32 devices in a mesh: dom: 8 (over z, x), rep: 4 (over y, core).
Axes of the slice: x: 2, y: 2, z: 4, core: 2. Of those that a mesh axis runs over, the one named last changes fastest.
Arguments:
- inputs: bfloat16 [4, 2048, 768], P('rep', 'dom'), may hold values from -6 to 6
- cotangent: bfloat16 [4, 2048, 576], P('rep', 'dom'), may hold values from -6 to 6
- conv_one: bfloat16 [2, 64, 128], replicated, may hold values from -1 to 1
- conv_two: bfloat16 [2, 64, 128], replicated, may hold values from -1 to 1
- mix_weight: bfloat16 [3, 64, 64], replicated, may hold values from -2 to 2
- send_rows: int32 [8, 8, 128], P('dom'), may hold values from 0 to 255, as said below
- counts: int32 [8, 8], P('dom'), may hold values from 0 to 128, as said below
- tile_cols: int32 [16, 12], P('dom'), may hold values from 0 to 9, as said below
- tile_vals: bfloat16 [16, 12, 128, 128], P('dom'), may hold values from -0.15625 to 0.15625
Outputs:
- output: bfloat16 [4, 2048, 576], P('rep', 'dom')
- grad_input: bfloat16 [4, 2048, 768], P('rep', 'dom')
- grad_conv_one: float32 [2, 64, 128], replicated
- grad_conv_two: float32 [2, 64, 128], replicated
- grad_mix: float32 [3, 64, 64], replicated
The draws below stay inside these ranges and needn't reach their ends.
Inputs may be any that keep to these rules, and one draw needn't show every extreme that they name: `send_rows`: rows of the source partition; entries in slots at or beyond counts are arbitrary rows. `counts`: zero for a partition with itself; every partition fills one block completely. `tile_cols`: entries below 2 are own row tiles, entry 2 + q is the block from partition q. Each partition's tiles name each of its own row tiles once and the block from the partition before it; which other blocks are named differs from partition to partition.
All inputs are finite; a program needn't handle non-finite values.
Results may differ from the reference program's by a relative error of at most 0.0075.
Values may be sent and summed in bfloat16 or wider, within the bound.
A program may use at most 128 MiB of HBM per device.

```python
import math
import jax
import jax.numpy as jnp
from jax import lax

C = 64
STEPS = 12
OUT_STEPS = 9
NODE_DEV = 256
BLOCK = 128
NT = 12
PARTS_SIZE = 8
NODES = 2048
WINDOWS = 4
RTILES = 2
CTILES = 10


def draw_send_rows(key, part):
    return jax.random.randint(key, (PARTS_SIZE, PARTS_SIZE, BLOCK), 0, NODE_DEV, dtype=jnp.int32)


def draw_counts(key, part):
    drawn_counts = jax.random.randint(key, (PARTS_SIZE, PARTS_SIZE), 0, BLOCK + 1, dtype=jnp.int32)
    source = jnp.arange(PARTS_SIZE)[:, None]
    target = jnp.arange(PARTS_SIZE)[None, :]
    drawn_counts = jnp.where(target == (source + 1) % PARTS_SIZE, BLOCK, drawn_counts)
    return jnp.where(target == source, 0, drawn_counts).astype(jnp.int32)


def partition_tiles(sub_key, index):
    slot_total = RTILES * NT
    rest_slots = slot_total - RTILES
    order_key, shuffle_key = jax.random.split(sub_key)
    offsets = (1 + jax.random.permutation(order_key, PARTS_SIZE - 1)).astype(jnp.int32)
    offsets = jnp.concatenate([jnp.zeros((1,), jnp.int32), offsets])
    block_order = ((index - 1 - offsets) % PARTS_SIZE).astype(jnp.int32)
    positions = (jnp.arange(rest_slots) % PARTS_SIZE).astype(jnp.int32)
    picked_blocks = jnp.take(block_order, positions)
    slots = jnp.concatenate([jnp.arange(RTILES).astype(jnp.int32), RTILES + picked_blocks])
    shuffle = jax.random.permutation(shuffle_key, slot_total).astype(jnp.int32)
    return jnp.take(slots, shuffle).astype(jnp.int32)


def draw_tile_cols(key, part):
    sub_keys = jax.random.split(jax.random.fold_in(key, 17), PARTS_SIZE)
    indices = jnp.arange(PARTS_SIZE).astype(jnp.int32)
    drawn = jax.vmap(partition_tiles)(sub_keys, indices)
    return drawn.reshape(PARTS_SIZE * RTILES, NT).astype(jnp.int32)


def steps_of(own_key, extent, cuts, least, high):
    def one(position, parts):
        heights = jax.random.uniform(jax.random.fold_in(jax.random.fold_in(own_key, 6), position), (parts,), jnp.float32, least / len(cuts), high / len(cuts))
        return jnp.repeat(jnp.exp(heights), extent[position] // parts).reshape((-1,) + (1,) * (len(extent) - position - 1))

    factor_of = one(*cuts[0])
    for cut in cuts[1:]:
        factor_of = factor_of * one(*cut)
    return factor_of


def normal_values(own_key, shape, deviation, reach, cuts=(), kind=jnp.bfloat16):
    result = jax.random.normal(own_key, shape, jnp.float32) * deviation
    if len(cuts) > 0:
        result = steps_of(own_key, shape, cuts, -0.22, 0.18) * result
    return jnp.clip(result, min=-reach, max=reach).astype(kind)


def setup_inputs(seed: int = 0) -> dict:
    key_list = jax.random.split(jax.random.key(seed), 10)
    return {
        "inputs": normal_values(key_list[0], (WINDOWS, NODES, STEPS * C), 1.0, 6.0, ((0, 4), (1, 8))),
        "cotangent": normal_values(key_list[1], (WINDOWS, NODES, OUT_STEPS * C), 1.0, 6.0, ((0, 4), (1, 8))),
        "conv_one": normal_values(key_list[2], (2, C, 2 * C), (C // 2) ** -0.5, 1.0),
        "conv_two": normal_values(key_list[3], (2, C, 2 * C), (C // 2) ** -0.5, 1.0),
        "mix_weight": normal_values(key_list[4], (3, C, C), (C // 8) ** -0.5, 2.0),
        "send_rows": draw_send_rows(jax.random.fold_in(key_list[9], 71), 0),
        "counts": draw_counts(jax.random.fold_in(key_list[9], 71), 0),
        "tile_cols": draw_tile_cols(jax.random.fold_in(key_list[9], 71), 0),
        "tile_vals": normal_values(key_list[8], (PARTS_SIZE * RTILES, NT, BLOCK, BLOCK), (NT * BLOCK) ** -0.5, 0.15625, ((0, 8),)),
    }


HIGHEST = lax.Precision.HIGHEST

def gated_conv(signal, weight, dilation):
    earlier_steps = signal[:, :-dilation]
    later_steps = signal[:, dilation:]
    preact = jnp.einsum('rsc,co->rso', earlier_steps, weight[0], precision=HIGHEST)
    preact = preact + jnp.einsum('rsc,co->rso', later_steps, weight[1], precision=HIGHEST)
    halfway = weight.shape[1]
    return jnp.tanh(preact[..., :halfway]) * jax.nn.sigmoid(preact[..., halfway:])

def temporal(signal, conv_one, conv_two):
    first = gated_conv(signal, conv_one, 1).astype(jnp.bfloat16)
    first = lax.optimization_barrier(first)
    return gated_conv(first.astype(jnp.float32), conv_two, 2)

def spread(extended, cols, vals):
    row_tiles, count_slots, tile_rows, _ = vals.shape
    blocks = extended.reshape(-1, tile_rows, extended.shape[1])
    summed = jnp.zeros((row_tiles, tile_rows, extended.shape[1]), jnp.float32)
    for slot_index in range(count_slots):
        picked = blocks[cols[:, slot_index]].astype(jnp.float32)
        summed = summed + jnp.einsum('rab,rbm->ram', vals[:, slot_index].astype(jnp.float32), picked, precision=HIGHEST)
    return summed.reshape(row_tiles * tile_rows, -1)

def spread_back(grads, cols, vals, col_tiles):
    row_tiles, count_slots, tile_rows, _ = vals.shape
    blocks = grads.reshape(row_tiles, tile_rows, grads.shape[1]).astype(jnp.float32)
    summed = jnp.zeros((col_tiles, tile_rows, grads.shape[1]), jnp.float32)
    for slot_index in range(count_slots):
        contribution = jnp.einsum('rab,ram->rbm', vals[:, slot_index].astype(jnp.float32), blocks, precision=HIGHEST)
        summed = summed + jax.ops.segment_sum(contribution, cols[:, slot_index], num_segments=col_tiles)
    return summed.reshape(col_tiles * tile_rows, -1)

def partition_rows(values, partitions):
    windows, nodes, feats = values.shape
    shaped = values.reshape(windows, partitions, nodes // partitions, feats).transpose(1, 2, 0, 3)
    return shaped.reshape(partitions, nodes // partitions, windows * feats)

def window_rows(values, windows):
    partitions, local_nodes, merged = values.shape
    shaped = values.reshape(partitions, local_nodes, windows, merged // windows).transpose(2, 0, 1, 3)
    return shaped.reshape(windows, partitions * local_nodes, merged // windows)

def reference(inputs, cotangent, conv_one, conv_two, mix_weight, send_rows, counts, tile_cols, tile_vals):
    windows, nodes, flat = inputs.shape
    channels = mix_weight.shape[1]
    history = flat // channels
    kept_steps = history - 3
    partitions = PARTS_SIZE
    local_nodes = nodes // partitions
    merged = windows * kept_steps * channels
    live_slots = jnp.arange(BLOCK)[None, None, :] < counts[:, :, None]
    cols = tile_cols.reshape(partitions, RTILES, NT)
    vals = tile_vals.reshape(partitions, RTILES, NT, BLOCK, BLOCK)
    every_part = jnp.arange(partitions).astype(jnp.int32)
    signal = inputs.reshape(windows * nodes, history, channels).astype(jnp.float32)
    hidden, pullback = jax.vjp(temporal, signal, conv_one.astype(jnp.float32), conv_two.astype(jnp.float32))
    node_hidden = partition_rows(hidden.astype(jnp.bfloat16).reshape(windows, nodes, kept_steps * channels), partitions)

    def hop(values):
        picked = jax.vmap(lambda table, index: table[index])(values, send_rows)
        sent = jnp.where(live_slots[..., None], picked, jnp.zeros((), values.dtype))

        def one_partition(index):
            halo = lax.dynamic_index_in_dim(sent, index, 1, keepdims=False).reshape(-1, merged)
            extended = jnp.concatenate([values[index], halo], axis=0)
            return spread(extended, cols[index], vals[index])
        return lax.map(one_partition, every_part)

    def hop_back(grads):

        def one_partition(index):
            return spread_back(grads[index], cols[index], vals[index], CTILES)
        ext_grads = lax.map(one_partition, every_part)
        local_part = ext_grads[:, :local_nodes]
        pieces = ext_grads[:, local_nodes:].reshape(partitions, partitions, BLOCK, merged).astype(jnp.bfloat16)

        def gather_to(index):
            piece = lax.dynamic_index_in_dim(pieces, index, 1, keepdims=False).astype(jnp.float32)
            piece = jnp.where(live_slots[index][..., None], piece, 0.0)
            return jax.ops.segment_sum(piece.reshape(-1, merged), send_rows[index].reshape(-1), num_segments=local_nodes)
        return local_part + lax.map(gather_to, every_part)
    first_hop = hop(node_hidden).astype(jnp.bfloat16)
    second_hop = hop(first_hop).astype(jnp.bfloat16)

    def channel_rows(values):
        return values.reshape(partitions, local_nodes, windows * kept_steps, channels).astype(jnp.float32)
    terms = (channel_rows(node_hidden), channel_rows(first_hop), channel_rows(second_hop))
    mix_full = mix_weight.astype(jnp.float32)
    mixed = jnp.einsum('pnkc,cd->pnkd', terms[0], mix_full[0], precision=HIGHEST)
    mixed = mixed + jnp.einsum('pnkc,cd->pnkd', terms[1], mix_full[1], precision=HIGHEST)
    mixed = mixed + jnp.einsum('pnkc,cd->pnkd', terms[2], mix_full[2], precision=HIGHEST)
    residual = channel_rows(partition_rows(inputs[:, :, 3 * channels:], partitions))
    output = window_rows((mixed + residual).astype(jnp.bfloat16).reshape(partitions, local_nodes, merged), windows)
    scaling = math.sqrt(windows * nodes * kept_steps)
    cot_rows = channel_rows(partition_rows(cotangent, partitions))
    grad_mix = jnp.stack([jnp.einsum('pnkc,pnkd->cd', term, cot_rows, precision=HIGHEST) for term in terms]) / scaling

    def through(index):
        return jnp.einsum('pnkd,cd->pnkc', cot_rows, mix_full[index], precision=HIGHEST).reshape(partitions, local_nodes, merged)
    grad_second = through(2).astype(jnp.bfloat16)
    grad_first = (through(1) + hop_back(grad_second)).astype(jnp.bfloat16)
    grad_hidden = through(0) + hop_back(grad_first)
    grad_rows = window_rows(grad_hidden, windows).reshape(windows * nodes, kept_steps, channels)
    grad_signal, grad_one, grad_two = pullback(grad_rows)
    padding = jnp.zeros((windows, nodes, 3 * channels), jnp.float32)
    grad_input = grad_signal.reshape(windows, nodes, flat) + jnp.concatenate([padding, cotangent.astype(jnp.float32)], axis=2)
    return (output, grad_input.astype(jnp.bfloat16), grad_one / scaling, grad_two / scaling, grad_mix)
```

```python
import functools
import math

import jax
import jax.numpy as jnp
from jax import lax
from jax.experimental import pallas as pl
from jax.experimental.pallas import tpu as pltpu
from jax.sharding import PartitionSpec as P

F32 = jnp.float32
BF16 = jnp.bfloat16
BLK = 128
VM = pl.BlockSpec(memory_space=pltpu.VMEM)
SM = pl.BlockSpec(memory_space=pltpu.SMEM)
LIMIT = pltpu.CompilerParams(vmem_limit_bytes=56 * 1024 * 1024)


def dot(a, b):
    return jnp.dot(a, b, preferred_element_type=F32)


def dot_t0(a, b):
    return lax.dot_general(a, b, (((0,), (0,)), ((), ())), preferred_element_type=F32)


def dot_t1(a, b):
    return lax.dot_general(a, b, (((1,), (1,)), ((), ())), preferred_element_type=F32)


def pair(k):
    return slice(k * 128, (k + 1) * 128)


def window2(k):
    return slice(k * 128, (k + 2) * 128)


def block_map(weight_ref, index, out_ref):
    c = weight_ref.shape[1]
    w = weight_ref[index]
    out_ref[...] = jnp.zeros(out_ref.shape, BF16)
    out_ref[0:c, 0:c] = w
    out_ref[c : 2 * c, c : 2 * c] = w


def band_blocks(dilation):
    if dilation == 1:
        return ((0, 1, 0), (0, 2, 1), (1, 2, 0), (1, 3, 1))
    return ((0, 0, 0), (0, 1, 1), (1, 2, 0), (1, 3, 1))


def band_map(conv_ref, dilation, out_ref):
    c = conv_ref.shape[1]
    out_ref[...] = jnp.zeros(out_ref.shape, BF16)
    for tap, i, o in band_blocks(dilation):
        w = conv_ref[tap]
        rows = slice(i * c, (i + 1) * c)
        out_ref[rows, o * c : (o + 1) * c] = w[:, :c]
        out_ref[rows, (o + 2) * c : (o + 3) * c] = w[:, c:]


def band_grad(total, dilation, out_ref):
    c = out_ref.shape[1]
    for tap in range(2):
        for half in range(2):
            acc = None
            for t, i, o in band_blocks(dilation):
                if t != tap:
                    continue
                col = (o + 2 * half) * c
                part = total[i * c : (i + 1) * c, col : col + c]
                acc = part if acc is None else acc + part
            out_ref[tap, :, half * c : (half + 1) * c] = acc


def activations(pre):
    filt = jnp.tanh(pre[:, :128])
    gates = 0.5 * jnp.tanh(0.5 * pre[:, 128:]) + 0.5
    return filt, gates


def earlier(ref, k):
    if k == 0:
        x = ref[:, 0:128]
        return jnp.concatenate([jnp.zeros_like(x), x], axis=1)
    return ref[:, window2(k - 1)]


def build_tiles(cols_ref, vals_ref, acc_ref, dense_ref):
    rtiles, slots = vals_ref.shape[0], vals_ref.shape[1]
    ctiles = dense_ref.shape[1] // BLK
    for r in range(rtiles):
        acc_ref[...] = jnp.zeros(acc_ref.shape, F32)
        for j in range(slots):
            c = cols_ref[r, j]
            acc_ref[c] = acc_ref[c] + vals_ref[r, j].astype(F32)
        for c in range(ctiles):
            dense_ref[r * BLK : (r + 1) * BLK, c * BLK : (c + 1) * BLK] = acc_ref[c].astype(BF16)


def build_picks(send_ref, counts_ref, picks_ref):
    parts = send_ref.shape[0]
    nodes = picks_ref.shape[0]
    lane = lax.broadcasted_iota(jnp.int32, (1, BLK), 1)
    rows = lax.broadcasted_iota(jnp.int32, (nodes, BLK), 0)
    for q in range(parts):
        wanted = jnp.where(lane < counts_ref[0, q], send_ref[q : q + 1, :], -1)
        hit = rows == wanted
        picks_ref[:, q * BLK : (q + 1) * BLK] = jnp.where(hit, 1.0, 0.0).astype(BF16)


def prepare_body(cot_ref, mix_ref, send_ref, counts_ref, cols_ref, vals_ref,
                 dense_ref, picks_ref, cot_out, base_ref, pieces_ref,
                 acc_ref, map_ref, g_ref):
    nodes = cot_ref.shape[1]
    parts = send_ref.shape[0]
    c = mix_ref.shape[1]
    build_tiles(cols_ref, vals_ref, acc_ref, dense_ref)
    build_picks(send_ref, counts_ref, picks_ref)
    wide = cot_ref[...].astype(F32).T
    wide = jnp.concatenate([jnp.zeros((nodes, c), F32), wide], axis=1).astype(BF16)
    cot_out[...] = wide
    pairs = cot_out.shape[1] // 128
    block_map(mix_ref, 2, map_ref)
    m = map_ref[...]
    for k in range(pairs):
        g_ref[:, pair(k)] = dot_t1(cot_out[:, pair(k)], m).astype(BF16)
    block_map(mix_ref, 1, map_ref)
    m = map_ref[...]
    g = g_ref[...]
    pack_rows(g, dense_ref, nodes, parts, pieces_ref)
    base_ref[...] = dot_t0(dense_ref[:, :nodes], g)
    for k in range(pairs):
        base_ref[:, pair(k)] += dot_t1(cot_out[:, pair(k)], m)


def pack_rows(values, table_ref, start, parts, out_ref):
    flipped = values.astype(F32).T.astype(BF16)
    for q in range(parts):
        table = table_ref[:, start + q * BLK : start + (q + 1) * BLK]
        out_ref[q] = dot(flipped, table).astype(BF16)


def from_blocks(total, table_ref, start, parts, arrived_ref):
    for q in range(parts):
        table = table_ref[:, start + q * BLK : start + (q + 1) * BLK]
        total = total + dot_t1(table, arrived_ref[q])
    return total


def forward_part(x_ref, conv1_ref, conv2_ref, first_ref, hidden_ref, band_ref):
    pairs = x_ref.shape[1] // 128
    band_map(conv1_ref, 1, band_ref)
    b = band_ref[...]
    for k in range(pairs):
        filt, gates = activations(dot(earlier(x_ref, k), b))
        first_ref[:, pair(k)] = (filt * gates).astype(BF16)
    band_map(conv2_ref, 2, band_ref)
    b = band_ref[...]
    for k in range(1, pairs):
        filt, gates = activations(dot(earlier(first_ref, k), b))
        hidden_ref[:, pair(k - 1)] = (filt * gates).astype(BF16)


def gate_grad(pre, up):
    filt, gates = activations(pre)
    d_filt = up * gates * (1.0 - filt * filt)
    d_gate = up * filt * gates * (1.0 - gates)
    return jnp.concatenate([d_filt, d_gate], axis=1).astype(BF16)


def backward_part(x_ref, first_ref, cot_ref, conv1_ref, conv2_ref, grad_ref, g1_ref, g2_ref,
                  band_ref, up_ref, mid_ref):
    pairs = x_ref.shape[1] // 128
    band_map(conv2_ref, 2, band_ref)
    b = band_ref[...]
    total = None
    carry = None
    for k in range(1, pairs):
        both = earlier(first_ref, k)
        d = gate_grad(dot(both, b), up_ref[:, pair(k - 1)])
        part = dot_t0(both, d)
        total = part if total is None else total + part
        back = dot_t1(d, b)
        low = back[:, :128] if carry is None else carry + back[:, :128]
        mid_ref[:, pair(k - 1)] = low.astype(BF16)
        carry = back[:, 128:]
    mid_ref[:, pair(pairs - 1)] = carry.astype(BF16)
    band_grad(total, 2, g2_ref)
    band_map(conv1_ref, 1, band_ref)
    b = band_ref[...]
    total = None
    carry = None
    for k in range(pairs):
        both = earlier(x_ref, k)
        d = gate_grad(dot(both, b), mid_ref[:, pair(k)].astype(F32))
        part = dot_t0(both, d)
        total = part if total is None else total + part
        back = dot_t1(d, b)
        if k > 0:
            low = carry + back[:, :128]
            if k > 1:
                low = low + cot_ref[:, pair(k - 2)].astype(F32)
            grad_ref[:, pair(k - 1)] = low.astype(BF16)
        carry = back[:, 128:]
    last = carry + cot_ref[:, pair(pairs - 2)].astype(F32)
    grad_ref[:, pair(pairs - 1)] = last.astype(BF16)
    band_grad(total, 1, g1_ref)


def mix_grad(term_ref, cot_ref, c):
    acc = None
    for k in range(cot_ref.shape[1] // 128):
        part = dot_t0(term_ref[:, pair(k)], cot_ref[:, pair(k)])
        acc = part if acc is None else acc + part
    return acc[:c, :c] + acc[c:, c:]


def early_part(hidden_ref, hop_ref, x_ref, cot_ref, mix_ref, gm_ref, map0, map1, wide_ref):
    c = mix_ref.shape[1]
    block_map(mix_ref, 0, map0)
    block_map(mix_ref, 1, map1)
    for k in range(cot_ref.shape[1] // 128):
        acc = x_ref[:, pair(k + 1)].astype(F32)
        acc = acc + dot(hidden_ref[:, pair(k)], map0[...])
        wide_ref[:, pair(k)] = acc + dot(hop_ref[:, pair(k)], map1[...])
    gm_ref[0] = mix_grad(hidden_ref, cot_ref, c)
    gm_ref[1] = mix_grad(hop_ref, cot_ref, c)


def main_body(parts, reps, scale,
              x_ref, cot_ref, conv1_ref, conv2_ref, mix_ref, dense_ref, picks_ref, base_ref,
              pieces_ref,
              out_ref, grad_ref, sum_ref,
              first_ref, hidden_ref, hop_ref, second_ref, up_ref, mid_ref, band_ref,
              map0, map1, map2, g1_ref, g2_ref, gm_ref,
              wide_ref, send1, send2, send3, recv0, recv1, recv2, recv3,
              pack_ref, got_ref, part_ref, reps_ref, sums_ref,
              ssem, rsem, asem, arsem, bsem, brsem):
    me = lax.axis_index("dom")
    mine = lax.axis_index("rep")
    nodes = x_ref.shape[0]
    c = mix_ref.shape[1]
    pairs = cot_ref.shape[1] // 128
    feats = cot_ref.shape[1]

    barrier = pltpu.get_barrier_semaphore()
    for o in range(1, parts):
        pl.semaphore_signal(barrier, inc=1, device_id={"dom": lax.rem(me + o, parts)},
                            device_id_type=pl.DeviceIdType.MESH)
    for o in range(1, reps):
        pl.semaphore_signal(barrier, inc=1, device_id={"rep": lax.rem(mine + o, reps)},
                            device_id_type=pl.DeviceIdType.MESH)
    pl.semaphore_wait(barrier, parts - 1 + reps - 1)

    def copies(level, src, dst):
        made = []
        for o in sorted(range(1, parts), key=lambda o: abs(2 * o - parts)):
            peer = lax.rem(me + o, parts)
            made.append(pltpu.make_async_remote_copy(
                src_ref=src.at[peer, pl.ds(c, feats - c)],
                dst_ref=dst.at[me, pl.ds(c, feats - c)],
                send_sem=ssem.at[level, o],
                recv_sem=rsem.at[level, o],
                device_id={"dom": peer},
                device_id_type=pl.DeviceIdType.MESH,
            ))
        for m in made:
            m.start()
        return made

    def arrive(made):
        for m in made:
            m.wait_recv()

    round0 = copies(0, pieces_ref, recv0)
    for buf in (recv0, recv1, recv2, recv3):
        buf[:, 0:c, :] = jnp.zeros((parts, c, BLK), BF16)
        buf[me] = jnp.zeros((feats, BLK), BF16)

    forward_part(x_ref, conv1_ref, conv2_ref, first_ref, hidden_ref, band_ref)
    pack_rows(hidden_ref[...], picks_ref, 0, parts, send1)
    round1 = copies(1, send1, recv1)

    arrive(round0)
    g = from_blocks(base_ref[...], picks_ref, 0, parts, recv0).astype(BF16)
    pack_rows(g, dense_ref, nodes, parts, send2)
    round2 = copies(2, send2, recv2)
    up_ref[...] = dot_t0(dense_ref[:, :nodes], g)
    block_map(mix_ref, 0, map0)
    for k in range(pairs):
        up_ref[:, pair(k)] += dot_t1(cot_ref[:, pair(k)], map0[...])

    own = dot(dense_ref[:, :nodes], hidden_ref[...])
    arrive(round1)
    hop_ref[...] = from_blocks(own, dense_ref, nodes, parts, recv1).astype(BF16)
    pack_rows(hop_ref[...], picks_ref, 0, parts, send3)
    round3 = copies(3, send3, recv3)

    arrive(round2)
    up_ref[...] = from_blocks(up_ref[...], picks_ref, 0, parts, recv2)
    backward_part(x_ref, first_ref, cot_ref, conv1_ref, conv2_ref, grad_ref, g1_ref, g2_ref,
                  band_ref, up_ref, mid_ref)

    early_part(hidden_ref, hop_ref, x_ref, cot_ref, mix_ref, gm_ref, map0, map1, wide_ref)
    block_map(mix_ref, 2, map2)
    own = dot(dense_ref[:, :nodes], hop_ref[...])
    arrive(round3)
    second_ref[...] = from_blocks(own, dense_ref, nodes, parts, recv3).astype(BF16)
    gm_ref[2] = mix_grad(second_ref, cot_ref, c)

    per = pack_ref.shape[1]
    flat = pack_ref
    flat[...] = jnp.zeros(flat.shape, F32)

    def put(first_row, value):
        rows = value.shape[0]
        done = 0
        while done < rows:
            slot, at = divmod(first_row + done, per)
            step = min(per - at, rows - done)
            flat[slot, at : at + step, :] = value[done : done + step]
            done += step

    put(0, g1_ref[0])
    put(c, g1_ref[1])
    put(2 * c, g2_ref[0])
    put(3 * c, g2_ref[1])
    put(4 * c, jnp.concatenate([gm_ref[0], gm_ref[1]], axis=1))
    put(5 * c, jnp.concatenate([gm_ref[2], jnp.zeros((c, c), F32)], axis=1))

    scatter = []
    for o in range(1, parts):
        peer = lax.rem(me + o, parts)
        scatter.append(pltpu.make_async_remote_copy(
            src_ref=pack_ref.at[peer], dst_ref=got_ref.at[me],
            send_sem=asem.at[0, o], recv_sem=arsem.at[0, o],
            device_id={"dom": peer}, device_id_type=pl.DeviceIdType.MESH))
    for m in scatter:
        m.start()
    for k in range(pairs):
        wide_ref[:, pair(k)] += dot(second_ref[:, pair(k)], map2[...])
    out_ref[...] = wide_ref[...].T[c:].astype(BF16)
    got_ref[me] = pack_ref[me]
    arrive(scatter)
    total = got_ref[0]
    for q in range(1, parts):
        total = total + got_ref[q]
    part_ref[...] = total
    around = []
    for o in range(1, reps):
        peer = lax.rem(mine + o, reps)
        around.append(pltpu.make_async_remote_copy(
            src_ref=part_ref, dst_ref=reps_ref.at[mine],
            send_sem=bsem.at[o], recv_sem=brsem.at[o],
            device_id={"rep": peer}, device_id_type=pl.DeviceIdType.MESH))
    for m in around:
        m.start()
    reps_ref[mine] = total
    arrive(around)
    total = reps_ref[0]
    for q in range(1, reps):
        total = total + reps_ref[q]
    for m in around:
        m.wait_send()
    part_ref[...] = total * (1.0 / scale)
    final = []
    for o in range(1, parts):
        peer = lax.rem(me + o, parts)
        final.append(pltpu.make_async_remote_copy(
            src_ref=part_ref, dst_ref=sums_ref.at[me],
            send_sem=asem.at[1, o], recv_sem=arsem.at[1, o],
            device_id={"dom": peer}, device_id_type=pl.DeviceIdType.MESH))
    for m in final:
        m.start()
    sums_ref[me] = part_ref[...]
    arrive(final)

    sum_ref[...] = sums_ref[...]
    for m in round0 + round1 + round2 + round3 + scatter + final:
        m.wait_send()


def shards(inputs, cotangent, conv_one, conv_two, mix_weight, send_rows, counts, tile_cols,
           tile_vals):
    windows, nodes, flat = inputs.shape
    channels = mix_weight.shape[1]
    parts = lax.axis_size("dom")
    reps = lax.axis_size("rep")
    kept = flat // channels - 3
    wide = flat - 2 * channels
    halo = parts * BLK
    blocks = (parts, wide, BLK)
    prepared = [((nodes, nodes + halo), BF16), ((nodes, halo), BF16), ((nodes, wide), BF16),
                ((nodes, wide), F32), (blocks, BF16)]
    dense, picks, cot_wide, base, pieces = pl.pallas_call(
        prepare_body,
        out_shape=[jax.ShapeDtypeStruct(s, d) for s, d in prepared],
        in_specs=[VM, VM, VM, SM, SM, VM],
        out_specs=[VM] * 5,
        scratch_shapes=[pltpu.VMEM((parts + nodes // BLK, BLK, BLK), F32),
                        pltpu.VMEM((128, 128), BF16), pltpu.VMEM((nodes, wide), BF16)],
        compiler_params=LIMIT,
        name="prepare",
    )(cotangent[0].T, mix_weight, send_rows[0], counts, tile_cols, tile_vals)
    scaling = math.sqrt(float(windows * reps * nodes * parts * kept))
    unit = 8 * parts
    per = -(-6 * channels // unit) * unit // parts
    results = [((kept * channels, nodes), BF16), ((nodes, flat), BF16), ((parts, per, BLK), F32)]
    scratch = [((nodes, flat), BF16), ((nodes, wide), BF16), ((nodes, wide), BF16),
               ((nodes, wide), BF16), ((nodes, wide), F32), ((nodes, flat), BF16),
               ((256, 256), BF16), ((128, 128), BF16), ((128, 128), BF16), ((128, 128), BF16),
               (conv_one.shape, F32), (conv_two.shape, F32), (mix_weight.shape, F32)]
    scratch += [((nodes, wide), F32)] + [(blocks, BF16)] * 7
    scratch += [((parts, per, BLK), F32), ((parts, per, BLK), F32), ((per, BLK), F32),
                ((reps, per, BLK), F32), ((parts, per, BLK), F32)]
    dma = pltpu.SemaphoreType.DMA
    output, grad_input, packed = pl.pallas_call(
        functools.partial(main_body, parts, reps, scaling),
        out_shape=[jax.ShapeDtypeStruct(s, d) for s, d in results],
        in_specs=[VM] * 9,
        out_specs=[VM] * 3,
        scratch_shapes=[pltpu.VMEM(s, d) for s, d in scratch]
        + [dma((4, parts)), dma((4, parts)), dma((2, parts)), dma((2, parts)), dma((reps,)),
           dma((reps,))],
        compiler_params=pltpu.CompilerParams(
            vmem_limit_bytes=60 * 1024 * 1024, collective_id=0, has_side_effects=True),
        name="layer",
    )(inputs[0], cot_wide, conv_one, conv_two, mix_weight, dense, picks, base, pieces)
    c = channels
    rows = packed.reshape(parts * per, BLK)
    gm = jnp.stack([rows[4 * c : 5 * c, :c], rows[4 * c : 5 * c, c:], rows[5 * c : 6 * c, :c]])
    return (
        output.T[None],
        grad_input[None],
        rows[: 2 * c].reshape(conv_one.shape),
        rows[2 * c : 4 * c].reshape(conv_two.shape),
        gm,
    )


def place_tiles(cols_ref, vals_ref, acc_ref, dense_ref, me, parts):
    rtiles, slots = vals_ref.shape[0], vals_ref.shape[1]
    ctiles = dense_ref.shape[1] // BLK
    for r in range(rtiles):
        acc_ref[...] = jnp.zeros(acc_ref.shape, F32)
        for j in range(slots):
            col = cols_ref[r, j]
            off = lax.rem(me - (col - rtiles) + 2 * parts, parts)
            c = jnp.where(col < rtiles, col, jnp.where(off == 0, ctiles, rtiles - 1 + off))
            acc_ref[c] = acc_ref[c] + vals_ref[r, j].astype(F32)
        for c in range(ctiles):
            dense_ref[r * BLK : (r + 1) * BLK, c * BLK : (c + 1) * BLK] = acc_ref[c].astype(BF16)


def setup_body(parts, send_ref, counts_ref, cols_ref, vals_ref, dense_ref, wanted_ref, acc_ref):
    me = lax.axis_index("dom")
    place_tiles(cols_ref, vals_ref, acc_ref, dense_ref, me, parts)
    lane = lax.broadcasted_iota(jnp.int32, (1, BLK), 1)
    for o in range(parts):
        t = lax.rem(me + o, parts)
        wanted_ref[o : o + 1, :] = jnp.where(
            lane < counts_ref[0, t], send_ref[pl.ds(t, 1), :], -1)


def chunk(first, size):
    return pl.ds(pl.multiple_of(first, size), size)


def steps_body(parts, reps, scale,
               x_ref, cot_ref, conv1_ref, conv2_ref, mix_ref, dense_ref, wanted_ref,
               out_ref, grad_ref, sum_ref,
               xt_ref, first_ref, hid_ref, d1_ref, d2_ref, mid_ref,
               band1, band1t, band2, band2t, maps, mapst,
               adj_ref, lists_ref, picks_ref,
               cf_ref, hf_ref, f1_ref, f2_ref, ga_ref, gb_ref, own_ref, part_t, ext_ref,
               gh_ref, mx_ref, ghs_ref, mxs_ref,
               g1_ref, g2_ref, gm_ref, pack_ref, got_ref, part_ref, reps_ref, sums_ref,
               lsend, lrecv, fsend, frecv, esend, erecv, tsend, trecv,
               asem, arsem, bsem, brsem):
    me = lax.axis_index("dom")
    mine = lax.axis_index("rep")
    nodes = x_ref.shape[0]
    c = mix_ref.shape[1]
    pairs = x_ref.shape[1] // 128
    rows = nodes // reps
    mesh_ids = pl.DeviceIdType.MESH
    holder = lax.rem(parts // 2 - reps // 2 + mine + parts, parts)
    extra = parts * c
    zs = parts // 2
    z, xx = me // 2, lax.rem(me, 2)
    yy, core = mine // 2, lax.rem(mine, 2)

    barrier = pltpu.get_barrier_semaphore()
    for o in range(1, parts):
        pl.semaphore_signal(barrier, inc=1, device_id={"dom": lax.rem(me + o, parts)},
                            device_id_type=mesh_ids)
    for o in range(1, reps):
        pl.semaphore_signal(barrier, inc=1, device_id={"rep": lax.rem(mine + o, reps)},
                            device_id_type=mesh_ids)
    pl.semaphore_wait(barrier, parts - 1 + reps - 1)

    def remote(src, dst, ssem, rsem, **where):
        return pltpu.make_async_remote_copy(
            src_ref=src, dst_ref=dst, send_sem=ssem, recv_sem=rsem,
            device_id=where, device_id_type=mesh_ids)

    order = sorted(range(1, parts), key=lambda o: abs(2 * o - parts))

    def piece(p, r):
        return adj_ref.at[p, chunk(r * rows, rows)]

    def source_z(t, way):
        return z - t if way == 0 else z + t

    def valid(t, way):
        if t == 0:
            return z >= 0
        return z >= t if way == 0 else z + t < zs

    def slot(t, way):
        return 0 if t == 0 else 2 * t - 1 + way

    def base(t, way):
        return source_z(t, way) * 2 + xx

    def cross(t, way):
        return source_z(t, way) * 2 + 1 - xx

    yrep = (1 - yy) * 2 + core
    crep = yy * 2 + 1 - core
    cyrep = (1 - yy) * 2 + 1 - core

    def along(t, way, out_way):
        src = dense_ref.at[chunk(mine * rows, rows)] if t == 0 else piece(base(t, way), mine)
        to = (z + 1 if out_way == 0 else z - 1) * 2 + xx
        return remote(src, piece(base(t, way), mine), tsend.at[out_way, slot(t, way)],
                      trecv.at[0, slot(t + 1, out_way)], dom=to)

    def across(t, way):
        src = dense_ref.at[chunk(mine * rows, rows)] if t == 0 else piece(base(t, way), mine)
        return remote(src, piece(base(t, way), mine), tsend.at[2, slot(t, way)],
                      trecv.at[2, slot(t, way)], dom=z * 2 + 1 - xx)

    def hand(kind, p, r, t, way, to):
        return remote(piece(p, r), piece(p, r), tsend.at[kind, slot(t, way)],
                      trecv.at[kind, slot(t, way)], rep=to)

    def arrived(kind, p, r, t, way, **where):
        remote(piece(p, r), piece(p, r), tsend.at[kind, slot(t, way)],
               trecv.at[kind, slot(t, way)], **where).wait_recv()

    def ways(t):
        return (0,) if t == 0 else (0, 1)

    def lane_sends(t, way):
        made = []
        outs = (0, 1) if t == 0 else (way,)
        for w in outs:
            made.append((z + 1 < zs if w == 0 else z >= 1, along(t, way, w)))
        made.append((None, across(t, way)))
        return made

    def base_sends(t, way):
        return [] if t == 0 else [(None, hand(3, base(t, way), mine, t, way, yrep)),
                                  (None, hand(4, base(t, way), mine, t, way, crep))]

    def cross_sends(t, way):
        return [(None, hand(5, cross(t, way), mine, t, way, yrep)),
                (None, hand(6, cross(t, way), mine, t, way, crep))]

    def ybase_sends(t, way):
        return [] if t == 0 else [(None, hand(7, base(t, way), yrep, t, way, crep))]

    def ycross_sends(t, way):
        return [(None, hand(8, cross(t, way), yrep, t, way, crep))]

    def go(sends, wait=False):
        for cond, copy in sends:
            act = copy.wait_send if wait else copy.start
            if cond is None:
                act()
            else:
                pl.when(cond)(act)

    def on_base(t, way):
        @pl.when(valid(t, way))
        def _():
            arrived(0, base(t, way), mine, t, way, rep=crep)
            go(lane_sends(t, way) + base_sends(t, way))

    def on_cross(t, way):
        @pl.when(valid(t, way))
        def _():
            arrived(2, cross(t, way), mine, t, way, rep=crep)
            go(cross_sends(t, way))

    def on_ybase(t, way):
        @pl.when(valid(t, way))
        def _():
            arrived(3, base(t, way), yrep, t, way, rep=crep)
            go(ybase_sends(t, way))

    def on_ycross(t, way):
        @pl.when(valid(t, way))
        def _():
            arrived(5, cross(t, way), yrep, t, way, rep=crep)
            go(ycross_sends(t, way))

    relay = []
    for s in range(1, zs + 2):
        for handler, t, least in ((on_base, s, 1), (on_cross, s - 1, 0), (on_ybase, s - 1, 1),
                                  (on_ycross, s - 2, 0)):
            if least <= t < zs:
                for w in ways(t):
                    relay.append(functools.partial(handler, t, w))
    relay.reverse()

    def step_relay(count=1):
        for _ in range(count):
            if relay:
                relay.pop()()

    def scatter_field(level, src, first, dst):
        made = []
        for o in order:
            peer = lax.rem(me + o, parts)
            made.append(remote(src.at[chunk(first + peer * c, c)], dst.at[me, pl.ds(0, c)],
                               fsend.at[level, o], frecv.at[level, o], dom=peer))
        for m in made:
            m.start()
        off = lax.rem(holder - me + parts, parts)
        last = remote(src.at[pl.ds(first + extra, c)], dst.at[me, pl.ds(c, c)],
                      esend.at[level, 0], erecv.at[level, off], dom=holder)
        pl.when(me != holder)(last.start)
        dst[me, 0:c, :] = src[chunk(first + me * c, c), :]

        @pl.when(me == holder)
        def _():
            dst[me, c : 2 * c, :] = src[first + extra : first + extra + c, :]

        @pl.when(me != holder)
        def _():
            dst[:, c : 2 * c, :] = jnp.zeros((parts, c, nodes), BF16)
        return made, last

    def field_arrives(level, made, src, dst):
        for m in made:
            m.wait_recv()

        @pl.when(me == holder)
        def _():
            for o in range(1, parts):
                q = lax.rem(me - o + parts, parts)
                remote(dst.at[q, pl.ds(c, c)], dst.at[q, pl.ds(c, c)], esend.at[level, 0],
                       erecv.at[level, o], dom=q).wait_recv()

    def home_copies(level, o, src, first, dst):
        q = lax.rem(me + o, parts)
        one = remote(src.at[q, pl.ds(0, c)], dst.at[chunk(first + me * c, c)],
                     fsend.at[level, o], frecv.at[level, o], dom=q)
        two = remote(src.at[q, pl.ds(c, c)], dst.at[pl.ds(first + extra, c)],
                     esend.at[level, o], erecv.at[level, 0], dom=q)
        return one, two

    def go_home(level, o, src, first, dst):
        if o:
            one, two = home_copies(level, o, src, first, dst)
            one.start()
            pl.when(me == holder)(two.start)
            return
        dst[chunk(first + me * c, c), :] = src[me, 0:c, :]

        @pl.when(me == holder)
        def _():
            dst[first + extra : first + extra + c, :] = src[me, c : 2 * c, :]

    def home_arrives(level, src, first, dst):
        for o in range(1, parts):
            home_copies(level, o, src, first, dst)[0].wait_recv()
        pl.when(me != holder)(home_copies(level, 1, src, first, dst)[1].wait_recv)

    def home_sent(level, src, first, dst):
        for o in range(1, parts):
            one, two = home_copies(level, o, src, first, dst)
            one.wait_send()
            pl.when(me == holder)(two.wait_send)

    go(lane_sends(0, 0))
    cot_round = scatter_field(0, cot_ref, 0, cf_ref)
    lists = []
    for o in order:
        peer = lax.rem(me + o, parts)
        lists.append(remote(wanted_ref, lists_ref.at[me], lsend.at[o], lrecv.at[o], dom=peer))
    for m in lists:
        m.start()
    lists_ref[me] = wanted_ref[...]
    adj_ref[me] = dense_ref[...]

    for k in range(pairs):
        xt_ref[pair(k), :] = x_ref[:, pair(k)].astype(F32).T.astype(BF16)
    for conv, dil, nat, tra in ((conv1_ref, 1, band1, band1t), (conv2_ref, 2, band2, band2t)):
        band_map(conv, dil, nat)
        tra[...] = nat[...].astype(F32).T.astype(BF16)

    def earlier_t(ref, k):
        if k == 0:
            v = ref[0:128, :]
            return jnp.concatenate([jnp.zeros_like(v), v], axis=0)
        return ref[window2(k - 1), :]

    def gated(pre, d_ref, k):
        filt = jnp.tanh(pre[:128])
        gates = 0.5 * jnp.tanh(0.5 * pre[128:]) + 0.5
        d_ref[k, 0:128, :] = gates * (1.0 - filt * filt)
        d_ref[k, 128:256, :] = filt * gates * (1.0 - gates)
        return (filt * gates).astype(BF16)

    for k in range(pairs):
        first_ref[pair(k), :] = gated(dot(band1t[...], earlier_t(xt_ref, k)), d1_ref, k)
        if k % 2:
            step_relay()
    for k in range(1, pairs):
        hid_ref[pair(k - 1), :] = gated(dot(band2t[...], earlier_t(first_ref, k)), d2_ref, k)
        step_relay()
    hid_round = scatter_field(1, hid_ref, c, hf_ref)
    step_relay()

    for i in range(3):
        block_map(mix_ref, i, maps.at[i])
        mapst[i] = maps[i].astype(F32).T.astype(BF16)
    gh_ref[0:c, :] = jnp.zeros((c, nodes), BF16)

    for m in lists:
        m.wait_recv()
    node = lax.broadcasted_iota(jnp.int32, (nodes, BLK), 0)
    for q in range(parts):
        for o in range(1, parts):
            hit = node == lists_ref[q, o : o + 1, :]
            picks_ref[q, :, (o - 1) * BLK : o * BLK] = jnp.where(hit, 1.0, 0.0).astype(BF16)
        step_relay(2)

    field_arrives(0, cot_round[0], cot_ref, cf_ref)
    for q in range(parts):
        ga_ref[q] = dot(maps[2], cf_ref[q]).astype(BF16)
    step_relay(len(relay))
    for t in range(zs):
        for w in ways(t):
            @pl.when(valid(t, w))
            def _():
                if t:
                    arrived(4, base(t, w), crep, t, w, rep=crep)
                    arrived(7, base(t, w), cyrep, t, w, rep=crep)
                arrived(6, cross(t, w), crep, t, w, rep=crep)
                arrived(8, cross(t, w), cyrep, t, w, rep=crep)

    def back_pieces(g_ref):
        for p in range(parts):
            t = dot(g_ref[p], adj_ref[p])
            own_ref[p] = t[:, :nodes]
            for o in range(1, parts):
                at = nodes + (o - 1) * BLK
                part_t[(p - o) % parts, :, (o - 1) * BLK : o * BLK] = t[:, at : at + BLK].astype(BF16)

    def back_owner(q, weight):
        total = own_ref[q] + dot_t1(part_t[q], picks_ref[q])
        return (total + dot(weight, cf_ref[q])).astype(BF16)

    back_pieces(ga_ref)
    for q in range(parts):
        gb_ref[q] = back_owner(q, maps[1])
    back_pieces(gb_ref)
    for o in order + [0]:
        q = lax.rem(me + o, parts)
        ghs_ref[q] = back_owner(q, maps[0])
        go_home(2, o, ghs_ref, c, gh_ref)

    field_arrives(1, hid_round[0], hid_ref, hf_ref)

    def extend(f_ref):
        for q in range(parts):
            ext_ref[q, :, 0:nodes] = f_ref[q]
            halo = dot(f_ref[q], picks_ref[q]).astype(BF16)
            for o in range(1, parts):
                at = nodes + (o - 1) * BLK
                ext_ref[(q + o) % parts, :, at : at + BLK] = halo[:, (o - 1) * BLK : o * BLK]

    extend(hf_ref)
    for p in range(parts):
        f1_ref[p] = dot_t1(ext_ref[p], adj_ref[p]).astype(BF16)
    extend(f1_ref)
    for o in order + [0]:
        q = lax.rem(me + o, parts)
        second = dot_t1(ext_ref[q], adj_ref[q]).astype(BF16)
        f2_ref[q] = second
        mixed = dot(mapst[0], hf_ref[q]) + dot(mapst[1], f1_ref[q]) + dot(mapst[2], second)
        mxs_ref[q] = mixed.astype(BF16)
        go_home(3, o, mxs_ref, 0, mx_ref)
    for i, f_ref in enumerate((hf_ref, f1_ref, f2_ref)):
        acc = None
        for q in range(parts):
            part = dot_t1(f_ref[q], cf_ref[q])
            acc = part if acc is None else acc + part
        gm_ref[i] = acc[:c, :c] + acc[c:, c:]

    home_arrives(2, ghs_ref, c, gh_ref)

    def conv_back(sig_ref, d_ref, up_of, band, low_of, first_pair, dilation, out):
        total, carry = None, None
        b = band[...]
        for k in range(first_pair, pairs):
            up = up_of(k)
            both = earlier_t(sig_ref, k)
            d = jnp.concatenate([up * d_ref[k, 0:128, :], up * d_ref[k, 128:256, :]], axis=0)
            d = d.astype(BF16)
            part = dot_t1(both, d)
            total = part if total is None else total + part
            back = dot(b, d)
            if k > 0:
                low_of(k - 1, back[:128] if carry is None else carry + back[:128])
            carry = back[128:]
        low_of(pairs - 1, carry)
        band_grad(total, dilation, out)

    def set_mid(k, low):
        mid_ref[pair(k), :] = low.astype(BF16)

    def set_grad(k, low):
        if k == 1:
            low = low + jnp.concatenate([jnp.zeros((c, nodes), F32), cot_ref[0:c, :].astype(F32)], axis=0)
        elif k > 1:
            low = low + cot_ref[(2 * k - 3) * c : (2 * k - 1) * c, :].astype(F32)
        grad_ref[:, pair(k)] = low.T.astype(BF16)

    conv_back(first_ref, d2_ref, lambda k: gh_ref[pair(k - 1), :].astype(F32), band2, set_mid, 1, 2, g2_ref)
    conv_back(xt_ref, d1_ref, lambda k: mid_ref[pair(k), :].astype(F32), band1, set_grad, 0, 1, g1_ref)

    per = pack_ref.shape[1]
    flat = pack_ref
    flat[...] = jnp.zeros(flat.shape, F32)

    def put(first_row, value):
        count = value.shape[0]
        done = 0
        while done < count:
            place, at = divmod(first_row + done, per)
            step = min(per - at, count - done)
            flat[place, at : at + step, :] = value[done : done + step]
            done += step

    put(0, g1_ref[0])
    put(c, g1_ref[1])
    put(2 * c, g2_ref[0])
    put(3 * c, g2_ref[1])
    put(4 * c, jnp.concatenate([gm_ref[0], gm_ref[1]], axis=1))
    put(5 * c, jnp.concatenate([gm_ref[2], jnp.zeros((c, c), F32)], axis=1))

    scatter = []
    for o in order:
        peer = lax.rem(me + o, parts)
        scatter.append(remote(pack_ref.at[peer], got_ref.at[me], asem.at[0, o], arsem.at[0, o], dom=peer))
    for m in scatter:
        m.start()
    home_arrives(3, mxs_ref, 0, mx_ref)
    kept = out_ref.shape[0]
    out_ref[...] = (mx_ref[...].astype(F32) + xt_ref[pairs * 128 - kept :, :].astype(F32)).astype(BF16)
    got_ref[me] = pack_ref[me]
    for m in scatter:
        m.wait_recv()
    total = got_ref[0]
    for q in range(1, parts):
        total = total + got_ref[q]
    part_ref[...] = total
    around = []
    for o in range(1, reps):
        peer = lax.rem(mine + o, reps)
        around.append(remote(part_ref, reps_ref.at[mine], bsem.at[o], brsem.at[o], rep=peer))
    for m in around:
        m.start()
    reps_ref[mine] = total
    for m in around:
        m.wait_recv()
    total = reps_ref[0]
    for q in range(1, reps):
        total = total + reps_ref[q]
    for m in around:
        m.wait_send()
    part_ref[...] = total * (1.0 / scale)
    final = []
    for o in order:
        peer = lax.rem(me + o, parts)
        final.append(remote(part_ref, sums_ref.at[me], asem.at[1, o], arsem.at[1, o], dom=peer))
    for m in final:
        m.start()
    sums_ref[me] = part_ref[...]

    for m in cot_round[0] + hid_round[0] + lists + scatter:
        m.wait_send()
    pl.when(me != holder)(cot_round[1].wait_send)
    pl.when(me != holder)(hid_round[1].wait_send)
    home_sent(2, ghs_ref, c, gh_ref)
    home_sent(3, mxs_ref, 0, mx_ref)
    for t in range(zs):
        for w in ways(t):
            @pl.when(valid(t, w))
            def _():
                go(lane_sends(t, w) + base_sends(t, w) + cross_sends(t, w) + ybase_sends(t, w)
                   + ycross_sends(t, w), wait=True)
    for m in final:
        m.wait_recv()
    sum_ref[...] = sums_ref[...]
    for m in final:
        m.wait_send()


def step_shards(inputs, cotangent, conv_one, conv_two, mix_weight, send_rows, counts, tile_cols,
                tile_vals):
    windows, nodes, flat = inputs.shape
    channels = mix_weight.shape[1]
    parts = lax.axis_size("dom")
    reps = lax.axis_size("rep")
    kept = flat // channels - 3
    c = channels
    pairs = flat // 128
    halo = (parts - 1) * BLK
    ext = nodes + halo
    dense, wanted = pl.pallas_call(
        functools.partial(setup_body, parts),
        out_shape=[jax.ShapeDtypeStruct((nodes, ext), BF16),
                   jax.ShapeDtypeStruct((parts, BLK), jnp.int32)],
        in_specs=[VM, SM, SM, VM],
        out_specs=[VM] * 2,
        scratch_shapes=[pltpu.VMEM((ext // BLK + 1, BLK, BLK), F32)],
        compiler_params=LIMIT,
        name="setup",
    )(send_rows[0], counts, tile_cols, tile_vals)
    scaling = math.sqrt(float(windows * reps * nodes * parts * kept))
    unit = 8 * parts
    per = -(-6 * channels // unit) * unit // parts
    results = [((kept * c, nodes), BF16), ((nodes, flat), BF16), ((parts, per, BLK), F32)]
    field = (parts, 2 * c, nodes)
    wide = flat - 2 * c
    scratch = [((flat, nodes), BF16), ((flat, nodes), BF16), ((wide, nodes), BF16),
               ((pairs, 256, nodes), F32), ((pairs, 256, nodes), F32), ((flat, nodes), BF16)]
    scratch += [((256, 256), BF16)] * 4 + [((3, 128, 128), BF16)] * 2
    scratch += [((parts, nodes, ext), BF16), ((parts, parts, BLK), jnp.int32),
                ((parts, nodes, halo), BF16)]
    scratch += [(field, BF16)] * 6 + [(field, F32), ((parts, 2 * c, halo), BF16),
                                      ((parts, 2 * c, ext), BF16)]
    scratch += [((wide, nodes), BF16), ((kept * c, nodes), BF16), (field, BF16), (field, BF16)]
    scratch += [(conv_one.shape, F32), (conv_two.shape, F32), (mix_weight.shape, F32)]
    scratch += [((parts, per, BLK), F32), ((parts, per, BLK), F32), ((per, BLK), F32),
                ((reps, per, BLK), F32), ((parts, per, BLK), F32)]
    dma = pltpu.SemaphoreType.DMA
    sems = [(parts,), (parts,), (4, parts), (4, parts), (4, parts), (4, parts),
            (9, parts), (9, parts), (2, parts), (2, parts), (reps,), (reps,)]
    output, grad_input, packed = pl.pallas_call(
        functools.partial(steps_body, parts, reps, scaling),
        out_shape=[jax.ShapeDtypeStruct(s, d) for s, d in results],
        in_specs=[VM] * 7,
        out_specs=[VM] * 3,
        scratch_shapes=[pltpu.VMEM(s, d) for s, d in scratch] + [dma(s) for s in sems],
        compiler_params=pltpu.CompilerParams(
            vmem_limit_bytes=60 * 1024 * 1024, collective_id=1, has_side_effects=True),
        name="steps",
    )(inputs[0], cotangent[0].T, conv_one, conv_two, mix_weight, dense, wanted)
    table = packed.reshape(parts * per, BLK)
    gm = jnp.stack([table[4 * c : 5 * c, :c], table[4 * c : 5 * c, c:], table[5 * c : 6 * c, :c]])
    return (
        output.T[None],
        grad_input[None],
        table[: 2 * c].reshape(conv_one.shape),
        table[2 * c : 4 * c].reshape(conv_two.shape),
        gm,
    )


def solution(mesh):
    placed = (
        P("rep", "dom", None),
        P("rep", "dom", None),
        P(),
        P(),
        P(),
        P("dom", None, None),
        P("dom", None),
        P("dom", None),
        P("dom", None, None, None),
    )
    parts, reps = mesh.shape["dom"], mesh.shape["rep"]

    def layer(*args):
        kept = args[0].shape[2] // args[4].shape[1] - 3
        by_step = parts % 2 == 0 and reps == 4 and parts == kept - 1
        return step_shards(*args) if by_step else shards(*args)

    return jax.shard_map(
        layer,
        mesh=mesh,
        in_specs=placed,
        out_specs=(P("rep", "dom", None), P("rep", "dom", None), P(), P(), P()),
        check_vma=False,
    )
```

```python
import functools
import math

import jax
import jax.numpy as jnp
from jax import lax
from jax.experimental import pallas as pl
from jax.experimental.pallas import tpu as pltpu
from jax.sharding import PartitionSpec as P

F32 = jnp.float32
BF16 = jnp.bfloat16
BLK = 128
VM = pl.BlockSpec(memory_space=pltpu.VMEM)
SM = pl.BlockSpec(memory_space=pltpu.SMEM)
LIMIT = pltpu.CompilerParams(vmem_limit_bytes=56 * 1024 * 1024)


def dot(a, b):
    return jnp.dot(a, b, preferred_element_type=F32)


def dot_t0(a, b):
    return lax.dot_general(a, b, (((0,), (0,)), ((), ())), preferred_element_type=F32)


def dot_t1(a, b):
    return lax.dot_general(a, b, (((1,), (1,)), ((), ())), preferred_element_type=F32)


def pair(k):
    return slice(k * 128, (k + 1) * 128)


def window2(k):
    return slice(k * 128, (k + 2) * 128)


def block_map(weight_ref, index, out_ref):
    c = weight_ref.shape[1]
    w = weight_ref[index]
    out_ref[...] = jnp.zeros(out_ref.shape, BF16)
    out_ref[0:c, 0:c] = w
    out_ref[c : 2 * c, c : 2 * c] = w


def band_blocks(dilation):
    if dilation == 1:
        return ((0, 1, 0), (0, 2, 1), (1, 2, 0), (1, 3, 1))
    return ((0, 0, 0), (0, 1, 1), (1, 2, 0), (1, 3, 1))


def band_map(conv_ref, dilation, out_ref):
    c = conv_ref.shape[1]
    out_ref[...] = jnp.zeros(out_ref.shape, BF16)
    for tap, i, o in band_blocks(dilation):
        w = conv_ref[tap]
        rows = slice(i * c, (i + 1) * c)
        out_ref[rows, o * c : (o + 1) * c] = w[:, :c]
        out_ref[rows, (o + 2) * c : (o + 3) * c] = w[:, c:]


def band_grad(total, dilation, out_ref):
    c = out_ref.shape[1]
    for tap in range(2):
        for half in range(2):
            acc = None
            for t, i, o in band_blocks(dilation):
                if t != tap:
                    continue
                col = (o + 2 * half) * c
                part = total[i * c : (i + 1) * c, col : col + c]
                acc = part if acc is None else acc + part
            out_ref[tap, :, half * c : (half + 1) * c] = acc


def activations(pre):
    filt = jnp.tanh(pre[:, :128])
    gates = 0.5 * jnp.tanh(0.5 * pre[:, 128:]) + 0.5
    return filt, gates


def earlier(ref, k):
    if k == 0:
        x = ref[:, 0:128]
        return jnp.concatenate([jnp.zeros_like(x), x], axis=1)
    return ref[:, window2(k - 1)]


def build_tiles(cols_ref, vals_ref, acc_ref, dense_ref):
    rtiles, slots = vals_ref.shape[0], vals_ref.shape[1]
    ctiles = dense_ref.shape[1] // BLK
    for r in range(rtiles):
        acc_ref[...] = jnp.zeros(acc_ref.shape, F32)
        for j in range(slots):
            c = cols_ref[r, j]
            acc_ref[c] = acc_ref[c] + vals_ref[r, j].astype(F32)
        for c in range(ctiles):
            dense_ref[r * BLK : (r + 1) * BLK, c * BLK : (c + 1) * BLK] = acc_ref[c].astype(BF16)


def build_picks(send_ref, counts_ref, picks_ref):
    parts = send_ref.shape[0]
    nodes = picks_ref.shape[0]
    lane = lax.broadcasted_iota(jnp.int32, (1, BLK), 1)
    rows = lax.broadcasted_iota(jnp.int32, (nodes, BLK), 0)
    for q in range(parts):
        wanted = jnp.where(lane < counts_ref[0, q], send_ref[q : q + 1, :], -1)
        hit = rows == wanted
        picks_ref[:, q * BLK : (q + 1) * BLK] = jnp.where(hit, 1.0, 0.0).astype(BF16)


def prepare_body(cot_ref, mix_ref, send_ref, counts_ref, cols_ref, vals_ref,
                 dense_ref, picks_ref, cot_out, base_ref, pieces_ref,
                 acc_ref, map_ref, g_ref):
    nodes = cot_ref.shape[1]
    parts = send_ref.shape[0]
    c = mix_ref.shape[1]
    build_tiles(cols_ref, vals_ref, acc_ref, dense_ref)
    build_picks(send_ref, counts_ref, picks_ref)
    wide = cot_ref[...].astype(F32).T
    wide = jnp.concatenate([jnp.zeros((nodes, c), F32), wide], axis=1).astype(BF16)
    cot_out[...] = wide
    pairs = cot_out.shape[1] // 128
    block_map(mix_ref, 2, map_ref)
    m = map_ref[...]
    for k in range(pairs):
        g_ref[:, pair(k)] = dot_t1(cot_out[:, pair(k)], m).astype(BF16)
    block_map(mix_ref, 1, map_ref)
    m = map_ref[...]
    g = g_ref[...]
    pack_rows(g, dense_ref, nodes, parts, pieces_ref)
    base_ref[...] = dot_t0(dense_ref[:, :nodes], g)
    for k in range(pairs):
        base_ref[:, pair(k)] += dot_t1(cot_out[:, pair(k)], m)


def pack_rows(values, table_ref, start, parts, out_ref):
    flipped = values.astype(F32).T.astype(BF16)
    for q in range(parts):
        table = table_ref[:, start + q * BLK : start + (q + 1) * BLK]
        out_ref[q] = dot(flipped, table).astype(BF16)


def from_blocks(total, table_ref, start, parts, arrived_ref):
    for q in range(parts):
        table = table_ref[:, start + q * BLK : start + (q + 1) * BLK]
        total = total + dot_t1(table, arrived_ref[q])
    return total


def forward_part(x_ref, conv1_ref, conv2_ref, first_ref, hidden_ref, band_ref):
    pairs = x_ref.shape[1] // 128
    band_map(conv1_ref, 1, band_ref)
    b = band_ref[...]
    for k in range(pairs):
        filt, gates = activations(dot(earlier(x_ref, k), b))
        first_ref[:, pair(k)] = (filt * gates).astype(BF16)
    band_map(conv2_ref, 2, band_ref)
    b = band_ref[...]
    for k in range(1, pairs):
        filt, gates = activations(dot(earlier(first_ref, k), b))
        hidden_ref[:, pair(k - 1)] = (filt * gates).astype(BF16)


def gate_grad(pre, up):
    filt, gates = activations(pre)
    d_filt = up * gates * (1.0 - filt * filt)
    d_gate = up * filt * gates * (1.0 - gates)
    return jnp.concatenate([d_filt, d_gate], axis=1).astype(BF16)


def backward_part(x_ref, first_ref, cot_ref, conv1_ref, conv2_ref, grad_ref, g1_ref, g2_ref,
                  band_ref, up_ref, mid_ref):
    pairs = x_ref.shape[1] // 128
    band_map(conv2_ref, 2, band_ref)
    b = band_ref[...]
    total = None
    carry = None
    for k in range(1, pairs):
        both = earlier(first_ref, k)
        d = gate_grad(dot(both, b), up_ref[:, pair(k - 1)])
        part = dot_t0(both, d)
        total = part if total is None else total + part
        back = dot_t1(d, b)
        low = back[:, :128] if carry is None else carry + back[:, :128]
        mid_ref[:, pair(k - 1)] = low.astype(BF16)
        carry = back[:, 128:]
    mid_ref[:, pair(pairs - 1)] = carry.astype(BF16)
    band_grad(total, 2, g2_ref)
    band_map(conv1_ref, 1, band_ref)
    b = band_ref[...]
    total = None
    carry = None
    for k in range(pairs):
        both = earlier(x_ref, k)
        d = gate_grad(dot(both, b), mid_ref[:, pair(k)].astype(F32))
        part = dot_t0(both, d)
        total = part if total is None else total + part
        back = dot_t1(d, b)
        if k > 0:
            low = carry + back[:, :128]
            if k > 1:
                low = low + cot_ref[:, pair(k - 2)].astype(F32)
            grad_ref[:, pair(k - 1)] = low.astype(BF16)
        carry = back[:, 128:]
    last = carry + cot_ref[:, pair(pairs - 2)].astype(F32)
    grad_ref[:, pair(pairs - 1)] = last.astype(BF16)
    band_grad(total, 1, g1_ref)


def mix_grad(term_ref, cot_ref, c):
    acc = None
    for k in range(cot_ref.shape[1] // 128):
        part = dot_t0(term_ref[:, pair(k)], cot_ref[:, pair(k)])
        acc = part if acc is None else acc + part
    return acc[:c, :c] + acc[c:, c:]


def early_part(hidden_ref, hop_ref, x_ref, cot_ref, mix_ref, gm_ref, map0, map1, wide_ref):
    c = mix_ref.shape[1]
    block_map(mix_ref, 0, map0)
    block_map(mix_ref, 1, map1)
    for k in range(cot_ref.shape[1] // 128):
        acc = x_ref[:, pair(k + 1)].astype(F32)
        acc = acc + dot(hidden_ref[:, pair(k)], map0[...])
        wide_ref[:, pair(k)] = acc + dot(hop_ref[:, pair(k)], map1[...])
    gm_ref[0] = mix_grad(hidden_ref, cot_ref, c)
    gm_ref[1] = mix_grad(hop_ref, cot_ref, c)


def main_body(parts, reps, scale,
              x_ref, cot_ref, conv1_ref, conv2_ref, mix_ref, dense_ref, picks_ref, base_ref,
              pieces_ref,
              out_ref, grad_ref, sum_ref,
              first_ref, hidden_ref, hop_ref, second_ref, up_ref, mid_ref, band_ref,
              map0, map1, map2, g1_ref, g2_ref, gm_ref,
              wide_ref, send1, send2, send3, recv0, recv1, recv2, recv3,
              pack_ref, got_ref, part_ref, reps_ref, sums_ref,
              ssem, rsem, asem, arsem, bsem, brsem):
    me = lax.axis_index("dom")
    mine = lax.axis_index("rep")
    nodes = x_ref.shape[0]
    c = mix_ref.shape[1]
    pairs = cot_ref.shape[1] // 128
    feats = cot_ref.shape[1]

    barrier = pltpu.get_barrier_semaphore()
    for o in range(1, parts):
        pl.semaphore_signal(barrier, inc=1, device_id={"dom": lax.rem(me + o, parts)},
                            device_id_type=pl.DeviceIdType.MESH)
    for o in range(1, reps):
        pl.semaphore_signal(barrier, inc=1, device_id={"rep": lax.rem(mine + o, reps)},
                            device_id_type=pl.DeviceIdType.MESH)
    pl.semaphore_wait(barrier, parts - 1 + reps - 1)

    def copies(level, src, dst):
        made = []
        for o in sorted(range(1, parts), key=lambda o: abs(2 * o - parts)):
            peer = lax.rem(me + o, parts)
            made.append(pltpu.make_async_remote_copy(
                src_ref=src.at[peer, pl.ds(c, feats - c)],
                dst_ref=dst.at[me, pl.ds(c, feats - c)],
                send_sem=ssem.at[level, o],
                recv_sem=rsem.at[level, o],
                device_id={"dom": peer},
                device_id_type=pl.DeviceIdType.MESH,
            ))
        for m in made:
            m.start()
        return made

    def arrive(made):
        for m in made:
            m.wait_recv()

    round0 = copies(0, pieces_ref, recv0)
    for buf in (recv0, recv1, recv2, recv3):
        buf[:, 0:c, :] = jnp.zeros((parts, c, BLK), BF16)
        buf[me] = jnp.zeros((feats, BLK), BF16)

    forward_part(x_ref, conv1_ref, conv2_ref, first_ref, hidden_ref, band_ref)
    pack_rows(hidden_ref[...], picks_ref, 0, parts, send1)
    round1 = copies(1, send1, recv1)

    arrive(round0)
    g = from_blocks(base_ref[...], picks_ref, 0, parts, recv0).astype(BF16)
    pack_rows(g, dense_ref, nodes, parts, send2)
    round2 = copies(2, send2, recv2)
    up_ref[...] = dot_t0(dense_ref[:, :nodes], g)
    block_map(mix_ref, 0, map0)
    for k in range(pairs):
        up_ref[:, pair(k)] += dot_t1(cot_ref[:, pair(k)], map0[...])

    own = dot(dense_ref[:, :nodes], hidden_ref[...])
    arrive(round1)
    hop_ref[...] = from_blocks(own, dense_ref, nodes, parts, recv1).astype(BF16)
    pack_rows(hop_ref[...], picks_ref, 0, parts, send3)
    round3 = copies(3, send3, recv3)

    arrive(round2)
    up_ref[...] = from_blocks(up_ref[...], picks_ref, 0, parts, recv2)
    backward_part(x_ref, first_ref, cot_ref, conv1_ref, conv2_ref, grad_ref, g1_ref, g2_ref,
                  band_ref, up_ref, mid_ref)

    early_part(hidden_ref, hop_ref, x_ref, cot_ref, mix_ref, gm_ref, map0, map1, wide_ref)
    block_map(mix_ref, 2, map2)
    own = dot(dense_ref[:, :nodes], hop_ref[...])
    arrive(round3)
    second_ref[...] = from_blocks(own, dense_ref, nodes, parts, recv3).astype(BF16)
    gm_ref[2] = mix_grad(second_ref, cot_ref, c)

    per = pack_ref.shape[1]
    flat = pack_ref
    flat[...] = jnp.zeros(flat.shape, F32)

    def put(first_row, value):
        rows = value.shape[0]
        done = 0
        while done < rows:
            slot, at = divmod(first_row + done, per)
            step = min(per - at, rows - done)
            flat[slot, at : at + step, :] = value[done : done + step]
            done += step

    put(0, g1_ref[0])
    put(c, g1_ref[1])
    put(2 * c, g2_ref[0])
    put(3 * c, g2_ref[1])
    put(4 * c, jnp.concatenate([gm_ref[0], gm_ref[1]], axis=1))
    put(5 * c, jnp.concatenate([gm_ref[2], jnp.zeros((c, c), F32)], axis=1))

    scatter = []
    for o in range(1, parts):
        peer = lax.rem(me + o, parts)
        scatter.append(pltpu.make_async_remote_copy(
            src_ref=pack_ref.at[peer], dst_ref=got_ref.at[me],
            send_sem=asem.at[0, o], recv_sem=arsem.at[0, o],
            device_id={"dom": peer}, device_id_type=pl.DeviceIdType.MESH))
    for m in scatter:
        m.start()
    for k in range(pairs):
        wide_ref[:, pair(k)] += dot(second_ref[:, pair(k)], map2[...])
    out_ref[...] = wide_ref[...].T[c:].astype(BF16)
    got_ref[me] = pack_ref[me]
    arrive(scatter)
    total = got_ref[0]
    for q in range(1, parts):
        total = total + got_ref[q]
    part_ref[...] = total
    around = []
    for o in range(1, reps):
        peer = lax.rem(mine + o, reps)
        around.append(pltpu.make_async_remote_copy(
            src_ref=part_ref, dst_ref=reps_ref.at[mine],
            send_sem=bsem.at[o], recv_sem=brsem.at[o],
            device_id={"rep": peer}, device_id_type=pl.DeviceIdType.MESH))
    for m in around:
        m.start()
    reps_ref[mine] = total
    arrive(around)
    total = reps_ref[0]
    for q in range(1, reps):
        total = total + reps_ref[q]
    for m in around:
        m.wait_send()
    part_ref[...] = total * (1.0 / scale)
    final = []
    for o in range(1, parts):
        peer = lax.rem(me + o, parts)
        final.append(pltpu.make_async_remote_copy(
            src_ref=part_ref, dst_ref=sums_ref.at[me],
            send_sem=asem.at[1, o], recv_sem=arsem.at[1, o],
            device_id={"dom": peer}, device_id_type=pl.DeviceIdType.MESH))
    for m in final:
        m.start()
    sums_ref[me] = part_ref[...]
    arrive(final)

    sum_ref[...] = sums_ref[...]
    for m in round0 + round1 + round2 + round3 + scatter + final:
        m.wait_send()


def shards(inputs, cotangent, conv_one, conv_two, mix_weight, send_rows, counts, tile_cols,
           tile_vals):
    windows, nodes, flat = inputs.shape
    channels = mix_weight.shape[1]
    parts = lax.axis_size("dom")
    reps = lax.axis_size("rep")
    kept = flat // channels - 3
    wide = flat - 2 * channels
    halo = parts * BLK
    blocks = (parts, wide, BLK)
    prepared = [((nodes, nodes + halo), BF16), ((nodes, halo), BF16), ((nodes, wide), BF16),
                ((nodes, wide), F32), (blocks, BF16)]
    dense, picks, cot_wide, base, pieces = pl.pallas_call(
        prepare_body,
        out_shape=[jax.ShapeDtypeStruct(s, d) for s, d in prepared],
        in_specs=[VM, VM, VM, SM, SM, VM],
        out_specs=[VM] * 5,
        scratch_shapes=[pltpu.VMEM((parts + nodes // BLK, BLK, BLK), F32),
                        pltpu.VMEM((128, 128), BF16), pltpu.VMEM((nodes, wide), BF16)],
        compiler_params=LIMIT,
        name="prepare",
    )(cotangent[0].T, mix_weight, send_rows[0], counts, tile_cols, tile_vals)
    scaling = math.sqrt(float(windows * reps * nodes * parts * kept))
    unit = 8 * parts
    per = -(-6 * channels // unit) * unit // parts
    results = [((kept * channels, nodes), BF16), ((nodes, flat), BF16), ((parts, per, BLK), F32)]
    scratch = [((nodes, flat), BF16), ((nodes, wide), BF16), ((nodes, wide), BF16),
               ((nodes, wide), BF16), ((nodes, wide), F32), ((nodes, flat), BF16),
               ((256, 256), BF16), ((128, 128), BF16), ((128, 128), BF16), ((128, 128), BF16),
               (conv_one.shape, F32), (conv_two.shape, F32), (mix_weight.shape, F32)]
    scratch += [((nodes, wide), F32)] + [(blocks, BF16)] * 7
    scratch += [((parts, per, BLK), F32), ((parts, per, BLK), F32), ((per, BLK), F32),
                ((reps, per, BLK), F32), ((parts, per, BLK), F32)]
    dma = pltpu.SemaphoreType.DMA
    output, grad_input, packed = pl.pallas_call(
        functools.partial(main_body, parts, reps, scaling),
        out_shape=[jax.ShapeDtypeStruct(s, d) for s, d in results],
        in_specs=[VM] * 9,
        out_specs=[VM] * 3,
        scratch_shapes=[pltpu.VMEM(s, d) for s, d in scratch]
        + [dma((4, parts)), dma((4, parts)), dma((2, parts)), dma((2, parts)), dma((reps,)),
           dma((reps,))],
        compiler_params=pltpu.CompilerParams(
            vmem_limit_bytes=60 * 1024 * 1024, collective_id=0, has_side_effects=True),
        name="layer",
    )(inputs[0], cot_wide, conv_one, conv_two, mix_weight, dense, picks, base, pieces)
    c = channels
    rows = packed.reshape(parts * per, BLK)
    gm = jnp.stack([rows[4 * c : 5 * c, :c], rows[4 * c : 5 * c, c:], rows[5 * c : 6 * c, :c]])
    return (
        output.T[None],
        grad_input[None],
        rows[: 2 * c].reshape(conv_one.shape),
        rows[2 * c : 4 * c].reshape(conv_two.shape),
        gm,
    )


def place_tiles(cols_ref, vals_ref, acc_ref, dense_ref, me, parts):
    rtiles, slots = vals_ref.shape[0], vals_ref.shape[1]
    ctiles = dense_ref.shape[1] // BLK
    for r in range(rtiles):
        acc_ref[...] = jnp.zeros(acc_ref.shape, F32)
        for j in range(slots):
            col = cols_ref[r, j]
            off = lax.rem(me - (col - rtiles) + 2 * parts, parts)
            c = jnp.where(col < rtiles, col, jnp.where(off == 0, ctiles, rtiles - 1 + off))
            acc_ref[c] = acc_ref[c] + vals_ref[r, j].astype(F32)
        for c in range(ctiles):
            dense_ref[r * BLK : (r + 1) * BLK, c * BLK : (c + 1) * BLK] = acc_ref[c].astype(BF16)


def setup_body(parts, send_ref, counts_ref, cols_ref, vals_ref, dense_ref, wanted_ref, acc_ref):
    me = lax.axis_index("dom")
    place_tiles(cols_ref, vals_ref, acc_ref, dense_ref, me, parts)
    lane = lax.broadcasted_iota(jnp.int32, (1, BLK), 1)
    for o in range(parts):
        t = lax.rem(me + o, parts)
        wanted_ref[o : o + 1, :] = jnp.where(
            lane < counts_ref[0, t], send_ref[pl.ds(t, 1), :], -1)


def chunk(first, size):
    return pl.ds(pl.multiple_of(first, size), size)


def steps_body(parts, reps, scale,
               x_ref, cot_ref, conv1_ref, conv2_ref, mix_ref, dense_ref, wanted_ref,
               out_ref, grad_ref, one_out, two_out, mix_out,
               xt_ref, first_ref, hid_ref, d1_ref, d2_ref, mid_ref,
               band1, band1t, band2, band2t, maps, mapst,
               adj_ref, lists_ref, picks_ref,
               cf_ref, hf_ref, f1_ref, c1_ref, own_ref, part_t, ext_ref,
               gh_ref, mx_ref, ghs_ref, mxs_ref,
               g1_ref, g2_ref, pack0, got0, half0, reps0, full0, sums0,
               pack1, got1, half1, reps1, full1, sums1,
               lsend, lrecv, fsend, frecv, esend, erecv, tsend, trecv,
               asem, arsem, bsem, brsem):
    me = lax.axis_index("dom")
    mine = lax.axis_index("rep")
    nodes = x_ref.shape[0]
    c = mix_ref.shape[1]
    pairs = x_ref.shape[1] // 128
    rows = nodes // reps
    mesh_ids = pl.DeviceIdType.MESH
    holder = lax.rem(parts // 2 - reps // 2 + mine + parts, parts)
    extra = parts * c
    zs = parts // 2
    z, xx = me // 2, lax.rem(me, 2)
    yy, core = mine // 2, lax.rem(mine, 2)

    barrier = pltpu.get_barrier_semaphore()
    for o in range(1, parts):
        pl.semaphore_signal(barrier, inc=1, device_id={"dom": lax.rem(me + o, parts)},
                            device_id_type=mesh_ids)
    for o in range(1, reps):
        pl.semaphore_signal(barrier, inc=1, device_id={"rep": lax.rem(mine + o, reps)},
                            device_id_type=mesh_ids)
    pl.semaphore_wait(barrier, parts - 1 + reps - 1)

    def remote(src, dst, ssem, rsem, **where):
        return pltpu.make_async_remote_copy(
            src_ref=src, dst_ref=dst, send_sem=ssem, recv_sem=rsem,
            device_id=where, device_id_type=mesh_ids)

    order = sorted(range(1, parts), key=lambda o: abs(2 * o - parts))

    def piece(p, r):
        return adj_ref.at[p, chunk(r * rows, rows)]

    def source_z(t, way):
        return z - t if way == 0 else z + t

    def valid(t, way):
        if t == 0:
            return z >= 0
        return z >= t if way == 0 else z + t < zs

    def slot(t, way):
        return 0 if t == 0 else 2 * t - 1 + way

    def base(t, way):
        return source_z(t, way) * 2 + xx

    def cross(t, way):
        return source_z(t, way) * 2 + 1 - xx

    yrep = (1 - yy) * 2 + core
    crep = yy * 2 + 1 - core
    cyrep = (1 - yy) * 2 + 1 - core

    def along(t, way, out_way):
        src = dense_ref.at[chunk(mine * rows, rows)] if t == 0 else piece(base(t, way), mine)
        to = (z + 1 if out_way == 0 else z - 1) * 2 + xx
        return remote(src, piece(base(t, way), mine), tsend.at[out_way, slot(t, way)],
                      trecv.at[0, slot(t + 1, out_way)], dom=to)

    def across(t, way):
        src = dense_ref.at[chunk(mine * rows, rows)] if t == 0 else piece(base(t, way), mine)
        return remote(src, piece(base(t, way), mine), tsend.at[2, slot(t, way)],
                      trecv.at[2, slot(t, way)], dom=z * 2 + 1 - xx)

    def hand(kind, p, r, t, way, to):
        return remote(piece(p, r), piece(p, r), tsend.at[kind, slot(t, way)],
                      trecv.at[kind, slot(t, way)], rep=to)

    def arrived(kind, p, r, t, way, **where):
        remote(piece(p, r), piece(p, r), tsend.at[kind, slot(t, way)],
               trecv.at[kind, slot(t, way)], **where).wait_recv()

    def ways(t):
        return (0,) if t == 0 else (0, 1)

    def lane_sends(t, way):
        made = []
        outs = (0, 1) if t == 0 else (way,)
        for w in outs:
            made.append((z + 1 < zs if w == 0 else z >= 1, along(t, way, w)))
        made.append((None, across(t, way)))
        return made

    def base_sends(t, way):
        return [] if t == 0 else [(None, hand(3, base(t, way), mine, t, way, yrep)),
                                  (None, hand(4, base(t, way), mine, t, way, crep))]

    def cross_sends(t, way):
        return [(None, hand(5, cross(t, way), mine, t, way, yrep)),
                (None, hand(6, cross(t, way), mine, t, way, crep))]

    def ybase_sends(t, way):
        return [] if t == 0 else [(None, hand(7, base(t, way), yrep, t, way, crep))]

    def ycross_sends(t, way):
        return [(None, hand(8, cross(t, way), yrep, t, way, crep))]

    def go(sends, wait=False):
        for cond, copy in sends:
            act = copy.wait_send if wait else copy.start
            if cond is None:
                act()
            else:
                pl.when(cond)(act)

    def on_base(t, way):
        @pl.when(valid(t, way))
        def _():
            arrived(0, base(t, way), mine, t, way, rep=crep)
            go(lane_sends(t, way) + base_sends(t, way))

    def on_cross(t, way):
        @pl.when(valid(t, way))
        def _():
            arrived(2, cross(t, way), mine, t, way, rep=crep)
            go(cross_sends(t, way))

    def on_ybase(t, way):
        @pl.when(valid(t, way))
        def _():
            arrived(3, base(t, way), yrep, t, way, rep=crep)
            go(ybase_sends(t, way))

    def on_ycross(t, way):
        @pl.when(valid(t, way))
        def _():
            arrived(5, cross(t, way), yrep, t, way, rep=crep)
            go(ycross_sends(t, way))

    relay = []
    for s in range(1, zs + 2):
        for handler, t, least in ((on_base, s, 1), (on_cross, s - 1, 0), (on_ybase, s - 1, 1),
                                  (on_ycross, s - 2, 0)):
            if least <= t < zs:
                for w in ways(t):
                    relay.append(functools.partial(handler, t, w))
    relay.reverse()

    def step_relay(count=1):
        for _ in range(count):
            if relay:
                relay.pop()()

    def scatter_field(level, src, first, dst):
        made = []
        for o in order:
            peer = lax.rem(me + o, parts)
            made.append(remote(src.at[chunk(first + peer * c, c)], dst.at[me, pl.ds(0, c)],
                               fsend.at[level, o], frecv.at[level, o], dom=peer))
        for m in made:
            m.start()
        off = lax.rem(holder - me + parts, parts)
        last = remote(src.at[pl.ds(first + extra, c)], dst.at[me, pl.ds(c, c)],
                      esend.at[level, 0], erecv.at[level, off], dom=holder)
        pl.when(me != holder)(last.start)
        dst[me, 0:c, :] = src[chunk(first + me * c, c), :]

        @pl.when(me == holder)
        def _():
            dst[me, c : 2 * c, :] = src[first + extra : first + extra + c, :]

        @pl.when(me != holder)
        def _():
            dst[:, c : 2 * c, :] = jnp.zeros((parts, c, nodes), BF16)
        return made, last

    def field_arrives(level, made, src, dst):
        for m in made:
            m.wait_recv()

        @pl.when(me == holder)
        def _():
            for o in range(1, parts):
                q = lax.rem(me - o + parts, parts)
                remote(dst.at[q, pl.ds(c, c)], dst.at[q, pl.ds(c, c)], esend.at[level, 0],
                       erecv.at[level, o], dom=q).wait_recv()

    def home_copies(level, o, src, first, dst):
        q = lax.rem(me + o, parts)
        one = remote(src.at[q, pl.ds(0, c)], dst.at[chunk(first + me * c, c)],
                     fsend.at[level, o], frecv.at[level, o], dom=q)
        two = remote(src.at[q, pl.ds(c, c)], dst.at[pl.ds(first + extra, c)],
                     esend.at[level, o], erecv.at[level, 0], dom=q)
        return one, two

    def go_home(level, o, src, first, dst):
        if o:
            one, two = home_copies(level, o, src, first, dst)
            one.start()
            pl.when(me == holder)(two.start)
            return
        dst[chunk(first + me * c, c), :] = src[me, 0:c, :]

        @pl.when(me == holder)
        def _():
            dst[first + extra : first + extra + c, :] = src[me, c : 2 * c, :]

    def home_arrives(level, src, first, dst):
        for o in range(1, parts):
            home_copies(level, o, src, first, dst)[0].wait_recv()
        pl.when(me != holder)(home_copies(level, 1, src, first, dst)[1].wait_recv)

    def home_sent(level, src, first, dst):
        for o in range(1, parts):
            one, two = home_copies(level, o, src, first, dst)
            one.wait_send()
            pl.when(me == holder)(two.wait_send)

    go(lane_sends(0, 0))
    cot_round = scatter_field(0, cot_ref, 0, cf_ref)
    lists = []
    for o in order:
        peer = lax.rem(me + o, parts)
        lists.append(remote(wanted_ref, lists_ref.at[me], lsend.at[o], lrecv.at[o], dom=peer))
    for m in lists:
        m.start()
    lists_ref[me] = wanted_ref[...]
    adj_ref[me] = dense_ref[...]

    for k in range(pairs):
        xt_ref[pair(k), :] = x_ref[:, pair(k)].astype(F32).T.astype(BF16)
    for conv, dil, nat, tra in ((conv1_ref, 1, band1, band1t), (conv2_ref, 2, band2, band2t)):
        band_map(conv, dil, nat)
        tra[...] = nat[...].astype(F32).T.astype(BF16)

    def earlier_t(ref, k):
        if k == 0:
            v = ref[0:128, :]
            return jnp.concatenate([jnp.zeros_like(v), v], axis=0)
        return ref[window2(k - 1), :]

    def gated(pre, d_ref, k):
        filt = jnp.tanh(pre[:128])
        gates = 0.5 * jnp.tanh(0.5 * pre[128:]) + 0.5
        d_ref[k, 0:128, :] = gates * (1.0 - filt * filt)
        d_ref[k, 128:256, :] = filt * gates * (1.0 - gates)
        return (filt * gates).astype(BF16)

    for k in range(pairs):
        first_ref[pair(k), :] = gated(dot(band1t[...], earlier_t(xt_ref, k)), d1_ref, k)
        if k % 2:
            step_relay()
    for k in range(1, pairs):
        hid_ref[pair(k - 1), :] = gated(dot(band2t[...], earlier_t(first_ref, k)), d2_ref, k)
        step_relay()
    hid_round = scatter_field(1, hid_ref, c, hf_ref)
    step_relay()

    for i in range(3):
        block_map(mix_ref, i, maps.at[i])
        mapst[i] = maps[i].astype(F32).T.astype(BF16)
    gh_ref[0:c, :] = jnp.zeros((c, nodes), BF16)

    for m in lists:
        m.wait_recv()
    node = lax.broadcasted_iota(jnp.int32, (nodes, BLK), 0)
    for q in range(parts):
        for o in range(1, parts):
            hit = node == lists_ref[q, o : o + 1, :]
            picks_ref[q, :, (o - 1) * BLK : o * BLK] = jnp.where(hit, 1.0, 0.0).astype(BF16)
        step_relay(2)

    field_arrives(0, cot_round[0], cot_ref, cf_ref)
    step_relay(len(relay))
    for t in range(zs):
        for w in ways(t):
            @pl.when(valid(t, w))
            def _():
                if t:
                    arrived(4, base(t, w), crep, t, w, rep=crep)
                    arrived(7, base(t, w), cyrep, t, w, rep=crep)
                arrived(6, cross(t, w), crep, t, w, rep=crep)
                arrived(8, cross(t, w), cyrep, t, w, rep=crep)

    def back_pieces(g_ref):
        for p in range(parts):
            t = dot(g_ref[p], adj_ref[p])
            own_ref[p] = t[:, :nodes]
            for o in range(1, parts):
                at = nodes + (o - 1) * BLK
                part_t[(p - o) % parts, :, (o - 1) * BLK : o * BLK] = t[:, at : at + BLK].astype(BF16)

    def back_owner(q):
        return (own_ref[q] + dot_t1(part_t[q], picks_ref[q])).astype(BF16)

    back_pieces(cf_ref)
    for q in range(parts):
        c1_ref[q] = back_owner(q)
    back_pieces(c1_ref)
    field_arrives(1, hid_round[0], hid_ref, hf_ref)
    mix = [None] * 3
    for o in order + [0]:
        q = lax.rem(me + o, parts)
        moved = (cf_ref[q], c1_ref[q], back_owner(q))
        grads = [dot(maps[i], moved[i]) for i in range(3)]
        ghs_ref[q] = (grads[0] + grads[1] + grads[2]).astype(BF16)
        go_home(2, o, ghs_ref, c, gh_ref)
        for i in range(3):
            more = dot_t1(hf_ref[q], moved[i])
            mix[i] = more if mix[i] is None else mix[i] + more
    mix = [m[:c, :c] + m[c:, c:] for m in mix]

    def reducer(g, pack, got, half, total_reps, full, sums):
        def around_dom(stage, src_of, dst):
            return [remote(src_of(lax.rem(me + o, parts)), dst.at[me], asem.at[2 * g + stage, o],
                           arsem.at[2 * g + stage, o], dom=lax.rem(me + o, parts)) for o in order]

        def around_rep():
            return [remote(half, total_reps.at[mine], bsem.at[g, o], brsem.at[g, o],
                           rep=lax.rem(mine + o, reps)) for o in range(1, reps)]

        def shares():
            return around_dom(0, lambda peer: pack.at[peer], got)

        def back():
            return around_dom(1, lambda peer: full, sums)

        def first():
            for m in shares():
                m.start()
            got[me] = pack[me]

        def second():
            for m in shares():
                m.wait_recv()
            total = got[0]
            for q in range(1, parts):
                total = total + got[q]
            half[...] = total
            for m in around_rep():
                m.start()
            total_reps[mine] = total

        def third():
            for m in around_rep():
                m.wait_recv()
            total = total_reps[0]
            for q in range(1, reps):
                total = total + total_reps[q]
            full[...] = total * (1.0 / scale)
            for m in back():
                m.start()
            sums[me] = full[...]

        def last():
            for m in back():
                m.wait_recv()

        def sent():
            for m in shares() + around_rep() + back():
                m.wait_send()

        return first, second, third, last, sent

    def put(pack, first_row, value):
        per = pack.shape[1]
        count, done = value.shape[0], 0
        while done < count:
            place, at = divmod(first_row + done, per)
            step = min(per - at, count - done)
            pack[place, at : at + step, :] = value[done : done + step]
            done += step

    early = reducer(0, pack0, got0, half0, reps0, full0, sums0)
    late = reducer(1, pack1, got1, half1, reps1, full1, sums1)
    put(pack0, 0, jnp.concatenate([mix[0], mix[1]], axis=1))
    put(pack0, c, jnp.concatenate([mix[2], jnp.zeros((c, c), F32)], axis=1))
    early[0]()

    def extend(f_ref):
        for q in range(parts):
            ext_ref[q, :, 0:nodes] = f_ref[q]
            halo = dot(f_ref[q], picks_ref[q]).astype(BF16)
            for o in range(1, parts):
                at = nodes + (o - 1) * BLK
                ext_ref[(q + o) % parts, :, at : at + BLK] = halo[:, (o - 1) * BLK : o * BLK]

    extend(hf_ref)
    for p in range(parts):
        f1_ref[p] = dot_t1(ext_ref[p], adj_ref[p]).astype(BF16)
    early[1]()

    home_arrives(2, ghs_ref, c, gh_ref)

    def conv_back(sig_ref, d_ref, up_of, band, low_of, first_pair, dilation, out):
        total, carry = None, None
        b = band[...]
        for k in range(first_pair, pairs):
            up = up_of(k)
            both = earlier_t(sig_ref, k)
            d = jnp.concatenate([up * d_ref[k, 0:128, :], up * d_ref[k, 128:256, :]], axis=0)
            d = d.astype(BF16)
            part = dot_t1(both, d)
            total = part if total is None else total + part
            back = dot(b, d)
            if k > 0:
                low_of(k - 1, back[:128] if carry is None else carry + back[:128])
            carry = back[128:]
        low_of(pairs - 1, carry)
        band_grad(total, dilation, out)

    def set_mid(k, low):
        mid_ref[pair(k), :] = low.astype(BF16)

    def set_grad(k, low):
        if k == 1:
            low = low + jnp.concatenate([jnp.zeros((c, nodes), F32), cot_ref[0:c, :].astype(F32)], axis=0)
        elif k > 1:
            low = low + cot_ref[(2 * k - 3) * c : (2 * k - 1) * c, :].astype(F32)
        grad_ref[:, pair(k)] = low.T.astype(BF16)

    conv_back(first_ref, d2_ref, lambda k: gh_ref[pair(k - 1), :].astype(F32), band2, set_mid, 1, 2, g2_ref)
    early[2]()
    conv_back(xt_ref, d1_ref, lambda k: mid_ref[pair(k), :].astype(F32), band1, set_grad, 0, 1, g1_ref)

    for tap in range(2):
        put(pack1, tap * c, g1_ref[tap])
        put(pack1, (2 + tap) * c, g2_ref[tap])
    late[0]()

    extend(f1_ref)
    for o in order + [0]:
        q = lax.rem(me + o, parts)
        second = dot_t1(ext_ref[q], adj_ref[q]).astype(BF16)
        mixed = dot(mapst[0], hf_ref[q]) + dot(mapst[1], f1_ref[q]) + dot(mapst[2], second)
        mxs_ref[q] = mixed.astype(BF16)
        go_home(3, o, mxs_ref, 0, mx_ref)
    late[1]()
    early[3]()
    per = sums0.shape[1]
    for i in range(2 * c // per):
        block, at = divmod(i * per, c)
        for j in range(2 - block):
            mix_out[2 * block + j, at : at + per, :] = sums0[i, :, j * c : (j + 1) * c]
    late[2]()
    home_arrives(3, mxs_ref, 0, mx_ref)
    kept = out_ref.shape[0]
    out_ref[...] = (mx_ref[...].astype(F32) + xt_ref[pairs * 128 - kept :, :].astype(F32)).astype(BF16)

    for m in cot_round[0] + hid_round[0] + lists:
        m.wait_send()
    pl.when(me != holder)(cot_round[1].wait_send)
    pl.when(me != holder)(hid_round[1].wait_send)
    home_sent(2, ghs_ref, c, gh_ref)
    home_sent(3, mxs_ref, 0, mx_ref)
    for t in range(zs):
        for w in ways(t):
            @pl.when(valid(t, w))
            def _():
                go(lane_sends(t, w) + base_sends(t, w) + cross_sends(t, w) + ybase_sends(t, w)
                   + ycross_sends(t, w), wait=True)
    late[3]()
    per = sums1.shape[1]
    for i in range(4 * c // per):
        tap, at = divmod(i * per, c)
        where = one_out if tap < 2 else two_out
        where[tap % 2, at : at + per, :] = sums1[i]
    early[4]()
    late[4]()


def finish_body(*refs):
    half = len(refs) // 2
    srcs, dsts, sem = refs[:half], refs[half : 2 * half], refs[-1]
    copies = [pltpu.make_async_copy(a, b, sem.at[i]) for i, (a, b) in enumerate(zip(srcs, dsts))]
    for m in copies:
        m.start()
    for m in copies:
        m.wait()


def step_shards(inputs, cotangent, conv_one, conv_two, mix_weight, send_rows, counts, tile_cols,
                tile_vals):
    windows, nodes, flat = inputs.shape
    channels = mix_weight.shape[1]
    parts = lax.axis_size("dom")
    reps = lax.axis_size("rep")
    kept = flat // channels - 3
    c = channels
    pairs = flat // 128
    halo = (parts - 1) * BLK
    ext = nodes + halo
    dense, wanted = pl.pallas_call(
        functools.partial(setup_body, parts),
        out_shape=[jax.ShapeDtypeStruct((nodes, ext), BF16),
                   jax.ShapeDtypeStruct((parts, BLK), jnp.int32)],
        in_specs=[VM, SM, SM, VM],
        out_specs=[VM] * 2,
        scratch_shapes=[pltpu.VMEM((ext // BLK + 1, BLK, BLK), F32)],
        compiler_params=LIMIT,
        name="setup",
    )(send_rows[0], counts, tile_cols, tile_vals)
    scaling = math.sqrt(float(windows * reps * nodes * parts * kept))
    results = [((kept * c, nodes), BF16), ((nodes, flat), BF16), (conv_one.shape, F32),
               (conv_two.shape, F32), (mix_weight.shape, F32)]
    field = (parts, 2 * c, nodes)
    wide = flat - 2 * c
    scratch = [((flat, nodes), BF16), ((flat, nodes), BF16), ((wide, nodes), BF16),
               ((pairs, 256, nodes), F32), ((pairs, 256, nodes), F32), ((flat, nodes), BF16)]
    scratch += [((256, 256), BF16)] * 4 + [((3, 128, 128), BF16)] * 2
    scratch += [((parts, nodes, ext), BF16), ((parts, parts, BLK), jnp.int32),
                ((parts, nodes, halo), BF16)]
    scratch += [(field, BF16)] * 4 + [(field, F32), ((parts, 2 * c, halo), BF16),
                                      ((parts, 2 * c, ext), BF16)]
    scratch += [((wide, nodes), BF16), ((kept * c, nodes), BF16), (field, BF16), (field, BF16)]
    scratch += [(conv_one.shape, F32), (conv_two.shape, F32)]
    for total in (2 * c, 4 * c):
        per = total // parts
        scratch += [((parts, per, BLK), F32), ((parts, per, BLK), F32), ((per, BLK), F32),
                    ((reps, per, BLK), F32), ((per, BLK), F32), ((parts, per, BLK), F32)]
    dma = pltpu.SemaphoreType.DMA
    sems = [(parts,), (parts,), (4, parts), (4, parts), (4, parts), (4, parts),
            (9, parts), (9, parts), (4, parts), (4, parts), (2, reps), (2, reps)]
    made = pl.pallas_call(
        functools.partial(steps_body, parts, reps, scaling),
        out_shape=[jax.ShapeDtypeStruct(s, d) for s, d in results],
        in_specs=[VM] * 7,
        out_specs=[VM] * 5,
        scratch_shapes=[pltpu.VMEM(s, d) for s, d in scratch] + [dma(s) for s in sems],
        compiler_params=pltpu.CompilerParams(
            vmem_limit_bytes=60 * 1024 * 1024, collective_id=1, has_side_effects=True),
        name="steps",
    )(inputs[0], cotangent[0].T, conv_one, conv_two, mix_weight, dense, wanted)
    hbm = pl.BlockSpec(memory_space=pl.ANY)
    output, grad_input, one, two, mix = pl.pallas_call(
        finish_body,
        out_shape=[jax.ShapeDtypeStruct(s, d) for s, d in results],
        in_specs=[hbm] * 5,
        out_specs=[hbm] * 5,
        scratch_shapes=[dma((5,))],
        name="finish",
    )(*made)
    return output.T[None], grad_input[None], one, two, mix


def solution(mesh):
    placed = (
        P("rep", "dom", None),
        P("rep", "dom", None),
        P(),
        P(),
        P(),
        P("dom", None, None),
        P("dom", None),
        P("dom", None),
        P("dom", None, None, None),
    )
    parts, reps = mesh.shape["dom"], mesh.shape["rep"]

    def layer(*args):
        kept = args[0].shape[2] // args[4].shape[1] - 3
        by_step = parts % 2 == 0 and reps == 4 and parts == kept - 1
        return step_shards(*args) if by_step else shards(*args)

    return jax.shard_map(
        layer,
        mesh=mesh,
        in_specs=placed,
        out_specs=(P("rep", "dom", None), P("rep", "dom", None), P(), P(), P()),
        check_vma=False,
    )
```

```python
import functools
import math

import jax
import jax.numpy as jnp
from jax import lax
from jax.experimental import pallas as pl
from jax.experimental.pallas import tpu as pltpu
from jax.sharding import PartitionSpec as P

F32 = jnp.float32
BF16 = jnp.bfloat16
BLK = 128
VM = pl.BlockSpec(memory_space=pltpu.VMEM)
SM = pl.BlockSpec(memory_space=pltpu.SMEM)
LIMIT = pltpu.CompilerParams(vmem_limit_bytes=56 * 1024 * 1024)


def dot(a, b):
    return jnp.dot(a, b, preferred_element_type=F32)


def dot_t0(a, b):
    return lax.dot_general(a, b, (((0,), (0,)), ((), ())), preferred_element_type=F32)


def dot_t1(a, b):
    return lax.dot_general(a, b, (((1,), (1,)), ((), ())), preferred_element_type=F32)


def pair(k):
    return slice(k * 128, (k + 1) * 128)


def window2(k):
    return slice(k * 128, (k + 2) * 128)


def block_map(weight_ref, index, out_ref):
    c = weight_ref.shape[1]
    w = weight_ref[index]
    out_ref[...] = jnp.zeros(out_ref.shape, BF16)
    out_ref[0:c, 0:c] = w
    out_ref[c : 2 * c, c : 2 * c] = w


def band_blocks(dilation):
    if dilation == 1:
        return ((0, 1, 0), (0, 2, 1), (1, 2, 0), (1, 3, 1))
    return ((0, 0, 0), (0, 1, 1), (1, 2, 0), (1, 3, 1))


def band_map(conv_ref, dilation, out_ref):
    c = conv_ref.shape[1]
    out_ref[...] = jnp.zeros(out_ref.shape, BF16)
    for tap, i, o in band_blocks(dilation):
        w = conv_ref[tap]
        rows = slice(i * c, (i + 1) * c)
        out_ref[rows, o * c : (o + 1) * c] = w[:, :c]
        out_ref[rows, (o + 2) * c : (o + 3) * c] = w[:, c:]


def band_grad(total, dilation, out_ref):
    c = out_ref.shape[1]
    for tap in range(2):
        for half in range(2):
            acc = None
            for t, i, o in band_blocks(dilation):
                if t != tap:
                    continue
                col = (o + 2 * half) * c
                part = total[i * c : (i + 1) * c, col : col + c]
                acc = part if acc is None else acc + part
            out_ref[tap, :, half * c : (half + 1) * c] = acc


def activations(pre):
    filt = jnp.tanh(pre[:, :128])
    gates = 0.5 * jnp.tanh(0.5 * pre[:, 128:]) + 0.5
    return filt, gates


def earlier(ref, k):
    if k == 0:
        x = ref[:, 0:128]
        return jnp.concatenate([jnp.zeros_like(x), x], axis=1)
    return ref[:, window2(k - 1)]


def build_tiles(cols_ref, vals_ref, acc_ref, dense_ref):
    rtiles, slots = vals_ref.shape[0], vals_ref.shape[1]
    ctiles = dense_ref.shape[1] // BLK
    for r in range(rtiles):
        acc_ref[...] = jnp.zeros(acc_ref.shape, F32)
        for j in range(slots):
            c = cols_ref[r, j]
            acc_ref[c] = acc_ref[c] + vals_ref[r, j].astype(F32)
        for c in range(ctiles):
            dense_ref[r * BLK : (r + 1) * BLK, c * BLK : (c + 1) * BLK] = acc_ref[c].astype(BF16)


def build_picks(send_ref, counts_ref, picks_ref):
    parts = send_ref.shape[0]
    nodes = picks_ref.shape[0]
    lane = lax.broadcasted_iota(jnp.int32, (1, BLK), 1)
    rows = lax.broadcasted_iota(jnp.int32, (nodes, BLK), 0)
    for q in range(parts):
        wanted = jnp.where(lane < counts_ref[0, q], send_ref[q : q + 1, :], -1)
        hit = rows == wanted
        picks_ref[:, q * BLK : (q + 1) * BLK] = jnp.where(hit, 1.0, 0.0).astype(BF16)


def prepare_body(cot_ref, mix_ref, send_ref, counts_ref, cols_ref, vals_ref,
                 dense_ref, picks_ref, cot_out, base_ref, pieces_ref,
                 acc_ref, map_ref, g_ref):
    nodes = cot_ref.shape[1]
    parts = send_ref.shape[0]
    c = mix_ref.shape[1]
    build_tiles(cols_ref, vals_ref, acc_ref, dense_ref)
    build_picks(send_ref, counts_ref, picks_ref)
    wide = cot_ref[...].astype(F32).T
    wide = jnp.concatenate([jnp.zeros((nodes, c), F32), wide], axis=1).astype(BF16)
    cot_out[...] = wide
    pairs = cot_out.shape[1] // 128
    block_map(mix_ref, 2, map_ref)
    m = map_ref[...]
    for k in range(pairs):
        g_ref[:, pair(k)] = dot_t1(cot_out[:, pair(k)], m).astype(BF16)
    block_map(mix_ref, 1, map_ref)
    m = map_ref[...]
    g = g_ref[...]
    pack_rows(g, dense_ref, nodes, parts, pieces_ref)
    base_ref[...] = dot_t0(dense_ref[:, :nodes], g)
    for k in range(pairs):
        base_ref[:, pair(k)] += dot_t1(cot_out[:, pair(k)], m)


def pack_rows(values, table_ref, start, parts, out_ref):
    flipped = values.astype(F32).T.astype(BF16)
    for q in range(parts):
        table = table_ref[:, start + q * BLK : start + (q + 1) * BLK]
        out_ref[q] = dot(flipped, table).astype(BF16)


def from_blocks(total, table_ref, start, parts, arrived_ref):
    for q in range(parts):
        table = table_ref[:, start + q * BLK : start + (q + 1) * BLK]
        total = total + dot_t1(table, arrived_ref[q])
    return total


def forward_part(x_ref, conv1_ref, conv2_ref, first_ref, hidden_ref, band_ref):
    pairs = x_ref.shape[1] // 128
    band_map(conv1_ref, 1, band_ref)
    b = band_ref[...]
    for k in range(pairs):
        filt, gates = activations(dot(earlier(x_ref, k), b))
        first_ref[:, pair(k)] = (filt * gates).astype(BF16)
    band_map(conv2_ref, 2, band_ref)
    b = band_ref[...]
    for k in range(1, pairs):
        filt, gates = activations(dot(earlier(first_ref, k), b))
        hidden_ref[:, pair(k - 1)] = (filt * gates).astype(BF16)


def gate_grad(pre, up):
    filt, gates = activations(pre)
    d_filt = up * gates * (1.0 - filt * filt)
    d_gate = up * filt * gates * (1.0 - gates)
    return jnp.concatenate([d_filt, d_gate], axis=1).astype(BF16)


def backward_part(x_ref, first_ref, cot_ref, conv1_ref, conv2_ref, grad_ref, g1_ref, g2_ref,
                  band_ref, up_ref, mid_ref):
    pairs = x_ref.shape[1] // 128
    band_map(conv2_ref, 2, band_ref)
    b = band_ref[...]
    total = None
    carry = None
    for k in range(1, pairs):
        both = earlier(first_ref, k)
        d = gate_grad(dot(both, b), up_ref[:, pair(k - 1)])
        part = dot_t0(both, d)
        total = part if total is None else total + part
        back = dot_t1(d, b)
        low = back[:, :128] if carry is None else carry + back[:, :128]
        mid_ref[:, pair(k - 1)] = low.astype(BF16)
        carry = back[:, 128:]
    mid_ref[:, pair(pairs - 1)] = carry.astype(BF16)
    band_grad(total, 2, g2_ref)
    band_map(conv1_ref, 1, band_ref)
    b = band_ref[...]
    total = None
    carry = None
    for k in range(pairs):
        both = earlier(x_ref, k)
        d = gate_grad(dot(both, b), mid_ref[:, pair(k)].astype(F32))
        part = dot_t0(both, d)
        total = part if total is None else total + part
        back = dot_t1(d, b)
        if k > 0:
            low = carry + back[:, :128]
            if k > 1:
                low = low + cot_ref[:, pair(k - 2)].astype(F32)
            grad_ref[:, pair(k - 1)] = low.astype(BF16)
        carry = back[:, 128:]
    last = carry + cot_ref[:, pair(pairs - 2)].astype(F32)
    grad_ref[:, pair(pairs - 1)] = last.astype(BF16)
    band_grad(total, 1, g1_ref)


def mix_grad(term_ref, cot_ref, c):
    acc = None
    for k in range(cot_ref.shape[1] // 128):
        part = dot_t0(term_ref[:, pair(k)], cot_ref[:, pair(k)])
        acc = part if acc is None else acc + part
    return acc[:c, :c] + acc[c:, c:]


def early_part(hidden_ref, hop_ref, x_ref, cot_ref, mix_ref, gm_ref, map0, map1, wide_ref):
    c = mix_ref.shape[1]
    block_map(mix_ref, 0, map0)
    block_map(mix_ref, 1, map1)
    for k in range(cot_ref.shape[1] // 128):
        acc = x_ref[:, pair(k + 1)].astype(F32)
        acc = acc + dot(hidden_ref[:, pair(k)], map0[...])
        wide_ref[:, pair(k)] = acc + dot(hop_ref[:, pair(k)], map1[...])
    gm_ref[0] = mix_grad(hidden_ref, cot_ref, c)
    gm_ref[1] = mix_grad(hop_ref, cot_ref, c)


def main_body(parts, reps, scale,
              x_ref, cot_ref, conv1_ref, conv2_ref, mix_ref, dense_ref, picks_ref, base_ref,
              pieces_ref,
              out_ref, grad_ref, sum_ref,
              first_ref, hidden_ref, hop_ref, second_ref, up_ref, mid_ref, band_ref,
              map0, map1, map2, g1_ref, g2_ref, gm_ref,
              wide_ref, send1, send2, send3, recv0, recv1, recv2, recv3,
              pack_ref, got_ref, part_ref, reps_ref, sums_ref,
              ssem, rsem, asem, arsem, bsem, brsem):
    me = lax.axis_index("dom")
    mine = lax.axis_index("rep")
    nodes = x_ref.shape[0]
    c = mix_ref.shape[1]
    pairs = cot_ref.shape[1] // 128
    feats = cot_ref.shape[1]

    barrier = pltpu.get_barrier_semaphore()
    for o in range(1, parts):
        pl.semaphore_signal(barrier, inc=1, device_id={"dom": lax.rem(me + o, parts)},
                            device_id_type=pl.DeviceIdType.MESH)
    for o in range(1, reps):
        pl.semaphore_signal(barrier, inc=1, device_id={"rep": lax.rem(mine + o, reps)},
                            device_id_type=pl.DeviceIdType.MESH)
    pl.semaphore_wait(barrier, parts - 1 + reps - 1)

    def copies(level, src, dst):
        made = []
        for o in sorted(range(1, parts), key=lambda o: abs(2 * o - parts)):
            peer = lax.rem(me + o, parts)
            made.append(pltpu.make_async_remote_copy(
                src_ref=src.at[peer, pl.ds(c, feats - c)],
                dst_ref=dst.at[me, pl.ds(c, feats - c)],
                send_sem=ssem.at[level, o],
                recv_sem=rsem.at[level, o],
                device_id={"dom": peer},
                device_id_type=pl.DeviceIdType.MESH,
            ))
        for m in made:
            m.start()
        return made

    def arrive(made):
        for m in made:
            m.wait_recv()

    round0 = copies(0, pieces_ref, recv0)
    for buf in (recv0, recv1, recv2, recv3):
        buf[:, 0:c, :] = jnp.zeros((parts, c, BLK), BF16)
        buf[me] = jnp.zeros((feats, BLK), BF16)

    forward_part(x_ref, conv1_ref, conv2_ref, first_ref, hidden_ref, band_ref)
    pack_rows(hidden_ref[...], picks_ref, 0, parts, send1)
    round1 = copies(1, send1, recv1)

    arrive(round0)
    g = from_blocks(base_ref[...], picks_ref, 0, parts, recv0).astype(BF16)
    pack_rows(g, dense_ref, nodes, parts, send2)
    round2 = copies(2, send2, recv2)
    up_ref[...] = dot_t0(dense_ref[:, :nodes], g)
    block_map(mix_ref, 0, map0)
    for k in range(pairs):
        up_ref[:, pair(k)] += dot_t1(cot_ref[:, pair(k)], map0[...])

    own = dot(dense_ref[:, :nodes], hidden_ref[...])
    arrive(round1)
    hop_ref[...] = from_blocks(own, dense_ref, nodes, parts, recv1).astype(BF16)
    pack_rows(hop_ref[...], picks_ref, 0, parts, send3)
    round3 = copies(3, send3, recv3)

    arrive(round2)
    up_ref[...] = from_blocks(up_ref[...], picks_ref, 0, parts, recv2)
    backward_part(x_ref, first_ref, cot_ref, conv1_ref, conv2_ref, grad_ref, g1_ref, g2_ref,
                  band_ref, up_ref, mid_ref)

    early_part(hidden_ref, hop_ref, x_ref, cot_ref, mix_ref, gm_ref, map0, map1, wide_ref)
    block_map(mix_ref, 2, map2)
    own = dot(dense_ref[:, :nodes], hop_ref[...])
    arrive(round3)
    second_ref[...] = from_blocks(own, dense_ref, nodes, parts, recv3).astype(BF16)
    gm_ref[2] = mix_grad(second_ref, cot_ref, c)

    per = pack_ref.shape[1]
    flat = pack_ref
    flat[...] = jnp.zeros(flat.shape, F32)

    def put(first_row, value):
        rows = value.shape[0]
        done = 0
        while done < rows:
            slot, at = divmod(first_row + done, per)
            step = min(per - at, rows - done)
            flat[slot, at : at + step, :] = value[done : done + step]
            done += step

    put(0, g1_ref[0])
    put(c, g1_ref[1])
    put(2 * c, g2_ref[0])
    put(3 * c, g2_ref[1])
    put(4 * c, jnp.concatenate([gm_ref[0], gm_ref[1]], axis=1))
    put(5 * c, jnp.concatenate([gm_ref[2], jnp.zeros((c, c), F32)], axis=1))

    scatter = []
    for o in range(1, parts):
        peer = lax.rem(me + o, parts)
        scatter.append(pltpu.make_async_remote_copy(
            src_ref=pack_ref.at[peer], dst_ref=got_ref.at[me],
            send_sem=asem.at[0, o], recv_sem=arsem.at[0, o],
            device_id={"dom": peer}, device_id_type=pl.DeviceIdType.MESH))
    for m in scatter:
        m.start()
    for k in range(pairs):
        wide_ref[:, pair(k)] += dot(second_ref[:, pair(k)], map2[...])
    out_ref[...] = wide_ref[...].T[c:].astype(BF16)
    got_ref[me] = pack_ref[me]
    arrive(scatter)
    total = got_ref[0]
    for q in range(1, parts):
        total = total + got_ref[q]
    part_ref[...] = total
    around = []
    for o in range(1, reps):
        peer = lax.rem(mine + o, reps)
        around.append(pltpu.make_async_remote_copy(
            src_ref=part_ref, dst_ref=reps_ref.at[mine],
            send_sem=bsem.at[o], recv_sem=brsem.at[o],
            device_id={"rep": peer}, device_id_type=pl.DeviceIdType.MESH))
    for m in around:
        m.start()
    reps_ref[mine] = total
    arrive(around)
    total = reps_ref[0]
    for q in range(1, reps):
        total = total + reps_ref[q]
    for m in around:
        m.wait_send()
    part_ref[...] = total * (1.0 / scale)
    final = []
    for o in range(1, parts):
        peer = lax.rem(me + o, parts)
        final.append(pltpu.make_async_remote_copy(
            src_ref=part_ref, dst_ref=sums_ref.at[me],
            send_sem=asem.at[1, o], recv_sem=arsem.at[1, o],
            device_id={"dom": peer}, device_id_type=pl.DeviceIdType.MESH))
    for m in final:
        m.start()
    sums_ref[me] = part_ref[...]
    arrive(final)

    sum_ref[...] = sums_ref[...]
    for m in round0 + round1 + round2 + round3 + scatter + final:
        m.wait_send()


def shards(inputs, cotangent, conv_one, conv_two, mix_weight, send_rows, counts, tile_cols,
           tile_vals):
    windows, nodes, flat = inputs.shape
    channels = mix_weight.shape[1]
    parts = lax.axis_size("dom")
    reps = lax.axis_size("rep")
    kept = flat // channels - 3
    wide = flat - 2 * channels
    halo = parts * BLK
    blocks = (parts, wide, BLK)
    prepared = [((nodes, nodes + halo), BF16), ((nodes, halo), BF16), ((nodes, wide), BF16),
                ((nodes, wide), F32), (blocks, BF16)]
    dense, picks, cot_wide, base, pieces = pl.pallas_call(
        prepare_body,
        out_shape=[jax.ShapeDtypeStruct(s, d) for s, d in prepared],
        in_specs=[VM, VM, VM, SM, SM, VM],
        out_specs=[VM] * 5,
        scratch_shapes=[pltpu.VMEM((parts + nodes // BLK, BLK, BLK), F32),
                        pltpu.VMEM((128, 128), BF16), pltpu.VMEM((nodes, wide), BF16)],
        compiler_params=LIMIT,
        name="prepare",
    )(cotangent[0].T, mix_weight, send_rows[0], counts, tile_cols, tile_vals)
    scaling = math.sqrt(float(windows * reps * nodes * parts * kept))
    unit = 8 * parts
    per = -(-6 * channels // unit) * unit // parts
    results = [((kept * channels, nodes), BF16), ((nodes, flat), BF16), ((parts, per, BLK), F32)]
    scratch = [((nodes, flat), BF16), ((nodes, wide), BF16), ((nodes, wide), BF16),
               ((nodes, wide), BF16), ((nodes, wide), F32), ((nodes, flat), BF16),
               ((256, 256), BF16), ((128, 128), BF16), ((128, 128), BF16), ((128, 128), BF16),
               (conv_one.shape, F32), (conv_two.shape, F32), (mix_weight.shape, F32)]
    scratch += [((nodes, wide), F32)] + [(blocks, BF16)] * 7
    scratch += [((parts, per, BLK), F32), ((parts, per, BLK), F32), ((per, BLK), F32),
                ((reps, per, BLK), F32), ((parts, per, BLK), F32)]
    dma = pltpu.SemaphoreType.DMA
    output, grad_input, packed = pl.pallas_call(
        functools.partial(main_body, parts, reps, scaling),
        out_shape=[jax.ShapeDtypeStruct(s, d) for s, d in results],
        in_specs=[VM] * 9,
        out_specs=[VM] * 3,
        scratch_shapes=[pltpu.VMEM(s, d) for s, d in scratch]
        + [dma((4, parts)), dma((4, parts)), dma((2, parts)), dma((2, parts)), dma((reps,)),
           dma((reps,))],
        compiler_params=pltpu.CompilerParams(
            vmem_limit_bytes=60 * 1024 * 1024, collective_id=0, has_side_effects=True),
        name="layer",
    )(inputs[0], cot_wide, conv_one, conv_two, mix_weight, dense, picks, base, pieces)
    c = channels
    rows = packed.reshape(parts * per, BLK)
    gm = jnp.stack([rows[4 * c : 5 * c, :c], rows[4 * c : 5 * c, c:], rows[5 * c : 6 * c, :c]])
    return (
        output.T[None],
        grad_input[None],
        rows[: 2 * c].reshape(conv_one.shape),
        rows[2 * c : 4 * c].reshape(conv_two.shape),
        gm,
    )


def place_tiles(me, parts, cols_ref, vals_ref, dense_ref):
    rtiles, slots = vals_ref.shape[0], vals_ref.shape[1]
    for r in range(rtiles):
        for c in range(dense_ref.shape[1] // BLK):
            named = c if c < rtiles else rtiles + lax.rem(me - (c - rtiles + 1) + parts, parts)
            total = None
            for j in range(slots):
                keep = jnp.where(cols_ref[r, j] == named, 1.0, 0.0)
                part = vals_ref[r, j].astype(F32) * keep
                total = part if total is None else total + part
            dense_ref[r * BLK : (r + 1) * BLK, c * BLK : (c + 1) * BLK] = total.astype(BF16)


def chunk(first, size):
    return pl.ds(pl.multiple_of(first, size), size)


def steps_body(parts, reps, scale,
               x_ref, cot_ref, conv1_ref, conv2_ref, mix_ref, send_ref, counts_ref, cols_ref, vals_ref,
               out_ref, grad_ref, one_out, two_out, mix_out,
               dense_ref, wanted_ref, xt_ref, first_ref, hid_ref, d1_ref, d2_ref, mid_ref,
               band1, band1t, band2, band2t, maps, mapst,
               adj_ref, lists_ref, picks_ref,
               cf_ref, hf_ref, f1_ref, c1_ref, own_ref, part_t, ext_ref,
               gh_ref, mx_ref, ghs_ref, mxs_ref,
               g1_ref, g2_ref, pack0, got0, half0, reps0, full0, sums0,
               pack1, got1, half1, reps1, full1, sums1,
               lsend, lrecv, fsend, frecv, esend, erecv, tsend, trecv,
               asem, arsem, bsem, brsem):
    me = lax.axis_index("dom")
    mine = lax.axis_index("rep")
    nodes = x_ref.shape[0]
    c = mix_ref.shape[1]
    pairs = x_ref.shape[1] // 128
    rows = nodes // reps
    mesh_ids = pl.DeviceIdType.MESH
    holder = lax.rem(parts // 2 - reps // 2 + mine + parts, parts)
    extra = parts * c
    zs = parts // 2
    z, xx = me // 2, lax.rem(me, 2)
    yy, core = mine // 2, lax.rem(mine, 2)

    barrier = pltpu.get_barrier_semaphore()
    for o in range(1, parts):
        pl.semaphore_signal(barrier, inc=1, device_id={"dom": lax.rem(me + o, parts)},
                            device_id_type=mesh_ids)
    for o in range(1, reps):
        pl.semaphore_signal(barrier, inc=1, device_id={"rep": lax.rem(mine + o, reps)},
                            device_id_type=mesh_ids)
    place_tiles(me, parts, cols_ref, vals_ref, dense_ref)
    lane = lax.broadcasted_iota(jnp.int32, (1, BLK), 1)
    for o in range(parts):
        t = lax.rem(me + o, parts)
        wanted_ref[o : o + 1, :] = jnp.where(
            lane < counts_ref[0, t], send_ref[pl.ds(t, 1), :], -1)
    pl.semaphore_wait(barrier, parts - 1 + reps - 1)

    def remote(src, dst, ssem, rsem, **where):
        return pltpu.make_async_remote_copy(
            src_ref=src, dst_ref=dst, send_sem=ssem, recv_sem=rsem,
            device_id=where, device_id_type=mesh_ids)

    order = sorted(range(1, parts), key=lambda o: abs(2 * o - parts))

    def piece(p, r):
        return adj_ref.at[p, chunk(r * rows, rows)]

    def source_z(t, way):
        return z - t if way == 0 else z + t

    def valid(t, way):
        if t == 0:
            return z >= 0
        return z >= t if way == 0 else z + t < zs

    def slot(t, way):
        return 0 if t == 0 else 2 * t - 1 + way

    def base(t, way):
        return source_z(t, way) * 2 + xx

    def cross(t, way):
        return source_z(t, way) * 2 + 1 - xx

    yrep = (1 - yy) * 2 + core
    crep = yy * 2 + 1 - core
    cyrep = (1 - yy) * 2 + 1 - core

    def along(t, way, out_way):
        src = dense_ref.at[chunk(mine * rows, rows)] if t == 0 else piece(base(t, way), mine)
        to = (z + 1 if out_way == 0 else z - 1) * 2 + xx
        return remote(src, piece(base(t, way), mine), tsend.at[out_way, slot(t, way)],
                      trecv.at[0, slot(t + 1, out_way)], dom=to)

    def across(t, way):
        src = dense_ref.at[chunk(mine * rows, rows)] if t == 0 else piece(base(t, way), mine)
        return remote(src, piece(base(t, way), mine), tsend.at[2, slot(t, way)],
                      trecv.at[2, slot(t, way)], dom=z * 2 + 1 - xx)

    def hand(kind, p, r, t, way, to):
        return remote(piece(p, r), piece(p, r), tsend.at[kind, slot(t, way)],
                      trecv.at[kind, slot(t, way)], rep=to)

    def arrived(kind, p, r, t, way, **where):
        remote(piece(p, r), piece(p, r), tsend.at[kind, slot(t, way)],
               trecv.at[kind, slot(t, way)], **where).wait_recv()

    def ways(t):
        return (0,) if t == 0 else (0, 1)

    def lane_sends(t, way):
        made = []
        outs = (0, 1) if t == 0 else (way,)
        for w in outs:
            made.append((z + 1 < zs if w == 0 else z >= 1, along(t, way, w)))
        made.append((None, across(t, way)))
        return made

    def base_sends(t, way):
        return [] if t == 0 else [(None, hand(3, base(t, way), mine, t, way, yrep)),
                                  (None, hand(4, base(t, way), mine, t, way, crep))]

    def cross_sends(t, way):
        return [(None, hand(5, cross(t, way), mine, t, way, yrep)),
                (None, hand(6, cross(t, way), mine, t, way, crep))]

    def ybase_sends(t, way):
        return [] if t == 0 else [(None, hand(7, base(t, way), yrep, t, way, crep))]

    def ycross_sends(t, way):
        return [(None, hand(8, cross(t, way), yrep, t, way, crep))]

    def go(sends, wait=False):
        for cond, copy in sends:
            act = copy.wait_send if wait else copy.start
            if cond is None:
                act()
            else:
                pl.when(cond)(act)

    def on_base(t, way):
        @pl.when(valid(t, way))
        def _():
            arrived(0, base(t, way), mine, t, way, rep=crep)
            go(lane_sends(t, way) + base_sends(t, way))

    def on_cross(t, way):
        @pl.when(valid(t, way))
        def _():
            arrived(2, cross(t, way), mine, t, way, rep=crep)
            go(cross_sends(t, way))

    def on_ybase(t, way):
        @pl.when(valid(t, way))
        def _():
            arrived(3, base(t, way), yrep, t, way, rep=crep)
            go(ybase_sends(t, way))

    def on_ycross(t, way):
        @pl.when(valid(t, way))
        def _():
            arrived(5, cross(t, way), yrep, t, way, rep=crep)
            go(ycross_sends(t, way))

    relay = []
    for s in range(1, zs + 2):
        for handler, t, least in ((on_base, s, 1), (on_cross, s - 1, 0), (on_ybase, s - 1, 1),
                                  (on_ycross, s - 2, 0)):
            if least <= t < zs:
                for w in ways(t):
                    relay.append(functools.partial(handler, t, w))
    relay.reverse()

    def step_relay(count=1):
        for _ in range(count):
            if relay:
                relay.pop()()

    def scatter_field(level, src, first, dst):
        made = []
        for o in order:
            peer = lax.rem(me + o, parts)
            made.append(remote(src.at[chunk(first + peer * c, c)], dst.at[me, pl.ds(0, c)],
                               fsend.at[level, o], frecv.at[level, o], dom=peer))
        for m in made:
            m.start()
        off = lax.rem(holder - me + parts, parts)
        last = remote(src.at[pl.ds(first + extra, c)], dst.at[me, pl.ds(c, c)],
                      esend.at[level, 0], erecv.at[level, off], dom=holder)
        pl.when(me != holder)(last.start)
        dst[me, 0:c, :] = src[chunk(first + me * c, c), :]

        @pl.when(me == holder)
        def _():
            dst[me, c : 2 * c, :] = src[first + extra : first + extra + c, :]

        @pl.when(me != holder)
        def _():
            dst[:, c : 2 * c, :] = jnp.zeros((parts, c, nodes), BF16)
        return made, last

    def field_arrives(level, made, src, dst):
        for m in made:
            m.wait_recv()

        @pl.when(me == holder)
        def _():
            for o in range(1, parts):
                q = lax.rem(me - o + parts, parts)
                remote(dst.at[q, pl.ds(c, c)], dst.at[q, pl.ds(c, c)], esend.at[level, 0],
                       erecv.at[level, o], dom=q).wait_recv()

    def home_copies(level, o, src, first, dst):
        q = lax.rem(me + o, parts)
        one = remote(src.at[q, pl.ds(0, c)], dst.at[chunk(first + me * c, c)],
                     fsend.at[level, o], frecv.at[level, o], dom=q)
        two = remote(src.at[q, pl.ds(c, c)], dst.at[pl.ds(first + extra, c)],
                     esend.at[level, o], erecv.at[level, 0], dom=q)
        return one, two

    def go_home(level, o, src, first, dst):
        if o:
            one, two = home_copies(level, o, src, first, dst)
            one.start()
            pl.when(me == holder)(two.start)
            return
        dst[chunk(first + me * c, c), :] = src[me, 0:c, :]

        @pl.when(me == holder)
        def _():
            dst[first + extra : first + extra + c, :] = src[me, c : 2 * c, :]

    def home_arrives(level, src, first, dst):
        for o in range(1, parts):
            home_copies(level, o, src, first, dst)[0].wait_recv()
        pl.when(me != holder)(home_copies(level, 1, src, first, dst)[1].wait_recv)

    def home_sent(level, src, first, dst):
        for o in range(1, parts):
            one, two = home_copies(level, o, src, first, dst)
            one.wait_send()
            pl.when(me == holder)(two.wait_send)

    go(lane_sends(0, 0))
    cot_round = scatter_field(0, cot_ref, 0, cf_ref)
    lists = []
    for o in order:
        peer = lax.rem(me + o, parts)
        lists.append(remote(wanted_ref, lists_ref.at[me], lsend.at[o], lrecv.at[o], dom=peer))
    for m in lists:
        m.start()
    lists_ref[me] = wanted_ref[...]
    adj_ref[me] = dense_ref[...]

    for k in range(pairs):
        xt_ref[pair(k), :] = x_ref[:, pair(k)].astype(F32).T.astype(BF16)
    for conv, dil, nat, tra in ((conv1_ref, 1, band1, band1t), (conv2_ref, 2, band2, band2t)):
        band_map(conv, dil, nat)
        tra[...] = nat[...].astype(F32).T.astype(BF16)

    def earlier_t(ref, k):
        if k == 0:
            v = ref[0:128, :]
            return jnp.concatenate([jnp.zeros_like(v), v], axis=0)
        return ref[window2(k - 1), :]

    def gated(pre, d_ref, k):
        filt = jnp.tanh(pre[:128])
        gates = 0.5 * jnp.tanh(0.5 * pre[128:]) + 0.5
        d_ref[k, 0:128, :] = gates * (1.0 - filt * filt)
        d_ref[k, 128:256, :] = filt * gates * (1.0 - gates)
        return (filt * gates).astype(BF16)

    for k in range(pairs):
        first_ref[pair(k), :] = gated(dot(band1t[...], earlier_t(xt_ref, k)), d1_ref, k)
        if k % 2:
            step_relay()
    for k in range(1, pairs):
        hid_ref[pair(k - 1), :] = gated(dot(band2t[...], earlier_t(first_ref, k)), d2_ref, k)
        step_relay()
    hid_round = scatter_field(1, hid_ref, c, hf_ref)
    step_relay()

    for i in range(3):
        block_map(mix_ref, i, maps.at[i])
        mapst[i] = maps[i].astype(F32).T.astype(BF16)
    gh_ref[0:c, :] = jnp.zeros((c, nodes), BF16)

    for m in lists:
        m.wait_recv()
    node = lax.broadcasted_iota(jnp.int32, (nodes, BLK), 0)
    for q in range(parts):
        for o in range(1, parts):
            hit = node == lists_ref[q, o : o + 1, :]
            picks_ref[q, :, (o - 1) * BLK : o * BLK] = jnp.where(hit, 1.0, 0.0).astype(BF16)
        step_relay(2)

    field_arrives(0, cot_round[0], cot_ref, cf_ref)
    step_relay(len(relay))
    for t in range(zs):
        for w in ways(t):
            @pl.when(valid(t, w))
            def _():
                if t:
                    arrived(4, base(t, w), crep, t, w, rep=crep)
                    arrived(7, base(t, w), cyrep, t, w, rep=crep)
                arrived(6, cross(t, w), crep, t, w, rep=crep)
                arrived(8, cross(t, w), cyrep, t, w, rep=crep)

    def back_pieces(g_ref):
        for p in range(parts):
            t = dot(g_ref[p], adj_ref[p])
            own_ref[p] = t[:, :nodes]
            for o in range(1, parts):
                at = nodes + (o - 1) * BLK
                part_t[(p - o) % parts, :, (o - 1) * BLK : o * BLK] = t[:, at : at + BLK].astype(BF16)

    def back_owner(q):
        return (own_ref[q] + dot_t1(part_t[q], picks_ref[q])).astype(BF16)

    back_pieces(cf_ref)
    for q in range(parts):
        c1_ref[q] = back_owner(q)
    back_pieces(c1_ref)
    field_arrives(1, hid_round[0], hid_ref, hf_ref)
    mix = [None] * 3
    for o in order + [0]:
        q = lax.rem(me + o, parts)
        moved = (cf_ref[q], c1_ref[q], back_owner(q))
        grads = [dot(maps[i], moved[i]) for i in range(3)]
        ghs_ref[q] = (grads[0] + grads[1] + grads[2]).astype(BF16)
        go_home(2, o, ghs_ref, c, gh_ref)
        for i in range(3):
            more = dot_t1(hf_ref[q], moved[i])
            mix[i] = more if mix[i] is None else mix[i] + more
    mix = [m[:c, :c] + m[c:, c:] for m in mix]

    def reducer(g, pack, got, half, total_reps, full, sums):
        def around_dom(stage, src_of, dst):
            return [remote(src_of(lax.rem(me + o, parts)), dst.at[me], asem.at[2 * g + stage, o],
                           arsem.at[2 * g + stage, o], dom=lax.rem(me + o, parts)) for o in order]

        def around_rep():
            return [remote(half, total_reps.at[mine], bsem.at[g, o], brsem.at[g, o],
                           rep=lax.rem(mine + o, reps)) for o in range(1, reps)]

        def shares():
            return around_dom(0, lambda peer: pack.at[peer], got)

        def back():
            return around_dom(1, lambda peer: full, sums)

        def first():
            for m in shares():
                m.start()
            got[me] = pack[me]

        def second():
            for m in shares():
                m.wait_recv()
            total = got[0]
            for q in range(1, parts):
                total = total + got[q]
            half[...] = total
            for m in around_rep():
                m.start()
            total_reps[mine] = total

        def third():
            for m in around_rep():
                m.wait_recv()
            total = total_reps[0]
            for q in range(1, reps):
                total = total + total_reps[q]
            full[...] = total * (1.0 / scale)
            for m in back():
                m.start()
            sums[me] = full[...]

        def last():
            for m in back():
                m.wait_recv()

        def sent():
            for m in shares() + around_rep() + back():
                m.wait_send()

        return first, second, third, last, sent

    def put(pack, first_row, value):
        per = pack.shape[1]
        count, done = value.shape[0], 0
        while done < count:
            place, at = divmod(first_row + done, per)
            step = min(per - at, count - done)
            pack[place, at : at + step, :] = value[done : done + step]
            done += step

    early = reducer(0, pack0, got0, half0, reps0, full0, sums0)
    late = reducer(1, pack1, got1, half1, reps1, full1, sums1)
    put(pack0, 0, jnp.concatenate([mix[0], mix[1]], axis=1))
    put(pack0, c, jnp.concatenate([mix[2], jnp.zeros((c, c), F32)], axis=1))
    early[0]()

    def extend(f_ref):
        for q in range(parts):
            ext_ref[q, :, 0:nodes] = f_ref[q]
            halo = dot(f_ref[q], picks_ref[q]).astype(BF16)
            for o in range(1, parts):
                at = nodes + (o - 1) * BLK
                ext_ref[(q + o) % parts, :, at : at + BLK] = halo[:, (o - 1) * BLK : o * BLK]

    extend(hf_ref)
    for p in range(parts):
        f1_ref[p] = dot_t1(ext_ref[p], adj_ref[p]).astype(BF16)
    early[1]()
    extend(f1_ref)
    for o in order + [0]:
        q = lax.rem(me + o, parts)
        second = dot_t1(ext_ref[q], adj_ref[q]).astype(BF16)
        mixed = dot(mapst[0], hf_ref[q]) + dot(mapst[1], f1_ref[q]) + dot(mapst[2], second)
        mxs_ref[q] = mixed.astype(BF16)
        go_home(3, o, mxs_ref, 0, mx_ref)
    early[2]()

    home_arrives(2, ghs_ref, c, gh_ref)

    def conv_back(sig_ref, d_ref, up_of, band, low_of, first_pair, dilation, out):
        total, carry = None, None
        b = band[...]
        for k in range(first_pair, pairs):
            up = up_of(k)
            both = earlier_t(sig_ref, k)
            d = jnp.concatenate([up * d_ref[k, 0:128, :], up * d_ref[k, 128:256, :]], axis=0)
            d = d.astype(BF16)
            part = dot_t1(both, d)
            total = part if total is None else total + part
            back = dot(b, d)
            if k > 0:
                low_of(k - 1, back[:128] if carry is None else carry + back[:128])
            carry = back[128:]
        low_of(pairs - 1, carry)
        band_grad(total, dilation, out)

    def set_mid(k, low):
        mid_ref[pair(k), :] = low.astype(BF16)

    def set_grad(k, low):
        if k == 1:
            low = low + jnp.concatenate([jnp.zeros((c, nodes), F32), cot_ref[0:c, :].astype(F32)], axis=0)
        elif k > 1:
            low = low + cot_ref[(2 * k - 3) * c : (2 * k - 1) * c, :].astype(F32)
        grad_ref[:, pair(k)] = low.T.astype(BF16)

    conv_back(first_ref, d2_ref, lambda k: gh_ref[pair(k - 1), :].astype(F32), band2, set_mid, 1, 2, g2_ref)
    conv_back(xt_ref, d1_ref, lambda k: mid_ref[pair(k), :].astype(F32), band1, set_grad, 0, 1, g1_ref)

    for tap in range(2):
        put(pack1, tap * c, g1_ref[tap])
        put(pack1, (2 + tap) * c, g2_ref[tap])
    late[0]()

    early[3]()
    per = sums0.shape[1]
    for i in range(2 * c // per):
        block, at = divmod(i * per, c)
        for j in range(2 - block):
            mix_out[2 * block + j, at : at + per, :] = sums0[i, :, j * c : (j + 1) * c]
    late[1]()
    home_arrives(3, mxs_ref, 0, mx_ref)
    kept = out_ref.shape[0]
    out_ref[...] = (mx_ref[...].astype(F32) + xt_ref[pairs * 128 - kept :, :].astype(F32)).astype(BF16)
    late[2]()

    for m in cot_round[0] + hid_round[0] + lists:
        m.wait_send()
    pl.when(me != holder)(cot_round[1].wait_send)
    pl.when(me != holder)(hid_round[1].wait_send)
    home_sent(2, ghs_ref, c, gh_ref)
    home_sent(3, mxs_ref, 0, mx_ref)
    for t in range(zs):
        for w in ways(t):
            @pl.when(valid(t, w))
            def _():
                go(lane_sends(t, w) + base_sends(t, w) + cross_sends(t, w) + ybase_sends(t, w)
                   + ycross_sends(t, w), wait=True)
    late[3]()
    per = sums1.shape[1]
    for i in range(4 * c // per):
        tap, at = divmod(i * per, c)
        where = one_out if tap < 2 else two_out
        where[tap % 2, at : at + per, :] = sums1[i]
    early[4]()
    late[4]()


def finish_body(*refs):
    half = len(refs) // 2
    for a, b in zip(refs[:half], refs[half:]):
        b[...] = a[...]


def step_shards(inputs, cotangent, conv_one, conv_two, mix_weight, send_rows, counts, tile_cols,
                tile_vals):
    windows, nodes, flat = inputs.shape
    channels = mix_weight.shape[1]
    parts = lax.axis_size("dom")
    reps = lax.axis_size("rep")
    kept = flat // channels - 3
    c = channels
    pairs = flat // 128
    halo = (parts - 1) * BLK
    ext = nodes + halo
    scaling = math.sqrt(float(windows * reps * nodes * parts * kept))
    results = [((kept * c, nodes), BF16), ((nodes, flat), BF16), (conv_one.shape, F32),
               (conv_two.shape, F32), (mix_weight.shape, F32)]
    field = (parts, 2 * c, nodes)
    wide = flat - 2 * c
    scratch = [((nodes, ext), BF16), ((parts, BLK), jnp.int32),
               ((flat, nodes), BF16), ((flat, nodes), BF16), ((wide, nodes), BF16),
               ((pairs, 256, nodes), F32), ((pairs, 256, nodes), F32), ((flat, nodes), BF16)]
    scratch += [((256, 256), BF16)] * 4 + [((3, 128, 128), BF16)] * 2
    scratch += [((parts, nodes, ext), BF16), ((parts, parts, BLK), jnp.int32),
                ((parts, nodes, halo), BF16)]
    scratch += [(field, BF16)] * 4 + [(field, F32), ((parts, 2 * c, halo), BF16),
                                      ((parts, 2 * c, ext), BF16)]
    scratch += [((wide, nodes), BF16), ((kept * c, nodes), BF16), (field, BF16), (field, BF16)]
    scratch += [(conv_one.shape, F32), (conv_two.shape, F32)]
    for total in (2 * c, 4 * c):
        per = total // parts
        scratch += [((parts, per, BLK), F32), ((parts, per, BLK), F32), ((per, BLK), F32),
                    ((reps, per, BLK), F32), ((per, BLK), F32), ((parts, per, BLK), F32)]
    dma = pltpu.SemaphoreType.DMA
    sems = [(parts,), (parts,), (4, parts), (4, parts), (4, parts), (4, parts),
            (9, parts), (9, parts), (4, parts), (4, parts), (2, reps), (2, reps)]
    made = pl.pallas_call(
        functools.partial(steps_body, parts, reps, scaling),
        out_shape=[jax.ShapeDtypeStruct(s, d) for s, d in results],
        in_specs=[VM] * 6 + [SM, SM, VM],
        out_specs=[VM] * 5,
        scratch_shapes=[pltpu.VMEM(s, d) for s, d in scratch] + [dma(s) for s in sems],
        compiler_params=pltpu.CompilerParams(
            vmem_limit_bytes=60 * 1024 * 1024, collective_id=1, has_side_effects=True),
        name="steps",
    )(inputs[0], cotangent[0].T, conv_one, conv_two, mix_weight, send_rows[0], counts, tile_cols,
      tile_vals)
    output, grad_input, one, two, mix = pl.pallas_call(
        finish_body,
        out_shape=[jax.ShapeDtypeStruct(s, d) for s, d in results],
        in_specs=[VM] * 5,
        out_specs=[VM] * 5,
        compiler_params=LIMIT,
        name="finish",
    )(*made)
    return output.T[None], grad_input[None], one, two, mix


def solution(mesh):
    placed = (
        P("rep", "dom", None),
        P("rep", "dom", None),
        P(),
        P(),
        P(),
        P("dom", None, None),
        P("dom", None),
        P("dom", None),
        P("dom", None, None, None),
    )
    parts, reps = mesh.shape["dom"], mesh.shape["rep"]

    def layer(*args):
        kept = args[0].shape[2] // args[4].shape[1] - 3
        by_step = parts % 2 == 0 and reps == 4 and parts == kept - 1
        return step_shards(*args) if by_step else shards(*args)

    return jax.shard_map(
        layer,
        mesh=mesh,
        in_specs=placed,
        out_specs=(P("rep", "dom", None), P("rep", "dom", None), P(), P(), P()),
        check_vma=False,
    )
```

```python
import functools
import math

import jax
import jax.numpy as jnp
from jax import lax
from jax.experimental import pallas as pl
from jax.experimental.pallas import tpu as pltpu
from jax.sharding import PartitionSpec as P

F32 = jnp.float32
BF16 = jnp.bfloat16
BLK = 128
VM = pl.BlockSpec(memory_space=pltpu.VMEM)
SM = pl.BlockSpec(memory_space=pltpu.SMEM)
LIMIT = pltpu.CompilerParams(vmem_limit_bytes=56 * 1024 * 1024)


def dot(a, b):
    return jnp.dot(a, b, preferred_element_type=F32)


def dot_t0(a, b):
    return lax.dot_general(a, b, (((0,), (0,)), ((), ())), preferred_element_type=F32)


def dot_t1(a, b):
    return lax.dot_general(a, b, (((1,), (1,)), ((), ())), preferred_element_type=F32)


def pair(k):
    return slice(k * 128, (k + 1) * 128)


def window2(k):
    return slice(k * 128, (k + 2) * 128)


def block_map(weight_ref, index, out_ref):
    c = weight_ref.shape[1]
    w = weight_ref[index]
    out_ref[...] = jnp.zeros(out_ref.shape, BF16)
    out_ref[0:c, 0:c] = w
    out_ref[c : 2 * c, c : 2 * c] = w


def band_blocks(dilation):
    if dilation == 1:
        return ((0, 1, 0), (0, 2, 1), (1, 2, 0), (1, 3, 1))
    return ((0, 0, 0), (0, 1, 1), (1, 2, 0), (1, 3, 1))


def band_map(conv_ref, dilation, out_ref):
    c = conv_ref.shape[1]
    out_ref[...] = jnp.zeros(out_ref.shape, BF16)
    for tap, i, o in band_blocks(dilation):
        w = conv_ref[tap]
        rows = slice(i * c, (i + 1) * c)
        out_ref[rows, o * c : (o + 1) * c] = w[:, :c]
        out_ref[rows, (o + 2) * c : (o + 3) * c] = w[:, c:]


def band_grad(total, dilation, out_ref):
    c = out_ref.shape[1]
    for tap in range(2):
        for half in range(2):
            acc = None
            for t, i, o in band_blocks(dilation):
                if t != tap:
                    continue
                col = (o + 2 * half) * c
                part = total[i * c : (i + 1) * c, col : col + c]
                acc = part if acc is None else acc + part
            out_ref[tap, :, half * c : (half + 1) * c] = acc


def activations(pre):
    filt = jnp.tanh(pre[:, :128])
    gates = 0.5 * jnp.tanh(0.5 * pre[:, 128:]) + 0.5
    return filt, gates


def earlier(ref, k):
    if k == 0:
        x = ref[:, 0:128]
        return jnp.concatenate([jnp.zeros_like(x), x], axis=1)
    return ref[:, window2(k - 1)]


def build_tiles(cols_ref, vals_ref, acc_ref, dense_ref):
    rtiles, slots = vals_ref.shape[0], vals_ref.shape[1]
    ctiles = dense_ref.shape[1] // BLK
    for r in range(rtiles):
        acc_ref[...] = jnp.zeros(acc_ref.shape, F32)
        for j in range(slots):
            c = cols_ref[r, j]
            acc_ref[c] = acc_ref[c] + vals_ref[r, j].astype(F32)
        for c in range(ctiles):
            dense_ref[r * BLK : (r + 1) * BLK, c * BLK : (c + 1) * BLK] = acc_ref[c].astype(BF16)


def build_picks(send_ref, counts_ref, picks_ref):
    parts = send_ref.shape[0]
    nodes = picks_ref.shape[0]
    lane = lax.broadcasted_iota(jnp.int32, (1, BLK), 1)
    rows = lax.broadcasted_iota(jnp.int32, (nodes, BLK), 0)
    for q in range(parts):
        wanted = jnp.where(lane < counts_ref[0, q], send_ref[q : q + 1, :], -1)
        hit = rows == wanted
        picks_ref[:, q * BLK : (q + 1) * BLK] = jnp.where(hit, 1.0, 0.0).astype(BF16)


def prepare_body(cot_ref, mix_ref, send_ref, counts_ref, cols_ref, vals_ref,
                 dense_ref, picks_ref, cot_out, base_ref, pieces_ref,
                 acc_ref, map_ref, g_ref):
    nodes = cot_ref.shape[1]
    parts = send_ref.shape[0]
    c = mix_ref.shape[1]
    build_tiles(cols_ref, vals_ref, acc_ref, dense_ref)
    build_picks(send_ref, counts_ref, picks_ref)
    wide = cot_ref[...].astype(F32).T
    wide = jnp.concatenate([jnp.zeros((nodes, c), F32), wide], axis=1).astype(BF16)
    cot_out[...] = wide
    pairs = cot_out.shape[1] // 128
    block_map(mix_ref, 2, map_ref)
    m = map_ref[...]
    for k in range(pairs):
        g_ref[:, pair(k)] = dot_t1(cot_out[:, pair(k)], m).astype(BF16)
    block_map(mix_ref, 1, map_ref)
    m = map_ref[...]
    g = g_ref[...]
    pack_rows(g, dense_ref, nodes, parts, pieces_ref)
    base_ref[...] = dot_t0(dense_ref[:, :nodes], g)
    for k in range(pairs):
        base_ref[:, pair(k)] += dot_t1(cot_out[:, pair(k)], m)


def pack_rows(values, table_ref, start, parts, out_ref):
    flipped = values.astype(F32).T.astype(BF16)
    for q in range(parts):
        table = table_ref[:, start + q * BLK : start + (q + 1) * BLK]
        out_ref[q] = dot(flipped, table).astype(BF16)


def from_blocks(total, table_ref, start, parts, arrived_ref):
    for q in range(parts):
        table = table_ref[:, start + q * BLK : start + (q + 1) * BLK]
        total = total + dot_t1(table, arrived_ref[q])
    return total


def forward_part(x_ref, conv1_ref, conv2_ref, first_ref, hidden_ref, band_ref):
    pairs = x_ref.shape[1] // 128
    band_map(conv1_ref, 1, band_ref)
    b = band_ref[...]
    for k in range(pairs):
        filt, gates = activations(dot(earlier(x_ref, k), b))
        first_ref[:, pair(k)] = (filt * gates).astype(BF16)
    band_map(conv2_ref, 2, band_ref)
    b = band_ref[...]
    for k in range(1, pairs):
        filt, gates = activations(dot(earlier(first_ref, k), b))
        hidden_ref[:, pair(k - 1)] = (filt * gates).astype(BF16)


def gate_grad(pre, up):
    filt, gates = activations(pre)
    d_filt = up * gates * (1.0 - filt * filt)
    d_gate = up * filt * gates * (1.0 - gates)
    return jnp.concatenate([d_filt, d_gate], axis=1).astype(BF16)


def backward_part(x_ref, first_ref, cot_ref, conv1_ref, conv2_ref, grad_ref, g1_ref, g2_ref,
                  band_ref, up_ref, mid_ref):
    pairs = x_ref.shape[1] // 128
    band_map(conv2_ref, 2, band_ref)
    b = band_ref[...]
    total = None
    carry = None
    for k in range(1, pairs):
        both = earlier(first_ref, k)
        d = gate_grad(dot(both, b), up_ref[:, pair(k - 1)])
        part = dot_t0(both, d)
        total = part if total is None else total + part
        back = dot_t1(d, b)
        low = back[:, :128] if carry is None else carry + back[:, :128]
        mid_ref[:, pair(k - 1)] = low.astype(BF16)
        carry = back[:, 128:]
    mid_ref[:, pair(pairs - 1)] = carry.astype(BF16)
    band_grad(total, 2, g2_ref)
    band_map(conv1_ref, 1, band_ref)
    b = band_ref[...]
    total = None
    carry = None
    for k in range(pairs):
        both = earlier(x_ref, k)
        d = gate_grad(dot(both, b), mid_ref[:, pair(k)].astype(F32))
        part = dot_t0(both, d)
        total = part if total is None else total + part
        back = dot_t1(d, b)
        if k > 0:
            low = carry + back[:, :128]
            if k > 1:
                low = low + cot_ref[:, pair(k - 2)].astype(F32)
            grad_ref[:, pair(k - 1)] = low.astype(BF16)
        carry = back[:, 128:]
    last = carry + cot_ref[:, pair(pairs - 2)].astype(F32)
    grad_ref[:, pair(pairs - 1)] = last.astype(BF16)
    band_grad(total, 1, g1_ref)


def mix_grad(term_ref, cot_ref, c):
    acc = None
    for k in range(cot_ref.shape[1] // 128):
        part = dot_t0(term_ref[:, pair(k)], cot_ref[:, pair(k)])
        acc = part if acc is None else acc + part
    return acc[:c, :c] + acc[c:, c:]


def early_part(hidden_ref, hop_ref, x_ref, cot_ref, mix_ref, gm_ref, map0, map1, wide_ref):
    c = mix_ref.shape[1]
    block_map(mix_ref, 0, map0)
    block_map(mix_ref, 1, map1)
    for k in range(cot_ref.shape[1] // 128):
        acc = x_ref[:, pair(k + 1)].astype(F32)
        acc = acc + dot(hidden_ref[:, pair(k)], map0[...])
        wide_ref[:, pair(k)] = acc + dot(hop_ref[:, pair(k)], map1[...])
    gm_ref[0] = mix_grad(hidden_ref, cot_ref, c)
    gm_ref[1] = mix_grad(hop_ref, cot_ref, c)


def main_body(parts, reps, scale,
              x_ref, cot_ref, conv1_ref, conv2_ref, mix_ref, dense_ref, picks_ref, base_ref,
              pieces_ref,
              out_ref, grad_ref, sum_ref,
              first_ref, hidden_ref, hop_ref, second_ref, up_ref, mid_ref, band_ref,
              map0, map1, map2, g1_ref, g2_ref, gm_ref,
              wide_ref, send1, send2, send3, recv0, recv1, recv2, recv3,
              pack_ref, got_ref, part_ref, reps_ref, sums_ref,
              ssem, rsem, asem, arsem, bsem, brsem):
    me = lax.axis_index("dom")
    mine = lax.axis_index("rep")
    nodes = x_ref.shape[0]
    c = mix_ref.shape[1]
    pairs = cot_ref.shape[1] // 128
    feats = cot_ref.shape[1]

    barrier = pltpu.get_barrier_semaphore()
    for o in range(1, parts):
        pl.semaphore_signal(barrier, inc=1, device_id={"dom": lax.rem(me + o, parts)},
                            device_id_type=pl.DeviceIdType.MESH)
    for o in range(1, reps):
        pl.semaphore_signal(barrier, inc=1, device_id={"rep": lax.rem(mine + o, reps)},
                            device_id_type=pl.DeviceIdType.MESH)
    pl.semaphore_wait(barrier, parts - 1 + reps - 1)

    def copies(level, src, dst):
        made = []
        for o in sorted(range(1, parts), key=lambda o: abs(2 * o - parts)):
            peer = lax.rem(me + o, parts)
            made.append(pltpu.make_async_remote_copy(
                src_ref=src.at[peer, pl.ds(c, feats - c)],
                dst_ref=dst.at[me, pl.ds(c, feats - c)],
                send_sem=ssem.at[level, o],
                recv_sem=rsem.at[level, o],
                device_id={"dom": peer},
                device_id_type=pl.DeviceIdType.MESH,
            ))
        for m in made:
            m.start()
        return made

    def arrive(made):
        for m in made:
            m.wait_recv()

    round0 = copies(0, pieces_ref, recv0)
    for buf in (recv0, recv1, recv2, recv3):
        buf[:, 0:c, :] = jnp.zeros((parts, c, BLK), BF16)
        buf[me] = jnp.zeros((feats, BLK), BF16)

    forward_part(x_ref, conv1_ref, conv2_ref, first_ref, hidden_ref, band_ref)
    pack_rows(hidden_ref[...], picks_ref, 0, parts, send1)
    round1 = copies(1, send1, recv1)

    arrive(round0)
    g = from_blocks(base_ref[...], picks_ref, 0, parts, recv0).astype(BF16)
    pack_rows(g, dense_ref, nodes, parts, send2)
    round2 = copies(2, send2, recv2)
    up_ref[...] = dot_t0(dense_ref[:, :nodes], g)
    block_map(mix_ref, 0, map0)
    for k in range(pairs):
        up_ref[:, pair(k)] += dot_t1(cot_ref[:, pair(k)], map0[...])

    own = dot(dense_ref[:, :nodes], hidden_ref[...])
    arrive(round1)
    hop_ref[...] = from_blocks(own, dense_ref, nodes, parts, recv1).astype(BF16)
    pack_rows(hop_ref[...], picks_ref, 0, parts, send3)
    round3 = copies(3, send3, recv3)

    arrive(round2)
    up_ref[...] = from_blocks(up_ref[...], picks_ref, 0, parts, recv2)
    backward_part(x_ref, first_ref, cot_ref, conv1_ref, conv2_ref, grad_ref, g1_ref, g2_ref,
                  band_ref, up_ref, mid_ref)

    early_part(hidden_ref, hop_ref, x_ref, cot_ref, mix_ref, gm_ref, map0, map1, wide_ref)
    block_map(mix_ref, 2, map2)
    own = dot(dense_ref[:, :nodes], hop_ref[...])
    arrive(round3)
    second_ref[...] = from_blocks(own, dense_ref, nodes, parts, recv3).astype(BF16)
    gm_ref[2] = mix_grad(second_ref, cot_ref, c)

    per = pack_ref.shape[1]
    flat = pack_ref
    flat[...] = jnp.zeros(flat.shape, F32)

    def put(first_row, value):
        rows = value.shape[0]
        done = 0
        while done < rows:
            slot, at = divmod(first_row + done, per)
            step = min(per - at, rows - done)
            flat[slot, at : at + step, :] = value[done : done + step]
            done += step

    put(0, g1_ref[0])
    put(c, g1_ref[1])
    put(2 * c, g2_ref[0])
    put(3 * c, g2_ref[1])
    put(4 * c, jnp.concatenate([gm_ref[0], gm_ref[1]], axis=1))
    put(5 * c, jnp.concatenate([gm_ref[2], jnp.zeros((c, c), F32)], axis=1))

    scatter = []
    for o in range(1, parts):
        peer = lax.rem(me + o, parts)
        scatter.append(pltpu.make_async_remote_copy(
            src_ref=pack_ref.at[peer], dst_ref=got_ref.at[me],
            send_sem=asem.at[0, o], recv_sem=arsem.at[0, o],
            device_id={"dom": peer}, device_id_type=pl.DeviceIdType.MESH))
    for m in scatter:
        m.start()
    for k in range(pairs):
        wide_ref[:, pair(k)] += dot(second_ref[:, pair(k)], map2[...])
    out_ref[...] = wide_ref[...].T[c:].astype(BF16)
    got_ref[me] = pack_ref[me]
    arrive(scatter)
    total = got_ref[0]
    for q in range(1, parts):
        total = total + got_ref[q]
    part_ref[...] = total
    around = []
    for o in range(1, reps):
        peer = lax.rem(mine + o, reps)
        around.append(pltpu.make_async_remote_copy(
            src_ref=part_ref, dst_ref=reps_ref.at[mine],
            send_sem=bsem.at[o], recv_sem=brsem.at[o],
            device_id={"rep": peer}, device_id_type=pl.DeviceIdType.MESH))
    for m in around:
        m.start()
    reps_ref[mine] = total
    arrive(around)
    total = reps_ref[0]
    for q in range(1, reps):
        total = total + reps_ref[q]
    for m in around:
        m.wait_send()
    part_ref[...] = total * (1.0 / scale)
    final = []
    for o in range(1, parts):
        peer = lax.rem(me + o, parts)
        final.append(pltpu.make_async_remote_copy(
            src_ref=part_ref, dst_ref=sums_ref.at[me],
            send_sem=asem.at[1, o], recv_sem=arsem.at[1, o],
            device_id={"dom": peer}, device_id_type=pl.DeviceIdType.MESH))
    for m in final:
        m.start()
    sums_ref[me] = part_ref[...]
    arrive(final)

    sum_ref[...] = sums_ref[...]
    for m in round0 + round1 + round2 + round3 + scatter + final:
        m.wait_send()


def shards(inputs, cotangent, conv_one, conv_two, mix_weight, send_rows, counts, tile_cols,
           tile_vals):
    windows, nodes, flat = inputs.shape
    channels = mix_weight.shape[1]
    parts = lax.axis_size("dom")
    reps = lax.axis_size("rep")
    kept = flat // channels - 3
    wide = flat - 2 * channels
    halo = parts * BLK
    blocks = (parts, wide, BLK)
    prepared = [((nodes, nodes + halo), BF16), ((nodes, halo), BF16), ((nodes, wide), BF16),
                ((nodes, wide), F32), (blocks, BF16)]
    dense, picks, cot_wide, base, pieces = pl.pallas_call(
        prepare_body,
        out_shape=[jax.ShapeDtypeStruct(s, d) for s, d in prepared],
        in_specs=[VM, VM, VM, SM, SM, VM],
        out_specs=[VM] * 5,
        scratch_shapes=[pltpu.VMEM((parts + nodes // BLK, BLK, BLK), F32),
                        pltpu.VMEM((128, 128), BF16), pltpu.VMEM((nodes, wide), BF16)],
        compiler_params=LIMIT,
        name="prepare",
    )(cotangent[0].T, mix_weight, send_rows[0], counts, tile_cols, tile_vals)
    scaling = math.sqrt(float(windows * reps * nodes * parts * kept))
    unit = 8 * parts
    per = -(-6 * channels // unit) * unit // parts
    results = [((kept * channels, nodes), BF16), ((nodes, flat), BF16), ((parts, per, BLK), F32)]
    scratch = [((nodes, flat), BF16), ((nodes, wide), BF16), ((nodes, wide), BF16),
               ((nodes, wide), BF16), ((nodes, wide), F32), ((nodes, flat), BF16),
               ((256, 256), BF16), ((128, 128), BF16), ((128, 128), BF16), ((128, 128), BF16),
               (conv_one.shape, F32), (conv_two.shape, F32), (mix_weight.shape, F32)]
    scratch += [((nodes, wide), F32)] + [(blocks, BF16)] * 7
    scratch += [((parts, per, BLK), F32), ((parts, per, BLK), F32), ((per, BLK), F32),
                ((reps, per, BLK), F32), ((parts, per, BLK), F32)]
    dma = pltpu.SemaphoreType.DMA
    output, grad_input, packed = pl.pallas_call(
        functools.partial(main_body, parts, reps, scaling),
        out_shape=[jax.ShapeDtypeStruct(s, d) for s, d in results],
        in_specs=[VM] * 9,
        out_specs=[VM] * 3,
        scratch_shapes=[pltpu.VMEM(s, d) for s, d in scratch]
        + [dma((4, parts)), dma((4, parts)), dma((2, parts)), dma((2, parts)), dma((reps,)),
           dma((reps,))],
        compiler_params=pltpu.CompilerParams(
            vmem_limit_bytes=60 * 1024 * 1024, collective_id=0, has_side_effects=True),
        name="layer",
    )(inputs[0], cot_wide, conv_one, conv_two, mix_weight, dense, picks, base, pieces)
    c = channels
    rows = packed.reshape(parts * per, BLK)
    gm = jnp.stack([rows[4 * c : 5 * c, :c], rows[4 * c : 5 * c, c:], rows[5 * c : 6 * c, :c]])
    return (
        output.T[None],
        grad_input[None],
        rows[: 2 * c].reshape(conv_one.shape),
        rows[2 * c : 4 * c].reshape(conv_two.shape),
        gm,
    )


def place_tiles(me, parts, cols_ref, vals_ref, dense_ref):
    rtiles, slots = vals_ref.shape[0], vals_ref.shape[1]
    for r in range(rtiles):
        for c in range(dense_ref.shape[1] // BLK):
            named = c if c < rtiles else rtiles + lax.rem(me - (c - rtiles + 1) + parts, parts)
            total = None
            for j in range(slots):
                keep = jnp.where(cols_ref[r, j] == named, 1.0, 0.0)
                part = vals_ref[r, j].astype(F32) * keep
                total = part if total is None else total + part
            dense_ref[r * BLK : (r + 1) * BLK, c * BLK : (c + 1) * BLK] = total.astype(BF16)


def chunk(first, size):
    return pl.ds(pl.multiple_of(first, size), size)


def steps_body(parts, reps, scale,
               x_ref, cot_ref, conv1_ref, conv2_ref, mix_ref, send_ref, counts_ref, cols_ref, vals_ref,
               out_ref, grad_ref, one_out, two_out, mix_out,
               dense_ref, wanted_ref, xt_ref, first_ref, hid_ref, d1_ref, d2_ref, mid_ref,
               band1, band1t, band2, band2t, maps, mapst,
               adj_ref, lists_ref, picks_ref,
               cf_ref, hf_ref, f1_ref, c1_ref, own_ref, part_t, ext_ref,
               gh_ref, mx_ref, ghs_ref, mxs_ref,
               g1_ref, g2_ref, pack0, got0, half0, dom0, full0, sums0,
               pack1, got1, half1, dom1, full1, sums1,
               lsend, lrecv, fsend, frecv, esend, erecv, tsend, trecv,
               asem, arsem, bsem, brsem):
    me = lax.axis_index("dom")
    mine = lax.axis_index("rep")
    nodes = x_ref.shape[0]
    c = mix_ref.shape[1]
    pairs = x_ref.shape[1] // 128
    rows = nodes // reps
    mesh_ids = pl.DeviceIdType.MESH
    holder = lax.rem(parts // 2 - reps // 2 + mine + parts, parts)
    extra = parts * c
    zs = parts // 2
    z, xx = me // 2, lax.rem(me, 2)
    yy, core = mine // 2, lax.rem(mine, 2)

    barrier = pltpu.get_barrier_semaphore()
    for o in range(1, parts):
        pl.semaphore_signal(barrier, inc=1, device_id={"dom": lax.rem(me + o, parts)},
                            device_id_type=mesh_ids)
    for o in range(1, reps):
        pl.semaphore_signal(barrier, inc=1, device_id={"rep": lax.rem(mine + o, reps)},
                            device_id_type=mesh_ids)
    place_tiles(me, parts, cols_ref, vals_ref, dense_ref)
    lane = lax.broadcasted_iota(jnp.int32, (1, BLK), 1)
    for o in range(parts):
        t = lax.rem(me + o, parts)
        wanted_ref[o : o + 1, :] = jnp.where(
            lane < counts_ref[0, t], send_ref[pl.ds(t, 1), :], -1)
    pl.semaphore_wait(barrier, parts - 1 + reps - 1)

    def remote(src, dst, ssem, rsem, **where):
        return pltpu.make_async_remote_copy(
            src_ref=src, dst_ref=dst, send_sem=ssem, recv_sem=rsem,
            device_id=where, device_id_type=mesh_ids)

    order = sorted(range(1, parts), key=lambda o: abs(2 * o - parts))

    def piece(p, r):
        return adj_ref.at[p, chunk(r * rows, rows)]

    def source_z(t, way):
        return z - t if way == 0 else z + t

    def valid(t, way):
        if t == 0:
            return z >= 0
        return z >= t if way == 0 else z + t < zs

    def slot(t, way):
        return 0 if t == 0 else 2 * t - 1 + way

    def base(t, way):
        return source_z(t, way) * 2 + xx

    def cross(t, way):
        return source_z(t, way) * 2 + 1 - xx

    yrep = (1 - yy) * 2 + core
    crep = yy * 2 + 1 - core
    cyrep = (1 - yy) * 2 + 1 - core

    def along(t, way, out_way):
        src = dense_ref.at[chunk(mine * rows, rows)] if t == 0 else piece(base(t, way), mine)
        to = (z + 1 if out_way == 0 else z - 1) * 2 + xx
        return remote(src, piece(base(t, way), mine), tsend.at[out_way, slot(t, way)],
                      trecv.at[0, slot(t + 1, out_way)], dom=to)

    def across(t, way):
        src = dense_ref.at[chunk(mine * rows, rows)] if t == 0 else piece(base(t, way), mine)
        return remote(src, piece(base(t, way), mine), tsend.at[2, slot(t, way)],
                      trecv.at[2, slot(t, way)], dom=z * 2 + 1 - xx)

    def hand(kind, p, r, t, way, to):
        return remote(piece(p, r), piece(p, r), tsend.at[kind, slot(t, way)],
                      trecv.at[kind, slot(t, way)], rep=to)

    def arrived(kind, p, r, t, way, **where):
        remote(piece(p, r), piece(p, r), tsend.at[kind, slot(t, way)],
               trecv.at[kind, slot(t, way)], **where).wait_recv()

    def ways(t):
        return (0,) if t == 0 else (0, 1)

    def lane_sends(t, way):
        made = []
        outs = (0, 1) if t == 0 else (way,)
        for w in outs:
            made.append((z + 1 < zs if w == 0 else z >= 1, along(t, way, w)))
        made.append((None, across(t, way)))
        return made

    def base_sends(t, way):
        return [] if t == 0 else [(None, hand(3, base(t, way), mine, t, way, yrep)),
                                  (None, hand(4, base(t, way), mine, t, way, crep))]

    def cross_sends(t, way):
        return [(None, hand(5, cross(t, way), mine, t, way, yrep)),
                (None, hand(6, cross(t, way), mine, t, way, crep))]

    def ybase_sends(t, way):
        return [] if t == 0 else [(None, hand(7, base(t, way), yrep, t, way, crep))]

    def ycross_sends(t, way):
        return [(None, hand(8, cross(t, way), yrep, t, way, crep))]

    def go(sends, wait=False):
        for cond, copy in sends:
            act = copy.wait_send if wait else copy.start
            if cond is None:
                act()
            else:
                pl.when(cond)(act)

    def on_base(t, way):
        @pl.when(valid(t, way))
        def _():
            arrived(0, base(t, way), mine, t, way, rep=crep)
            go(lane_sends(t, way) + base_sends(t, way))

    def on_cross(t, way):
        @pl.when(valid(t, way))
        def _():
            arrived(2, cross(t, way), mine, t, way, rep=crep)
            go(cross_sends(t, way))

    def on_ybase(t, way):
        @pl.when(valid(t, way))
        def _():
            arrived(3, base(t, way), yrep, t, way, rep=crep)
            go(ybase_sends(t, way))

    def on_ycross(t, way):
        @pl.when(valid(t, way))
        def _():
            arrived(5, cross(t, way), yrep, t, way, rep=crep)
            go(ycross_sends(t, way))

    relay = []
    for s in range(1, zs + 2):
        for handler, t, least in ((on_base, s, 1), (on_cross, s - 1, 0), (on_ybase, s - 1, 1),
                                  (on_ycross, s - 2, 0)):
            if least <= t < zs:
                for w in ways(t):
                    relay.append(functools.partial(handler, t, w))
    relay.reverse()

    def step_relay(count=1):
        for _ in range(count):
            if relay:
                relay.pop()()

    def scatter_field(level, src, first, dst):
        made = []
        for o in order:
            peer = lax.rem(me + o, parts)
            made.append(remote(src.at[chunk(first + peer * c, c)], dst.at[me, pl.ds(0, c)],
                               fsend.at[level, o], frecv.at[level, o], dom=peer))
        for m in made:
            m.start()
        off = lax.rem(holder - me + parts, parts)
        last = remote(src.at[pl.ds(first + extra, c)], dst.at[me, pl.ds(c, c)],
                      esend.at[level, 0], erecv.at[level, off], dom=holder)
        pl.when(me != holder)(last.start)
        dst[me, 0:c, :] = src[chunk(first + me * c, c), :]

        @pl.when(me == holder)
        def _():
            dst[me, c : 2 * c, :] = src[first + extra : first + extra + c, :]

        @pl.when(me != holder)
        def _():
            dst[:, c : 2 * c, :] = jnp.zeros((parts, c, nodes), BF16)
        return made, last

    def field_arrives(level, made, src, dst):
        for m in made:
            m.wait_recv()

        @pl.when(me == holder)
        def _():
            for o in range(1, parts):
                q = lax.rem(me - o + parts, parts)
                remote(dst.at[q, pl.ds(c, c)], dst.at[q, pl.ds(c, c)], esend.at[level, 0],
                       erecv.at[level, o], dom=q).wait_recv()

    def home_copies(level, o, src, first, dst):
        q = lax.rem(me + o, parts)
        one = remote(src.at[q, pl.ds(0, c)], dst.at[chunk(first + me * c, c)],
                     fsend.at[level, o], frecv.at[level, o], dom=q)
        two = remote(src.at[q, pl.ds(c, c)], dst.at[pl.ds(first + extra, c)],
                     esend.at[level, o], erecv.at[level, 0], dom=q)
        return one, two

    def go_home(level, o, src, first, dst):
        if o:
            one, two = home_copies(level, o, src, first, dst)
            one.start()
            pl.when(me == holder)(two.start)
            return
        dst[chunk(first + me * c, c), :] = src[me, 0:c, :]

        @pl.when(me == holder)
        def _():
            dst[first + extra : first + extra + c, :] = src[me, c : 2 * c, :]

    def home_arrives(level, src, first, dst):
        for o in range(1, parts):
            home_copies(level, o, src, first, dst)[0].wait_recv()
        pl.when(me != holder)(home_copies(level, 1, src, first, dst)[1].wait_recv)

    def home_sent(level, src, first, dst):
        for o in range(1, parts):
            one, two = home_copies(level, o, src, first, dst)
            one.wait_send()
            pl.when(me == holder)(two.wait_send)

    go(lane_sends(0, 0))
    cot_round = scatter_field(0, cot_ref, 0, cf_ref)
    lists = []
    for o in order:
        peer = lax.rem(me + o, parts)
        lists.append(remote(wanted_ref, lists_ref.at[me], lsend.at[o], lrecv.at[o], dom=peer))
    for m in lists:
        m.start()
    lists_ref[me] = wanted_ref[...]
    adj_ref[me] = dense_ref[...]

    for k in range(pairs):
        xt_ref[pair(k), :] = x_ref[:, pair(k)].astype(F32).T.astype(BF16)
    for conv, dil, nat, tra in ((conv1_ref, 1, band1, band1t), (conv2_ref, 2, band2, band2t)):
        band_map(conv, dil, nat)
        tra[...] = nat[...].astype(F32).T.astype(BF16)

    def earlier_t(ref, k):
        if k == 0:
            v = ref[0:128, :]
            return jnp.concatenate([jnp.zeros_like(v), v], axis=0)
        return ref[window2(k - 1), :]

    def gated(pre, d_ref, k):
        filt = jnp.tanh(pre[:128])
        gates = 0.5 * jnp.tanh(0.5 * pre[128:]) + 0.5
        d_ref[k, 0:128, :] = gates * (1.0 - filt * filt)
        d_ref[k, 128:256, :] = filt * gates * (1.0 - gates)
        return (filt * gates).astype(BF16)

    for k in range(pairs):
        first_ref[pair(k), :] = gated(dot(band1t[...], earlier_t(xt_ref, k)), d1_ref, k)
        if k % 2:
            step_relay()
    for k in range(1, pairs):
        hid_ref[pair(k - 1), :] = gated(dot(band2t[...], earlier_t(first_ref, k)), d2_ref, k)
        step_relay()
    hid_round = scatter_field(1, hid_ref, c, hf_ref)
    step_relay()

    for i in range(3):
        block_map(mix_ref, i, maps.at[i])
        mapst[i] = maps[i].astype(F32).T.astype(BF16)
    gh_ref[0:c, :] = jnp.zeros((c, nodes), BF16)

    for m in lists:
        m.wait_recv()
    node = lax.broadcasted_iota(jnp.int32, (nodes, BLK), 0)
    for q in range(parts):
        for o in range(1, parts):
            hit = node == lists_ref[q, o : o + 1, :]
            picks_ref[q, :, (o - 1) * BLK : o * BLK] = jnp.where(hit, 1.0, 0.0).astype(BF16)
        step_relay(2)

    field_arrives(0, cot_round[0], cot_ref, cf_ref)
    step_relay(len(relay))
    for t in range(zs):
        for w in ways(t):
            @pl.when(valid(t, w))
            def _():
                if t:
                    arrived(4, base(t, w), crep, t, w, rep=crep)
                    arrived(7, base(t, w), cyrep, t, w, rep=crep)
                arrived(6, cross(t, w), crep, t, w, rep=crep)
                arrived(8, cross(t, w), cyrep, t, w, rep=crep)

    def back_pieces(g_ref):
        for p in range(parts):
            t = dot(g_ref[p], adj_ref[p])
            own_ref[p] = t[:, :nodes]
            for o in range(1, parts):
                at = nodes + (o - 1) * BLK
                part_t[(p - o) % parts, :, (o - 1) * BLK : o * BLK] = t[:, at : at + BLK].astype(BF16)

    def back_owner(q):
        return (own_ref[q] + dot_t1(part_t[q], picks_ref[q])).astype(BF16)

    back_pieces(cf_ref)
    for q in range(parts):
        c1_ref[q] = back_owner(q)
    back_pieces(c1_ref)
    field_arrives(1, hid_round[0], hid_ref, hf_ref)
    mix = [None] * 3
    for o in order + [0]:
        q = lax.rem(me + o, parts)
        moved = (cf_ref[q], c1_ref[q], back_owner(q))
        grads = [dot(maps[i], moved[i]) for i in range(3)]
        ghs_ref[q] = (grads[0] + grads[1] + grads[2]).astype(BF16)
        go_home(2, o, ghs_ref, c, gh_ref)
        for i in range(3):
            more = dot_t1(hf_ref[q], moved[i])
            mix[i] = more if mix[i] is None else mix[i] + more
    mix = [m[:c, :c] + m[c:, c:] for m in mix]

    def reducer(g, pack, got, half, got_dom, full, sums):
        def over_rep(stage, src_of, dst):
            return [remote(src_of(lax.rem(mine + o, reps)), dst.at[mine], bsem.at[2 * g + stage, o],
                           brsem.at[2 * g + stage, o], rep=lax.rem(mine + o, reps)) for o in range(1, reps)]

        def over_dom(stage, src_of, dst):
            return [remote(src_of(lax.rem(me + o, parts)), dst, asem.at[2 * g + stage, o],
                           arsem.at[2 * g + stage, o], dom=lax.rem(me + o, parts)) for o in order]

        steps = (lambda: over_rep(0, lambda peer: pack.at[peer], got),
                 lambda: over_dom(0, lambda peer: half.at[peer], got_dom.at[me]),
                 lambda: over_dom(1, lambda peer: full, sums.at[mine, me]),
                 lambda: over_rep(1, lambda peer: sums.at[mine], sums))

        def start(i):
            for m in steps[i]():
                m.start()

        def arrive(i):
            for m in steps[i]():
                m.wait_recv()

        def first():
            start(0)
            got[mine] = pack[mine]

        def second():
            arrive(0)
            total = got[0]
            for q in range(1, reps):
                total = total + got[q]
            share = half.shape[1]
            for q in range(parts):
                half[q] = total[q * share : (q + 1) * share]
            start(1)
            got_dom[me] = half[me]

        def third():
            arrive(1)
            total = got_dom[0]
            for q in range(1, parts):
                total = total + got_dom[q]
            full[...] = total * (1.0 / scale)
            start(2)
            sums[mine, me] = full[...]

        def fourth():
            arrive(2)
            start(3)

        def last():
            arrive(3)

        def sent():
            for i in range(4):
                for m in steps[i]():
                    m.wait_send()

        return first, second, third, fourth, last, sent

    early = reducer(0, pack0, got0, half0, dom0, full0, sums0)
    late = reducer(1, pack1, got1, half1, dom1, full1, sums1)
    pack0[...] = jnp.zeros(pack0.shape, F32)
    for i in range(3):
        pack0[i, :, 0:c] = mix[i]
    early[0]()

    def extend(f_ref):
        for q in range(parts):
            ext_ref[q, :, 0:nodes] = f_ref[q]
            halo = dot(f_ref[q], picks_ref[q]).astype(BF16)
            for o in range(1, parts):
                at = nodes + (o - 1) * BLK
                ext_ref[(q + o) % parts, :, at : at + BLK] = halo[:, (o - 1) * BLK : o * BLK]

    extend(hf_ref)
    for p in range(parts):
        f1_ref[p] = dot_t1(ext_ref[p], adj_ref[p]).astype(BF16)
    early[1]()
    extend(f1_ref)
    for o in order + [0]:
        q = lax.rem(me + o, parts)
        second = dot_t1(ext_ref[q], adj_ref[q]).astype(BF16)
        mixed = dot(mapst[0], hf_ref[q]) + dot(mapst[1], f1_ref[q]) + dot(mapst[2], second)
        mxs_ref[q] = mixed.astype(BF16)
        go_home(3, o, mxs_ref, 0, mx_ref)
    early[2]()

    home_arrives(2, ghs_ref, c, gh_ref)

    def conv_back(sig_ref, d_ref, up_of, band, low_of, first_pair, dilation, out):
        total, carry = None, None
        b = band[...]
        for k in range(first_pair, pairs):
            up = up_of(k)
            both = earlier_t(sig_ref, k)
            d = jnp.concatenate([up * d_ref[k, 0:128, :], up * d_ref[k, 128:256, :]], axis=0)
            d = d.astype(BF16)
            part = dot_t1(both, d)
            total = part if total is None else total + part
            back = dot(b, d)
            if k > 0:
                low_of(k - 1, back[:128] if carry is None else carry + back[:128])
            carry = back[128:]
        low_of(pairs - 1, carry)
        band_grad(total, dilation, out)

    def set_mid(k, low):
        mid_ref[pair(k), :] = low.astype(BF16)

    def set_grad(k, low):
        if k == 1:
            low = low + jnp.concatenate([jnp.zeros((c, nodes), F32), cot_ref[0:c, :].astype(F32)], axis=0)
        elif k > 1:
            low = low + cot_ref[(2 * k - 3) * c : (2 * k - 1) * c, :].astype(F32)
        grad_ref[:, pair(k)] = low.T.astype(BF16)

    conv_back(first_ref, d2_ref, lambda k: gh_ref[pair(k - 1), :].astype(F32), band2, set_mid, 1, 2, g2_ref)
    early[3]()
    conv_back(xt_ref, d1_ref, lambda k: mid_ref[pair(k), :].astype(F32), band1, set_grad, 0, 1, g1_ref)

    for tap in range(2):
        pack1[tap] = g1_ref[tap]
        pack1[2 + tap] = g2_ref[tap]
    late[0]()
    early[4]()
    share = sums0.shape[2]
    for d in range(parts):
        for i in range(3):
            mix_out[i, d * share : (d + 1) * share, :] = sums0[i, d, :, 0:c]
    late[1]()
    home_arrives(3, mxs_ref, 0, mx_ref)
    kept = out_ref.shape[0]
    out_ref[...] = (mx_ref[...].astype(F32) + xt_ref[pairs * 128 - kept :, :].astype(F32)).astype(BF16)
    late[2]()

    for m in cot_round[0] + hid_round[0] + lists:
        m.wait_send()
    pl.when(me != holder)(cot_round[1].wait_send)
    pl.when(me != holder)(hid_round[1].wait_send)
    home_sent(2, ghs_ref, c, gh_ref)
    home_sent(3, mxs_ref, 0, mx_ref)
    for t in range(zs):
        for w in ways(t):
            @pl.when(valid(t, w))
            def _():
                go(lane_sends(t, w) + base_sends(t, w) + cross_sends(t, w) + ybase_sends(t, w)
                   + ycross_sends(t, w), wait=True)
    late[3]()
    early[5]()
    late[4]()
    for d in range(parts):
        for tap in range(2):
            one_out[tap, d * share : (d + 1) * share, :] = sums1[tap, d]
            two_out[tap, d * share : (d + 1) * share, :] = sums1[2 + tap, d]
    late[5]()


def finish_body(*refs):
    half = len(refs) // 2
    for a, b in zip(refs[:half], refs[half:]):
        b[...] = a[...]


def step_shards(inputs, cotangent, conv_one, conv_two, mix_weight, send_rows, counts, tile_cols,
                tile_vals):
    windows, nodes, flat = inputs.shape
    channels = mix_weight.shape[1]
    parts = lax.axis_size("dom")
    reps = lax.axis_size("rep")
    kept = flat // channels - 3
    c = channels
    pairs = flat // 128
    halo = (parts - 1) * BLK
    ext = nodes + halo
    scaling = math.sqrt(float(windows * reps * nodes * parts * kept))
    results = [((kept * c, nodes), BF16), ((nodes, flat), BF16), (conv_one.shape, F32),
               (conv_two.shape, F32), (mix_weight.shape, F32)]
    field = (parts, 2 * c, nodes)
    wide = flat - 2 * c
    scratch = [((nodes, ext), BF16), ((parts, BLK), jnp.int32),
               ((flat, nodes), BF16), ((flat, nodes), BF16), ((wide, nodes), BF16),
               ((pairs, 256, nodes), F32), ((pairs, 256, nodes), F32), ((flat, nodes), BF16)]
    scratch += [((256, 256), BF16)] * 4 + [((3, 128, 128), BF16)] * 2
    scratch += [((parts, nodes, ext), BF16), ((parts, parts, BLK), jnp.int32),
                ((parts, nodes, halo), BF16)]
    scratch += [(field, BF16)] * 4 + [(field, F32), ((parts, 2 * c, halo), BF16),
                                      ((parts, 2 * c, ext), BF16)]
    scratch += [((wide, nodes), BF16), ((kept * c, nodes), BF16), (field, BF16), (field, BF16)]
    scratch += [(conv_one.shape, F32), (conv_two.shape, F32)]
    share = c // parts
    for _ in range(2):
        scratch += [((reps, c, BLK), F32), ((reps, c, BLK), F32), ((parts, share, BLK), F32),
                    ((parts, share, BLK), F32), ((share, BLK), F32), ((reps, parts, share, BLK), F32)]
    dma = pltpu.SemaphoreType.DMA
    sems = [(parts,), (parts,), (4, parts), (4, parts), (4, parts), (4, parts),
            (9, parts), (9, parts), (4, parts), (4, parts), (4, reps), (4, reps)]
    made = pl.pallas_call(
        functools.partial(steps_body, parts, reps, scaling),
        out_shape=[jax.ShapeDtypeStruct(s, d) for s, d in results],
        in_specs=[VM] * 6 + [SM, SM, VM],
        out_specs=[VM] * 5,
        scratch_shapes=[pltpu.VMEM(s, d) for s, d in scratch] + [dma(s) for s in sems],
        compiler_params=pltpu.CompilerParams(
            vmem_limit_bytes=60 * 1024 * 1024, collective_id=1, has_side_effects=True),
        name="steps",
    )(inputs[0], cotangent[0].T, conv_one, conv_two, mix_weight, send_rows[0], counts, tile_cols,
      tile_vals)
    output, grad_input, one, two, mix = pl.pallas_call(
        finish_body,
        out_shape=[jax.ShapeDtypeStruct(s, d) for s, d in results],
        in_specs=[VM] * 5,
        out_specs=[VM] * 5,
        compiler_params=LIMIT,
        name="finish",
    )(*made)
    return output.T[None], grad_input[None], one, two, mix


def solution(mesh):
    placed = (
        P("rep", "dom", None),
        P("rep", "dom", None),
        P(),
        P(),
        P(),
        P("dom", None, None),
        P("dom", None),
        P("dom", None),
        P("dom", None, None, None),
    )
    parts, reps = mesh.shape["dom"], mesh.shape["rep"]

    def layer(*args):
        kept = args[0].shape[2] // args[4].shape[1] - 3
        by_step = parts % 2 == 0 and reps == 4 and parts == kept - 1
        return step_shards(*args) if by_step else shards(*args)

    return jax.shard_map(
        layer,
        mesh=mesh,
        in_specs=placed,
        out_specs=(P("rep", "dom", None), P("rep", "dom", None), P(), P(), P()),
        check_vma=False,
    )
```

```python
import functools
import math

import jax
import jax.numpy as jnp
from jax import lax
from jax.experimental import pallas as pl
from jax.experimental.pallas import tpu as pltpu
from jax.sharding import PartitionSpec as P

F32 = jnp.float32
BF16 = jnp.bfloat16
BLK = 128
VM = pl.BlockSpec(memory_space=pltpu.VMEM)
SM = pl.BlockSpec(memory_space=pltpu.SMEM)
LIMIT = pltpu.CompilerParams(vmem_limit_bytes=56 * 1024 * 1024)


def dot(a, b):
    return jnp.dot(a, b, preferred_element_type=F32)


def dot_t0(a, b):
    return lax.dot_general(a, b, (((0,), (0,)), ((), ())), preferred_element_type=F32)


def dot_t1(a, b):
    return lax.dot_general(a, b, (((1,), (1,)), ((), ())), preferred_element_type=F32)


def pair(k):
    return slice(k * 128, (k + 1) * 128)


def window2(k):
    return slice(k * 128, (k + 2) * 128)


def block_map(weight_ref, index, out_ref):
    c = weight_ref.shape[1]
    w = weight_ref[index]
    out_ref[...] = jnp.zeros(out_ref.shape, BF16)
    out_ref[0:c, 0:c] = w
    out_ref[c : 2 * c, c : 2 * c] = w


def band_blocks(dilation):
    if dilation == 1:
        return ((0, 1, 0), (0, 2, 1), (1, 2, 0), (1, 3, 1))
    return ((0, 0, 0), (0, 1, 1), (1, 2, 0), (1, 3, 1))


def band_map(conv_ref, dilation, out_ref):
    c = conv_ref.shape[1]
    out_ref[...] = jnp.zeros(out_ref.shape, BF16)
    for tap, i, o in band_blocks(dilation):
        w = conv_ref[tap]
        rows = slice(i * c, (i + 1) * c)
        out_ref[rows, o * c : (o + 1) * c] = w[:, :c]
        out_ref[rows, (o + 2) * c : (o + 3) * c] = w[:, c:]


def band_grad(total, dilation, out_ref):
    c = out_ref.shape[1]
    for tap in range(2):
        for half in range(2):
            acc = None
            for t, i, o in band_blocks(dilation):
                if t != tap:
                    continue
                col = (o + 2 * half) * c
                part = total[i * c : (i + 1) * c, col : col + c]
                acc = part if acc is None else acc + part
            out_ref[tap, :, half * c : (half + 1) * c] = acc


def activations(pre):
    filt = jnp.tanh(pre[:, :128])
    gates = 0.5 * jnp.tanh(0.5 * pre[:, 128:]) + 0.5
    return filt, gates


def earlier(ref, k):
    if k == 0:
        x = ref[:, 0:128]
        return jnp.concatenate([jnp.zeros_like(x), x], axis=1)
    return ref[:, window2(k - 1)]


def build_tiles(cols_ref, vals_ref, acc_ref, dense_ref):
    rtiles, slots = vals_ref.shape[0], vals_ref.shape[1]
    ctiles = dense_ref.shape[1] // BLK
    for r in range(rtiles):
        acc_ref[...] = jnp.zeros(acc_ref.shape, F32)
        for j in range(slots):
            c = cols_ref[r, j]
            acc_ref[c] = acc_ref[c] + vals_ref[r, j].astype(F32)
        for c in range(ctiles):
            dense_ref[r * BLK : (r + 1) * BLK, c * BLK : (c + 1) * BLK] = acc_ref[c].astype(BF16)


def build_picks(send_ref, counts_ref, picks_ref):
    parts = send_ref.shape[0]
    nodes = picks_ref.shape[0]
    lane = lax.broadcasted_iota(jnp.int32, (1, BLK), 1)
    rows = lax.broadcasted_iota(jnp.int32, (nodes, BLK), 0)
    for q in range(parts):
        wanted = jnp.where(lane < counts_ref[0, q], send_ref[q : q + 1, :], -1)
        hit = rows == wanted
        picks_ref[:, q * BLK : (q + 1) * BLK] = jnp.where(hit, 1.0, 0.0).astype(BF16)


def prepare_body(cot_ref, mix_ref, send_ref, counts_ref, cols_ref, vals_ref,
                 dense_ref, picks_ref, cot_out, base_ref, pieces_ref,
                 acc_ref, map_ref, g_ref):
    nodes = cot_ref.shape[1]
    parts = send_ref.shape[0]
    c = mix_ref.shape[1]
    build_tiles(cols_ref, vals_ref, acc_ref, dense_ref)
    build_picks(send_ref, counts_ref, picks_ref)
    wide = cot_ref[...].astype(F32).T
    wide = jnp.concatenate([jnp.zeros((nodes, c), F32), wide], axis=1).astype(BF16)
    cot_out[...] = wide
    pairs = cot_out.shape[1] // 128
    block_map(mix_ref, 2, map_ref)
    m = map_ref[...]
    for k in range(pairs):
        g_ref[:, pair(k)] = dot_t1(cot_out[:, pair(k)], m).astype(BF16)
    block_map(mix_ref, 1, map_ref)
    m = map_ref[...]
    g = g_ref[...]
    pack_rows(g, dense_ref, nodes, parts, pieces_ref)
    base_ref[...] = dot_t0(dense_ref[:, :nodes], g)
    for k in range(pairs):
        base_ref[:, pair(k)] += dot_t1(cot_out[:, pair(k)], m)


def pack_rows(values, table_ref, start, parts, out_ref):
    flipped = values.astype(F32).T.astype(BF16)
    for q in range(parts):
        table = table_ref[:, start + q * BLK : start + (q + 1) * BLK]
        out_ref[q] = dot(flipped, table).astype(BF16)


def from_blocks(total, table_ref, start, parts, arrived_ref):
    for q in range(parts):
        table = table_ref[:, start + q * BLK : start + (q + 1) * BLK]
        total = total + dot_t1(table, arrived_ref[q])
    return total


def forward_part(x_ref, conv1_ref, conv2_ref, first_ref, hidden_ref, band_ref):
    pairs = x_ref.shape[1] // 128
    band_map(conv1_ref, 1, band_ref)
    b = band_ref[...]
    for k in range(pairs):
        filt, gates = activations(dot(earlier(x_ref, k), b))
        first_ref[:, pair(k)] = (filt * gates).astype(BF16)
    band_map(conv2_ref, 2, band_ref)
    b = band_ref[...]
    for k in range(1, pairs):
        filt, gates = activations(dot(earlier(first_ref, k), b))
        hidden_ref[:, pair(k - 1)] = (filt * gates).astype(BF16)


def gate_grad(pre, up):
    filt, gates = activations(pre)
    d_filt = up * gates * (1.0 - filt * filt)
    d_gate = up * filt * gates * (1.0 - gates)
    return jnp.concatenate([d_filt, d_gate], axis=1).astype(BF16)


def backward_part(x_ref, first_ref, cot_ref, conv1_ref, conv2_ref, grad_ref, g1_ref, g2_ref,
                  band_ref, up_ref, mid_ref):
    pairs = x_ref.shape[1] // 128
    band_map(conv2_ref, 2, band_ref)
    b = band_ref[...]
    total = None
    carry = None
    for k in range(1, pairs):
        both = earlier(first_ref, k)
        d = gate_grad(dot(both, b), up_ref[:, pair(k - 1)])
        part = dot_t0(both, d)
        total = part if total is None else total + part
        back = dot_t1(d, b)
        low = back[:, :128] if carry is None else carry + back[:, :128]
        mid_ref[:, pair(k - 1)] = low.astype(BF16)
        carry = back[:, 128:]
    mid_ref[:, pair(pairs - 1)] = carry.astype(BF16)
    band_grad(total, 2, g2_ref)
    band_map(conv1_ref, 1, band_ref)
    b = band_ref[...]
    total = None
    carry = None
    for k in range(pairs):
        both = earlier(x_ref, k)
        d = gate_grad(dot(both, b), mid_ref[:, pair(k)].astype(F32))
        part = dot_t0(both, d)
        total = part if total is None else total + part
        back = dot_t1(d, b)
        if k > 0:
            low = carry + back[:, :128]
            if k > 1:
                low = low + cot_ref[:, pair(k - 2)].astype(F32)
            grad_ref[:, pair(k - 1)] = low.astype(BF16)
        carry = back[:, 128:]
    last = carry + cot_ref[:, pair(pairs - 2)].astype(F32)
    grad_ref[:, pair(pairs - 1)] = last.astype(BF16)
    band_grad(total, 1, g1_ref)


def mix_grad(term_ref, cot_ref, c):
    acc = None
    for k in range(cot_ref.shape[1] // 128):
        part = dot_t0(term_ref[:, pair(k)], cot_ref[:, pair(k)])
        acc = part if acc is None else acc + part
    return acc[:c, :c] + acc[c:, c:]


def early_part(hidden_ref, hop_ref, x_ref, cot_ref, mix_ref, gm_ref, map0, map1, wide_ref):
    c = mix_ref.shape[1]
    block_map(mix_ref, 0, map0)
    block_map(mix_ref, 1, map1)
    for k in range(cot_ref.shape[1] // 128):
        acc = x_ref[:, pair(k + 1)].astype(F32)
        acc = acc + dot(hidden_ref[:, pair(k)], map0[...])
        wide_ref[:, pair(k)] = acc + dot(hop_ref[:, pair(k)], map1[...])
    gm_ref[0] = mix_grad(hidden_ref, cot_ref, c)
    gm_ref[1] = mix_grad(hop_ref, cot_ref, c)


def main_body(parts, reps, scale,
              x_ref, cot_ref, conv1_ref, conv2_ref, mix_ref, dense_ref, picks_ref, base_ref,
              pieces_ref,
              out_ref, grad_ref, sum_ref,
              first_ref, hidden_ref, hop_ref, second_ref, up_ref, mid_ref, band_ref,
              map0, map1, map2, g1_ref, g2_ref, gm_ref,
              wide_ref, send1, send2, send3, recv0, recv1, recv2, recv3,
              pack_ref, got_ref, part_ref, reps_ref, sums_ref,
              ssem, rsem, asem, arsem, bsem, brsem):
    me = lax.axis_index("dom")
    mine = lax.axis_index("rep")
    nodes = x_ref.shape[0]
    c = mix_ref.shape[1]
    pairs = cot_ref.shape[1] // 128
    feats = cot_ref.shape[1]

    barrier = pltpu.get_barrier_semaphore()
    for o in range(1, parts):
        pl.semaphore_signal(barrier, inc=1, device_id={"dom": lax.rem(me + o, parts)},
                            device_id_type=pl.DeviceIdType.MESH)
    for o in range(1, reps):
        pl.semaphore_signal(barrier, inc=1, device_id={"rep": lax.rem(mine + o, reps)},
                            device_id_type=pl.DeviceIdType.MESH)
    pl.semaphore_wait(barrier, parts - 1 + reps - 1)

    def copies(level, src, dst):
        made = []
        for o in sorted(range(1, parts), key=lambda o: abs(2 * o - parts)):
            peer = lax.rem(me + o, parts)
            made.append(pltpu.make_async_remote_copy(
                src_ref=src.at[peer, pl.ds(c, feats - c)],
                dst_ref=dst.at[me, pl.ds(c, feats - c)],
                send_sem=ssem.at[level, o],
                recv_sem=rsem.at[level, o],
                device_id={"dom": peer},
                device_id_type=pl.DeviceIdType.MESH,
            ))
        for m in made:
            m.start()
        return made

    def arrive(made):
        for m in made:
            m.wait_recv()

    round0 = copies(0, pieces_ref, recv0)
    for buf in (recv0, recv1, recv2, recv3):
        buf[:, 0:c, :] = jnp.zeros((parts, c, BLK), BF16)
        buf[me] = jnp.zeros((feats, BLK), BF16)

    forward_part(x_ref, conv1_ref, conv2_ref, first_ref, hidden_ref, band_ref)
    pack_rows(hidden_ref[...], picks_ref, 0, parts, send1)
    round1 = copies(1, send1, recv1)

    arrive(round0)
    g = from_blocks(base_ref[...], picks_ref, 0, parts, recv0).astype(BF16)
    pack_rows(g, dense_ref, nodes, parts, send2)
    round2 = copies(2, send2, recv2)
    up_ref[...] = dot_t0(dense_ref[:, :nodes], g)
    block_map(mix_ref, 0, map0)
    for k in range(pairs):
        up_ref[:, pair(k)] += dot_t1(cot_ref[:, pair(k)], map0[...])

    own = dot(dense_ref[:, :nodes], hidden_ref[...])
    arrive(round1)
    hop_ref[...] = from_blocks(own, dense_ref, nodes, parts, recv1).astype(BF16)
    pack_rows(hop_ref[...], picks_ref, 0, parts, send3)
    round3 = copies(3, send3, recv3)

    arrive(round2)
    up_ref[...] = from_blocks(up_ref[...], picks_ref, 0, parts, recv2)
    backward_part(x_ref, first_ref, cot_ref, conv1_ref, conv2_ref, grad_ref, g1_ref, g2_ref,
                  band_ref, up_ref, mid_ref)

    early_part(hidden_ref, hop_ref, x_ref, cot_ref, mix_ref, gm_ref, map0, map1, wide_ref)
    block_map(mix_ref, 2, map2)
    own = dot(dense_ref[:, :nodes], hop_ref[...])
    arrive(round3)
    second_ref[...] = from_blocks(own, dense_ref, nodes, parts, recv3).astype(BF16)
    gm_ref[2] = mix_grad(second_ref, cot_ref, c)

    per = pack_ref.shape[1]
    flat = pack_ref
    flat[...] = jnp.zeros(flat.shape, F32)

    def put(first_row, value):
        rows = value.shape[0]
        done = 0
        while done < rows:
            slot, at = divmod(first_row + done, per)
            step = min(per - at, rows - done)
            flat[slot, at : at + step, :] = value[done : done + step]
            done += step

    put(0, g1_ref[0])
    put(c, g1_ref[1])
    put(2 * c, g2_ref[0])
    put(3 * c, g2_ref[1])
    put(4 * c, jnp.concatenate([gm_ref[0], gm_ref[1]], axis=1))
    put(5 * c, jnp.concatenate([gm_ref[2], jnp.zeros((c, c), F32)], axis=1))

    scatter = []
    for o in range(1, parts):
        peer = lax.rem(me + o, parts)
        scatter.append(pltpu.make_async_remote_copy(
            src_ref=pack_ref.at[peer], dst_ref=got_ref.at[me],
            send_sem=asem.at[0, o], recv_sem=arsem.at[0, o],
            device_id={"dom": peer}, device_id_type=pl.DeviceIdType.MESH))
    for m in scatter:
        m.start()
    for k in range(pairs):
        wide_ref[:, pair(k)] += dot(second_ref[:, pair(k)], map2[...])
    out_ref[...] = wide_ref[...].T[c:].astype(BF16)
    got_ref[me] = pack_ref[me]
    arrive(scatter)
    total = got_ref[0]
    for q in range(1, parts):
        total = total + got_ref[q]
    part_ref[...] = total
    around = []
    for o in range(1, reps):
        peer = lax.rem(mine + o, reps)
        around.append(pltpu.make_async_remote_copy(
            src_ref=part_ref, dst_ref=reps_ref.at[mine],
            send_sem=bsem.at[o], recv_sem=brsem.at[o],
            device_id={"rep": peer}, device_id_type=pl.DeviceIdType.MESH))
    for m in around:
        m.start()
    reps_ref[mine] = total
    arrive(around)
    total = reps_ref[0]
    for q in range(1, reps):
        total = total + reps_ref[q]
    for m in around:
        m.wait_send()
    part_ref[...] = total * (1.0 / scale)
    final = []
    for o in range(1, parts):
        peer = lax.rem(me + o, parts)
        final.append(pltpu.make_async_remote_copy(
            src_ref=part_ref, dst_ref=sums_ref.at[me],
            send_sem=asem.at[1, o], recv_sem=arsem.at[1, o],
            device_id={"dom": peer}, device_id_type=pl.DeviceIdType.MESH))
    for m in final:
        m.start()
    sums_ref[me] = part_ref[...]
    arrive(final)

    sum_ref[...] = sums_ref[...]
    for m in round0 + round1 + round2 + round3 + scatter + final:
        m.wait_send()


def shards(inputs, cotangent, conv_one, conv_two, mix_weight, send_rows, counts, tile_cols,
           tile_vals):
    windows, nodes, flat = inputs.shape
    channels = mix_weight.shape[1]
    parts = lax.axis_size("dom")
    reps = lax.axis_size("rep")
    kept = flat // channels - 3
    wide = flat - 2 * channels
    halo = parts * BLK
    blocks = (parts, wide, BLK)
    prepared = [((nodes, nodes + halo), BF16), ((nodes, halo), BF16), ((nodes, wide), BF16),
                ((nodes, wide), F32), (blocks, BF16)]
    dense, picks, cot_wide, base, pieces = pl.pallas_call(
        prepare_body,
        out_shape=[jax.ShapeDtypeStruct(s, d) for s, d in prepared],
        in_specs=[VM, VM, VM, SM, SM, VM],
        out_specs=[VM] * 5,
        scratch_shapes=[pltpu.VMEM((parts + nodes // BLK, BLK, BLK), F32),
                        pltpu.VMEM((128, 128), BF16), pltpu.VMEM((nodes, wide), BF16)],
        compiler_params=LIMIT,
        name="prepare",
    )(cotangent[0].T, mix_weight, send_rows[0], counts, tile_cols, tile_vals)
    scaling = math.sqrt(float(windows * reps * nodes * parts * kept))
    unit = 8 * parts
    per = -(-6 * channels // unit) * unit // parts
    results = [((kept * channels, nodes), BF16), ((nodes, flat), BF16), ((parts, per, BLK), F32)]
    scratch = [((nodes, flat), BF16), ((nodes, wide), BF16), ((nodes, wide), BF16),
               ((nodes, wide), BF16), ((nodes, wide), F32), ((nodes, flat), BF16),
               ((256, 256), BF16), ((128, 128), BF16), ((128, 128), BF16), ((128, 128), BF16),
               (conv_one.shape, F32), (conv_two.shape, F32), (mix_weight.shape, F32)]
    scratch += [((nodes, wide), F32)] + [(blocks, BF16)] * 7
    scratch += [((parts, per, BLK), F32), ((parts, per, BLK), F32), ((per, BLK), F32),
                ((reps, per, BLK), F32), ((parts, per, BLK), F32)]
    dma = pltpu.SemaphoreType.DMA
    output, grad_input, packed = pl.pallas_call(
        functools.partial(main_body, parts, reps, scaling),
        out_shape=[jax.ShapeDtypeStruct(s, d) for s, d in results],
        in_specs=[VM] * 9,
        out_specs=[VM] * 3,
        scratch_shapes=[pltpu.VMEM(s, d) for s, d in scratch]
        + [dma((4, parts)), dma((4, parts)), dma((2, parts)), dma((2, parts)), dma((reps,)),
           dma((reps,))],
        compiler_params=pltpu.CompilerParams(
            vmem_limit_bytes=60 * 1024 * 1024, collective_id=0, has_side_effects=True),
        name="layer",
    )(inputs[0], cot_wide, conv_one, conv_two, mix_weight, dense, picks, base, pieces)
    c = channels
    rows = packed.reshape(parts * per, BLK)
    gm = jnp.stack([rows[4 * c : 5 * c, :c], rows[4 * c : 5 * c, c:], rows[5 * c : 6 * c, :c]])
    return (
        output.T[None],
        grad_input[None],
        rows[: 2 * c].reshape(conv_one.shape),
        rows[2 * c : 4 * c].reshape(conv_two.shape),
        gm,
    )


def place_tiles(me, parts, cols_ref, vals_ref, dense_ref):
    rtiles, slots = vals_ref.shape[0], vals_ref.shape[1]
    for r in range(rtiles):
        for c in range(dense_ref.shape[1] // BLK):
            named = c if c < rtiles else rtiles + lax.rem(me - (c - rtiles + 1) + parts, parts)
            total = None
            for j in range(slots):
                keep = jnp.where(cols_ref[r, j] == named, 1.0, 0.0)
                part = vals_ref[r, j].astype(F32) * keep
                total = part if total is None else total + part
            dense_ref[r * BLK : (r + 1) * BLK, c * BLK : (c + 1) * BLK] = total.astype(BF16)


def chunk(first, size):
    return pl.ds(pl.multiple_of(first, size), size)


def steps_body(parts, reps, scale,
               x_ref, cot_ref, conv1_ref, conv2_ref, mix_ref, send_ref, counts_ref, cols_ref, vals_ref,
               out_ref, grad_ref, one_out, two_out, mix_out,
               dense_ref, wanted_ref, xt_ref, first_ref, hid_ref, d1_ref, d2_ref, mid_ref,
               band1, band1t, band2, band2t, maps, mapst,
               adj_ref, lists_ref, picks_ref,
               cf_ref, hf_ref, f1_ref, c1_ref, own_ref, part_t, ext_ref,
               gh_ref, mx_ref, ghs_ref, mxs_ref,
               g1_ref, g2_ref, pack0, got0, half0, all0, full0, sums0,
               pack1, got1, half1, all1, full1, sums1,
               lsend, lrecv, fsend, frecv, esend, erecv, tsend, trecv,
               asem, arsem, bsem, brsem):
    me = lax.axis_index("dom")
    mine = lax.axis_index("rep")
    nodes = x_ref.shape[0]
    c = mix_ref.shape[1]
    pairs = x_ref.shape[1] // 128
    rows = nodes // reps
    mesh_ids = pl.DeviceIdType.MESH
    holder = lax.rem(parts // 2 - reps // 2 + mine + parts, parts)
    extra = parts * c
    zs = parts // 2
    z, xx = me // 2, lax.rem(me, 2)
    yy, core = mine // 2, lax.rem(mine, 2)
    chips = parts * reps // 2
    chip = me * 2 + yy

    barrier = pltpu.get_barrier_semaphore()
    for o in range(1, chips):
        peer = lax.rem(chip + o, chips)
        pl.semaphore_signal(barrier, inc=1, device_id={"dom": peer // 2, "rep": lax.rem(peer, 2) * 2 + core},
                            device_id_type=mesh_ids)
    pl.semaphore_signal(barrier, inc=1, device_id={"rep": yy * 2 + 1 - core}, device_id_type=mesh_ids)
    place_tiles(me, parts, cols_ref, vals_ref, dense_ref)
    lane = lax.broadcasted_iota(jnp.int32, (1, BLK), 1)
    for o in range(parts):
        t = lax.rem(me + o, parts)
        wanted_ref[o : o + 1, :] = jnp.where(
            lane < counts_ref[0, t], send_ref[pl.ds(t, 1), :], -1)
    pl.semaphore_wait(barrier, chips)

    def remote(src, dst, ssem, rsem, **where):
        return pltpu.make_async_remote_copy(
            src_ref=src, dst_ref=dst, send_sem=ssem, recv_sem=rsem,
            device_id=where, device_id_type=mesh_ids)

    order = sorted(range(1, parts), key=lambda o: abs(2 * o - parts))

    def piece(p, r):
        return adj_ref.at[p, chunk(r * rows, rows)]

    def source_z(t, way):
        return z - t if way == 0 else z + t

    def valid(t, way):
        if t == 0:
            return z >= 0
        return z >= t if way == 0 else z + t < zs

    def slot(t, way):
        return 0 if t == 0 else 2 * t - 1 + way

    def base(t, way):
        return source_z(t, way) * 2 + xx

    def cross(t, way):
        return source_z(t, way) * 2 + 1 - xx

    yrep = (1 - yy) * 2 + core
    crep = yy * 2 + 1 - core
    cyrep = (1 - yy) * 2 + 1 - core

    def along(t, way, out_way):
        src = dense_ref.at[chunk(mine * rows, rows)] if t == 0 else piece(base(t, way), mine)
        to = (z + 1 if out_way == 0 else z - 1) * 2 + xx
        return remote(src, piece(base(t, way), mine), tsend.at[out_way, slot(t, way)],
                      trecv.at[0, slot(t + 1, out_way)], dom=to)

    def across(t, way):
        src = dense_ref.at[chunk(mine * rows, rows)] if t == 0 else piece(base(t, way), mine)
        return remote(src, piece(base(t, way), mine), tsend.at[2, slot(t, way)],
                      trecv.at[2, slot(t, way)], dom=z * 2 + 1 - xx)

    def hand(kind, p, r, t, way, to):
        return remote(piece(p, r), piece(p, r), tsend.at[kind, slot(t, way)],
                      trecv.at[kind, slot(t, way)], rep=to)

    def arrived(kind, p, r, t, way, **where):
        remote(piece(p, r), piece(p, r), tsend.at[kind, slot(t, way)],
               trecv.at[kind, slot(t, way)], **where).wait_recv()

    def ways(t):
        return (0,) if t == 0 else (0, 1)

    def lane_sends(t, way):
        made = []
        outs = (0, 1) if t == 0 else (way,)
        for w in outs:
            made.append((z + 1 < zs if w == 0 else z >= 1, along(t, way, w)))
        made.append((None, across(t, way)))
        return made

    def base_sends(t, way):
        return [] if t == 0 else [(None, hand(3, base(t, way), mine, t, way, yrep)),
                                  (None, hand(4, base(t, way), mine, t, way, crep))]

    def cross_sends(t, way):
        return [(None, hand(5, cross(t, way), mine, t, way, yrep)),
                (None, hand(6, cross(t, way), mine, t, way, crep))]

    def ybase_sends(t, way):
        return [] if t == 0 else [(None, hand(7, base(t, way), yrep, t, way, crep))]

    def ycross_sends(t, way):
        return [(None, hand(8, cross(t, way), yrep, t, way, crep))]

    def go(sends, wait=False):
        for cond, copy in sends:
            act = copy.wait_send if wait else copy.start
            if cond is None:
                act()
            else:
                pl.when(cond)(act)

    def on_base(t, way):
        @pl.when(valid(t, way))
        def _():
            arrived(0, base(t, way), mine, t, way, rep=crep)
            go(lane_sends(t, way) + base_sends(t, way))

    def on_cross(t, way):
        @pl.when(valid(t, way))
        def _():
            arrived(2, cross(t, way), mine, t, way, rep=crep)
            go(cross_sends(t, way))

    def on_ybase(t, way):
        @pl.when(valid(t, way))
        def _():
            arrived(3, base(t, way), yrep, t, way, rep=crep)
            go(ybase_sends(t, way))

    def on_ycross(t, way):
        @pl.when(valid(t, way))
        def _():
            arrived(5, cross(t, way), yrep, t, way, rep=crep)
            go(ycross_sends(t, way))

    relay = []
    for s in range(1, zs + 2):
        for handler, t, least in ((on_base, s, 1), (on_cross, s - 1, 0), (on_ybase, s - 1, 1),
                                  (on_ycross, s - 2, 0)):
            if least <= t < zs:
                for w in ways(t):
                    relay.append(functools.partial(handler, t, w))
    relay.reverse()

    def step_relay(count=1):
        for _ in range(count):
            if relay:
                relay.pop()()

    def scatter_field(level, src, first, dst):
        made = []
        for o in order:
            peer = lax.rem(me + o, parts)
            made.append(remote(src.at[chunk(first + peer * c, c)], dst.at[me, pl.ds(0, c)],
                               fsend.at[level, o], frecv.at[level, o], dom=peer))
        for m in made:
            m.start()
        off = lax.rem(holder - me + parts, parts)
        last = remote(src.at[pl.ds(first + extra, c)], dst.at[me, pl.ds(c, c)],
                      esend.at[level, 0], erecv.at[level, off], dom=holder)
        pl.when(me != holder)(last.start)
        dst[me, 0:c, :] = src[chunk(first + me * c, c), :]

        @pl.when(me == holder)
        def _():
            dst[me, c : 2 * c, :] = src[first + extra : first + extra + c, :]

        @pl.when(me != holder)
        def _():
            dst[:, c : 2 * c, :] = jnp.zeros((parts, c, nodes), BF16)
        return made, last

    def field_arrives(level, made, src, dst):
        for m in made:
            m.wait_recv()

        @pl.when(me == holder)
        def _():
            for o in range(1, parts):
                q = lax.rem(me - o + parts, parts)
                remote(dst.at[q, pl.ds(c, c)], dst.at[q, pl.ds(c, c)], esend.at[level, 0],
                       erecv.at[level, o], dom=q).wait_recv()

    def home_copies(level, o, src, first, dst):
        q = lax.rem(me + o, parts)
        one = remote(src.at[q, pl.ds(0, c)], dst.at[chunk(first + me * c, c)],
                     fsend.at[level, o], frecv.at[level, o], dom=q)
        two = remote(src.at[q, pl.ds(c, c)], dst.at[pl.ds(first + extra, c)],
                     esend.at[level, o], erecv.at[level, 0], dom=q)
        return one, two

    def go_home(level, o, src, first, dst):
        if o:
            one, two = home_copies(level, o, src, first, dst)
            one.start()
            pl.when(me == holder)(two.start)
            return
        dst[chunk(first + me * c, c), :] = src[me, 0:c, :]

        @pl.when(me == holder)
        def _():
            dst[first + extra : first + extra + c, :] = src[me, c : 2 * c, :]

    def home_arrives(level, src, first, dst):
        for o in range(1, parts):
            home_copies(level, o, src, first, dst)[0].wait_recv()
        pl.when(me != holder)(home_copies(level, 1, src, first, dst)[1].wait_recv)

    def home_sent(level, src, first, dst):
        for o in range(1, parts):
            one, two = home_copies(level, o, src, first, dst)
            one.wait_send()
            pl.when(me == holder)(two.wait_send)

    go(lane_sends(0, 0))
    cot_round = scatter_field(0, cot_ref, 0, cf_ref)
    lists = []
    for o in order:
        peer = lax.rem(me + o, parts)
        lists.append(remote(wanted_ref, lists_ref.at[me], lsend.at[o], lrecv.at[o], dom=peer))
    for m in lists:
        m.start()
    lists_ref[me] = wanted_ref[...]
    adj_ref[me] = dense_ref[...]

    for k in range(pairs):
        xt_ref[pair(k), :] = x_ref[:, pair(k)].astype(F32).T.astype(BF16)
    for conv, dil, nat, tra in ((conv1_ref, 1, band1, band1t), (conv2_ref, 2, band2, band2t)):
        band_map(conv, dil, nat)
        tra[...] = nat[...].astype(F32).T.astype(BF16)

    def earlier_t(ref, k):
        if k == 0:
            v = ref[0:128, :]
            return jnp.concatenate([jnp.zeros_like(v), v], axis=0)
        return ref[window2(k - 1), :]

    def gated(pre, d_ref, k):
        filt = jnp.tanh(pre[:128])
        gates = 0.5 * jnp.tanh(0.5 * pre[128:]) + 0.5
        d_ref[k, 0:128, :] = gates * (1.0 - filt * filt)
        d_ref[k, 128:256, :] = filt * gates * (1.0 - gates)
        return (filt * gates).astype(BF16)

    for k in range(pairs):
        first_ref[pair(k), :] = gated(dot(band1t[...], earlier_t(xt_ref, k)), d1_ref, k)
        if k % 2:
            step_relay()
    for k in range(1, pairs):
        hid_ref[pair(k - 1), :] = gated(dot(band2t[...], earlier_t(first_ref, k)), d2_ref, k)
        step_relay()
    hid_round = scatter_field(1, hid_ref, c, hf_ref)
    step_relay()

    for i in range(3):
        block_map(mix_ref, i, maps.at[i])
        mapst[i] = maps[i].astype(F32).T.astype(BF16)
    gh_ref[0:c, :] = jnp.zeros((c, nodes), BF16)

    for m in lists:
        m.wait_recv()
    node = lax.broadcasted_iota(jnp.int32, (nodes, BLK), 0)
    for q in range(parts):
        for o in range(1, parts):
            hit = node == lists_ref[q, o : o + 1, :]
            picks_ref[q, :, (o - 1) * BLK : o * BLK] = jnp.where(hit, 1.0, 0.0).astype(BF16)
        step_relay(2)

    field_arrives(0, cot_round[0], cot_ref, cf_ref)
    step_relay(len(relay))
    for t in range(zs):
        for w in ways(t):
            @pl.when(valid(t, w))
            def _():
                if t:
                    arrived(4, base(t, w), crep, t, w, rep=crep)
                    arrived(7, base(t, w), cyrep, t, w, rep=crep)
                arrived(6, cross(t, w), crep, t, w, rep=crep)
                arrived(8, cross(t, w), cyrep, t, w, rep=crep)

    def back_pieces(g_ref):
        for p in range(parts):
            t = dot(g_ref[p], adj_ref[p])
            own_ref[p] = t[:, :nodes]
            for o in range(1, parts):
                at = nodes + (o - 1) * BLK
                part_t[(p - o) % parts, :, (o - 1) * BLK : o * BLK] = t[:, at : at + BLK].astype(BF16)

    def back_owner(q):
        return (own_ref[q] + dot_t1(part_t[q], picks_ref[q])).astype(BF16)

    back_pieces(cf_ref)
    for q in range(parts):
        c1_ref[q] = back_owner(q)
    back_pieces(c1_ref)
    field_arrives(1, hid_round[0], hid_ref, hf_ref)
    mix = [None] * 3
    for o in order + [0]:
        q = lax.rem(me + o, parts)
        moved = (cf_ref[q], c1_ref[q], back_owner(q))
        grads = [dot(maps[i], moved[i]) for i in range(3)]
        ghs_ref[q] = (grads[0] + grads[1] + grads[2]).astype(BF16)
        go_home(2, o, ghs_ref, c, gh_ref)
        for i in range(3):
            more = dot_t1(hf_ref[q], moved[i])
            mix[i] = more if mix[i] is None else mix[i] + more
    mix = [m[:c, :c] + m[c:, c:] for m in mix]

    def reducer(g, pack, got, half, got_all, full, sums):
        def over_core(stage, src, dst):
            return [remote(src, dst, bsem.at[2 * g + stage], brsem.at[2 * g + stage], rep=crep)]

        def over_chips(stage, src_of, dst):
            made = []
            for o in range(1, chips):
                peer = lax.rem(chip + o, chips)
                made.append(remote(src_of(peer), dst, asem.at[2 * g + stage, o], arsem.at[2 * g + stage, o],
                                   dom=peer // 2, rep=lax.rem(peer, 2) * 2 + core))
            return made

        steps = (lambda: over_core(0, pack.at[1 - core], got),
                 lambda: over_chips(0, lambda peer: half.at[peer], got_all.at[chip]),
                 lambda: over_chips(1, lambda peer: full, sums.at[core, chip]),
                 lambda: over_core(1, sums.at[core], sums.at[core]))

        def start(i):
            for m in steps[i]():
                m.start()

        def arrive(i):
            for m in steps[i]():
                m.wait_recv()

        def first():
            start(0)

        def second():
            arrive(0)
            total = pack[core] + got[...]
            share = half.shape[1]
            for q in range(chips):
                half[q] = total[q * share : (q + 1) * share]
            start(1)
            got_all[chip] = half[chip]

        def third():
            arrive(1)
            total = got_all[0]
            for q in range(1, chips):
                total = total + got_all[q]
            full[...] = total * (1.0 / scale)
            start(2)
            sums[core, chip] = full[...]

        def fourth():
            arrive(2)
            start(3)

        def last():
            arrive(3)

        def sent():
            for i in range(4):
                for m in steps[i]():
                    m.wait_send()

        return first, second, third, fourth, last, sent

    early = reducer(0, pack0, got0, half0, all0, full0, sums0)
    late = reducer(1, pack1, got1, half1, all1, full1, sums1)
    pack0[...] = jnp.zeros(pack0.shape, F32)
    for i in range(3):
        pack0[i // 2, (i % 2) * c : (i % 2 + 1) * c, 0:c] = mix[i]
    early[0]()

    def extend(f_ref):
        for q in range(parts):
            ext_ref[q, :, 0:nodes] = f_ref[q]
            halo = dot(f_ref[q], picks_ref[q]).astype(BF16)
            for o in range(1, parts):
                at = nodes + (o - 1) * BLK
                ext_ref[(q + o) % parts, :, at : at + BLK] = halo[:, (o - 1) * BLK : o * BLK]

    extend(hf_ref)
    for p in range(parts):
        f1_ref[p] = dot_t1(ext_ref[p], adj_ref[p]).astype(BF16)
    extend(f1_ref)
    for o in order + [0]:
        q = lax.rem(me + o, parts)
        second = dot_t1(ext_ref[q], adj_ref[q]).astype(BF16)
        mixed = dot(mapst[0], hf_ref[q]) + dot(mapst[1], f1_ref[q]) + dot(mapst[2], second)
        mxs_ref[q] = mixed.astype(BF16)
        go_home(3, o, mxs_ref, 0, mx_ref)
    early[1]()

    home_arrives(2, ghs_ref, c, gh_ref)

    def conv_back(sig_ref, d_ref, up_of, band, low_of, first_pair, dilation, out):
        total, carry = None, None
        b = band[...]
        for k in range(first_pair, pairs):
            up = up_of(k)
            both = earlier_t(sig_ref, k)
            d = jnp.concatenate([up * d_ref[k, 0:128, :], up * d_ref[k, 128:256, :]], axis=0)
            d = d.astype(BF16)
            part = dot_t1(both, d)
            total = part if total is None else total + part
            back = dot(b, d)
            if k > 0:
                low_of(k - 1, back[:128] if carry is None else carry + back[:128])
            carry = back[128:]
        low_of(pairs - 1, carry)
        band_grad(total, dilation, out)

    def set_mid(k, low):
        mid_ref[pair(k), :] = low.astype(BF16)

    def set_grad(k, low):
        if k == 1:
            low = low + jnp.concatenate([jnp.zeros((c, nodes), F32), cot_ref[0:c, :].astype(F32)], axis=0)
        elif k > 1:
            low = low + cot_ref[(2 * k - 3) * c : (2 * k - 1) * c, :].astype(F32)
        grad_ref[:, pair(k)] = low.T.astype(BF16)

    conv_back(first_ref, d2_ref, lambda k: gh_ref[pair(k - 1), :].astype(F32), band2, set_mid, 1, 2, g2_ref)
    conv_back(xt_ref, d1_ref, lambda k: mid_ref[pair(k), :].astype(F32), band1, set_grad, 0, 1, g1_ref)

    for tap in range(2):
        pack1[0, tap * c : (tap + 1) * c, :] = g1_ref[tap]
        pack1[1, tap * c : (tap + 1) * c, :] = g2_ref[tap]
    late[0]()
    early[2]()
    late[1]()
    home_arrives(3, mxs_ref, 0, mx_ref)
    kept = out_ref.shape[0]
    out_ref[...] = (mx_ref[...].astype(F32) + xt_ref[pairs * 128 - kept :, :].astype(F32)).astype(BF16)
    late[2]()
    early[3]()

    for m in cot_round[0] + hid_round[0] + lists:
        m.wait_send()
    pl.when(me != holder)(cot_round[1].wait_send)
    pl.when(me != holder)(hid_round[1].wait_send)
    home_sent(2, ghs_ref, c, gh_ref)
    home_sent(3, mxs_ref, 0, mx_ref)
    for t in range(zs):
        for w in ways(t):
            @pl.when(valid(t, w))
            def _():
                go(lane_sends(t, w) + base_sends(t, w) + cross_sends(t, w) + ybase_sends(t, w)
                   + ycross_sends(t, w), wait=True)
    late[3]()
    early[4]()
    share = sums0.shape[2]
    for q in range(chips):
        tap, at = divmod(q * share, c)
        mix_out[tap, at : at + share, :] = sums0[0, q, :, 0:c]
        if tap == 0:
            mix_out[2, at : at + share, :] = sums0[1, q, :, 0:c]
    early[5]()
    late[4]()
    for q in range(chips):
        tap, at = divmod(q * share, c)
        one_out[tap, at : at + share, :] = sums1[0, q]
        two_out[tap, at : at + share, :] = sums1[1, q]
    late[5]()


def finish_body(*refs):
    half = len(refs) // 2
    for a, b in zip(refs[:half], refs[half:]):
        b[...] = a[...]


def step_shards(inputs, cotangent, conv_one, conv_two, mix_weight, send_rows, counts, tile_cols,
                tile_vals):
    windows, nodes, flat = inputs.shape
    channels = mix_weight.shape[1]
    parts = lax.axis_size("dom")
    reps = lax.axis_size("rep")
    kept = flat // channels - 3
    c = channels
    pairs = flat // 128
    halo = (parts - 1) * BLK
    ext = nodes + halo
    scaling = math.sqrt(float(windows * reps * nodes * parts * kept))
    results = [((kept * c, nodes), BF16), ((nodes, flat), BF16), (conv_one.shape, F32),
               (conv_two.shape, F32), (mix_weight.shape, F32)]
    field = (parts, 2 * c, nodes)
    wide = flat - 2 * c
    scratch = [((nodes, ext), BF16), ((parts, BLK), jnp.int32),
               ((flat, nodes), BF16), ((flat, nodes), BF16), ((wide, nodes), BF16),
               ((pairs, 256, nodes), F32), ((pairs, 256, nodes), F32), ((flat, nodes), BF16)]
    scratch += [((256, 256), BF16)] * 4 + [((3, 128, 128), BF16)] * 2
    scratch += [((parts, nodes, ext), BF16), ((parts, parts, BLK), jnp.int32),
                ((parts, nodes, halo), BF16)]
    scratch += [(field, BF16)] * 4 + [(field, F32), ((parts, 2 * c, halo), BF16),
                                      ((parts, 2 * c, ext), BF16)]
    scratch += [((wide, nodes), BF16), ((kept * c, nodes), BF16), (field, BF16), (field, BF16)]
    scratch += [(conv_one.shape, F32), (conv_two.shape, F32)]
    chips = parts * reps // 2
    share = 2 * c // chips
    for _ in range(2):
        scratch += [((2, 2 * c, BLK), F32), ((2 * c, BLK), F32), ((chips, share, BLK), F32),
                    ((chips, share, BLK), F32), ((share, BLK), F32), ((2, chips, share, BLK), F32)]
    dma = pltpu.SemaphoreType.DMA
    sems = [(parts,), (parts,), (4, parts), (4, parts), (4, parts), (4, parts),
            (9, parts), (9, parts), (4, chips), (4, chips), (4,), (4,)]
    made = pl.pallas_call(
        functools.partial(steps_body, parts, reps, scaling),
        out_shape=[jax.ShapeDtypeStruct(s, d) for s, d in results],
        in_specs=[VM] * 6 + [SM, SM, VM],
        out_specs=[VM] * 5,
        scratch_shapes=[pltpu.VMEM(s, d) for s, d in scratch] + [dma(s) for s in sems],
        compiler_params=pltpu.CompilerParams(
            vmem_limit_bytes=60 * 1024 * 1024, collective_id=1, has_side_effects=True),
        name="steps",
    )(inputs[0], cotangent[0].T, conv_one, conv_two, mix_weight, send_rows[0], counts, tile_cols,
      tile_vals)
    output, grad_input, one, two, mix = pl.pallas_call(
        finish_body,
        out_shape=[jax.ShapeDtypeStruct(s, d) for s, d in results],
        in_specs=[VM] * 5,
        out_specs=[VM] * 5,
        compiler_params=LIMIT,
        name="finish",
    )(*made)
    return output.T[None], grad_input[None], one, two, mix


def solution(mesh):
    placed = (
        P("rep", "dom", None),
        P("rep", "dom", None),
        P(),
        P(),
        P(),
        P("dom", None, None),
        P("dom", None),
        P("dom", None),
        P("dom", None, None, None),
    )
    parts, reps = mesh.shape["dom"], mesh.shape["rep"]

    def layer(*args):
        kept = args[0].shape[2] // args[4].shape[1] - 3
        by_step = parts % 2 == 0 and reps == 4 and parts == kept - 1
        return step_shards(*args) if by_step else shards(*args)

    return jax.shard_map(
        layer,
        mesh=mesh,
        in_specs=placed,
        out_specs=(P("rep", "dom", None), P("rep", "dom", None), P(), P(), P()),
        check_vma=False,
    )
```

```python
import functools
import math

import jax
import jax.numpy as jnp
from jax import lax
from jax.experimental import pallas as pl
from jax.experimental.pallas import tpu as pltpu
from jax.sharding import PartitionSpec as P

F32 = jnp.float32
BF16 = jnp.bfloat16
BLK = 128
VM = pl.BlockSpec(memory_space=pltpu.VMEM)
SM = pl.BlockSpec(memory_space=pltpu.SMEM)
LIMIT = pltpu.CompilerParams(vmem_limit_bytes=56 * 1024 * 1024)


def dot(a, b):
    return jnp.dot(a, b, preferred_element_type=F32)


def dot_t0(a, b):
    return lax.dot_general(a, b, (((0,), (0,)), ((), ())), preferred_element_type=F32)


def dot_t1(a, b):
    return lax.dot_general(a, b, (((1,), (1,)), ((), ())), preferred_element_type=F32)


def pair(k):
    return slice(k * 128, (k + 1) * 128)


def window2(k):
    return slice(k * 128, (k + 2) * 128)


def block_map(weight_ref, index, out_ref):
    c = weight_ref.shape[1]
    w = weight_ref[index]
    out_ref[...] = jnp.zeros(out_ref.shape, BF16)
    out_ref[0:c, 0:c] = w
    out_ref[c : 2 * c, c : 2 * c] = w


def band_blocks(dilation):
    if dilation == 1:
        return ((0, 1, 0), (0, 2, 1), (1, 2, 0), (1, 3, 1))
    return ((0, 0, 0), (0, 1, 1), (1, 2, 0), (1, 3, 1))


def band_map(conv_ref, dilation, out_ref):
    c = conv_ref.shape[1]
    out_ref[...] = jnp.zeros(out_ref.shape, BF16)
    for tap, i, o in band_blocks(dilation):
        w = conv_ref[tap]
        rows = slice(i * c, (i + 1) * c)
        out_ref[rows, o * c : (o + 1) * c] = w[:, :c]
        out_ref[rows, (o + 2) * c : (o + 3) * c] = w[:, c:]


def band_grad(total, dilation, out_ref):
    c = out_ref.shape[1]
    for tap in range(2):
        for half in range(2):
            acc = None
            for t, i, o in band_blocks(dilation):
                if t != tap:
                    continue
                col = (o + 2 * half) * c
                part = total[i * c : (i + 1) * c, col : col + c]
                acc = part if acc is None else acc + part
            out_ref[tap, :, half * c : (half + 1) * c] = acc


def activations(pre):
    filt = jnp.tanh(pre[:, :128])
    gates = 0.5 * jnp.tanh(0.5 * pre[:, 128:]) + 0.5
    return filt, gates


def earlier(ref, k):
    if k == 0:
        x = ref[:, 0:128]
        return jnp.concatenate([jnp.zeros_like(x), x], axis=1)
    return ref[:, window2(k - 1)]


def build_tiles(cols_ref, vals_ref, acc_ref, dense_ref):
    rtiles, slots = vals_ref.shape[0], vals_ref.shape[1]
    ctiles = dense_ref.shape[1] // BLK
    for r in range(rtiles):
        acc_ref[...] = jnp.zeros(acc_ref.shape, F32)
        for j in range(slots):
            c = cols_ref[r, j]
            acc_ref[c] = acc_ref[c] + vals_ref[r, j].astype(F32)
        for c in range(ctiles):
            dense_ref[r * BLK : (r + 1) * BLK, c * BLK : (c + 1) * BLK] = acc_ref[c].astype(BF16)


def build_picks(send_ref, counts_ref, picks_ref):
    parts = send_ref.shape[0]
    nodes = picks_ref.shape[0]
    lane = lax.broadcasted_iota(jnp.int32, (1, BLK), 1)
    rows = lax.broadcasted_iota(jnp.int32, (nodes, BLK), 0)
    for q in range(parts):
        wanted = jnp.where(lane < counts_ref[0, q], send_ref[q : q + 1, :], -1)
        hit = rows == wanted
        picks_ref[:, q * BLK : (q + 1) * BLK] = jnp.where(hit, 1.0, 0.0).astype(BF16)


def prepare_body(cot_ref, mix_ref, send_ref, counts_ref, cols_ref, vals_ref,
                 dense_ref, picks_ref, cot_out, base_ref, pieces_ref,
                 acc_ref, map_ref, g_ref):
    nodes = cot_ref.shape[1]
    parts = send_ref.shape[0]
    c = mix_ref.shape[1]
    build_tiles(cols_ref, vals_ref, acc_ref, dense_ref)
    build_picks(send_ref, counts_ref, picks_ref)
    wide = cot_ref[...].astype(F32).T
    wide = jnp.concatenate([jnp.zeros((nodes, c), F32), wide], axis=1).astype(BF16)
    cot_out[...] = wide
    pairs = cot_out.shape[1] // 128
    block_map(mix_ref, 2, map_ref)
    m = map_ref[...]
    for k in range(pairs):
        g_ref[:, pair(k)] = dot_t1(cot_out[:, pair(k)], m).astype(BF16)
    block_map(mix_ref, 1, map_ref)
    m = map_ref[...]
    g = g_ref[...]
    pack_rows(g, dense_ref, nodes, parts, pieces_ref)
    base_ref[...] = dot_t0(dense_ref[:, :nodes], g)
    for k in range(pairs):
        base_ref[:, pair(k)] += dot_t1(cot_out[:, pair(k)], m)


def pack_rows(values, table_ref, start, parts, out_ref):
    flipped = values.astype(F32).T.astype(BF16)
    for q in range(parts):
        table = table_ref[:, start + q * BLK : start + (q + 1) * BLK]
        out_ref[q] = dot(flipped, table).astype(BF16)


def from_blocks(total, table_ref, start, parts, arrived_ref):
    for q in range(parts):
        table = table_ref[:, start + q * BLK : start + (q + 1) * BLK]
        total = total + dot_t1(table, arrived_ref[q])
    return total


def forward_part(x_ref, conv1_ref, conv2_ref, first_ref, hidden_ref, band_ref):
    pairs = x_ref.shape[1] // 128
    band_map(conv1_ref, 1, band_ref)
    b = band_ref[...]
    for k in range(pairs):
        filt, gates = activations(dot(earlier(x_ref, k), b))
        first_ref[:, pair(k)] = (filt * gates).astype(BF16)
    band_map(conv2_ref, 2, band_ref)
    b = band_ref[...]
    for k in range(1, pairs):
        filt, gates = activations(dot(earlier(first_ref, k), b))
        hidden_ref[:, pair(k - 1)] = (filt * gates).astype(BF16)


def gate_grad(pre, up):
    filt, gates = activations(pre)
    d_filt = up * gates * (1.0 - filt * filt)
    d_gate = up * filt * gates * (1.0 - gates)
    return jnp.concatenate([d_filt, d_gate], axis=1).astype(BF16)


def backward_part(x_ref, first_ref, cot_ref, conv1_ref, conv2_ref, grad_ref, g1_ref, g2_ref,
                  band_ref, up_ref, mid_ref):
    pairs = x_ref.shape[1] // 128
    band_map(conv2_ref, 2, band_ref)
    b = band_ref[...]
    total = None
    carry = None
    for k in range(1, pairs):
        both = earlier(first_ref, k)
        d = gate_grad(dot(both, b), up_ref[:, pair(k - 1)])
        part = dot_t0(both, d)
        total = part if total is None else total + part
        back = dot_t1(d, b)
        low = back[:, :128] if carry is None else carry + back[:, :128]
        mid_ref[:, pair(k - 1)] = low.astype(BF16)
        carry = back[:, 128:]
    mid_ref[:, pair(pairs - 1)] = carry.astype(BF16)
    band_grad(total, 2, g2_ref)
    band_map(conv1_ref, 1, band_ref)
    b = band_ref[...]
    total = None
    carry = None
    for k in range(pairs):
        both = earlier(x_ref, k)
        d = gate_grad(dot(both, b), mid_ref[:, pair(k)].astype(F32))
        part = dot_t0(both, d)
        total = part if total is None else total + part
        back = dot_t1(d, b)
        if k > 0:
            low = carry + back[:, :128]
            if k > 1:
                low = low + cot_ref[:, pair(k - 2)].astype(F32)
            grad_ref[:, pair(k - 1)] = low.astype(BF16)
        carry = back[:, 128:]
    last = carry + cot_ref[:, pair(pairs - 2)].astype(F32)
    grad_ref[:, pair(pairs - 1)] = last.astype(BF16)
    band_grad(total, 1, g1_ref)


def mix_grad(term_ref, cot_ref, c):
    acc = None
    for k in range(cot_ref.shape[1] // 128):
        part = dot_t0(term_ref[:, pair(k)], cot_ref[:, pair(k)])
        acc = part if acc is None else acc + part
    return acc[:c, :c] + acc[c:, c:]


def early_part(hidden_ref, hop_ref, x_ref, cot_ref, mix_ref, gm_ref, map0, map1, wide_ref):
    c = mix_ref.shape[1]
    block_map(mix_ref, 0, map0)
    block_map(mix_ref, 1, map1)
    for k in range(cot_ref.shape[1] // 128):
        acc = x_ref[:, pair(k + 1)].astype(F32)
        acc = acc + dot(hidden_ref[:, pair(k)], map0[...])
        wide_ref[:, pair(k)] = acc + dot(hop_ref[:, pair(k)], map1[...])
    gm_ref[0] = mix_grad(hidden_ref, cot_ref, c)
    gm_ref[1] = mix_grad(hop_ref, cot_ref, c)


def main_body(parts, reps, scale,
              x_ref, cot_ref, conv1_ref, conv2_ref, mix_ref, dense_ref, picks_ref, base_ref,
              pieces_ref,
              out_ref, grad_ref, sum_ref,
              first_ref, hidden_ref, hop_ref, second_ref, up_ref, mid_ref, band_ref,
              map0, map1, map2, g1_ref, g2_ref, gm_ref,
              wide_ref, send1, send2, send3, recv0, recv1, recv2, recv3,
              pack_ref, got_ref, part_ref, reps_ref, sums_ref,
              ssem, rsem, asem, arsem, bsem, brsem):
    me = lax.axis_index("dom")
    mine = lax.axis_index("rep")
    nodes = x_ref.shape[0]
    c = mix_ref.shape[1]
    pairs = cot_ref.shape[1] // 128
    feats = cot_ref.shape[1]

    barrier = pltpu.get_barrier_semaphore()
    for o in range(1, parts):
        pl.semaphore_signal(barrier, inc=1, device_id={"dom": lax.rem(me + o, parts)},
                            device_id_type=pl.DeviceIdType.MESH)
    for o in range(1, reps):
        pl.semaphore_signal(barrier, inc=1, device_id={"rep": lax.rem(mine + o, reps)},
                            device_id_type=pl.DeviceIdType.MESH)
    pl.semaphore_wait(barrier, parts - 1 + reps - 1)

    def copies(level, src, dst):
        made = []
        for o in sorted(range(1, parts), key=lambda o: abs(2 * o - parts)):
            peer = lax.rem(me + o, parts)
            made.append(pltpu.make_async_remote_copy(
                src_ref=src.at[peer, pl.ds(c, feats - c)],
                dst_ref=dst.at[me, pl.ds(c, feats - c)],
                send_sem=ssem.at[level, o],
                recv_sem=rsem.at[level, o],
                device_id={"dom": peer},
                device_id_type=pl.DeviceIdType.MESH,
            ))
        for m in made:
            m.start()
        return made

    def arrive(made):
        for m in made:
            m.wait_recv()

    round0 = copies(0, pieces_ref, recv0)
    for buf in (recv0, recv1, recv2, recv3):
        buf[:, 0:c, :] = jnp.zeros((parts, c, BLK), BF16)
        buf[me] = jnp.zeros((feats, BLK), BF16)

    forward_part(x_ref, conv1_ref, conv2_ref, first_ref, hidden_ref, band_ref)
    pack_rows(hidden_ref[...], picks_ref, 0, parts, send1)
    round1 = copies(1, send1, recv1)

    arrive(round0)
    g = from_blocks(base_ref[...], picks_ref, 0, parts, recv0).astype(BF16)
    pack_rows(g, dense_ref, nodes, parts, send2)
    round2 = copies(2, send2, recv2)
    up_ref[...] = dot_t0(dense_ref[:, :nodes], g)
    block_map(mix_ref, 0, map0)
    for k in range(pairs):
        up_ref[:, pair(k)] += dot_t1(cot_ref[:, pair(k)], map0[...])

    own = dot(dense_ref[:, :nodes], hidden_ref[...])
    arrive(round1)
    hop_ref[...] = from_blocks(own, dense_ref, nodes, parts, recv1).astype(BF16)
    pack_rows(hop_ref[...], picks_ref, 0, parts, send3)
    round3 = copies(3, send3, recv3)

    arrive(round2)
    up_ref[...] = from_blocks(up_ref[...], picks_ref, 0, parts, recv2)
    backward_part(x_ref, first_ref, cot_ref, conv1_ref, conv2_ref, grad_ref, g1_ref, g2_ref,
                  band_ref, up_ref, mid_ref)

    early_part(hidden_ref, hop_ref, x_ref, cot_ref, mix_ref, gm_ref, map0, map1, wide_ref)
    block_map(mix_ref, 2, map2)
    own = dot(dense_ref[:, :nodes], hop_ref[...])
    arrive(round3)
    second_ref[...] = from_blocks(own, dense_ref, nodes, parts, recv3).astype(BF16)
    gm_ref[2] = mix_grad(second_ref, cot_ref, c)

    per = pack_ref.shape[1]
    flat = pack_ref
    flat[...] = jnp.zeros(flat.shape, F32)

    def put(first_row, value):
        rows = value.shape[0]
        done = 0
        while done < rows:
            slot, at = divmod(first_row + done, per)
            step = min(per - at, rows - done)
            flat[slot, at : at + step, :] = value[done : done + step]
            done += step

    put(0, g1_ref[0])
    put(c, g1_ref[1])
    put(2 * c, g2_ref[0])
    put(3 * c, g2_ref[1])
    put(4 * c, jnp.concatenate([gm_ref[0], gm_ref[1]], axis=1))
    put(5 * c, jnp.concatenate([gm_ref[2], jnp.zeros((c, c), F32)], axis=1))

    scatter = []
    for o in range(1, parts):
        peer = lax.rem(me + o, parts)
        scatter.append(pltpu.make_async_remote_copy(
            src_ref=pack_ref.at[peer], dst_ref=got_ref.at[me],
            send_sem=asem.at[0, o], recv_sem=arsem.at[0, o],
            device_id={"dom": peer}, device_id_type=pl.DeviceIdType.MESH))
    for m in scatter:
        m.start()
    for k in range(pairs):
        wide_ref[:, pair(k)] += dot(second_ref[:, pair(k)], map2[...])
    out_ref[...] = wide_ref[...].T[c:].astype(BF16)
    got_ref[me] = pack_ref[me]
    arrive(scatter)
    total = got_ref[0]
    for q in range(1, parts):
        total = total + got_ref[q]
    part_ref[...] = total
    around = []
    for o in range(1, reps):
        peer = lax.rem(mine + o, reps)
        around.append(pltpu.make_async_remote_copy(
            src_ref=part_ref, dst_ref=reps_ref.at[mine],
            send_sem=bsem.at[o], recv_sem=brsem.at[o],
            device_id={"rep": peer}, device_id_type=pl.DeviceIdType.MESH))
    for m in around:
        m.start()
    reps_ref[mine] = total
    arrive(around)
    total = reps_ref[0]
    for q in range(1, reps):
        total = total + reps_ref[q]
    for m in around:
        m.wait_send()
    part_ref[...] = total * (1.0 / scale)
    final = []
    for o in range(1, parts):
        peer = lax.rem(me + o, parts)
        final.append(pltpu.make_async_remote_copy(
            src_ref=part_ref, dst_ref=sums_ref.at[me],
            send_sem=asem.at[1, o], recv_sem=arsem.at[1, o],
            device_id={"dom": peer}, device_id_type=pl.DeviceIdType.MESH))
    for m in final:
        m.start()
    sums_ref[me] = part_ref[...]
    arrive(final)

    sum_ref[...] = sums_ref[...]
    for m in round0 + round1 + round2 + round3 + scatter + final:
        m.wait_send()


def shards(inputs, cotangent, conv_one, conv_two, mix_weight, send_rows, counts, tile_cols,
           tile_vals):
    windows, nodes, flat = inputs.shape
    channels = mix_weight.shape[1]
    parts = lax.axis_size("dom")
    reps = lax.axis_size("rep")
    kept = flat // channels - 3
    wide = flat - 2 * channels
    halo = parts * BLK
    blocks = (parts, wide, BLK)
    prepared = [((nodes, nodes + halo), BF16), ((nodes, halo), BF16), ((nodes, wide), BF16),
                ((nodes, wide), F32), (blocks, BF16)]
    dense, picks, cot_wide, base, pieces = pl.pallas_call(
        prepare_body,
        out_shape=[jax.ShapeDtypeStruct(s, d) for s, d in prepared],
        in_specs=[VM, VM, VM, SM, SM, VM],
        out_specs=[VM] * 5,
        scratch_shapes=[pltpu.VMEM((parts + nodes // BLK, BLK, BLK), F32),
                        pltpu.VMEM((128, 128), BF16), pltpu.VMEM((nodes, wide), BF16)],
        compiler_params=LIMIT,
        name="prepare",
    )(cotangent[0].T, mix_weight, send_rows[0], counts, tile_cols, tile_vals)
    scaling = math.sqrt(float(windows * reps * nodes * parts * kept))
    unit = 8 * parts
    per = -(-6 * channels // unit) * unit // parts
    results = [((kept * channels, nodes), BF16), ((nodes, flat), BF16), ((parts, per, BLK), F32)]
    scratch = [((nodes, flat), BF16), ((nodes, wide), BF16), ((nodes, wide), BF16),
               ((nodes, wide), BF16), ((nodes, wide), F32), ((nodes, flat), BF16),
               ((256, 256), BF16), ((128, 128), BF16), ((128, 128), BF16), ((128, 128), BF16),
               (conv_one.shape, F32), (conv_two.shape, F32), (mix_weight.shape, F32)]
    scratch += [((nodes, wide), F32)] + [(blocks, BF16)] * 7
    scratch += [((parts, per, BLK), F32), ((parts, per, BLK), F32), ((per, BLK), F32),
                ((reps, per, BLK), F32), ((parts, per, BLK), F32)]
    dma = pltpu.SemaphoreType.DMA
    output, grad_input, packed = pl.pallas_call(
        functools.partial(main_body, parts, reps, scaling),
        out_shape=[jax.ShapeDtypeStruct(s, d) for s, d in results],
        in_specs=[VM] * 9,
        out_specs=[VM] * 3,
        scratch_shapes=[pltpu.VMEM(s, d) for s, d in scratch]
        + [dma((4, parts)), dma((4, parts)), dma((2, parts)), dma((2, parts)), dma((reps,)),
           dma((reps,))],
        compiler_params=pltpu.CompilerParams(
            vmem_limit_bytes=60 * 1024 * 1024, collective_id=0, has_side_effects=True),
        name="layer",
    )(inputs[0], cot_wide, conv_one, conv_two, mix_weight, dense, picks, base, pieces)
    c = channels
    rows = packed.reshape(parts * per, BLK)
    gm = jnp.stack([rows[4 * c : 5 * c, :c], rows[4 * c : 5 * c, c:], rows[5 * c : 6 * c, :c]])
    return (
        output.T[None],
        grad_input[None],
        rows[: 2 * c].reshape(conv_one.shape),
        rows[2 * c : 4 * c].reshape(conv_two.shape),
        gm,
    )


def place_tiles(me, parts, cols_ref, vals_ref, dense_ref):
    rtiles, slots = vals_ref.shape[0], vals_ref.shape[1]
    for r in range(rtiles):
        for c in range(dense_ref.shape[1] // BLK):
            named = c if c < rtiles else rtiles + lax.rem(me - (c - rtiles + 1) + parts, parts)
            total = None
            for j in range(slots):
                keep = jnp.where(cols_ref[r, j] == named, 1.0, 0.0)
                part = vals_ref[r, j].astype(F32) * keep
                total = part if total is None else total + part
            dense_ref[r * BLK : (r + 1) * BLK, c * BLK : (c + 1) * BLK] = total.astype(BF16)


def chunk(first, size):
    return pl.ds(pl.multiple_of(first, size), size)


def steps_body(parts, reps, scale,
               x_ref, cot_ref, conv1_ref, conv2_ref, mix_ref, send_ref, counts_ref, cols_ref, vals_ref,
               out_ref, grad_ref, one_out, two_out, mix_out,
               dense_ref, wanted_ref, xt_ref, first_ref, hid_ref, d1_ref, d2_ref, mid_ref,
               band1, band1t, band2, band2t, maps, mapst,
               adj_ref, lists_ref, picks_ref,
               cf_ref, hf_ref, f1_ref, c1_ref, own_ref, part_t, ext_ref,
               gh_ref, mx_ref, ghs_ref, mxs_ref,
               g1_ref, g2_ref, pack0, got0, half0, all0, full0, sums0,
               pack1, got1, half1, all1, full1, sums1,
               lsend, lrecv, fsend, frecv, esend, erecv, tsend, trecv,
               asem, arsem, bsem, brsem):
    me = lax.axis_index("dom")
    mine = lax.axis_index("rep")
    nodes = x_ref.shape[0]
    c = mix_ref.shape[1]
    pairs = x_ref.shape[1] // 128
    mesh_ids = pl.DeviceIdType.MESH
    holder = lax.rem(parts // 2 - reps // 2 + mine + parts, parts)
    extra = parts * c
    zs = parts // 2
    z, xx = me // 2, lax.rem(me, 2)
    yy, core = mine // 2, lax.rem(mine, 2)
    chips = parts * reps // 2
    chip = me * 2 + yy
    crep = yy * 2 + 1 - core

    barrier = pltpu.get_barrier_semaphore()
    for o in range(1, chips):
        peer = lax.rem(chip + o, chips)
        pl.semaphore_signal(barrier, inc=1, device_id={"dom": peer // 2, "rep": lax.rem(peer, 2) * 2 + core},
                            device_id_type=mesh_ids)
    pl.semaphore_signal(barrier, inc=1, device_id={"rep": yy * 2 + 1 - core}, device_id_type=mesh_ids)
    place_tiles(me, parts, cols_ref, vals_ref, dense_ref)
    lane = lax.broadcasted_iota(jnp.int32, (1, BLK), 1)
    for o in range(parts):
        t = lax.rem(me + o, parts)
        wanted_ref[o : o + 1, :] = jnp.where(
            lane < counts_ref[0, t], send_ref[pl.ds(t, 1), :], -1)
    pl.semaphore_wait(barrier, chips)

    def remote(src, dst, ssem, rsem, **where):
        return pltpu.make_async_remote_copy(
            src_ref=src, dst_ref=dst, send_sem=ssem, recv_sem=rsem,
            device_id=where, device_id_type=mesh_ids)

    order = sorted(range(1, parts), key=lambda o: abs(2 * o - parts))

    own_rows = 3 * (nodes // 16)
    both_rows = nodes // 2 - 2 * own_rows

    def span(sub, cc, y):
        at = cc * (nodes // 2) + (own_rows if sub else (own_rows + both_rows) * y)
        return pl.ds(pl.multiple_of(at, 16), both_rows if sub else own_rows)

    def piece(p, sub, cc, y):
        return adj_ref.at[p, span(sub, cc, y)]

    def source_z(t, way):
        return z - t if way == 0 else z + t

    def valid(t, way):
        if t == 0:
            return z >= 0
        return z >= t if way == 0 else z + t < zs

    def slot(t, way, sub):
        return 2 * (0 if t == 0 else 2 * t - 1 + way) + sub

    def base(t, way):
        return source_z(t, way) * 2 + xx

    def cross(t, way):
        return source_z(t, way) * 2 + 1 - xx

    def first_source(t, way, sub):
        return dense_ref.at[span(sub, core, yy)] if t == 0 else piece(base(t, way), sub, core, yy)

    def along(t, way, sub, out_way):
        to = (z + 1 if out_way == 0 else z - 1) * 2 + xx
        return remote(first_source(t, way, sub), piece(base(t, way), sub, core, yy),
                      tsend.at[out_way, slot(t, way, sub)], trecv.at[0, slot(t + 1, out_way, sub)], dom=to)

    def across(t, way, sub):
        return remote(first_source(t, way, sub), piece(base(t, way), sub, core, yy),
                      tsend.at[2, slot(t, way, sub)], trecv.at[2, slot(t, way, sub)], dom=z * 2 + 1 - xx)

    def hand(kind, part, t, way, sub, y):
        ref = piece(part(t, way), sub, core, y)
        to = (1 - yy) * 2 + core if kind in (3, 5) else crep
        return remote(ref, ref, tsend.at[kind, slot(t, way, sub)], trecv.at[kind, slot(t, way, sub)], rep=to)

    def arrived(kind, ref, t, way, sub):
        remote(ref, ref, tsend.at[kind, slot(t, way, sub)], trecv.at[kind, slot(t, way, sub)],
               rep=crep).wait_recv()

    def ways(t):
        return (0,) if t == 0 else (0, 1)

    def lane_sends(t, way, sub):
        made = []
        if t + 1 < zs:
            for w in (0, 1) if t == 0 else (way,):
                made.append((z + 1 < zs if w == 0 else z >= 1, along(t, way, sub, w)))
        made.append((None, across(t, way, sub)))
        return made

    def side_sends(t, way, sub, part, kind):
        if t == 0 and part is base:
            return []
        made = [(None, hand(kind, part, t, way, sub, yy))] if sub == 0 else []
        return made + [(None, hand(kind + 1, part, t, way, sub, yy))]

    def core_sends(t, way, part, kind):
        if t == 0 and part is base:
            return []
        return [(None, hand(kind, part, t, way, 0, 1 - yy))]

    def go(sends, wait=False):
        for cond, copy in sends:
            act = copy.wait_send if wait else copy.start
            if cond is None:
                act()
            else:
                pl.when(cond)(act)

    def on_base(t, way, sub):
        @pl.when(valid(t, way))
        def _():
            arrived(0, piece(base(t, way), sub, core, yy), t, way, sub)
            go(lane_sends(t, way, sub) + side_sends(t, way, sub, base, 3))

    def on_cross(t, way, sub):
        @pl.when(valid(t, way))
        def _():
            arrived(2, piece(cross(t, way), sub, core, yy), t, way, sub)
            go(side_sends(t, way, sub, cross, 5))

    def on_plane(t, way, part, kind):
        @pl.when(valid(t, way))
        def _():
            arrived(kind, piece(part(t, way), 0, core, 1 - yy), t, way, 0)
            go(core_sends(t, way, part, 7 if kind == 3 else 8))

    def on_tiles(t, way, part, kind, use):
        @pl.when(valid(t, way))
        def _():
            if t or part is cross:
                for sub in (0, 1):
                    arrived(kind + 1, piece(part(t, way), sub, 1 - core, yy), t, way, sub)
                arrived(7 if kind == 3 else 8, piece(part(t, way), 0, 1 - core, 1 - yy), t, way, 0)
            use(part(t, way))

    relay = []

    def step_relay(count=1):
        for _ in range(count):
            if relay:
                relay.pop()()

    def scatter_field(level, src, first, dst):
        made = []
        for o in order:
            peer = lax.rem(me + o, parts)
            made.append(remote(src.at[chunk(first + peer * c, c)], dst.at[me, pl.ds(0, c)],
                               fsend.at[level, o], frecv.at[level, o], dom=peer))
        for m in made:
            m.start()
        off = lax.rem(holder - me + parts, parts)
        last = remote(src.at[pl.ds(first + extra, c)], dst.at[me, pl.ds(c, c)],
                      esend.at[level, 0], erecv.at[level, off], dom=holder)
        pl.when(me != holder)(last.start)
        dst[me, 0:c, :] = src[chunk(first + me * c, c), :]

        @pl.when(me == holder)
        def _():
            dst[me, c : 2 * c, :] = src[first + extra : first + extra + c, :]

        @pl.when(me != holder)
        def _():
            dst[:, c : 2 * c, :] = jnp.zeros((parts, c, nodes), BF16)
        return made, last

    def field_arrives(level, made, src, dst):
        for m in made:
            m.wait_recv()

        @pl.when(me == holder)
        def _():
            for o in range(1, parts):
                q = lax.rem(me - o + parts, parts)
                remote(dst.at[q, pl.ds(c, c)], dst.at[q, pl.ds(c, c)], esend.at[level, 0],
                       erecv.at[level, o], dom=q).wait_recv()

    def home_copies(level, o, src, first, dst):
        q = lax.rem(me + o, parts)
        one = remote(src.at[q, pl.ds(0, c)], dst.at[chunk(first + me * c, c)],
                     fsend.at[level, o], frecv.at[level, o], dom=q)
        two = remote(src.at[q, pl.ds(c, c)], dst.at[pl.ds(first + extra, c)],
                     esend.at[level, o], erecv.at[level, 0], dom=q)
        return one, two

    def go_home(level, o, src, first, dst):
        if o:
            one, two = home_copies(level, o, src, first, dst)
            one.start()
            pl.when(me == holder)(two.start)
            return
        dst[chunk(first + me * c, c), :] = src[me, 0:c, :]

        @pl.when(me == holder)
        def _():
            dst[first + extra : first + extra + c, :] = src[me, c : 2 * c, :]

    def home_arrives(level, src, first, dst):
        for o in range(1, parts):
            home_copies(level, o, src, first, dst)[0].wait_recv()
        pl.when(me != holder)(home_copies(level, 1, src, first, dst)[1].wait_recv)

    def home_sent(level, src, first, dst):
        for o in range(1, parts):
            one, two = home_copies(level, o, src, first, dst)
            one.wait_send()
            pl.when(me == holder)(two.wait_send)

    go(lane_sends(0, 0, 0) + lane_sends(0, 0, 1))
    cot_round = scatter_field(0, cot_ref, 0, cf_ref)
    lists = []
    for o in order:
        peer = lax.rem(me + o, parts)
        lists.append(remote(wanted_ref, lists_ref.at[me], lsend.at[o], lrecv.at[o], dom=peer))
    for m in lists:
        m.start()
    lists_ref[me] = wanted_ref[...]
    adj_ref[me] = dense_ref[...]

    def back_piece(g_ref, p):
        t = dot(g_ref[p], adj_ref[p])
        own_ref[p] = t[:, :nodes]
        for o in range(1, parts):
            at = nodes + (o - 1) * BLK
            owner = lax.rem(p - o + parts, parts)
            part_t[owner, :, (o - 1) * BLK : o * BLK] = t[:, at : at + BLK].astype(BF16)

    hid_round = []

    def first_piece():
        field_arrives(0, cot_round[0], cot_ref, cf_ref)
        back_piece(cf_ref, me)

    def send_hidden():
        hid_round.extend(scatter_field(1, hid_ref, c, hf_ref))

    def add(handler, t, *rest):
        for w in ways(t):
            relay.append(functools.partial(handler, t, w, *rest))

    use = functools.partial(back_piece, cf_ref)
    for t in range(1, zs + 2):
        if t < zs:
            for sub in (0, 1):
                add(on_base, t, sub)
        if t <= zs:
            for sub in (0, 1):
                add(on_cross, t - 1, sub)
        if 2 <= t <= zs:
            add(on_plane, t - 1, base, 3)
        if t >= 2:
            add(on_plane, t - 2, cross, 5)
        if t == zs - 1:
            relay.append(send_hidden)
            relay.append(first_piece)
        if t >= zs:
            for u in range(t - zs, t - zs + 1):
                add(on_tiles, u, cross, 5, use)
                add(on_tiles, u + 1, base, 3, use)
    for u in range(2, zs):
        add(on_tiles, u, cross, 5, use)
        if u + 1 < zs:
            add(on_tiles, u + 1, base, 3, use)
    relay.reverse()

    for k in range(pairs):
        xt_ref[pair(k), :] = x_ref[:, pair(k)].astype(F32).T.astype(BF16)
    for conv, dil, nat, tra in ((conv1_ref, 1, band1, band1t), (conv2_ref, 2, band2, band2t)):
        band_map(conv, dil, nat)
        tra[...] = nat[...].astype(F32).T.astype(BF16)

    def earlier_t(ref, k):
        if k == 0:
            v = ref[0:128, :]
            return jnp.concatenate([jnp.zeros_like(v), v], axis=0)
        return ref[window2(k - 1), :]

    def gated(pre, d_ref, k):
        filt = jnp.tanh(pre[:128])
        gates = 0.5 * jnp.tanh(0.5 * pre[128:]) + 0.5
        d_ref[k, 0:128, :] = gates * (1.0 - filt * filt)
        d_ref[k, 128:256, :] = filt * gates * (1.0 - gates)
        return (filt * gates).astype(BF16)

    for k in range(pairs):
        first_ref[pair(k), :] = gated(dot(band1t[...], earlier_t(xt_ref, k)), d1_ref, k)
        if k % 2:
            step_relay()
    for k in range(1, pairs):
        hid_ref[pair(k - 1), :] = gated(dot(band2t[...], earlier_t(first_ref, k)), d2_ref, k)
        step_relay()

    for i in range(3):
        block_map(mix_ref, i, maps.at[i])
        mapst[i] = maps[i].astype(F32).T.astype(BF16)
    gh_ref[0:c, :] = jnp.zeros((c, nodes), BF16)

    for m in lists:
        m.wait_recv()
    node = lax.broadcasted_iota(jnp.int32, (nodes, BLK), 0)
    for q in range(parts):
        for o in range(1, parts):
            hit = node == lists_ref[q, o : o + 1, :]
            picks_ref[q, :, (o - 1) * BLK : o * BLK] = jnp.where(hit, 1.0, 0.0).astype(BF16)
        step_relay(2)

    step_relay(len(relay))

    def back_owner(q):
        return (own_ref[q] + dot_t1(part_t[q], picks_ref[q])).astype(BF16)

    for q in range(parts):
        c1_ref[q] = back_owner(q)
    for p in range(parts):
        back_piece(c1_ref, p)
    field_arrives(1, hid_round[0], hid_ref, hf_ref)
    mix = [None] * 3
    for o in order + [0]:
        q = lax.rem(me + o, parts)
        moved = (cf_ref[q], c1_ref[q], back_owner(q))
        grads = [dot(maps[i], moved[i]) for i in range(3)]
        ghs_ref[q] = (grads[0] + grads[1] + grads[2]).astype(BF16)
        go_home(2, o, ghs_ref, c, gh_ref)
        for i in range(3):
            more = dot_t1(hf_ref[q], moved[i])
            mix[i] = more if mix[i] is None else mix[i] + more
    mix = [m[:c, :c] + m[c:, c:] for m in mix]

    def reducer(g, pack, got, half, got_all, full, sums):
        def over_core(stage, src, dst):
            return [remote(src, dst, bsem.at[2 * g + stage], brsem.at[2 * g + stage], rep=crep)]

        def over_chips(stage, src_of, dst):
            made = []
            for o in range(1, chips):
                peer = lax.rem(chip + o, chips)
                made.append(remote(src_of(peer), dst, asem.at[2 * g + stage, o], arsem.at[2 * g + stage, o],
                                   dom=peer // 2, rep=lax.rem(peer, 2) * 2 + core))
            return made

        steps = (lambda: over_core(0, pack.at[1 - core], got),
                 lambda: over_chips(0, lambda peer: half.at[peer], got_all.at[chip]),
                 lambda: over_chips(1, lambda peer: full, sums.at[core, chip]),
                 lambda: over_core(1, sums.at[core], sums.at[core]))

        def start(i):
            for m in steps[i]():
                m.start()

        def arrive(i):
            for m in steps[i]():
                m.wait_recv()

        def first():
            start(0)

        def second():
            arrive(0)
            total = pack[core] + got[...]
            share = half.shape[1]
            for q in range(chips):
                half[q] = total[q * share : (q + 1) * share]
            start(1)
            got_all[chip] = half[chip]

        def third():
            arrive(1)
            total = got_all[0]
            for q in range(1, chips):
                total = total + got_all[q]
            full[...] = total * (1.0 / scale)
            start(2)
            sums[core, chip] = full[...]

        def fourth():
            arrive(2)
            start(3)

        def last():
            arrive(3)

        def sent():
            for i in range(4):
                for m in steps[i]():
                    m.wait_send()

        return first, second, third, fourth, last, sent

    early = reducer(0, pack0, got0, half0, all0, full0, sums0)
    late = reducer(1, pack1, got1, half1, all1, full1, sums1)
    pack0[...] = jnp.zeros(pack0.shape, F32)
    for i in range(3):
        pack0[i // 2, (i % 2) * c : (i % 2 + 1) * c, 0:c] = mix[i]
    early[0]()

    def extend(f_ref):
        for q in range(parts):
            ext_ref[q, :, 0:nodes] = f_ref[q]
            halo = dot(f_ref[q], picks_ref[q]).astype(BF16)
            for o in range(1, parts):
                at = nodes + (o - 1) * BLK
                ext_ref[(q + o) % parts, :, at : at + BLK] = halo[:, (o - 1) * BLK : o * BLK]

    extend(hf_ref)
    for p in range(parts):
        f1_ref[p] = dot_t1(ext_ref[p], adj_ref[p]).astype(BF16)
    extend(f1_ref)
    for o in order + [0]:
        q = lax.rem(me + o, parts)
        second = dot_t1(ext_ref[q], adj_ref[q]).astype(BF16)
        mixed = dot(mapst[0], hf_ref[q]) + dot(mapst[1], f1_ref[q]) + dot(mapst[2], second)
        mxs_ref[q] = mixed.astype(BF16)
        go_home(3, o, mxs_ref, 0, mx_ref)
    early[1]()

    home_arrives(2, ghs_ref, c, gh_ref)

    def conv_back(sig_ref, d_ref, up_of, band, low_of, first_pair, dilation, out):
        total, carry = None, None
        b = band[...]
        for k in range(first_pair, pairs):
            up = up_of(k)
            both = earlier_t(sig_ref, k)
            d = jnp.concatenate([up * d_ref[k, 0:128, :], up * d_ref[k, 128:256, :]], axis=0)
            d = d.astype(BF16)
            part = dot_t1(both, d)
            total = part if total is None else total + part
            back = dot(b, d)
            if k > 0:
                low_of(k - 1, back[:128] if carry is None else carry + back[:128])
            carry = back[128:]
        low_of(pairs - 1, carry)
        band_grad(total, dilation, out)

    def set_mid(k, low):
        mid_ref[pair(k), :] = low.astype(BF16)

    def set_grad(k, low):
        if k == 1:
            low = low + jnp.concatenate([jnp.zeros((c, nodes), F32), cot_ref[0:c, :].astype(F32)], axis=0)
        elif k > 1:
            low = low + cot_ref[(2 * k - 3) * c : (2 * k - 1) * c, :].astype(F32)
        grad_ref[:, pair(k)] = low.T.astype(BF16)

    conv_back(first_ref, d2_ref, lambda k: gh_ref[pair(k - 1), :].astype(F32), band2, set_mid, 1, 2, g2_ref)
    conv_back(xt_ref, d1_ref, lambda k: mid_ref[pair(k), :].astype(F32), band1, set_grad, 0, 1, g1_ref)

    for tap in range(2):
        pack1[0, tap * c : (tap + 1) * c, :] = g1_ref[tap]
        pack1[1, tap * c : (tap + 1) * c, :] = g2_ref[tap]
    late[0]()
    late[1]()
    early[2]()
    home_arrives(3, mxs_ref, 0, mx_ref)
    kept = out_ref.shape[0]
    out_ref[...] = (mx_ref[...].astype(F32) + xt_ref[pairs * 128 - kept :, :].astype(F32)).astype(BF16)
    late[2]()
    early[3]()

    for m in cot_round[0] + hid_round[0] + lists:
        m.wait_send()
    pl.when(me != holder)(cot_round[1].wait_send)
    pl.when(me != holder)(hid_round[1].wait_send)
    home_sent(2, ghs_ref, c, gh_ref)
    home_sent(3, mxs_ref, 0, mx_ref)
    for t in range(zs):
        for w in ways(t):
            @pl.when(valid(t, w))
            def _():
                for sub in (0, 1):
                    go(lane_sends(t, w, sub) + side_sends(t, w, sub, base, 3)
                       + side_sends(t, w, sub, cross, 5), wait=True)
                go(core_sends(t, w, base, 7) + core_sends(t, w, cross, 8), wait=True)
    late[3]()
    early[4]()
    share = sums0.shape[2]
    for q in range(chips):
        tap, at = divmod(q * share, c)
        mix_out[tap, at : at + share, :] = sums0[0, q, :, 0:c]
        if tap == 0:
            mix_out[2, at : at + share, :] = sums0[1, q, :, 0:c]
    early[5]()
    late[4]()
    for q in range(chips):
        tap, at = divmod(q * share, c)
        one_out[tap, at : at + share, :] = sums1[0, q]
        two_out[tap, at : at + share, :] = sums1[1, q]
    late[5]()


def finish_body(*refs):
    half = len(refs) // 2
    for a, b in zip(refs[:half], refs[half:]):
        b[...] = a[...]


def step_shards(inputs, cotangent, conv_one, conv_two, mix_weight, send_rows, counts, tile_cols,
                tile_vals):
    windows, nodes, flat = inputs.shape
    channels = mix_weight.shape[1]
    parts = lax.axis_size("dom")
    reps = lax.axis_size("rep")
    kept = flat // channels - 3
    c = channels
    pairs = flat // 128
    halo = (parts - 1) * BLK
    ext = nodes + halo
    scaling = math.sqrt(float(windows * reps * nodes * parts * kept))
    results = [((kept * c, nodes), BF16), ((nodes, flat), BF16), (conv_one.shape, F32),
               (conv_two.shape, F32), (mix_weight.shape, F32)]
    field = (parts, 2 * c, nodes)
    wide = flat - 2 * c
    scratch = [((nodes, ext), BF16), ((parts, BLK), jnp.int32),
               ((flat, nodes), BF16), ((flat, nodes), BF16), ((wide, nodes), BF16),
               ((pairs, 256, nodes), F32), ((pairs, 256, nodes), F32), ((flat, nodes), BF16)]
    scratch += [((256, 256), BF16)] * 4 + [((3, 128, 128), BF16)] * 2
    scratch += [((parts, nodes, ext), BF16), ((parts, parts, BLK), jnp.int32),
                ((parts, nodes, halo), BF16)]
    scratch += [(field, BF16)] * 4 + [(field, F32), ((parts, 2 * c, halo), BF16),
                                      ((parts, 2 * c, ext), BF16)]
    scratch += [((wide, nodes), BF16), ((kept * c, nodes), BF16), (field, BF16), (field, BF16)]
    scratch += [(conv_one.shape, F32), (conv_two.shape, F32)]
    chips = parts * reps // 2
    share = 2 * c // chips
    for _ in range(2):
        scratch += [((2, 2 * c, BLK), F32), ((2 * c, BLK), F32), ((chips, share, BLK), F32),
                    ((chips, share, BLK), F32), ((share, BLK), F32), ((2, chips, share, BLK), F32)]
    dma = pltpu.SemaphoreType.DMA
    sems = [(parts,), (parts,), (4, parts), (4, parts), (4, parts), (4, parts),
            (9, 2 * parts), (9, 2 * parts), (4, chips), (4, chips), (4,), (4,)]
    made = pl.pallas_call(
        functools.partial(steps_body, parts, reps, scaling),
        out_shape=[jax.ShapeDtypeStruct(s, d) for s, d in results],
        in_specs=[VM] * 6 + [SM, SM, VM],
        out_specs=[VM] * 5,
        scratch_shapes=[pltpu.VMEM(s, d) for s, d in scratch] + [dma(s) for s in sems],
        compiler_params=pltpu.CompilerParams(
            vmem_limit_bytes=60 * 1024 * 1024, collective_id=1, has_side_effects=True),
        name="steps",
    )(inputs[0], cotangent[0].T, conv_one, conv_two, mix_weight, send_rows[0], counts, tile_cols,
      tile_vals)
    output, grad_input, one, two, mix = pl.pallas_call(
        finish_body,
        out_shape=[jax.ShapeDtypeStruct(s, d) for s, d in results],
        in_specs=[VM] * 5,
        out_specs=[VM] * 5,
        compiler_params=LIMIT,
        name="finish",
    )(*made)
    return output.T[None], grad_input[None], one, two, mix


def solution(mesh):
    placed = (
        P("rep", "dom", None),
        P("rep", "dom", None),
        P(),
        P(),
        P(),
        P("dom", None, None),
        P("dom", None),
        P("dom", None),
        P("dom", None, None, None),
    )
    parts, reps = mesh.shape["dom"], mesh.shape["rep"]

    def layer(*args):
        kept = args[0].shape[2] // args[4].shape[1] - 3
        by_step = parts % 2 == 0 and reps == 4 and parts == kept - 1
        return step_shards(*args) if by_step else shards(*args)

    return jax.shard_map(
        layer,
        mesh=mesh,
        in_specs=placed,
        out_specs=(P("rep", "dom", None), P("rep", "dom", None), P(), P(), P()),
        check_vma=False,
    )
```

```python
import functools
import math

import jax
import jax.numpy as jnp
from jax import lax
from jax.experimental import pallas as pl
from jax.experimental.pallas import tpu as pltpu
from jax.sharding import PartitionSpec as P

F32 = jnp.float32
BF16 = jnp.bfloat16
BLK = 128
VM = pl.BlockSpec(memory_space=pltpu.VMEM)
SM = pl.BlockSpec(memory_space=pltpu.SMEM)
LIMIT = pltpu.CompilerParams(vmem_limit_bytes=56 * 1024 * 1024)


def dot(a, b):
    return jnp.dot(a, b, preferred_element_type=F32)


def dot_t0(a, b):
    return lax.dot_general(a, b, (((0,), (0,)), ((), ())), preferred_element_type=F32)


def dot_t1(a, b):
    return lax.dot_general(a, b, (((1,), (1,)), ((), ())), preferred_element_type=F32)


def pair(k):
    return slice(k * 128, (k + 1) * 128)


def window2(k):
    return slice(k * 128, (k + 2) * 128)


def block_map(weight_ref, index, out_ref):
    c = weight_ref.shape[1]
    w = weight_ref[index]
    out_ref[...] = jnp.zeros(out_ref.shape, BF16)
    out_ref[0:c, 0:c] = w
    out_ref[c : 2 * c, c : 2 * c] = w


def band_blocks(dilation):
    if dilation == 1:
        return ((0, 1, 0), (0, 2, 1), (1, 2, 0), (1, 3, 1))
    return ((0, 0, 0), (0, 1, 1), (1, 2, 0), (1, 3, 1))


def band_map(conv_ref, dilation, out_ref):
    c = conv_ref.shape[1]
    out_ref[...] = jnp.zeros(out_ref.shape, BF16)
    for tap, i, o in band_blocks(dilation):
        w = conv_ref[tap]
        rows = slice(i * c, (i + 1) * c)
        out_ref[rows, o * c : (o + 1) * c] = w[:, :c]
        out_ref[rows, (o + 2) * c : (o + 3) * c] = w[:, c:]


def band_grad(total, dilation, out_ref):
    c = out_ref.shape[1]
    for tap in range(2):
        for half in range(2):
            acc = None
            for t, i, o in band_blocks(dilation):
                if t != tap:
                    continue
                col = (o + 2 * half) * c
                part = total[i * c : (i + 1) * c, col : col + c]
                acc = part if acc is None else acc + part
            out_ref[tap, :, half * c : (half + 1) * c] = acc


def activations(pre):
    filt = jnp.tanh(pre[:, :128])
    gates = 0.5 * jnp.tanh(0.5 * pre[:, 128:]) + 0.5
    return filt, gates


def earlier(ref, k):
    if k == 0:
        x = ref[:, 0:128]
        return jnp.concatenate([jnp.zeros_like(x), x], axis=1)
    return ref[:, window2(k - 1)]


def build_tiles(cols_ref, vals_ref, acc_ref, dense_ref):
    rtiles, slots = vals_ref.shape[0], vals_ref.shape[1]
    ctiles = dense_ref.shape[1] // BLK
    for r in range(rtiles):
        acc_ref[...] = jnp.zeros(acc_ref.shape, F32)
        for j in range(slots):
            c = cols_ref[r, j]
            acc_ref[c] = acc_ref[c] + vals_ref[r, j].astype(F32)
        for c in range(ctiles):
            dense_ref[r * BLK : (r + 1) * BLK, c * BLK : (c + 1) * BLK] = acc_ref[c].astype(BF16)


def build_picks(send_ref, counts_ref, picks_ref):
    parts = send_ref.shape[0]
    nodes = picks_ref.shape[0]
    lane = lax.broadcasted_iota(jnp.int32, (1, BLK), 1)
    rows = lax.broadcasted_iota(jnp.int32, (nodes, BLK), 0)
    for q in range(parts):
        wanted = jnp.where(lane < counts_ref[0, q], send_ref[q : q + 1, :], -1)
        hit = rows == wanted
        picks_ref[:, q * BLK : (q + 1) * BLK] = jnp.where(hit, 1.0, 0.0).astype(BF16)


def prepare_body(cot_ref, mix_ref, send_ref, counts_ref, cols_ref, vals_ref,
                 dense_ref, picks_ref, cot_out, base_ref, pieces_ref,
                 acc_ref, map_ref, g_ref):
    nodes = cot_ref.shape[1]
    parts = send_ref.shape[0]
    c = mix_ref.shape[1]
    build_tiles(cols_ref, vals_ref, acc_ref, dense_ref)
    build_picks(send_ref, counts_ref, picks_ref)
    wide = cot_ref[...].astype(F32).T
    wide = jnp.concatenate([jnp.zeros((nodes, c), F32), wide], axis=1).astype(BF16)
    cot_out[...] = wide
    pairs = cot_out.shape[1] // 128
    block_map(mix_ref, 2, map_ref)
    m = map_ref[...]
    for k in range(pairs):
        g_ref[:, pair(k)] = dot_t1(cot_out[:, pair(k)], m).astype(BF16)
    block_map(mix_ref, 1, map_ref)
    m = map_ref[...]
    g = g_ref[...]
    pack_rows(g, dense_ref, nodes, parts, pieces_ref)
    base_ref[...] = dot_t0(dense_ref[:, :nodes], g)
    for k in range(pairs):
        base_ref[:, pair(k)] += dot_t1(cot_out[:, pair(k)], m)


def pack_rows(values, table_ref, start, parts, out_ref):
    flipped = values.astype(F32).T.astype(BF16)
    for q in range(parts):
        table = table_ref[:, start + q * BLK : start + (q + 1) * BLK]
        out_ref[q] = dot(flipped, table).astype(BF16)


def from_blocks(total, table_ref, start, parts, arrived_ref):
    for q in range(parts):
        table = table_ref[:, start + q * BLK : start + (q + 1) * BLK]
        total = total + dot_t1(table, arrived_ref[q])
    return total


def forward_part(x_ref, conv1_ref, conv2_ref, first_ref, hidden_ref, band_ref):
    pairs = x_ref.shape[1] // 128
    band_map(conv1_ref, 1, band_ref)
    b = band_ref[...]
    for k in range(pairs):
        filt, gates = activations(dot(earlier(x_ref, k), b))
        first_ref[:, pair(k)] = (filt * gates).astype(BF16)
    band_map(conv2_ref, 2, band_ref)
    b = band_ref[...]
    for k in range(1, pairs):
        filt, gates = activations(dot(earlier(first_ref, k), b))
        hidden_ref[:, pair(k - 1)] = (filt * gates).astype(BF16)


def gate_grad(pre, up):
    filt, gates = activations(pre)
    d_filt = up * gates * (1.0 - filt * filt)
    d_gate = up * filt * gates * (1.0 - gates)
    return jnp.concatenate([d_filt, d_gate], axis=1).astype(BF16)


def backward_part(x_ref, first_ref, cot_ref, conv1_ref, conv2_ref, grad_ref, g1_ref, g2_ref,
                  band_ref, up_ref, mid_ref):
    pairs = x_ref.shape[1] // 128
    band_map(conv2_ref, 2, band_ref)
    b = band_ref[...]
    total = None
    carry = None
    for k in range(1, pairs):
        both = earlier(first_ref, k)
        d = gate_grad(dot(both, b), up_ref[:, pair(k - 1)])
        part = dot_t0(both, d)
        total = part if total is None else total + part
        back = dot_t1(d, b)
        low = back[:, :128] if carry is None else carry + back[:, :128]
        mid_ref[:, pair(k - 1)] = low.astype(BF16)
        carry = back[:, 128:]
    mid_ref[:, pair(pairs - 1)] = carry.astype(BF16)
    band_grad(total, 2, g2_ref)
    band_map(conv1_ref, 1, band_ref)
    b = band_ref[...]
    total = None
    carry = None
    for k in range(pairs):
        both = earlier(x_ref, k)
        d = gate_grad(dot(both, b), mid_ref[:, pair(k)].astype(F32))
        part = dot_t0(both, d)
        total = part if total is None else total + part
        back = dot_t1(d, b)
        if k > 0:
            low = carry + back[:, :128]
            if k > 1:
                low = low + cot_ref[:, pair(k - 2)].astype(F32)
            grad_ref[:, pair(k - 1)] = low.astype(BF16)
        carry = back[:, 128:]
    last = carry + cot_ref[:, pair(pairs - 2)].astype(F32)
    grad_ref[:, pair(pairs - 1)] = last.astype(BF16)
    band_grad(total, 1, g1_ref)


def mix_grad(term_ref, cot_ref, c):
    acc = None
    for k in range(cot_ref.shape[1] // 128):
        part = dot_t0(term_ref[:, pair(k)], cot_ref[:, pair(k)])
        acc = part if acc is None else acc + part
    return acc[:c, :c] + acc[c:, c:]


def early_part(hidden_ref, hop_ref, x_ref, cot_ref, mix_ref, gm_ref, map0, map1, wide_ref):
    c = mix_ref.shape[1]
    block_map(mix_ref, 0, map0)
    block_map(mix_ref, 1, map1)
    for k in range(cot_ref.shape[1] // 128):
        acc = x_ref[:, pair(k + 1)].astype(F32)
        acc = acc + dot(hidden_ref[:, pair(k)], map0[...])
        wide_ref[:, pair(k)] = acc + dot(hop_ref[:, pair(k)], map1[...])
    gm_ref[0] = mix_grad(hidden_ref, cot_ref, c)
    gm_ref[1] = mix_grad(hop_ref, cot_ref, c)


def main_body(parts, reps, scale,
              x_ref, cot_ref, conv1_ref, conv2_ref, mix_ref, dense_ref, picks_ref, base_ref,
              pieces_ref,
              out_ref, grad_ref, sum_ref,
              first_ref, hidden_ref, hop_ref, second_ref, up_ref, mid_ref, band_ref,
              map0, map1, map2, g1_ref, g2_ref, gm_ref,
              wide_ref, send1, send2, send3, recv0, recv1, recv2, recv3,
              pack_ref, got_ref, part_ref, reps_ref, sums_ref,
              ssem, rsem, asem, arsem, bsem, brsem):
    me = lax.axis_index("dom")
    mine = lax.axis_index("rep")
    nodes = x_ref.shape[0]
    c = mix_ref.shape[1]
    pairs = cot_ref.shape[1] // 128
    feats = cot_ref.shape[1]

    barrier = pltpu.get_barrier_semaphore()
    for o in range(1, parts):
        pl.semaphore_signal(barrier, inc=1, device_id={"dom": lax.rem(me + o, parts)},
                            device_id_type=pl.DeviceIdType.MESH)
    for o in range(1, reps):
        pl.semaphore_signal(barrier, inc=1, device_id={"rep": lax.rem(mine + o, reps)},
                            device_id_type=pl.DeviceIdType.MESH)
    pl.semaphore_wait(barrier, parts - 1 + reps - 1)

    def copies(level, src, dst):
        made = []
        for o in sorted(range(1, parts), key=lambda o: abs(2 * o - parts)):
            peer = lax.rem(me + o, parts)
            made.append(pltpu.make_async_remote_copy(
                src_ref=src.at[peer, pl.ds(c, feats - c)],
                dst_ref=dst.at[me, pl.ds(c, feats - c)],
                send_sem=ssem.at[level, o],
                recv_sem=rsem.at[level, o],
                device_id={"dom": peer},
                device_id_type=pl.DeviceIdType.MESH,
            ))
        for m in made:
            m.start()
        return made

    def arrive(made):
        for m in made:
            m.wait_recv()

    round0 = copies(0, pieces_ref, recv0)
    for buf in (recv0, recv1, recv2, recv3):
        buf[:, 0:c, :] = jnp.zeros((parts, c, BLK), BF16)
        buf[me] = jnp.zeros((feats, BLK), BF16)

    forward_part(x_ref, conv1_ref, conv2_ref, first_ref, hidden_ref, band_ref)
    pack_rows(hidden_ref[...], picks_ref, 0, parts, send1)
    round1 = copies(1, send1, recv1)

    arrive(round0)
    g = from_blocks(base_ref[...], picks_ref, 0, parts, recv0).astype(BF16)
    pack_rows(g, dense_ref, nodes, parts, send2)
    round2 = copies(2, send2, recv2)
    up_ref[...] = dot_t0(dense_ref[:, :nodes], g)
    block_map(mix_ref, 0, map0)
    for k in range(pairs):
        up_ref[:, pair(k)] += dot_t1(cot_ref[:, pair(k)], map0[...])

    own = dot(dense_ref[:, :nodes], hidden_ref[...])
    arrive(round1)
    hop_ref[...] = from_blocks(own, dense_ref, nodes, parts, recv1).astype(BF16)
    pack_rows(hop_ref[...], picks_ref, 0, parts, send3)
    round3 = copies(3, send3, recv3)

    arrive(round2)
    up_ref[...] = from_blocks(up_ref[...], picks_ref, 0, parts, recv2)
    backward_part(x_ref, first_ref, cot_ref, conv1_ref, conv2_ref, grad_ref, g1_ref, g2_ref,
                  band_ref, up_ref, mid_ref)

    early_part(hidden_ref, hop_ref, x_ref, cot_ref, mix_ref, gm_ref, map0, map1, wide_ref)
    block_map(mix_ref, 2, map2)
    own = dot(dense_ref[:, :nodes], hop_ref[...])
    arrive(round3)
    second_ref[...] = from_blocks(own, dense_ref, nodes, parts, recv3).astype(BF16)
    gm_ref[2] = mix_grad(second_ref, cot_ref, c)

    per = pack_ref.shape[1]
    flat = pack_ref
    flat[...] = jnp.zeros(flat.shape, F32)

    def put(first_row, value):
        rows = value.shape[0]
        done = 0
        while done < rows:
            slot, at = divmod(first_row + done, per)
            step = min(per - at, rows - done)
            flat[slot, at : at + step, :] = value[done : done + step]
            done += step

    put(0, g1_ref[0])
    put(c, g1_ref[1])
    put(2 * c, g2_ref[0])
    put(3 * c, g2_ref[1])
    put(4 * c, jnp.concatenate([gm_ref[0], gm_ref[1]], axis=1))
    put(5 * c, jnp.concatenate([gm_ref[2], jnp.zeros((c, c), F32)], axis=1))

    scatter = []
    for o in range(1, parts):
        peer = lax.rem(me + o, parts)
        scatter.append(pltpu.make_async_remote_copy(
            src_ref=pack_ref.at[peer], dst_ref=got_ref.at[me],
            send_sem=asem.at[0, o], recv_sem=arsem.at[0, o],
            device_id={"dom": peer}, device_id_type=pl.DeviceIdType.MESH))
    for m in scatter:
        m.start()
    for k in range(pairs):
        wide_ref[:, pair(k)] += dot(second_ref[:, pair(k)], map2[...])
    out_ref[...] = wide_ref[...].T[c:].astype(BF16)
    got_ref[me] = pack_ref[me]
    arrive(scatter)
    total = got_ref[0]
    for q in range(1, parts):
        total = total + got_ref[q]
    part_ref[...] = total
    around = []
    for o in range(1, reps):
        peer = lax.rem(mine + o, reps)
        around.append(pltpu.make_async_remote_copy(
            src_ref=part_ref, dst_ref=reps_ref.at[mine],
            send_sem=bsem.at[o], recv_sem=brsem.at[o],
            device_id={"rep": peer}, device_id_type=pl.DeviceIdType.MESH))
    for m in around:
        m.start()
    reps_ref[mine] = total
    arrive(around)
    total = reps_ref[0]
    for q in range(1, reps):
        total = total + reps_ref[q]
    for m in around:
        m.wait_send()
    part_ref[...] = total * (1.0 / scale)
    final = []
    for o in range(1, parts):
        peer = lax.rem(me + o, parts)
        final.append(pltpu.make_async_remote_copy(
            src_ref=part_ref, dst_ref=sums_ref.at[me],
            send_sem=asem.at[1, o], recv_sem=arsem.at[1, o],
            device_id={"dom": peer}, device_id_type=pl.DeviceIdType.MESH))
    for m in final:
        m.start()
    sums_ref[me] = part_ref[...]
    arrive(final)

    sum_ref[...] = sums_ref[...]
    for m in round0 + round1 + round2 + round3 + scatter + final:
        m.wait_send()


def shards(inputs, cotangent, conv_one, conv_two, mix_weight, send_rows, counts, tile_cols,
           tile_vals):
    windows, nodes, flat = inputs.shape
    channels = mix_weight.shape[1]
    parts = lax.axis_size("dom")
    reps = lax.axis_size("rep")
    kept = flat // channels - 3
    wide = flat - 2 * channels
    halo = parts * BLK
    blocks = (parts, wide, BLK)
    prepared = [((nodes, nodes + halo), BF16), ((nodes, halo), BF16), ((nodes, wide), BF16),
                ((nodes, wide), F32), (blocks, BF16)]
    dense, picks, cot_wide, base, pieces = pl.pallas_call(
        prepare_body,
        out_shape=[jax.ShapeDtypeStruct(s, d) for s, d in prepared],
        in_specs=[VM, VM, VM, SM, SM, VM],
        out_specs=[VM] * 5,
        scratch_shapes=[pltpu.VMEM((parts + nodes // BLK, BLK, BLK), F32),
                        pltpu.VMEM((128, 128), BF16), pltpu.VMEM((nodes, wide), BF16)],
        compiler_params=LIMIT,
        name="prepare",
    )(cotangent[0].T, mix_weight, send_rows[0], counts, tile_cols, tile_vals)
    scaling = math.sqrt(float(windows * reps * nodes * parts * kept))
    unit = 8 * parts
    per = -(-6 * channels // unit) * unit // parts
    results = [((kept * channels, nodes), BF16), ((nodes, flat), BF16), ((parts, per, BLK), F32)]
    scratch = [((nodes, flat), BF16), ((nodes, wide), BF16), ((nodes, wide), BF16),
               ((nodes, wide), BF16), ((nodes, wide), F32), ((nodes, flat), BF16),
               ((256, 256), BF16), ((128, 128), BF16), ((128, 128), BF16), ((128, 128), BF16),
               (conv_one.shape, F32), (conv_two.shape, F32), (mix_weight.shape, F32)]
    scratch += [((nodes, wide), F32)] + [(blocks, BF16)] * 7
    scratch += [((parts, per, BLK), F32), ((parts, per, BLK), F32), ((per, BLK), F32),
                ((reps, per, BLK), F32), ((parts, per, BLK), F32)]
    dma = pltpu.SemaphoreType.DMA
    output, grad_input, packed = pl.pallas_call(
        functools.partial(main_body, parts, reps, scaling),
        out_shape=[jax.ShapeDtypeStruct(s, d) for s, d in results],
        in_specs=[VM] * 9,
        out_specs=[VM] * 3,
        scratch_shapes=[pltpu.VMEM(s, d) for s, d in scratch]
        + [dma((4, parts)), dma((4, parts)), dma((2, parts)), dma((2, parts)), dma((reps,)),
           dma((reps,))],
        compiler_params=pltpu.CompilerParams(
            vmem_limit_bytes=60 * 1024 * 1024, collective_id=0, has_side_effects=True),
        name="layer",
    )(inputs[0], cot_wide, conv_one, conv_two, mix_weight, dense, picks, base, pieces)
    c = channels
    rows = packed.reshape(parts * per, BLK)
    gm = jnp.stack([rows[4 * c : 5 * c, :c], rows[4 * c : 5 * c, c:], rows[5 * c : 6 * c, :c]])
    return (
        output.T[None],
        grad_input[None],
        rows[: 2 * c].reshape(conv_one.shape),
        rows[2 * c : 4 * c].reshape(conv_two.shape),
        gm,
    )


def place_tiles(r, me, parts, cols_ref, vals_ref, dense_ref):
    rtiles, slots = vals_ref.shape[0], vals_ref.shape[1]
    for c in range(dense_ref.shape[1] // BLK):
        named = c if c < rtiles else rtiles + lax.rem(me - (c - rtiles + 1) + parts, parts)
        total = None
        for j in range(slots):
            keep = jnp.where(cols_ref[r, j] == named, 1.0, 0.0)
            part = vals_ref[r, j].astype(F32) * keep
            total = part if total is None else total + part
        dense_ref[chunk(r * BLK, BLK), c * BLK : (c + 1) * BLK] = total.astype(BF16)


def chunk(first, size):
    return pl.ds(pl.multiple_of(first, size), size)


def steps_body(parts, reps, scale,
               x_ref, cot_ref, conv1_ref, conv2_ref, mix_ref, send_ref, counts_ref, cols_ref, vals_ref,
               out_ref, grad_ref, one_out, two_out, mix_out,
               dense_ref, wanted_ref, xt_ref, first_ref, hid_ref, d1_ref, d2_ref, mid_ref,
               band1, band1t, band2, band2t, maps, mapst,
               adj_ref, lists_ref, picks_ref,
               cf_ref, hf_ref, f1_ref, c1_ref, c2_ref, own_ref, part_t, ext_ref,
               gh_ref, mx_ref, ghs_ref, mxs_ref,
               g1_ref, g2_ref, pack0, got0, half0, all0, full0, sums0,
               pack1, got1, half1, all1, full1, sums1,
               lsend, lrecv, fsend, frecv, esend, erecv, tsend, trecv,
               asem, arsem, bsem, brsem):
    me = lax.axis_index("dom")
    mine = lax.axis_index("rep")
    nodes = x_ref.shape[0]
    c = mix_ref.shape[1]
    pairs = x_ref.shape[1] // 128
    mesh_ids = pl.DeviceIdType.MESH
    holder = lax.rem(parts // 2 - reps // 2 + mine + parts, parts)
    extra = parts * c
    zs = parts // 2
    z, xx = me // 2, lax.rem(me, 2)
    yy, core = mine // 2, lax.rem(mine, 2)
    chips = parts * reps // 2
    chip = me * 2 + yy
    crep = yy * 2 + 1 - core

    barrier = pltpu.get_barrier_semaphore()
    for o in range(1, chips):
        peer = lax.rem(chip + o, chips)
        pl.semaphore_signal(barrier, inc=1, device_id={"dom": peer // 2, "rep": lax.rem(peer, 2) * 2 + core},
                            device_id_type=mesh_ids)
    pl.semaphore_signal(barrier, inc=1, device_id={"rep": yy * 2 + 1 - core}, device_id_type=mesh_ids)
    place_tiles(core, me, parts, cols_ref, vals_ref, dense_ref)
    pl.semaphore_wait(barrier, chips)

    def remote(src, dst, ssem, rsem, **where):
        return pltpu.make_async_remote_copy(
            src_ref=src, dst_ref=dst, send_sem=ssem, recv_sem=rsem,
            device_id=where, device_id_type=mesh_ids)

    order = sorted(range(1, parts), key=lambda o: abs(2 * o - parts))

    own_rows = 3 * (nodes // 16)
    both_rows = nodes // 2 - 2 * own_rows

    def span(sub, cc, y):
        third = own_rows // 3
        first = (own_rows + both_rows) * y
        at, size = ((first, 2 * third), (first + 2 * third, third), (own_rows, both_rows))[sub]
        return pl.ds(pl.multiple_of(cc * (nodes // 2) + at, 16), size)

    def piece(p, sub, cc, y):
        return adj_ref.at[p, span(sub, cc, y)]

    def source_z(t, way):
        return z - t if way == 0 else z + t

    def valid(t, way):
        if t == 0:
            return z >= 0
        return z >= t if way == 0 else z + t < zs

    def slot(t, way, sub):
        return 3 * (0 if t == 0 else 2 * t - 1 + way) + sub

    def base(t, way):
        return source_z(t, way) * 2 + xx

    def cross(t, way):
        return source_z(t, way) * 2 + 1 - xx

    def first_source(t, way, sub):
        return dense_ref.at[span(sub, core, yy)] if t == 0 else piece(base(t, way), sub, core, yy)

    def along(t, way, sub, out_way):
        to = (z + 1 if out_way == 0 else z - 1) * 2 + xx
        return remote(first_source(t, way, sub), piece(base(t, way), sub, core, yy),
                      tsend.at[out_way, slot(t, way, sub)], trecv.at[0, slot(t + 1, out_way, sub)], dom=to)

    def across(t, way, sub):
        return remote(first_source(t, way, sub), piece(base(t, way), sub, core, yy),
                      tsend.at[2, slot(t, way, sub)], trecv.at[2, slot(t, way, sub)], dom=z * 2 + 1 - xx)

    def hand(kind, part, t, way, sub, y):
        ref = piece(part(t, way), sub, core, y)
        to = (1 - yy) * 2 + core if kind in (3, 5) else crep
        return remote(ref, ref, tsend.at[kind, slot(t, way, sub)], trecv.at[kind, slot(t, way, sub)], rep=to)

    def arrived(kind, ref, t, way, sub):
        remote(ref, ref, tsend.at[kind, slot(t, way, sub)], trecv.at[kind, slot(t, way, sub)],
               rep=crep).wait_recv()

    def ways(t):
        return (0,) if t == 0 else (0, 1)

    def lane_sends(t, way, sub):
        made = []
        if t + 1 < zs:
            for w in (0, 1) if t == 0 else (way,):
                made.append((z + 1 < zs if w == 0 else z >= 1, along(t, way, sub, w)))
        made.append((None, across(t, way, sub)))
        return made

    def side_sends(t, way, sub, part, kind):
        if t == 0 and part is base:
            return []
        made = [(None, hand(kind, part, t, way, sub, yy))] if sub < 2 else []
        return made + [(None, hand(kind + 1, part, t, way, sub, yy))]

    def core_sends(t, way, sub, part, kind):
        if t == 0 and part is base or sub == 2:
            return []
        return [(None, hand(kind, part, t, way, sub, 1 - yy))]

    def go(sends, wait=False):
        for cond, copy in sends:
            act = copy.wait_send if wait else copy.start
            if cond is None:
                act()
            else:
                pl.when(cond)(act)

    def on_base(t, way, sub):
        @pl.when(valid(t, way))
        def _():
            arrived(0, piece(base(t, way), sub, core, yy), t, way, sub)
            go(lane_sends(t, way, sub) + side_sends(t, way, sub, base, 3))

    def on_cross(t, way, sub):
        @pl.when(valid(t, way))
        def _():
            arrived(2, piece(cross(t, way), sub, core, yy), t, way, sub)
            go(side_sends(t, way, sub, cross, 5))

    def on_plane(t, way, sub, part, kind):
        @pl.when(valid(t, way))
        def _():
            arrived(kind, piece(part(t, way), sub, core, 1 - yy), t, way, sub)
            go(core_sends(t, way, sub, part, 7 if kind == 3 else 8))

    def on_tiles(t, way, part, kind, use):
        @pl.when(valid(t, way))
        def _():
            if t or part is cross:
                for sub in range(3):
                    arrived(kind + 1, piece(part(t, way), sub, 1 - core, yy), t, way, sub)
                for sub in range(2):
                    arrived(7 if kind == 3 else 8, piece(part(t, way), sub, 1 - core, 1 - yy), t, way, sub)
            use(part(t, way))

    relay = []

    def step_relay(count=1):
        for _ in range(count):
            if relay:
                relay.pop()()

    def scatter_field(level, src, first, dst):
        made = []
        for o in order:
            peer = lax.rem(me + o, parts)
            made.append(remote(src.at[chunk(first + peer * c, c)], dst.at[me, pl.ds(0, c)],
                               fsend.at[level, o], frecv.at[level, o], dom=peer))
        for m in made:
            m.start()
        off = lax.rem(holder - me + parts, parts)
        last = remote(src.at[pl.ds(first + extra, c)], dst.at[me, pl.ds(c, c)],
                      esend.at[level, 0], erecv.at[level, off], dom=holder)
        pl.when(me != holder)(last.start)
        dst[me, 0:c, :] = src[chunk(first + me * c, c), :]

        @pl.when(me == holder)
        def _():
            dst[me, c : 2 * c, :] = src[first + extra : first + extra + c, :]

        @pl.when(me != holder)
        def _():
            dst[:, c : 2 * c, :] = jnp.zeros((parts, c, nodes), BF16)
        return made, last

    def field_arrives(level, made, src, dst):
        for m in made:
            m.wait_recv()

        @pl.when(me == holder)
        def _():
            for o in range(1, parts):
                q = lax.rem(me - o + parts, parts)
                remote(dst.at[q, pl.ds(c, c)], dst.at[q, pl.ds(c, c)], esend.at[level, 0],
                       erecv.at[level, o], dom=q).wait_recv()

    def home_copies(level, o, src, first, dst):
        q = lax.rem(me + o, parts)
        one = remote(src.at[q, pl.ds(0, c)], dst.at[chunk(first + me * c, c)],
                     fsend.at[level, o], frecv.at[level, o], dom=q)
        two = remote(src.at[q, pl.ds(c, c)], dst.at[pl.ds(first + extra, c)],
                     esend.at[level, o], erecv.at[level, 0], dom=q)
        return one, two

    def go_home(level, o, src, first, dst):
        if o:
            one, two = home_copies(level, o, src, first, dst)
            one.start()
            pl.when(me == holder)(two.start)
            return
        dst[chunk(first + me * c, c), :] = src[me, 0:c, :]

        @pl.when(me == holder)
        def _():
            dst[first + extra : first + extra + c, :] = src[me, c : 2 * c, :]

    def home_arrives(level, src, first, dst):
        for o in range(1, parts):
            home_copies(level, o, src, first, dst)[0].wait_recv()
        pl.when(me != holder)(home_copies(level, 1, src, first, dst)[1].wait_recv)

    def home_sent(level, src, first, dst):
        for o in range(1, parts):
            one, two = home_copies(level, o, src, first, dst)
            one.wait_send()
            pl.when(me == holder)(two.wait_send)

    for sub in range(3):
        go(lane_sends(0, 0, sub))
    lane = lax.broadcasted_iota(jnp.int32, (1, BLK), 1)
    for o in range(parts):
        t = lax.rem(me + o, parts)
        wanted_ref[o : o + 1, :] = jnp.where(
            lane < counts_ref[0, t], send_ref[pl.ds(t, 1), :], -1)
    lists = []
    for o in order:
        peer = lax.rem(me + o, parts)
        lists.append(remote(wanted_ref, lists_ref.at[me], lsend.at[o], lrecv.at[o], dom=peer))
    for m in lists:
        m.start()
    lists_ref[me] = wanted_ref[...]
    place_tiles(1 - core, me, parts, cols_ref, vals_ref, dense_ref)
    adj_ref[me] = dense_ref[...]

    def back_piece(g_ref, p):
        t = dot(g_ref[p], adj_ref[p])
        own_ref[p] = t[:, :nodes]
        for o in range(1, parts):
            at = nodes + (o - 1) * BLK
            owner = lax.rem(p - o + parts, parts)
            part_t[owner, :, (o - 1) * BLK : o * BLK] = t[:, at : at + BLK].astype(BF16)

    hid_round, cot_round = [], []

    def first_piece():
        field_arrives(0, cot_round[0], cot_ref, cf_ref)
        back_piece(cf_ref, me)

    def send_cotangent():
        cot_round.extend(scatter_field(0, cot_ref, 0, cf_ref))

    def send_hidden():
        hid_round.extend(scatter_field(1, hid_ref, c, hf_ref))

    def add(handler, t, *rest):
        for w in ways(t):
            relay.append(functools.partial(handler, t, w, *rest))

    use = functools.partial(back_piece, cf_ref)
    for t in range(1, zs + 2):
        if t < zs:
            for sub in range(3):
                add(on_base, t, sub)
        if t <= zs:
            for sub in range(3):
                add(on_cross, t - 1, sub)
        if t == 2:
            relay.append(send_cotangent)
        for sub in range(2):
            if 2 <= t <= zs:
                add(on_plane, t - 1, sub, base, 3)
            if t >= 2:
                add(on_plane, t - 2, sub, cross, 5)
        if t == 4:
            relay.append(send_hidden)
        if t >= zs:
            if t == zs:
                relay.append(first_piece)
            add(on_tiles, t - zs, cross, 5, use)
            add(on_tiles, t - zs + 1, base, 3, use)
    for u in range(2, zs):
        add(on_tiles, u, cross, 5, use)
        if u + 1 < zs:
            add(on_tiles, u + 1, base, 3, use)
    relay.reverse()

    for k in range(pairs):
        xt_ref[pair(k), :] = x_ref[:, pair(k)].astype(F32).T.astype(BF16)
    for conv, dil, nat, tra in ((conv1_ref, 1, band1, band1t), (conv2_ref, 2, band2, band2t)):
        band_map(conv, dil, nat)
        tra[...] = nat[...].astype(F32).T.astype(BF16)

    def earlier_t(ref, k):
        if k == 0:
            v = ref[0:128, :]
            return jnp.concatenate([jnp.zeros_like(v), v], axis=0)
        return ref[window2(k - 1), :]

    def gated(pre, d_ref, k):
        filt = jnp.tanh(pre[:128])
        gates = 0.5 * jnp.tanh(0.5 * pre[128:]) + 0.5
        d_ref[k, 0:128, :] = gates * (1.0 - filt * filt)
        d_ref[k, 128:256, :] = filt * gates * (1.0 - gates)
        return (filt * gates).astype(BF16)

    for k in range(pairs):
        first_ref[pair(k), :] = gated(dot(band1t[...], earlier_t(xt_ref, k)), d1_ref, k)
        if k % 2:
            step_relay()
    for k in range(1, pairs):
        hid_ref[pair(k - 1), :] = gated(dot(band2t[...], earlier_t(first_ref, k)), d2_ref, k)
        step_relay()

    for i in range(3):
        block_map(mix_ref, i, maps.at[i])
        mapst[i] = maps[i].astype(F32).T.astype(BF16)
    gh_ref[0:c, :] = jnp.zeros((c, nodes), BF16)

    for m in lists:
        m.wait_recv()
    node = lax.broadcasted_iota(jnp.int32, (nodes, BLK), 0)
    for q in range(parts):
        for o in range(1, parts):
            hit = node == lists_ref[q, o : o + 1, :]
            picks_ref[q, :, (o - 1) * BLK : o * BLK] = jnp.where(hit, 1.0, 0.0).astype(BF16)
        step_relay(2)

    step_relay(len(relay))

    def back_owner(q):
        return (own_ref[q] + dot_t1(part_t[q], picks_ref[q])).astype(BF16)

    for q in range(parts):
        c1_ref[q] = back_owner(q)
    for p in range(parts):
        back_piece(c1_ref, p)
    for o in order + [0]:
        q = lax.rem(me + o, parts)
        c2 = back_owner(q)
        c2_ref[q] = c2
        grads = dot(maps[0], cf_ref[q]) + dot(maps[1], c1_ref[q]) + dot(maps[2], c2)
        ghs_ref[q] = grads.astype(BF16)
        go_home(2, o, ghs_ref, c, gh_ref)

    field_arrives(1, hid_round[0], hid_ref, hf_ref)
    mix = []
    for moved in (cf_ref, c1_ref, c2_ref):
        total = dot_t1(hf_ref[0], moved[0])
        for q in range(1, parts):
            total = total + dot_t1(hf_ref[q], moved[q])
        mix.append(total[:c, :c] + total[c:, c:])

    def reducer(g, pack, got, half, got_all, full, sums):
        def over_core(stage, src, dst):
            return [remote(src, dst, bsem.at[2 * g + stage], brsem.at[2 * g + stage], rep=crep)]

        def over_chips(stage, src_of, dst):
            made = []
            for o in range(1, chips):
                peer = lax.rem(chip + o, chips)
                made.append(remote(src_of(peer), dst, asem.at[2 * g + stage, o], arsem.at[2 * g + stage, o],
                                   dom=peer // 2, rep=lax.rem(peer, 2) * 2 + core))
            return made

        steps = (lambda: over_core(0, pack.at[1 - core], got),
                 lambda: over_chips(0, lambda peer: half.at[peer], got_all.at[chip]),
                 lambda: over_chips(1, lambda peer: full, sums.at[core, chip]),
                 lambda: over_core(1, sums.at[core], sums.at[core]))

        def start(i):
            for m in steps[i]():
                m.start()

        def arrive(i):
            for m in steps[i]():
                m.wait_recv()

        def first():
            start(0)

        def second():
            arrive(0)
            total = pack[core] + got[...]
            share = half.shape[1]
            for q in range(chips):
                half[q] = total[q * share : (q + 1) * share]
            start(1)
            got_all[chip] = half[chip]

        def third():
            arrive(1)
            total = got_all[0]
            for q in range(1, chips):
                total = total + got_all[q]
            full[...] = total * (1.0 / scale)
            start(2)
            sums[core, chip] = full[...]

        def fourth():
            arrive(2)
            start(3)

        def last():
            arrive(3)

        def sent():
            for i in range(4):
                for m in steps[i]():
                    m.wait_send()

        return first, second, third, fourth, last, sent

    early = reducer(0, pack0, got0, half0, all0, full0, sums0)
    late = reducer(1, pack1, got1, half1, all1, full1, sums1)
    pack0[...] = jnp.zeros(pack0.shape, F32)
    for i in range(3):
        pack0[i // 2, (i % 2) * c : (i % 2 + 1) * c, 0:c] = mix[i]
    early[0]()

    def extend(f_ref):
        for q in range(parts):
            ext_ref[q, :, 0:nodes] = f_ref[q]
            halo = dot(f_ref[q], picks_ref[q]).astype(BF16)
            for o in range(1, parts):
                at = nodes + (o - 1) * BLK
                ext_ref[(q + o) % parts, :, at : at + BLK] = halo[:, (o - 1) * BLK : o * BLK]

    extend(hf_ref)
    for p in range(parts):
        f1_ref[p] = dot_t1(ext_ref[p], adj_ref[p]).astype(BF16)
    extend(f1_ref)
    for o in order + [0]:
        q = lax.rem(me + o, parts)
        second = dot_t1(ext_ref[q], adj_ref[q]).astype(BF16)
        mixed = dot(mapst[0], hf_ref[q]) + dot(mapst[1], f1_ref[q]) + dot(mapst[2], second)
        mxs_ref[q] = mixed.astype(BF16)
        go_home(3, o, mxs_ref, 0, mx_ref)
    early[1]()

    home_arrives(2, ghs_ref, c, gh_ref)

    def conv_back(sig_ref, d_ref, up_of, band, low_of, first_pair, dilation, out):
        total, carry = None, None
        b = band[...]
        for k in range(first_pair, pairs):
            up = up_of(k)
            both = earlier_t(sig_ref, k)
            d = jnp.concatenate([up * d_ref[k, 0:128, :], up * d_ref[k, 128:256, :]], axis=0)
            d = d.astype(BF16)
            part = dot_t1(both, d)
            total = part if total is None else total + part
            back = dot(b, d)
            if k > 0:
                low_of(k - 1, back[:128] if carry is None else carry + back[:128])
            carry = back[128:]
        low_of(pairs - 1, carry)
        band_grad(total, dilation, out)

    def set_mid(k, low):
        mid_ref[pair(k), :] = low.astype(BF16)

    def set_grad(k, low):
        if k == 1:
            low = low + jnp.concatenate([jnp.zeros((c, nodes), F32), cot_ref[0:c, :].astype(F32)], axis=0)
        elif k > 1:
            low = low + cot_ref[(2 * k - 3) * c : (2 * k - 1) * c, :].astype(F32)
        grad_ref[:, pair(k)] = low.T.astype(BF16)

    conv_back(first_ref, d2_ref, lambda k: gh_ref[pair(k - 1), :].astype(F32), band2, set_mid, 1, 2, g2_ref)
    conv_back(xt_ref, d1_ref, lambda k: mid_ref[pair(k), :].astype(F32), band1, set_grad, 0, 1, g1_ref)

    for tap in range(2):
        pack1[0, tap * c : (tap + 1) * c, :] = g1_ref[tap]
        pack1[1, tap * c : (tap + 1) * c, :] = g2_ref[tap]
    late[0]()
    late[1]()
    early[2]()
    home_arrives(3, mxs_ref, 0, mx_ref)
    kept = out_ref.shape[0]
    out_ref[...] = (mx_ref[...].astype(F32) + xt_ref[pairs * 128 - kept :, :].astype(F32)).astype(BF16)
    late[2]()
    early[3]()

    for m in cot_round[0] + hid_round[0] + lists:
        m.wait_send()
    pl.when(me != holder)(cot_round[1].wait_send)
    pl.when(me != holder)(hid_round[1].wait_send)
    home_sent(2, ghs_ref, c, gh_ref)
    home_sent(3, mxs_ref, 0, mx_ref)
    for t in range(zs):
        for w in ways(t):
            @pl.when(valid(t, w))
            def _():
                for sub in range(3):
                    go(lane_sends(t, w, sub) + side_sends(t, w, sub, base, 3)
                       + side_sends(t, w, sub, cross, 5) + core_sends(t, w, sub, base, 7)
                       + core_sends(t, w, sub, cross, 8), wait=True)
    late[3]()
    early[4]()
    share = sums0.shape[2]
    for q in range(chips):
        tap, at = divmod(q * share, c)
        mix_out[tap, at : at + share, :] = sums0[0, q, :, 0:c]
        if tap == 0:
            mix_out[2, at : at + share, :] = sums0[1, q, :, 0:c]
    early[5]()
    late[4]()
    for q in range(chips):
        tap, at = divmod(q * share, c)
        one_out[tap, at : at + share, :] = sums1[0, q]
        two_out[tap, at : at + share, :] = sums1[1, q]
    late[5]()


def finish_body(*refs):
    half = len(refs) // 2
    for a, b in zip(refs[:half], refs[half:]):
        b[...] = a[...]


def step_shards(inputs, cotangent, conv_one, conv_two, mix_weight, send_rows, counts, tile_cols,
                tile_vals):
    windows, nodes, flat = inputs.shape
    channels = mix_weight.shape[1]
    parts = lax.axis_size("dom")
    reps = lax.axis_size("rep")
    kept = flat // channels - 3
    c = channels
    pairs = flat // 128
    halo = (parts - 1) * BLK
    ext = nodes + halo
    scaling = math.sqrt(float(windows * reps * nodes * parts * kept))
    results = [((kept * c, nodes), BF16), ((nodes, flat), BF16), (conv_one.shape, F32),
               (conv_two.shape, F32), (mix_weight.shape, F32)]
    field = (parts, 2 * c, nodes)
    wide = flat - 2 * c
    scratch = [((nodes, ext), BF16), ((parts, BLK), jnp.int32),
               ((flat, nodes), BF16), ((flat, nodes), BF16), ((wide, nodes), BF16),
               ((pairs, 256, nodes), F32), ((pairs, 256, nodes), F32), ((flat, nodes), BF16)]
    scratch += [((256, 256), BF16)] * 4 + [((3, 128, 128), BF16)] * 2
    scratch += [((parts, nodes, ext), BF16), ((parts, parts, BLK), jnp.int32),
                ((parts, nodes, halo), BF16)]
    scratch += [(field, BF16)] * 5 + [(field, F32), ((parts, 2 * c, halo), BF16),
                                      ((parts, 2 * c, ext), BF16)]
    scratch += [((wide, nodes), BF16), ((kept * c, nodes), BF16), (field, BF16), (field, BF16)]
    scratch += [(conv_one.shape, F32), (conv_two.shape, F32)]
    chips = parts * reps // 2
    share = 2 * c // chips
    for _ in range(2):
        scratch += [((2, 2 * c, BLK), F32), ((2 * c, BLK), F32), ((chips, share, BLK), F32),
                    ((chips, share, BLK), F32), ((share, BLK), F32), ((2, chips, share, BLK), F32)]
    dma = pltpu.SemaphoreType.DMA
    sems = [(parts,), (parts,), (4, parts), (4, parts), (4, parts), (4, parts),
            (9, 3 * parts), (9, 3 * parts), (4, chips), (4, chips), (4,), (4,)]
    made = pl.pallas_call(
        functools.partial(steps_body, parts, reps, scaling),
        out_shape=[jax.ShapeDtypeStruct(s, d) for s, d in results],
        in_specs=[VM] * 6 + [SM, SM, VM],
        out_specs=[VM] * 5,
        scratch_shapes=[pltpu.VMEM(s, d) for s, d in scratch] + [dma(s) for s in sems],
        compiler_params=pltpu.CompilerParams(
            vmem_limit_bytes=60 * 1024 * 1024, collective_id=1, has_side_effects=True),
        name="steps",
    )(inputs[0], cotangent[0].T, conv_one, conv_two, mix_weight, send_rows[0], counts, tile_cols,
      tile_vals)
    output, grad_input, one, two, mix = pl.pallas_call(
        finish_body,
        out_shape=[jax.ShapeDtypeStruct(s, d) for s, d in results],
        in_specs=[VM] * 5,
        out_specs=[VM] * 5,
        compiler_params=LIMIT,
        name="finish",
    )(*made)
    return output.T[None], grad_input[None], one, two, mix


def solution(mesh):
    placed = (
        P("rep", "dom", None),
        P("rep", "dom", None),
        P(),
        P(),
        P(),
        P("dom", None, None),
        P("dom", None),
        P("dom", None),
        P("dom", None, None, None),
    )
    parts, reps = mesh.shape["dom"], mesh.shape["rep"]

    def layer(*args):
        kept = args[0].shape[2] // args[4].shape[1] - 3
        by_step = parts % 2 == 0 and reps == 4 and parts == kept - 1
        return step_shards(*args) if by_step else shards(*args)

    return jax.shard_map(
        layer,
        mesh=mesh,
        in_specs=placed,
        out_specs=(P("rep", "dom", None), P("rep", "dom", None), P(), P(), P()),
        check_vma=False,
    )
```

```python
import functools
import math

import jax
import jax.numpy as jnp
from jax import lax
from jax.experimental import pallas as pl
from jax.experimental.pallas import tpu as pltpu
from jax.sharding import PartitionSpec as P

F32 = jnp.float32
BF16 = jnp.bfloat16
BLK = 128
VM = pl.BlockSpec(memory_space=pltpu.VMEM)
SM = pl.BlockSpec(memory_space=pltpu.SMEM)
LIMIT = pltpu.CompilerParams(vmem_limit_bytes=56 * 1024 * 1024)


def dot(a, b):
    return jnp.dot(a, b, preferred_element_type=F32)


def dot_t0(a, b):
    return lax.dot_general(a, b, (((0,), (0,)), ((), ())), preferred_element_type=F32)


def dot_t1(a, b):
    return lax.dot_general(a, b, (((1,), (1,)), ((), ())), preferred_element_type=F32)


def pair(k):
    return slice(k * 128, (k + 1) * 128)


def window2(k):
    return slice(k * 128, (k + 2) * 128)


def block_map(weight_ref, index, out_ref):
    c = weight_ref.shape[1]
    w = weight_ref[index]
    out_ref[...] = jnp.zeros(out_ref.shape, BF16)
    out_ref[0:c, 0:c] = w
    out_ref[c : 2 * c, c : 2 * c] = w


def band_blocks(dilation):
    if dilation == 1:
        return ((0, 1, 0), (0, 2, 1), (1, 2, 0), (1, 3, 1))
    return ((0, 0, 0), (0, 1, 1), (1, 2, 0), (1, 3, 1))


def band_map(conv_ref, dilation, out_ref):
    c = conv_ref.shape[1]
    out_ref[...] = jnp.zeros(out_ref.shape, BF16)
    for tap, i, o in band_blocks(dilation):
        w = conv_ref[tap]
        rows = slice(i * c, (i + 1) * c)
        out_ref[rows, o * c : (o + 1) * c] = w[:, :c]
        out_ref[rows, (o + 2) * c : (o + 3) * c] = w[:, c:]


def band_grad(total, dilation, out_ref):
    c = out_ref.shape[1]
    for tap in range(2):
        for half in range(2):
            acc = None
            for t, i, o in band_blocks(dilation):
                if t != tap:
                    continue
                col = (o + 2 * half) * c
                part = total[i * c : (i + 1) * c, col : col + c]
                acc = part if acc is None else acc + part
            out_ref[tap, :, half * c : (half + 1) * c] = acc


def activations(pre):
    filt = jnp.tanh(pre[:, :128])
    gates = 0.5 * jnp.tanh(0.5 * pre[:, 128:]) + 0.5
    return filt, gates


def earlier(ref, k):
    if k == 0:
        x = ref[:, 0:128]
        return jnp.concatenate([jnp.zeros_like(x), x], axis=1)
    return ref[:, window2(k - 1)]


def build_tiles(cols_ref, vals_ref, acc_ref, dense_ref):
    rtiles, slots = vals_ref.shape[0], vals_ref.shape[1]
    ctiles = dense_ref.shape[1] // BLK
    for r in range(rtiles):
        acc_ref[...] = jnp.zeros(acc_ref.shape, F32)
        for j in range(slots):
            c = cols_ref[r, j]
            acc_ref[c] = acc_ref[c] + vals_ref[r, j].astype(F32)
        for c in range(ctiles):
            dense_ref[r * BLK : (r + 1) * BLK, c * BLK : (c + 1) * BLK] = acc_ref[c].astype(BF16)


def build_picks(send_ref, counts_ref, picks_ref):
    parts = send_ref.shape[0]
    nodes = picks_ref.shape[0]
    lane = lax.broadcasted_iota(jnp.int32, (1, BLK), 1)
    rows = lax.broadcasted_iota(jnp.int32, (nodes, BLK), 0)
    for q in range(parts):
        wanted = jnp.where(lane < counts_ref[0, q], send_ref[q : q + 1, :], -1)
        hit = rows == wanted
        picks_ref[:, q * BLK : (q + 1) * BLK] = jnp.where(hit, 1.0, 0.0).astype(BF16)


def prepare_body(cot_ref, mix_ref, send_ref, counts_ref, cols_ref, vals_ref,
                 dense_ref, picks_ref, cot_out, base_ref, pieces_ref,
                 acc_ref, map_ref, g_ref):
    nodes = cot_ref.shape[1]
    parts = send_ref.shape[0]
    c = mix_ref.shape[1]
    build_tiles(cols_ref, vals_ref, acc_ref, dense_ref)
    build_picks(send_ref, counts_ref, picks_ref)
    wide = cot_ref[...].astype(F32).T
    wide = jnp.concatenate([jnp.zeros((nodes, c), F32), wide], axis=1).astype(BF16)
    cot_out[...] = wide
    pairs = cot_out.shape[1] // 128
    block_map(mix_ref, 2, map_ref)
    m = map_ref[...]
    for k in range(pairs):
        g_ref[:, pair(k)] = dot_t1(cot_out[:, pair(k)], m).astype(BF16)
    block_map(mix_ref, 1, map_ref)
    m = map_ref[...]
    g = g_ref[...]
    pack_rows(g, dense_ref, nodes, parts, pieces_ref)
    base_ref[...] = dot_t0(dense_ref[:, :nodes], g)
    for k in range(pairs):
        base_ref[:, pair(k)] += dot_t1(cot_out[:, pair(k)], m)


def pack_rows(values, table_ref, start, parts, out_ref):
    flipped = values.astype(F32).T.astype(BF16)
    for q in range(parts):
        table = table_ref[:, start + q * BLK : start + (q + 1) * BLK]
        out_ref[q] = dot(flipped, table).astype(BF16)


def from_blocks(total, table_ref, start, parts, arrived_ref):
    for q in range(parts):
        table = table_ref[:, start + q * BLK : start + (q + 1) * BLK]
        total = total + dot_t1(table, arrived_ref[q])
    return total


def forward_part(x_ref, conv1_ref, conv2_ref, first_ref, hidden_ref, band_ref):
    pairs = x_ref.shape[1] // 128
    band_map(conv1_ref, 1, band_ref)
    b = band_ref[...]
    for k in range(pairs):
        filt, gates = activations(dot(earlier(x_ref, k), b))
        first_ref[:, pair(k)] = (filt * gates).astype(BF16)
    band_map(conv2_ref, 2, band_ref)
    b = band_ref[...]
    for k in range(1, pairs):
        filt, gates = activations(dot(earlier(first_ref, k), b))
        hidden_ref[:, pair(k - 1)] = (filt * gates).astype(BF16)


def gate_grad(pre, up):
    filt, gates = activations(pre)
    d_filt = up * gates * (1.0 - filt * filt)
    d_gate = up * filt * gates * (1.0 - gates)
    return jnp.concatenate([d_filt, d_gate], axis=1).astype(BF16)


def backward_part(x_ref, first_ref, cot_ref, conv1_ref, conv2_ref, grad_ref, g1_ref, g2_ref,
                  band_ref, up_ref, mid_ref):
    pairs = x_ref.shape[1] // 128
    band_map(conv2_ref, 2, band_ref)
    b = band_ref[...]
    total = None
    carry = None
    for k in range(1, pairs):
        both = earlier(first_ref, k)
        d = gate_grad(dot(both, b), up_ref[:, pair(k - 1)])
        part = dot_t0(both, d)
        total = part if total is None else total + part
        back = dot_t1(d, b)
        low = back[:, :128] if carry is None else carry + back[:, :128]
        mid_ref[:, pair(k - 1)] = low.astype(BF16)
        carry = back[:, 128:]
    mid_ref[:, pair(pairs - 1)] = carry.astype(BF16)
    band_grad(total, 2, g2_ref)
    band_map(conv1_ref, 1, band_ref)
    b = band_ref[...]
    total = None
    carry = None
    for k in range(pairs):
        both = earlier(x_ref, k)
        d = gate_grad(dot(both, b), mid_ref[:, pair(k)].astype(F32))
        part = dot_t0(both, d)
        total = part if total is None else total + part
        back = dot_t1(d, b)
        if k > 0:
            low = carry + back[:, :128]
            if k > 1:
                low = low + cot_ref[:, pair(k - 2)].astype(F32)
            grad_ref[:, pair(k - 1)] = low.astype(BF16)
        carry = back[:, 128:]
    last = carry + cot_ref[:, pair(pairs - 2)].astype(F32)
    grad_ref[:, pair(pairs - 1)] = last.astype(BF16)
    band_grad(total, 1, g1_ref)


def mix_grad(term_ref, cot_ref, c):
    acc = None
    for k in range(cot_ref.shape[1] // 128):
        part = dot_t0(term_ref[:, pair(k)], cot_ref[:, pair(k)])
        acc = part if acc is None else acc + part
    return acc[:c, :c] + acc[c:, c:]


def early_part(hidden_ref, hop_ref, x_ref, cot_ref, mix_ref, gm_ref, map0, map1, wide_ref):
    c = mix_ref.shape[1]
    block_map(mix_ref, 0, map0)
    block_map(mix_ref, 1, map1)
    for k in range(cot_ref.shape[1] // 128):
        acc = x_ref[:, pair(k + 1)].astype(F32)
        acc = acc + dot(hidden_ref[:, pair(k)], map0[...])
        wide_ref[:, pair(k)] = acc + dot(hop_ref[:, pair(k)], map1[...])
    gm_ref[0] = mix_grad(hidden_ref, cot_ref, c)
    gm_ref[1] = mix_grad(hop_ref, cot_ref, c)


def main_body(parts, reps, scale,
              x_ref, cot_ref, conv1_ref, conv2_ref, mix_ref, dense_ref, picks_ref, base_ref,
              pieces_ref,
              out_ref, grad_ref, sum_ref,
              first_ref, hidden_ref, hop_ref, second_ref, up_ref, mid_ref, band_ref,
              map0, map1, map2, g1_ref, g2_ref, gm_ref,
              wide_ref, send1, send2, send3, recv0, recv1, recv2, recv3,
              pack_ref, got_ref, part_ref, reps_ref, sums_ref,
              ssem, rsem, asem, arsem, bsem, brsem):
    me = lax.axis_index("dom")
    mine = lax.axis_index("rep")
    nodes = x_ref.shape[0]
    c = mix_ref.shape[1]
    pairs = cot_ref.shape[1] // 128
    feats = cot_ref.shape[1]

    barrier = pltpu.get_barrier_semaphore()
    for o in range(1, parts):
        pl.semaphore_signal(barrier, inc=1, device_id={"dom": lax.rem(me + o, parts)},
                            device_id_type=pl.DeviceIdType.MESH)
    for o in range(1, reps):
        pl.semaphore_signal(barrier, inc=1, device_id={"rep": lax.rem(mine + o, reps)},
                            device_id_type=pl.DeviceIdType.MESH)
    pl.semaphore_wait(barrier, parts - 1 + reps - 1)

    def copies(level, src, dst):
        made = []
        for o in sorted(range(1, parts), key=lambda o: abs(2 * o - parts)):
            peer = lax.rem(me + o, parts)
            made.append(pltpu.make_async_remote_copy(
                src_ref=src.at[peer, pl.ds(c, feats - c)],
                dst_ref=dst.at[me, pl.ds(c, feats - c)],
                send_sem=ssem.at[level, o],
                recv_sem=rsem.at[level, o],
                device_id={"dom": peer},
                device_id_type=pl.DeviceIdType.MESH,
            ))
        for m in made:
            m.start()
        return made

    def arrive(made):
        for m in made:
            m.wait_recv()

    round0 = copies(0, pieces_ref, recv0)
    for buf in (recv0, recv1, recv2, recv3):
        buf[:, 0:c, :] = jnp.zeros((parts, c, BLK), BF16)
        buf[me] = jnp.zeros((feats, BLK), BF16)

    forward_part(x_ref, conv1_ref, conv2_ref, first_ref, hidden_ref, band_ref)
    pack_rows(hidden_ref[...], picks_ref, 0, parts, send1)
    round1 = copies(1, send1, recv1)

    arrive(round0)
    g = from_blocks(base_ref[...], picks_ref, 0, parts, recv0).astype(BF16)
    pack_rows(g, dense_ref, nodes, parts, send2)
    round2 = copies(2, send2, recv2)
    up_ref[...] = dot_t0(dense_ref[:, :nodes], g)
    block_map(mix_ref, 0, map0)
    for k in range(pairs):
        up_ref[:, pair(k)] += dot_t1(cot_ref[:, pair(k)], map0[...])

    own = dot(dense_ref[:, :nodes], hidden_ref[...])
    arrive(round1)
    hop_ref[...] = from_blocks(own, dense_ref, nodes, parts, recv1).astype(BF16)
    pack_rows(hop_ref[...], picks_ref, 0, parts, send3)
    round3 = copies(3, send3, recv3)

    arrive(round2)
    up_ref[...] = from_blocks(up_ref[...], picks_ref, 0, parts, recv2)
    backward_part(x_ref, first_ref, cot_ref, conv1_ref, conv2_ref, grad_ref, g1_ref, g2_ref,
                  band_ref, up_ref, mid_ref)

    early_part(hidden_ref, hop_ref, x_ref, cot_ref, mix_ref, gm_ref, map0, map1, wide_ref)
    block_map(mix_ref, 2, map2)
    own = dot(dense_ref[:, :nodes], hop_ref[...])
    arrive(round3)
    second_ref[...] = from_blocks(own, dense_ref, nodes, parts, recv3).astype(BF16)
    gm_ref[2] = mix_grad(second_ref, cot_ref, c)

    per = pack_ref.shape[1]
    flat = pack_ref
    flat[...] = jnp.zeros(flat.shape, F32)

    def put(first_row, value):
        rows = value.shape[0]
        done = 0
        while done < rows:
            slot, at = divmod(first_row + done, per)
            step = min(per - at, rows - done)
            flat[slot, at : at + step, :] = value[done : done + step]
            done += step

    put(0, g1_ref[0])
    put(c, g1_ref[1])
    put(2 * c, g2_ref[0])
    put(3 * c, g2_ref[1])
    put(4 * c, jnp.concatenate([gm_ref[0], gm_ref[1]], axis=1))
    put(5 * c, jnp.concatenate([gm_ref[2], jnp.zeros((c, c), F32)], axis=1))

    scatter = []
    for o in range(1, parts):
        peer = lax.rem(me + o, parts)
        scatter.append(pltpu.make_async_remote_copy(
            src_ref=pack_ref.at[peer], dst_ref=got_ref.at[me],
            send_sem=asem.at[0, o], recv_sem=arsem.at[0, o],
            device_id={"dom": peer}, device_id_type=pl.DeviceIdType.MESH))
    for m in scatter:
        m.start()
    for k in range(pairs):
        wide_ref[:, pair(k)] += dot(second_ref[:, pair(k)], map2[...])
    out_ref[...] = wide_ref[...].T[c:].astype(BF16)
    got_ref[me] = pack_ref[me]
    arrive(scatter)
    total = got_ref[0]
    for q in range(1, parts):
        total = total + got_ref[q]
    part_ref[...] = total
    around = []
    for o in range(1, reps):
        peer = lax.rem(mine + o, reps)
        around.append(pltpu.make_async_remote_copy(
            src_ref=part_ref, dst_ref=reps_ref.at[mine],
            send_sem=bsem.at[o], recv_sem=brsem.at[o],
            device_id={"rep": peer}, device_id_type=pl.DeviceIdType.MESH))
    for m in around:
        m.start()
    reps_ref[mine] = total
    arrive(around)
    total = reps_ref[0]
    for q in range(1, reps):
        total = total + reps_ref[q]
    for m in around:
        m.wait_send()
    part_ref[...] = total * (1.0 / scale)
    final = []
    for o in range(1, parts):
        peer = lax.rem(me + o, parts)
        final.append(pltpu.make_async_remote_copy(
            src_ref=part_ref, dst_ref=sums_ref.at[me],
            send_sem=asem.at[1, o], recv_sem=arsem.at[1, o],
            device_id={"dom": peer}, device_id_type=pl.DeviceIdType.MESH))
    for m in final:
        m.start()
    sums_ref[me] = part_ref[...]
    arrive(final)

    sum_ref[...] = sums_ref[...]
    for m in round0 + round1 + round2 + round3 + scatter + final:
        m.wait_send()


def shards(inputs, cotangent, conv_one, conv_two, mix_weight, send_rows, counts, tile_cols,
           tile_vals):
    windows, nodes, flat = inputs.shape
    channels = mix_weight.shape[1]
    parts = lax.axis_size("dom")
    reps = lax.axis_size("rep")
    kept = flat // channels - 3
    wide = flat - 2 * channels
    halo = parts * BLK
    blocks = (parts, wide, BLK)
    prepared = [((nodes, nodes + halo), BF16), ((nodes, halo), BF16), ((nodes, wide), BF16),
                ((nodes, wide), F32), (blocks, BF16)]
    dense, picks, cot_wide, base, pieces = pl.pallas_call(
        prepare_body,
        out_shape=[jax.ShapeDtypeStruct(s, d) for s, d in prepared],
        in_specs=[VM, VM, VM, SM, SM, VM],
        out_specs=[VM] * 5,
        scratch_shapes=[pltpu.VMEM((parts + nodes // BLK, BLK, BLK), F32),
                        pltpu.VMEM((128, 128), BF16), pltpu.VMEM((nodes, wide), BF16)],
        compiler_params=LIMIT,
        name="prepare",
    )(cotangent[0].T, mix_weight, send_rows[0], counts, tile_cols, tile_vals)
    scaling = math.sqrt(float(windows * reps * nodes * parts * kept))
    unit = 8 * parts
    per = -(-6 * channels // unit) * unit // parts
    results = [((kept * channels, nodes), BF16), ((nodes, flat), BF16), ((parts, per, BLK), F32)]
    scratch = [((nodes, flat), BF16), ((nodes, wide), BF16), ((nodes, wide), BF16),
               ((nodes, wide), BF16), ((nodes, wide), F32), ((nodes, flat), BF16),
               ((256, 256), BF16), ((128, 128), BF16), ((128, 128), BF16), ((128, 128), BF16),
               (conv_one.shape, F32), (conv_two.shape, F32), (mix_weight.shape, F32)]
    scratch += [((nodes, wide), F32)] + [(blocks, BF16)] * 7
    scratch += [((parts, per, BLK), F32), ((parts, per, BLK), F32), ((per, BLK), F32),
                ((reps, per, BLK), F32), ((parts, per, BLK), F32)]
    dma = pltpu.SemaphoreType.DMA
    output, grad_input, packed = pl.pallas_call(
        functools.partial(main_body, parts, reps, scaling),
        out_shape=[jax.ShapeDtypeStruct(s, d) for s, d in results],
        in_specs=[VM] * 9,
        out_specs=[VM] * 3,
        scratch_shapes=[pltpu.VMEM(s, d) for s, d in scratch]
        + [dma((4, parts)), dma((4, parts)), dma((2, parts)), dma((2, parts)), dma((reps,)),
           dma((reps,))],
        compiler_params=pltpu.CompilerParams(
            vmem_limit_bytes=60 * 1024 * 1024, collective_id=0, has_side_effects=True),
        name="layer",
    )(inputs[0], cot_wide, conv_one, conv_two, mix_weight, dense, picks, base, pieces)
    c = channels
    rows = packed.reshape(parts * per, BLK)
    gm = jnp.stack([rows[4 * c : 5 * c, :c], rows[4 * c : 5 * c, c:], rows[5 * c : 6 * c, :c]])
    return (
        output.T[None],
        grad_input[None],
        rows[: 2 * c].reshape(conv_one.shape),
        rows[2 * c : 4 * c].reshape(conv_two.shape),
        gm,
    )


def place_tiles(r, me, parts, cols_ref, vals_ref, dense_ref):
    rtiles, slots = vals_ref.shape[0], vals_ref.shape[1]
    for c in range(dense_ref.shape[1] // BLK):
        named = c if c < rtiles else rtiles + lax.rem(me - (c - rtiles + 1) + parts, parts)
        total = None
        for j in range(slots):
            keep = jnp.where(cols_ref[r, j] == named, 1.0, 0.0)
            part = vals_ref[r, j].astype(F32) * keep
            total = part if total is None else total + part
        dense_ref[chunk(r * BLK, BLK), c * BLK : (c + 1) * BLK] = total.astype(BF16)


def chunk(first, size):
    return pl.ds(pl.multiple_of(first, size), size)


def steps_body(parts, reps, scale,
               x_ref, cot_ref, conv1_ref, conv2_ref, mix_ref, send_ref, counts_ref, cols_ref, vals_ref,
               out_ref, grad_ref, one_out, two_out, mix_out,
               dense_ref, wanted_ref, xt_ref, first_ref, hid_ref, d1_ref, d2_ref, mid_ref, low_ref,
               band1, band1t, band2, band2t, maps, mapst,
               adj_ref, adj_t, lists_ref, picks_ref, picks_t,
               cf_ref, hf_ref, f1_ref, c1_ref, c2_ref, own_ref, part_t, ext_ref,
               gh_ref, mx_ref, ghs_ref, mxs_ref,
               g1_ref, g2_ref, pack0, got0, half0, all0, full0, sums0,
               pack1, got1, half1, all1, full1, sums1,
               lsend, lrecv, fsend, frecv, esend, erecv, tsend, trecv,
               asem, arsem, bsem, brsem):
    me = lax.axis_index("dom")
    mine = lax.axis_index("rep")
    nodes = x_ref.shape[0]
    c = mix_ref.shape[1]
    pairs = x_ref.shape[1] // 128
    mesh_ids = pl.DeviceIdType.MESH
    holder = lax.rem(parts // 2 - reps // 2 + mine + parts, parts)
    extra = parts * c
    zs = parts // 2
    z, xx = me // 2, lax.rem(me, 2)
    yy, core = mine // 2, lax.rem(mine, 2)
    chips = parts * reps // 2
    chip = me * 2 + yy
    crep = yy * 2 + 1 - core

    barrier = pltpu.get_barrier_semaphore()
    for o in range(1, chips):
        peer = lax.rem(chip + o, chips)
        pl.semaphore_signal(barrier, inc=1, device_id={"dom": peer // 2, "rep": lax.rem(peer, 2) * 2 + core},
                            device_id_type=mesh_ids)
    pl.semaphore_signal(barrier, inc=1, device_id={"rep": yy * 2 + 1 - core}, device_id_type=mesh_ids)
    place_tiles(core, me, parts, cols_ref, vals_ref, dense_ref)
    pl.semaphore_wait(barrier, chips)

    def remote(src, dst, ssem, rsem, **where):
        return pltpu.make_async_remote_copy(
            src_ref=src, dst_ref=dst, send_sem=ssem, recv_sem=rsem,
            device_id=where, device_id_type=mesh_ids)

    order = sorted(range(1, parts), key=lambda o: abs(2 * o - parts))

    own_rows = 3 * (nodes // 16)
    both_rows = nodes // 2 - 2 * own_rows

    def span(sub, cc, y):
        third = own_rows // 3
        first = (own_rows + both_rows) * y
        at, size = ((first, 2 * third), (first + 2 * third, third), (own_rows, both_rows))[sub]
        return pl.ds(pl.multiple_of(cc * (nodes // 2) + at, 16), size)

    def piece(p, sub, cc, y):
        return adj_ref.at[p, span(sub, cc, y)]

    def source_z(t, way):
        return z - t if way == 0 else z + t

    def valid(t, way):
        if t == 0:
            return z >= 0
        return z >= t if way == 0 else z + t < zs

    def slot(t, way, sub):
        return 3 * (0 if t == 0 else 2 * t - 1 + way) + sub

    def base(t, way):
        return source_z(t, way) * 2 + xx

    def cross(t, way):
        return source_z(t, way) * 2 + 1 - xx

    def first_source(t, way, sub):
        return dense_ref.at[span(sub, core, yy)] if t == 0 else piece(base(t, way), sub, core, yy)

    def along(t, way, sub, out_way):
        to = (z + 1 if out_way == 0 else z - 1) * 2 + xx
        return remote(first_source(t, way, sub), piece(base(t, way), sub, core, yy),
                      tsend.at[out_way, slot(t, way, sub)], trecv.at[0, slot(t + 1, out_way, sub)], dom=to)

    def across(t, way, sub):
        return remote(first_source(t, way, sub), piece(base(t, way), sub, core, yy),
                      tsend.at[2, slot(t, way, sub)], trecv.at[2, slot(t, way, sub)], dom=z * 2 + 1 - xx)

    def hand(kind, part, t, way, sub, y):
        ref = piece(part(t, way), sub, core, y)
        to = (1 - yy) * 2 + core if kind in (3, 5) else crep
        return remote(ref, ref, tsend.at[kind, slot(t, way, sub)], trecv.at[kind, slot(t, way, sub)], rep=to)

    def arrived(kind, ref, t, way, sub):
        remote(ref, ref, tsend.at[kind, slot(t, way, sub)], trecv.at[kind, slot(t, way, sub)],
               rep=crep).wait_recv()

    def ways(t):
        return (0,) if t == 0 else (0, 1)

    def lane_sends(t, way, sub):
        made = []
        if t + 1 < zs:
            for w in (0, 1) if t == 0 else (way,):
                made.append((z + 1 < zs if w == 0 else z >= 1, along(t, way, sub, w)))
        made.append((None, across(t, way, sub)))
        return made

    def side_sends(t, way, sub, part, kind):
        if t == 0 and part is base:
            return []
        made = [(None, hand(kind, part, t, way, sub, yy))] if sub < 2 else []
        return made + [(None, hand(kind + 1, part, t, way, sub, yy))]

    def core_sends(t, way, sub, part, kind):
        if t == 0 and part is base or sub == 2:
            return []
        return [(None, hand(kind, part, t, way, sub, 1 - yy))]

    def go(sends, wait=False):
        for cond, copy in sends:
            act = copy.wait_send if wait else copy.start
            if cond is None:
                act()
            else:
                pl.when(cond)(act)

    def on_base(t, way, sub):
        @pl.when(valid(t, way))
        def _():
            arrived(0, piece(base(t, way), sub, core, yy), t, way, sub)
            go(lane_sends(t, way, sub) + side_sends(t, way, sub, base, 3))

    def on_cross(t, way, sub):
        @pl.when(valid(t, way))
        def _():
            arrived(2, piece(cross(t, way), sub, core, yy), t, way, sub)
            go(side_sends(t, way, sub, cross, 5))

    def on_plane(t, way, sub, part, kind):
        @pl.when(valid(t, way))
        def _():
            arrived(kind, piece(part(t, way), sub, core, 1 - yy), t, way, sub)
            go(core_sends(t, way, sub, part, 7 if kind == 3 else 8))

    def on_tiles(t, way, part, kind, use):
        @pl.when(valid(t, way))
        def _():
            if t or part is cross:
                for sub in range(3):
                    arrived(kind + 1, piece(part(t, way), sub, 1 - core, yy), t, way, sub)
                for sub in range(2):
                    arrived(7 if kind == 3 else 8, piece(part(t, way), sub, 1 - core, 1 - yy), t, way, sub)
            use(part(t, way))

    relay = []

    def step_relay(count=1):
        for _ in range(count):
            if relay:
                relay.pop()()

    def scatter_field(level, src, first, dst):
        made = []
        for o in order:
            peer = lax.rem(me + o, parts)
            made.append(remote(src.at[chunk(first + peer * c, c)], dst.at[me, pl.ds(0, c)],
                               fsend.at[level, o], frecv.at[level, o], dom=peer))
        for m in made:
            m.start()
        off = lax.rem(holder - me + parts, parts)
        last = remote(src.at[pl.ds(first + extra, c)], dst.at[me, pl.ds(c, c)],
                      esend.at[level, 0], erecv.at[level, off], dom=holder)
        pl.when(me != holder)(last.start)
        dst[me, 0:c, :] = src[chunk(first + me * c, c), :]

        @pl.when(me == holder)
        def _():
            dst[me, c : 2 * c, :] = src[first + extra : first + extra + c, :]

        @pl.when(me != holder)
        def _():
            dst[:, c : 2 * c, :] = jnp.zeros((parts, c, nodes), BF16)
        return made, last

    def field_arrives(level, made, src, dst):
        for m in made:
            m.wait_recv()

        @pl.when(me == holder)
        def _():
            for o in range(1, parts):
                q = lax.rem(me - o + parts, parts)
                remote(dst.at[q, pl.ds(c, c)], dst.at[q, pl.ds(c, c)], esend.at[level, 0],
                       erecv.at[level, o], dom=q).wait_recv()

    def home_copies(level, o, src, first, dst):
        q = lax.rem(me + o, parts)
        one = remote(src.at[q, pl.ds(0, c)], dst.at[chunk(first + me * c, c)],
                     fsend.at[level, o], frecv.at[level, o], dom=q)
        two = remote(src.at[q, pl.ds(c, c)], dst.at[pl.ds(first + extra, c)],
                     esend.at[level, o], erecv.at[level, 0], dom=q)
        return one, two

    def go_home(level, o, src, first, dst):
        if o:
            one, two = home_copies(level, o, src, first, dst)
            one.start()
            pl.when(me == holder)(two.start)
            return
        dst[chunk(first + me * c, c), :] = src[me, 0:c, :]

        @pl.when(me == holder)
        def _():
            dst[first + extra : first + extra + c, :] = src[me, c : 2 * c, :]

    def home_arrives(level, src, first, dst):
        for o in range(1, parts):
            home_copies(level, o, src, first, dst)[0].wait_recv()
        pl.when(me != holder)(home_copies(level, 1, src, first, dst)[1].wait_recv)

    def home_sent(level, src, first, dst):
        for o in range(1, parts):
            one, two = home_copies(level, o, src, first, dst)
            one.wait_send()
            pl.when(me == holder)(two.wait_send)

    for sub in range(3):
        go(lane_sends(0, 0, sub))
    lane = lax.broadcasted_iota(jnp.int32, (1, BLK), 1)
    for o in range(parts):
        t = lax.rem(me + o, parts)
        wanted_ref[o : o + 1, :] = jnp.where(
            lane < counts_ref[0, t], send_ref[pl.ds(t, 1), :], -1)
    lists = []
    for o in order:
        peer = lax.rem(me + o, parts)
        lists.append(remote(wanted_ref, lists_ref.at[me], lsend.at[o], lrecv.at[o], dom=peer))
    for m in lists:
        m.start()
    lists_ref[me] = wanted_ref[...]
    place_tiles(1 - core, me, parts, cols_ref, vals_ref, dense_ref)
    adj_ref[me] = dense_ref[...]

    def back_piece(g_ref, p):
        t = dot(g_ref[p], adj_ref[p])
        own_ref[p] = t[:, :nodes]
        for o in range(1, parts):
            at = nodes + (o - 1) * BLK
            owner = lax.rem(p - o + parts, parts)
            part_t[owner, :, (o - 1) * BLK : o * BLK] = t[:, at : at + BLK].astype(BF16)

    def use(p):
        back_piece(cf_ref, p)
        adj_t[p] = adj_ref[p].T

    hid_round, cot_round = [], []

    def first_piece():
        field_arrives(0, cot_round[0], cot_ref, cf_ref)
        use(me)

    def send_cotangent():
        cot_round.extend(scatter_field(0, cot_ref, 0, cf_ref))

    def send_hidden():
        hid_round.extend(scatter_field(1, hid_ref, c, hf_ref))

    def add(handler, t, *rest):
        for w in ways(t):
            relay.append(functools.partial(handler, t, w, *rest))

    for t in range(1, zs + 2):
        if t < zs:
            for sub in range(3):
                add(on_base, t, sub)
        if t <= zs:
            for sub in range(3):
                add(on_cross, t - 1, sub)
        if t == 2:
            relay.append(send_cotangent)
        for sub in range(2):
            if 2 <= t <= zs:
                add(on_plane, t - 1, sub, base, 3)
            if t >= 2:
                add(on_plane, t - 2, sub, cross, 5)
        if t == 4:
            relay.append(send_hidden)
        if t >= zs:
            if t == zs:
                relay.append(first_piece)
            add(on_tiles, t - zs, cross, 5, use)
            add(on_tiles, t - zs + 1, base, 3, use)
    for u in range(2, zs):
        add(on_tiles, u, cross, 5, use)
        if u + 1 < zs:
            add(on_tiles, u + 1, base, 3, use)
    relay.reverse()

    for k in range(pairs):
        xt_ref[pair(k), :] = x_ref[:, pair(k)].T
    for conv, dil, nat, tra in ((conv1_ref, 1, band1, band1t), (conv2_ref, 2, band2, band2t)):
        band_map(conv, dil, nat)
        tra[...] = nat[...].T

    def earlier_t(ref, k):
        if k == 0:
            v = ref[0:128, :]
            return jnp.concatenate([jnp.zeros_like(v), v], axis=0)
        return ref[window2(k - 1), :]

    def gated(pre, d_ref, k):
        filt = jnp.tanh(pre[:128])
        gates = 0.5 * jnp.tanh(0.5 * pre[128:]) + 0.5
        d_ref[k, 0:128, :] = gates * (1.0 - filt * filt)
        d_ref[k, 128:256, :] = filt * gates * (1.0 - gates)
        return (filt * gates).astype(BF16)

    for k in range(pairs):
        first_ref[pair(k), :] = gated(dot(band1t[...], earlier_t(xt_ref, k)), d1_ref, k)
        if k % 2:
            step_relay()
    for k in range(1, pairs):
        hid_ref[pair(k - 1), :] = gated(dot(band2t[...], earlier_t(first_ref, k)), d2_ref, k)
        step_relay()

    for i in range(3):
        block_map(mix_ref, i, maps.at[i])
        mapst[i] = maps[i].T
    gh_ref[0:c, :] = jnp.zeros((c, nodes), BF16)

    for m in lists:
        m.wait_recv()
    node = lax.broadcasted_iota(jnp.int32, (nodes, BLK), 0)
    for q in range(parts):
        for o in range(1, parts):
            hit = node == lists_ref[q, o : o + 1, :]
            picks_ref[q, :, (o - 1) * BLK : o * BLK] = jnp.where(hit, 1.0, 0.0).astype(BF16)
        picks_t[q] = picks_ref[q].T
        step_relay(2)

    step_relay(len(relay))

    def back_owner(q):
        return (own_ref[q] + dot(part_t[q], picks_t[q])).astype(BF16)

    for q in range(parts):
        c1_ref[q] = back_owner(q)
    for p in range(parts):
        back_piece(c1_ref, p)
    for o in order + [0]:
        q = lax.rem(me + o, parts)
        c2 = back_owner(q)
        c2_ref[q] = c2
        grads = dot(maps[0], cf_ref[q]) + dot(maps[1], c1_ref[q]) + dot(maps[2], c2)
        ghs_ref[q] = grads.astype(BF16)
        go_home(2, o, ghs_ref, c, gh_ref)

    field_arrives(1, hid_round[0], hid_ref, hf_ref)
    mix = []
    for moved in (cf_ref, c1_ref, c2_ref):
        total = dot_t1(hf_ref[0], moved[0])
        for q in range(1, parts):
            total = total + dot_t1(hf_ref[q], moved[q])
        mix.append(total[:c, :c] + total[c:, c:])

    def reducer(g, pack, got, half, got_all, full, sums):
        def over_core(stage, src, dst):
            return [remote(src, dst, bsem.at[2 * g + stage], brsem.at[2 * g + stage], rep=crep)]

        def over_chips(stage, src_of, dst):
            made = []
            for o in range(1, chips):
                peer = lax.rem(chip + o, chips)
                made.append(remote(src_of(peer), dst, asem.at[2 * g + stage, o], arsem.at[2 * g + stage, o],
                                   dom=peer // 2, rep=lax.rem(peer, 2) * 2 + core))
            return made

        steps = (lambda: over_core(0, pack.at[1 - core], got),
                 lambda: over_chips(0, lambda peer: half.at[peer], got_all.at[chip]),
                 lambda: over_chips(1, lambda peer: full, sums.at[core, chip]),
                 lambda: over_core(1, sums.at[core], sums.at[core]))

        def start(i):
            for m in steps[i]():
                m.start()

        def arrive(i):
            for m in steps[i]():
                m.wait_recv()

        def first():
            start(0)

        def second():
            arrive(0)
            total = pack[core] + got[...]
            share = half.shape[1]
            for q in range(chips):
                half[q] = total[q * share : (q + 1) * share]
            start(1)
            got_all[chip] = half[chip]

        def third():
            arrive(1)
            total = got_all[0]
            for q in range(1, chips):
                total = total + got_all[q]
            full[...] = total * (1.0 / scale)
            start(2)
            sums[core, chip] = full[...]

        def fourth():
            arrive(2)
            start(3)

        def last():
            arrive(3)

        def sent():
            for i in range(4):
                for m in steps[i]():
                    m.wait_send()

        return first, second, third, fourth, last, sent

    early = reducer(0, pack0, got0, half0, all0, full0, sums0)
    late = reducer(1, pack1, got1, half1, all1, full1, sums1)
    pack0[...] = jnp.zeros(pack0.shape, F32)
    for i in range(3):
        pack0[i // 2, (i % 2) * c : (i % 2 + 1) * c, 0:c] = mix[i]
    early[0]()

    def extend(f_ref):
        for q in range(parts):
            ext_ref[q, :, 0:nodes] = f_ref[q]
            halo = dot(f_ref[q], picks_ref[q]).astype(BF16)
            for o in range(1, parts):
                at = nodes + (o - 1) * BLK
                ext_ref[(q + o) % parts, :, at : at + BLK] = halo[:, (o - 1) * BLK : o * BLK]

    extend(hf_ref)
    for p in range(parts):
        f1_ref[p] = dot(ext_ref[p], adj_t[p]).astype(BF16)
    extend(f1_ref)
    for o in order + [0]:
        q = lax.rem(me + o, parts)
        second = dot(ext_ref[q], adj_t[q]).astype(BF16)
        mixed = dot(mapst[0], hf_ref[q]) + dot(mapst[1], f1_ref[q]) + dot(mapst[2], second)
        mxs_ref[q] = mixed.astype(BF16)
        go_home(3, o, mxs_ref, 0, mx_ref)
    early[1]()

    home_arrives(2, ghs_ref, c, gh_ref)

    def conv_back(sig_ref, d_ref, up_of, band, low_of, first_pair, dilation, out):
        total, carry = None, None
        b = band[...]
        for k in range(first_pair, pairs):
            up = up_of(k)
            both = earlier_t(sig_ref, k)
            d = jnp.concatenate([up * d_ref[k, 0:128, :], up * d_ref[k, 128:256, :]], axis=0)
            d = d.astype(BF16)
            part = dot_t1(both, d)
            total = part if total is None else total + part
            back = dot(b, d)
            if k > 0:
                low_of(k - 1, back[:128] if carry is None else carry + back[:128])
            carry = back[128:]
        low_of(pairs - 1, carry)
        band_grad(total, dilation, out)

    def set_mid(k, low):
        mid_ref[pair(k), :] = low.astype(BF16)

    def set_grad(k, low):
        if k == 1:
            low = low + jnp.concatenate([jnp.zeros((c, nodes), F32), cot_ref[0:c, :].astype(F32)], axis=0)
        elif k > 1:
            low = low + cot_ref[(2 * k - 3) * c : (2 * k - 1) * c, :].astype(F32)
        low_ref[pair(k), :] = low.astype(BF16)

    conv_back(first_ref, d2_ref, lambda k: gh_ref[pair(k - 1), :].astype(F32), band2, set_mid, 1, 2, g2_ref)
    conv_back(xt_ref, d1_ref, lambda k: mid_ref[pair(k), :].astype(F32), band1, set_grad, 0, 1, g1_ref)

    for tap in range(2):
        pack1[0, tap * c : (tap + 1) * c, :] = g1_ref[tap]
        pack1[1, tap * c : (tap + 1) * c, :] = g2_ref[tap]
    late[0]()
    late[1]()
    for k in range(pairs):
        grad_ref[:, pair(k)] = low_ref[pair(k), :].T
    early[2]()
    home_arrives(3, mxs_ref, 0, mx_ref)
    kept = out_ref.shape[0]
    out_ref[...] = (mx_ref[...].astype(F32) + xt_ref[pairs * 128 - kept :, :].astype(F32)).astype(BF16)
    late[2]()
    early[3]()

    for m in cot_round[0] + hid_round[0] + lists:
        m.wait_send()
    pl.when(me != holder)(cot_round[1].wait_send)
    pl.when(me != holder)(hid_round[1].wait_send)
    home_sent(2, ghs_ref, c, gh_ref)
    home_sent(3, mxs_ref, 0, mx_ref)
    for t in range(zs):
        for w in ways(t):
            @pl.when(valid(t, w))
            def _():
                for sub in range(3):
                    go(lane_sends(t, w, sub) + side_sends(t, w, sub, base, 3)
                       + side_sends(t, w, sub, cross, 5) + core_sends(t, w, sub, base, 7)
                       + core_sends(t, w, sub, cross, 8), wait=True)
    late[3]()
    early[4]()
    share = sums0.shape[2]
    for q in range(chips):
        tap, at = divmod(q * share, c)
        mix_out[tap, at : at + share, :] = sums0[0, q, :, 0:c]
        if tap == 0:
            mix_out[2, at : at + share, :] = sums0[1, q, :, 0:c]
    early[5]()
    late[4]()
    for q in range(chips):
        tap, at = divmod(q * share, c)
        one_out[tap, at : at + share, :] = sums1[0, q]
        two_out[tap, at : at + share, :] = sums1[1, q]
    late[5]()


def finish_body(*refs):
    half = len(refs) // 2
    for a, b in zip(refs[:half], refs[half:]):
        b[...] = a[...]


def step_shards(inputs, cotangent, conv_one, conv_two, mix_weight, send_rows, counts, tile_cols,
                tile_vals):
    windows, nodes, flat = inputs.shape
    channels = mix_weight.shape[1]
    parts = lax.axis_size("dom")
    reps = lax.axis_size("rep")
    kept = flat // channels - 3
    c = channels
    pairs = flat // 128
    halo = (parts - 1) * BLK
    ext = nodes + halo
    scaling = math.sqrt(float(windows * reps * nodes * parts * kept))
    results = [((kept * c, nodes), BF16), ((nodes, flat), BF16), (conv_one.shape, F32),
               (conv_two.shape, F32), (mix_weight.shape, F32)]
    field = (parts, 2 * c, nodes)
    wide = flat - 2 * c
    scratch = [((nodes, ext), BF16), ((parts, BLK), jnp.int32),
               ((flat, nodes), BF16), ((flat, nodes), BF16), ((wide, nodes), BF16),
               ((pairs, 256, nodes), F32), ((pairs, 256, nodes), F32), ((flat, nodes), BF16),
               ((flat, nodes), BF16)]
    scratch += [((256, 256), BF16)] * 4 + [((3, 128, 128), BF16)] * 2
    scratch += [((parts, nodes, ext), BF16), ((parts, ext, nodes), BF16), ((parts, parts, BLK), jnp.int32),
                ((parts, nodes, halo), BF16), ((parts, halo, nodes), BF16)]
    scratch += [(field, BF16)] * 5 + [(field, F32), ((parts, 2 * c, halo), BF16),
                                      ((parts, 2 * c, ext), BF16)]
    scratch += [((wide, nodes), BF16), ((kept * c, nodes), BF16), (field, BF16), (field, BF16)]
    scratch += [(conv_one.shape, F32), (conv_two.shape, F32)]
    chips = parts * reps // 2
    share = 2 * c // chips
    for _ in range(2):
        scratch += [((2, 2 * c, BLK), F32), ((2 * c, BLK), F32), ((chips, share, BLK), F32),
                    ((chips, share, BLK), F32), ((share, BLK), F32), ((2, chips, share, BLK), F32)]
    dma = pltpu.SemaphoreType.DMA
    sems = [(parts,), (parts,), (4, parts), (4, parts), (4, parts), (4, parts),
            (9, 3 * parts), (9, 3 * parts), (4, chips), (4, chips), (4,), (4,)]
    made = pl.pallas_call(
        functools.partial(steps_body, parts, reps, scaling),
        out_shape=[jax.ShapeDtypeStruct(s, d) for s, d in results],
        in_specs=[VM] * 6 + [SM, SM, VM],
        out_specs=[VM] * 5,
        scratch_shapes=[pltpu.VMEM(s, d) for s, d in scratch] + [dma(s) for s in sems],
        compiler_params=pltpu.CompilerParams(
            vmem_limit_bytes=60 * 1024 * 1024, collective_id=1, has_side_effects=True),
        name="steps",
    )(inputs[0], cotangent[0].T, conv_one, conv_two, mix_weight, send_rows[0], counts, tile_cols,
      tile_vals)
    output, grad_input, one, two, mix = pl.pallas_call(
        finish_body,
        out_shape=[jax.ShapeDtypeStruct(s, d) for s, d in results],
        in_specs=[VM] * 5,
        out_specs=[VM] * 5,
        compiler_params=LIMIT,
        name="finish",
    )(*made)
    return output.T[None], grad_input[None], one, two, mix


def solution(mesh):
    placed = (
        P("rep", "dom", None),
        P("rep", "dom", None),
        P(),
        P(),
        P(),
        P("dom", None, None),
        P("dom", None),
        P("dom", None),
        P("dom", None, None, None),
    )
    parts, reps = mesh.shape["dom"], mesh.shape["rep"]

    def layer(*args):
        kept = args[0].shape[2] // args[4].shape[1] - 3
        by_step = parts % 2 == 0 and reps == 4 and parts == kept - 1
        return step_shards(*args) if by_step else shards(*args)

    return jax.shard_map(
        layer,
        mesh=mesh,
        in_specs=placed,
        out_specs=(P("rep", "dom", None), P("rep", "dom", None), P(), P(), P()),
        check_vma=False,
    )
```

```python
import functools
import math

import jax
import jax.numpy as jnp
from jax import lax
from jax.experimental import pallas as pl
from jax.experimental.pallas import tpu as pltpu
from jax.sharding import PartitionSpec as P

F32 = jnp.float32
BF16 = jnp.bfloat16
BLK = 128
VM = pl.BlockSpec(memory_space=pltpu.VMEM)
SM = pl.BlockSpec(memory_space=pltpu.SMEM)
LIMIT = pltpu.CompilerParams(vmem_limit_bytes=56 * 1024 * 1024)


def dot(a, b):
    return jnp.dot(a, b, preferred_element_type=F32)


def dot_t0(a, b):
    return lax.dot_general(a, b, (((0,), (0,)), ((), ())), preferred_element_type=F32)


def dot_t1(a, b):
    return lax.dot_general(a, b, (((1,), (1,)), ((), ())), preferred_element_type=F32)


def pair(k):
    return slice(k * 128, (k + 1) * 128)


def window2(k):
    return slice(k * 128, (k + 2) * 128)


def block_map(weight_ref, index, out_ref):
    c = weight_ref.shape[1]
    w = weight_ref[index]
    out_ref[...] = jnp.zeros(out_ref.shape, BF16)
    out_ref[0:c, 0:c] = w
    out_ref[c : 2 * c, c : 2 * c] = w


def band_blocks(dilation):
    if dilation == 1:
        return ((0, 1, 0), (0, 2, 1), (1, 2, 0), (1, 3, 1))
    return ((0, 0, 0), (0, 1, 1), (1, 2, 0), (1, 3, 1))


def band_map(conv_ref, dilation, out_ref):
    c = conv_ref.shape[1]
    out_ref[...] = jnp.zeros(out_ref.shape, BF16)
    for tap, i, o in band_blocks(dilation):
        w = conv_ref[tap]
        rows = slice(i * c, (i + 1) * c)
        out_ref[rows, o * c : (o + 1) * c] = w[:, :c]
        out_ref[rows, (o + 2) * c : (o + 3) * c] = w[:, c:]


def band_grad(total, dilation, out_ref):
    c = out_ref.shape[1]
    for tap in range(2):
        for half in range(2):
            acc = None
            for t, i, o in band_blocks(dilation):
                if t != tap:
                    continue
                col = (o + 2 * half) * c
                part = total[i * c : (i + 1) * c, col : col + c]
                acc = part if acc is None else acc + part
            out_ref[tap, :, half * c : (half + 1) * c] = acc


def activations(pre):
    filt = jnp.tanh(pre[:, :128])
    gates = 0.5 * jnp.tanh(0.5 * pre[:, 128:]) + 0.5
    return filt, gates


def earlier(ref, k):
    if k == 0:
        x = ref[:, 0:128]
        return jnp.concatenate([jnp.zeros_like(x), x], axis=1)
    return ref[:, window2(k - 1)]


def build_tiles(cols_ref, vals_ref, acc_ref, dense_ref):
    rtiles, slots = vals_ref.shape[0], vals_ref.shape[1]
    ctiles = dense_ref.shape[1] // BLK
    for r in range(rtiles):
        acc_ref[...] = jnp.zeros(acc_ref.shape, F32)
        for j in range(slots):
            c = cols_ref[r, j]
            acc_ref[c] = acc_ref[c] + vals_ref[r, j].astype(F32)
        for c in range(ctiles):
            dense_ref[r * BLK : (r + 1) * BLK, c * BLK : (c + 1) * BLK] = acc_ref[c].astype(BF16)


def build_picks(send_ref, counts_ref, picks_ref):
    parts = send_ref.shape[0]
    nodes = picks_ref.shape[0]
    lane = lax.broadcasted_iota(jnp.int32, (1, BLK), 1)
    rows = lax.broadcasted_iota(jnp.int32, (nodes, BLK), 0)
    for q in range(parts):
        wanted = jnp.where(lane < counts_ref[0, q], send_ref[q : q + 1, :], -1)
        hit = rows == wanted
        picks_ref[:, q * BLK : (q + 1) * BLK] = jnp.where(hit, 1.0, 0.0).astype(BF16)


def prepare_body(cot_ref, mix_ref, send_ref, counts_ref, cols_ref, vals_ref,
                 dense_ref, picks_ref, cot_out, base_ref, pieces_ref,
                 acc_ref, map_ref, g_ref):
    nodes = cot_ref.shape[1]
    parts = send_ref.shape[0]
    c = mix_ref.shape[1]
    build_tiles(cols_ref, vals_ref, acc_ref, dense_ref)
    build_picks(send_ref, counts_ref, picks_ref)
    wide = cot_ref[...].astype(F32).T
    wide = jnp.concatenate([jnp.zeros((nodes, c), F32), wide], axis=1).astype(BF16)
    cot_out[...] = wide
    pairs = cot_out.shape[1] // 128
    block_map(mix_ref, 2, map_ref)
    m = map_ref[...]
    for k in range(pairs):
        g_ref[:, pair(k)] = dot_t1(cot_out[:, pair(k)], m).astype(BF16)
    block_map(mix_ref, 1, map_ref)
    m = map_ref[...]
    g = g_ref[...]
    pack_rows(g, dense_ref, nodes, parts, pieces_ref)
    base_ref[...] = dot_t0(dense_ref[:, :nodes], g)
    for k in range(pairs):
        base_ref[:, pair(k)] += dot_t1(cot_out[:, pair(k)], m)


def pack_rows(values, table_ref, start, parts, out_ref):
    flipped = values.astype(F32).T.astype(BF16)
    for q in range(parts):
        table = table_ref[:, start + q * BLK : start + (q + 1) * BLK]
        out_ref[q] = dot(flipped, table).astype(BF16)


def from_blocks(total, table_ref, start, parts, arrived_ref):
    for q in range(parts):
        table = table_ref[:, start + q * BLK : start + (q + 1) * BLK]
        total = total + dot_t1(table, arrived_ref[q])
    return total


def forward_part(x_ref, conv1_ref, conv2_ref, first_ref, hidden_ref, band_ref):
    pairs = x_ref.shape[1] // 128
    band_map(conv1_ref, 1, band_ref)
    b = band_ref[...]
    for k in range(pairs):
        filt, gates = activations(dot(earlier(x_ref, k), b))
        first_ref[:, pair(k)] = (filt * gates).astype(BF16)
    band_map(conv2_ref, 2, band_ref)
    b = band_ref[...]
    for k in range(1, pairs):
        filt, gates = activations(dot(earlier(first_ref, k), b))
        hidden_ref[:, pair(k - 1)] = (filt * gates).astype(BF16)


def gate_grad(pre, up):
    filt, gates = activations(pre)
    d_filt = up * gates * (1.0 - filt * filt)
    d_gate = up * filt * gates * (1.0 - gates)
    return jnp.concatenate([d_filt, d_gate], axis=1).astype(BF16)


def backward_part(x_ref, first_ref, cot_ref, conv1_ref, conv2_ref, grad_ref, g1_ref, g2_ref,
                  band_ref, up_ref, mid_ref):
    pairs = x_ref.shape[1] // 128
    band_map(conv2_ref, 2, band_ref)
    b = band_ref[...]
    total = None
    carry = None
    for k in range(1, pairs):
        both = earlier(first_ref, k)
        d = gate_grad(dot(both, b), up_ref[:, pair(k - 1)])
        part = dot_t0(both, d)
        total = part if total is None else total + part
        back = dot_t1(d, b)
        low = back[:, :128] if carry is None else carry + back[:, :128]
        mid_ref[:, pair(k - 1)] = low.astype(BF16)
        carry = back[:, 128:]
    mid_ref[:, pair(pairs - 1)] = carry.astype(BF16)
    band_grad(total, 2, g2_ref)
    band_map(conv1_ref, 1, band_ref)
    b = band_ref[...]
    total = None
    carry = None
    for k in range(pairs):
        both = earlier(x_ref, k)
        d = gate_grad(dot(both, b), mid_ref[:, pair(k)].astype(F32))
        part = dot_t0(both, d)
        total = part if total is None else total + part
        back = dot_t1(d, b)
        if k > 0:
            low = carry + back[:, :128]
            if k > 1:
                low = low + cot_ref[:, pair(k - 2)].astype(F32)
            grad_ref[:, pair(k - 1)] = low.astype(BF16)
        carry = back[:, 128:]
    last = carry + cot_ref[:, pair(pairs - 2)].astype(F32)
    grad_ref[:, pair(pairs - 1)] = last.astype(BF16)
    band_grad(total, 1, g1_ref)


def mix_grad(term_ref, cot_ref, c):
    acc = None
    for k in range(cot_ref.shape[1] // 128):
        part = dot_t0(term_ref[:, pair(k)], cot_ref[:, pair(k)])
        acc = part if acc is None else acc + part
    return acc[:c, :c] + acc[c:, c:]


def early_part(hidden_ref, hop_ref, x_ref, cot_ref, mix_ref, gm_ref, map0, map1, wide_ref):
    c = mix_ref.shape[1]
    block_map(mix_ref, 0, map0)
    block_map(mix_ref, 1, map1)
    for k in range(cot_ref.shape[1] // 128):
        acc = x_ref[:, pair(k + 1)].astype(F32)
        acc = acc + dot(hidden_ref[:, pair(k)], map0[...])
        wide_ref[:, pair(k)] = acc + dot(hop_ref[:, pair(k)], map1[...])
    gm_ref[0] = mix_grad(hidden_ref, cot_ref, c)
    gm_ref[1] = mix_grad(hop_ref, cot_ref, c)


def main_body(parts, reps, scale,
              x_ref, cot_ref, conv1_ref, conv2_ref, mix_ref, dense_ref, picks_ref, base_ref,
              pieces_ref,
              out_ref, grad_ref, sum_ref,
              first_ref, hidden_ref, hop_ref, second_ref, up_ref, mid_ref, band_ref,
              map0, map1, map2, g1_ref, g2_ref, gm_ref,
              wide_ref, send1, send2, send3, recv0, recv1, recv2, recv3,
              pack_ref, got_ref, part_ref, reps_ref, sums_ref,
              ssem, rsem, asem, arsem, bsem, brsem):
    me = lax.axis_index("dom")
    mine = lax.axis_index("rep")
    nodes = x_ref.shape[0]
    c = mix_ref.shape[1]
    pairs = cot_ref.shape[1] // 128
    feats = cot_ref.shape[1]

    barrier = pltpu.get_barrier_semaphore()
    for o in range(1, parts):
        pl.semaphore_signal(barrier, inc=1, device_id={"dom": lax.rem(me + o, parts)},
                            device_id_type=pl.DeviceIdType.MESH)
    for o in range(1, reps):
        pl.semaphore_signal(barrier, inc=1, device_id={"rep": lax.rem(mine + o, reps)},
                            device_id_type=pl.DeviceIdType.MESH)
    pl.semaphore_wait(barrier, parts - 1 + reps - 1)

    def copies(level, src, dst):
        made = []
        for o in sorted(range(1, parts), key=lambda o: abs(2 * o - parts)):
            peer = lax.rem(me + o, parts)
            made.append(pltpu.make_async_remote_copy(
                src_ref=src.at[peer, pl.ds(c, feats - c)],
                dst_ref=dst.at[me, pl.ds(c, feats - c)],
                send_sem=ssem.at[level, o],
                recv_sem=rsem.at[level, o],
                device_id={"dom": peer},
                device_id_type=pl.DeviceIdType.MESH,
            ))
        for m in made:
            m.start()
        return made

    def arrive(made):
        for m in made:
            m.wait_recv()

    round0 = copies(0, pieces_ref, recv0)
    for buf in (recv0, recv1, recv2, recv3):
        buf[:, 0:c, :] = jnp.zeros((parts, c, BLK), BF16)
        buf[me] = jnp.zeros((feats, BLK), BF16)

    forward_part(x_ref, conv1_ref, conv2_ref, first_ref, hidden_ref, band_ref)
    pack_rows(hidden_ref[...], picks_ref, 0, parts, send1)
    round1 = copies(1, send1, recv1)

    arrive(round0)
    g = from_blocks(base_ref[...], picks_ref, 0, parts, recv0).astype(BF16)
    pack_rows(g, dense_ref, nodes, parts, send2)
    round2 = copies(2, send2, recv2)
    up_ref[...] = dot_t0(dense_ref[:, :nodes], g)
    block_map(mix_ref, 0, map0)
    for k in range(pairs):
        up_ref[:, pair(k)] += dot_t1(cot_ref[:, pair(k)], map0[...])

    own = dot(dense_ref[:, :nodes], hidden_ref[...])
    arrive(round1)
    hop_ref[...] = from_blocks(own, dense_ref, nodes, parts, recv1).astype(BF16)
    pack_rows(hop_ref[...], picks_ref, 0, parts, send3)
    round3 = copies(3, send3, recv3)

    arrive(round2)
    up_ref[...] = from_blocks(up_ref[...], picks_ref, 0, parts, recv2)
    backward_part(x_ref, first_ref, cot_ref, conv1_ref, conv2_ref, grad_ref, g1_ref, g2_ref,
                  band_ref, up_ref, mid_ref)

    early_part(hidden_ref, hop_ref, x_ref, cot_ref, mix_ref, gm_ref, map0, map1, wide_ref)
    block_map(mix_ref, 2, map2)
    own = dot(dense_ref[:, :nodes], hop_ref[...])
    arrive(round3)
    second_ref[...] = from_blocks(own, dense_ref, nodes, parts, recv3).astype(BF16)
    gm_ref[2] = mix_grad(second_ref, cot_ref, c)

    per = pack_ref.shape[1]
    flat = pack_ref
    flat[...] = jnp.zeros(flat.shape, F32)

    def put(first_row, value):
        rows = value.shape[0]
        done = 0
        while done < rows:
            slot, at = divmod(first_row + done, per)
            step = min(per - at, rows - done)
            flat[slot, at : at + step, :] = value[done : done + step]
            done += step

    put(0, g1_ref[0])
    put(c, g1_ref[1])
    put(2 * c, g2_ref[0])
    put(3 * c, g2_ref[1])
    put(4 * c, jnp.concatenate([gm_ref[0], gm_ref[1]], axis=1))
    put(5 * c, jnp.concatenate([gm_ref[2], jnp.zeros((c, c), F32)], axis=1))

    scatter = []
    for o in range(1, parts):
        peer = lax.rem(me + o, parts)
        scatter.append(pltpu.make_async_remote_copy(
            src_ref=pack_ref.at[peer], dst_ref=got_ref.at[me],
            send_sem=asem.at[0, o], recv_sem=arsem.at[0, o],
            device_id={"dom": peer}, device_id_type=pl.DeviceIdType.MESH))
    for m in scatter:
        m.start()
    for k in range(pairs):
        wide_ref[:, pair(k)] += dot(second_ref[:, pair(k)], map2[...])
    out_ref[...] = wide_ref[...].T[c:].astype(BF16)
    got_ref[me] = pack_ref[me]
    arrive(scatter)
    total = got_ref[0]
    for q in range(1, parts):
        total = total + got_ref[q]
    part_ref[...] = total
    around = []
    for o in range(1, reps):
        peer = lax.rem(mine + o, reps)
        around.append(pltpu.make_async_remote_copy(
            src_ref=part_ref, dst_ref=reps_ref.at[mine],
            send_sem=bsem.at[o], recv_sem=brsem.at[o],
            device_id={"rep": peer}, device_id_type=pl.DeviceIdType.MESH))
    for m in around:
        m.start()
    reps_ref[mine] = total
    arrive(around)
    total = reps_ref[0]
    for q in range(1, reps):
        total = total + reps_ref[q]
    for m in around:
        m.wait_send()
    part_ref[...] = total * (1.0 / scale)
    final = []
    for o in range(1, parts):
        peer = lax.rem(me + o, parts)
        final.append(pltpu.make_async_remote_copy(
            src_ref=part_ref, dst_ref=sums_ref.at[me],
            send_sem=asem.at[1, o], recv_sem=arsem.at[1, o],
            device_id={"dom": peer}, device_id_type=pl.DeviceIdType.MESH))
    for m in final:
        m.start()
    sums_ref[me] = part_ref[...]
    arrive(final)

    sum_ref[...] = sums_ref[...]
    for m in round0 + round1 + round2 + round3 + scatter + final:
        m.wait_send()


def shards(inputs, cotangent, conv_one, conv_two, mix_weight, send_rows, counts, tile_cols,
           tile_vals):
    windows, nodes, flat = inputs.shape
    channels = mix_weight.shape[1]
    parts = lax.axis_size("dom")
    reps = lax.axis_size("rep")
    kept = flat // channels - 3
    wide = flat - 2 * channels
    halo = parts * BLK
    blocks = (parts, wide, BLK)
    prepared = [((nodes, nodes + halo), BF16), ((nodes, halo), BF16), ((nodes, wide), BF16),
                ((nodes, wide), F32), (blocks, BF16)]
    dense, picks, cot_wide, base, pieces = pl.pallas_call(
        prepare_body,
        out_shape=[jax.ShapeDtypeStruct(s, d) for s, d in prepared],
        in_specs=[VM, VM, VM, SM, SM, VM],
        out_specs=[VM] * 5,
        scratch_shapes=[pltpu.VMEM((parts + nodes // BLK, BLK, BLK), F32),
                        pltpu.VMEM((128, 128), BF16), pltpu.VMEM((nodes, wide), BF16)],
        compiler_params=LIMIT,
        name="prepare",
    )(cotangent[0].T, mix_weight, send_rows[0], counts, tile_cols, tile_vals)
    scaling = math.sqrt(float(windows * reps * nodes * parts * kept))
    unit = 8 * parts
    per = -(-6 * channels // unit) * unit // parts
    results = [((kept * channels, nodes), BF16), ((nodes, flat), BF16), ((parts, per, BLK), F32)]
    scratch = [((nodes, flat), BF16), ((nodes, wide), BF16), ((nodes, wide), BF16),
               ((nodes, wide), BF16), ((nodes, wide), F32), ((nodes, flat), BF16),
               ((256, 256), BF16), ((128, 128), BF16), ((128, 128), BF16), ((128, 128), BF16),
               (conv_one.shape, F32), (conv_two.shape, F32), (mix_weight.shape, F32)]
    scratch += [((nodes, wide), F32)] + [(blocks, BF16)] * 7
    scratch += [((parts, per, BLK), F32), ((parts, per, BLK), F32), ((per, BLK), F32),
                ((reps, per, BLK), F32), ((parts, per, BLK), F32)]
    dma = pltpu.SemaphoreType.DMA
    output, grad_input, packed = pl.pallas_call(
        functools.partial(main_body, parts, reps, scaling),
        out_shape=[jax.ShapeDtypeStruct(s, d) for s, d in results],
        in_specs=[VM] * 9,
        out_specs=[VM] * 3,
        scratch_shapes=[pltpu.VMEM(s, d) for s, d in scratch]
        + [dma((4, parts)), dma((4, parts)), dma((2, parts)), dma((2, parts)), dma((reps,)),
           dma((reps,))],
        compiler_params=pltpu.CompilerParams(
            vmem_limit_bytes=60 * 1024 * 1024, collective_id=0, has_side_effects=True),
        name="layer",
    )(inputs[0], cot_wide, conv_one, conv_two, mix_weight, dense, picks, base, pieces)
    c = channels
    rows = packed.reshape(parts * per, BLK)
    gm = jnp.stack([rows[4 * c : 5 * c, :c], rows[4 * c : 5 * c, c:], rows[5 * c : 6 * c, :c]])
    return (
        output.T[None],
        grad_input[None],
        rows[: 2 * c].reshape(conv_one.shape),
        rows[2 * c : 4 * c].reshape(conv_two.shape),
        gm,
    )


def place_tiles(r, me, parts, cols_ref, vals_ref, dense_ref):
    rtiles, slots = vals_ref.shape[0], vals_ref.shape[1]
    for c in range(dense_ref.shape[1] // BLK):
        named = r if c == 0 else rtiles + lax.rem(me - c + parts, parts)
        total = None
        for row in range(rtiles) if c == 0 else (r,):
            for j in range(slots):
                keep = jnp.where(cols_ref[row, j] == named, 1.0, 0.0)
                part = vals_ref[row, j].astype(F32) * keep
                total = part if total is None else total + part
        dense_ref[chunk(r * BLK, BLK), c * BLK : (c + 1) * BLK] = total.astype(BF16)


def own_places(cols_ref):
    code = 0
    for j in range(cols_ref.shape[1]):
        code = code + jnp.where(cols_ref[1, j] == 0, 1, 0) + jnp.where(cols_ref[1, j] == 1, 2, 0)
    return code


def chunk(first, size):
    return pl.ds(pl.multiple_of(first, size), size)


def steps_body(parts, reps, scale,
               x_ref, cot_ref, conv1_ref, conv2_ref, mix_ref, send_ref, counts_ref, cols_ref, vals_ref,
               out_ref, grad_ref, one_out, two_out, mix_out,
               dense_ref, wanted_ref, xt_ref, first_ref, hid_ref, d1_ref, d2_ref, mid_ref, low_ref,
               band1, band1t, band2, band2t, maps, mapst,
               adj_ref, own_adj, adj_t, lists_ref, picks_ref, picks_t,
               cf_ref, hf_ref, f1_ref, c1_ref, c2_ref, own_ref, part_t, ext_ref,
               gh_ref, mx_ref, ghs_ref, mxs_ref,
               g1_ref, g2_ref, pack0, got0, half0, all0, full0, sums0,
               pack1, got1, half1, all1, full1, sums1,
               lsend, lrecv, fsend, frecv, esend, erecv, tsend, trecv,
               asem, arsem, bsem, brsem):
    me = lax.axis_index("dom")
    mine = lax.axis_index("rep")
    nodes = x_ref.shape[0]
    c = mix_ref.shape[1]
    pairs = x_ref.shape[1] // 128
    mesh_ids = pl.DeviceIdType.MESH
    holder = lax.rem(parts // 2 - reps // 2 + mine + parts, parts)
    extra = parts * c
    zs = parts // 2
    z, xx = me // 2, lax.rem(me, 2)
    yy, core = mine // 2, lax.rem(mine, 2)
    chips = parts * reps // 2
    chip = me * 2 + yy
    crep = yy * 2 + 1 - core

    barrier = pltpu.get_barrier_semaphore()
    for o in range(1, chips):
        peer = lax.rem(chip + o, chips)
        pl.semaphore_signal(barrier, inc=1, device_id={"dom": peer // 2, "rep": lax.rem(peer, 2) * 2 + core},
                            device_id_type=mesh_ids)
    pl.semaphore_signal(barrier, inc=1, device_id={"rep": yy * 2 + 1 - core}, device_id_type=mesh_ids)
    place_tiles(core, me, parts, cols_ref, vals_ref, dense_ref)
    pl.semaphore_wait(barrier, chips)

    def remote(src, dst, ssem, rsem, **where):
        return pltpu.make_async_remote_copy(
            src_ref=src, dst_ref=dst, send_sem=ssem, recv_sem=rsem,
            device_id=where, device_id_type=mesh_ids)

    order = sorted(range(1, parts), key=lambda o: abs(2 * o - parts))

    own_rows = 3 * (nodes // 16)
    both_rows = nodes // 2 - 2 * own_rows

    def span(sub, cc, y):
        third = own_rows // 3
        first = (own_rows + both_rows) * y
        at, size = ((first, 2 * third), (first + 2 * third, third), (own_rows, both_rows))[sub]
        return pl.ds(pl.multiple_of(cc * (nodes // 2) + at, 16), size)

    def piece(p, sub, cc, y):
        return adj_ref.at[p, span(sub, cc, y)]

    def source_z(t, way):
        return z - t if way == 0 else z + t

    def valid(t, way):
        if t == 0:
            return z >= 0
        return z >= t if way == 0 else z + t < zs

    def slot(t, way, sub):
        return 3 * (0 if t == 0 else 2 * t - 1 + way) + sub

    def base(t, way):
        return source_z(t, way) * 2 + xx

    def cross(t, way):
        return source_z(t, way) * 2 + 1 - xx

    def first_source(t, way, sub):
        return dense_ref.at[span(sub, core, yy)] if t == 0 else piece(base(t, way), sub, core, yy)

    def along(t, way, sub, out_way):
        to = (z + 1 if out_way == 0 else z - 1) * 2 + xx
        return remote(first_source(t, way, sub), piece(base(t, way), sub, core, yy),
                      tsend.at[out_way, slot(t, way, sub)], trecv.at[0, slot(t + 1, out_way, sub)], dom=to)

    def across(t, way, sub):
        return remote(first_source(t, way, sub), piece(base(t, way), sub, core, yy),
                      tsend.at[2, slot(t, way, sub)], trecv.at[2, slot(t, way, sub)], dom=z * 2 + 1 - xx)

    def hand(kind, part, t, way, sub, y):
        ref = piece(part(t, way), sub, core, y)
        to = (1 - yy) * 2 + core if kind in (3, 5) else crep
        return remote(ref, ref, tsend.at[kind, slot(t, way, sub)], trecv.at[kind, slot(t, way, sub)], rep=to)

    def arrived(kind, ref, t, way, sub):
        remote(ref, ref, tsend.at[kind, slot(t, way, sub)], trecv.at[kind, slot(t, way, sub)],
               rep=crep).wait_recv()

    def ways(t):
        return (0,) if t == 0 else (0, 1)

    def lane_sends(t, way, sub):
        made = []
        if t + 1 < zs:
            for w in (0, 1) if t == 0 else (way,):
                made.append((z + 1 < zs if w == 0 else z >= 1, along(t, way, sub, w)))
        made.append((None, across(t, way, sub)))
        return made

    def side_sends(t, way, sub, part, kind):
        if t == 0 and part is base:
            return []
        made = [(None, hand(kind, part, t, way, sub, yy))] if sub < 2 else []
        return made + [(None, hand(kind + 1, part, t, way, sub, yy))]

    def core_sends(t, way, sub, part, kind):
        if t == 0 and part is base or sub == 2:
            return []
        return [(None, hand(kind, part, t, way, sub, 1 - yy))]

    def go(sends, wait=False):
        for cond, copy in sends:
            act = copy.wait_send if wait else copy.start
            if cond is None:
                act()
            else:
                pl.when(cond)(act)

    def on_base(t, way, sub):
        @pl.when(valid(t, way))
        def _():
            arrived(0, piece(base(t, way), sub, core, yy), t, way, sub)
            go(lane_sends(t, way, sub) + side_sends(t, way, sub, base, 3))

    def on_cross(t, way, sub):
        @pl.when(valid(t, way))
        def _():
            arrived(2, piece(cross(t, way), sub, core, yy), t, way, sub)
            go(side_sends(t, way, sub, cross, 5))

    def on_plane(t, way, sub, part, kind):
        @pl.when(valid(t, way))
        def _():
            arrived(kind, piece(part(t, way), sub, core, 1 - yy), t, way, sub)
            go(core_sends(t, way, sub, part, 7 if kind == 3 else 8))

    def on_tiles(t, way, part, kind, use):
        @pl.when(valid(t, way))
        def _():
            if t or part is cross:
                for sub in range(3):
                    arrived(kind + 1, piece(part(t, way), sub, 1 - core, yy), t, way, sub)
                for sub in range(2):
                    arrived(7 if kind == 3 else 8, piece(part(t, way), sub, 1 - core, 1 - yy), t, way, sub)
            use(part(t, way))

    relay = []

    def step_relay(count=1):
        for _ in range(count):
            if relay:
                relay.pop()()

    def scatter_field(level, src, first, dst):
        made = []
        for o in order:
            peer = lax.rem(me + o, parts)
            made.append(remote(src.at[chunk(first + peer * c, c)], dst.at[me, pl.ds(0, c)],
                               fsend.at[level, o], frecv.at[level, o], dom=peer))
        for m in made:
            m.start()
        off = lax.rem(holder - me + parts, parts)
        last = remote(src.at[pl.ds(first + extra, c)], dst.at[me, pl.ds(c, c)],
                      esend.at[level, 0], erecv.at[level, off], dom=holder)
        pl.when(me != holder)(last.start)
        dst[me, 0:c, :] = src[chunk(first + me * c, c), :]

        @pl.when(me == holder)
        def _():
            dst[me, c : 2 * c, :] = src[first + extra : first + extra + c, :]

        @pl.when(me != holder)
        def _():
            dst[:, c : 2 * c, :] = jnp.zeros((parts, c, nodes), BF16)
        return made, last

    def field_arrives(level, made, src, dst):
        for m in made:
            m.wait_recv()

        @pl.when(me == holder)
        def _():
            for o in range(1, parts):
                q = lax.rem(me - o + parts, parts)
                remote(dst.at[q, pl.ds(c, c)], dst.at[q, pl.ds(c, c)], esend.at[level, 0],
                       erecv.at[level, o], dom=q).wait_recv()

    def home_copies(level, o, src, first, dst):
        q = lax.rem(me + o, parts)
        one = remote(src.at[q, pl.ds(0, c)], dst.at[chunk(first + me * c, c)],
                     fsend.at[level, o], frecv.at[level, o], dom=q)
        two = remote(src.at[q, pl.ds(c, c)], dst.at[pl.ds(first + extra, c)],
                     esend.at[level, o], erecv.at[level, 0], dom=q)
        return one, two

    def go_home(level, o, src, first, dst):
        if o:
            one, two = home_copies(level, o, src, first, dst)
            one.start()
            pl.when(me == holder)(two.start)
            return
        dst[chunk(first + me * c, c), :] = src[me, 0:c, :]

        @pl.when(me == holder)
        def _():
            dst[first + extra : first + extra + c, :] = src[me, c : 2 * c, :]

    def home_arrives(level, src, first, dst):
        for o in range(1, parts):
            home_copies(level, o, src, first, dst)[0].wait_recv()
        pl.when(me != holder)(home_copies(level, 1, src, first, dst)[1].wait_recv)

    def home_sent(level, src, first, dst):
        for o in range(1, parts):
            one, two = home_copies(level, o, src, first, dst)
            one.wait_send()
            pl.when(me == holder)(two.wait_send)

    for sub in range(3):
        go(lane_sends(0, 0, sub))
    lane = lax.broadcasted_iota(jnp.int32, (1, BLK), 1)
    for o in range(1, parts):
        t = lax.rem(me + o, parts)
        wanted_ref[o : o + 1, :] = jnp.where(
            lane < counts_ref[0, t], send_ref[pl.ds(t, 1), :], -1)
    wanted_ref[0:1, :] = jnp.zeros((1, BLK), jnp.int32) + own_places(cols_ref)
    lists = []
    for o in order:
        peer = lax.rem(me + o, parts)
        lists.append(remote(wanted_ref, lists_ref.at[me], lsend.at[o], lrecv.at[o], dom=peer))
    for m in lists:
        m.start()
    lists_ref[me] = wanted_ref[...]
    place_tiles(1 - core, me, parts, cols_ref, vals_ref, dense_ref)
    adj_ref[me] = dense_ref[...]

    def back_piece(g_ref, p):
        own_ref[p] = dot(g_ref[p], own_adj[p])
        t = dot(g_ref[p], adj_ref[p, :, BLK:])
        for o in range(1, parts):
            at = (o - 1) * BLK
            owner = lax.rem(p - o + parts, parts)
            part_t[owner, :, at : at + BLK] = t[:, at : at + BLK].astype(BF16)

    def use(p):
        code = lists_ref[p, 0:1, :]
        for col in range(2):
            tile = adj_ref[p, col * BLK : (col + 1) * BLK, 0:BLK]
            second = jnp.where(jnp.bitwise_and(code, col + 1) > 0, 1.0, 0.0)
            for row, keep in enumerate((1.0 - second, second)):
                own_adj[p, row * BLK : (row + 1) * BLK, col * BLK : (col + 1) * BLK] = (
                    tile.astype(F32) * keep).astype(BF16)
        back_piece(cf_ref, p)
        adj_t[p, 0:nodes, :] = own_adj[p].T
        adj_t[p, nodes:, :] = adj_ref[p, :, BLK:].T

    hid_round, cot_round = [], []

    def first_piece():
        field_arrives(0, cot_round[0], cot_ref, cf_ref)
        use(me)

    def send_cotangent():
        cot_round.extend(scatter_field(0, cot_ref, 0, cf_ref))

    def send_hidden():
        hid_round.extend(scatter_field(1, hid_ref, c, hf_ref))

    def add(handler, t, *rest):
        for w in ways(t):
            relay.append(functools.partial(handler, t, w, *rest))

    for t in range(1, zs + 2):
        if t < zs:
            for sub in range(3):
                add(on_base, t, sub)
        if t <= zs:
            for sub in range(3):
                add(on_cross, t - 1, sub)
        if t == 2:
            relay.append(send_cotangent)
        for sub in range(2):
            if 2 <= t <= zs:
                add(on_plane, t - 1, sub, base, 3)
            if t >= 2:
                add(on_plane, t - 2, sub, cross, 5)
        if t == zs + 1:
            relay.append(send_hidden)
        if t >= zs:
            if t == zs:
                relay.append(first_piece)
            add(on_tiles, t - zs, cross, 5, use)
            add(on_tiles, t - zs + 1, base, 3, use)
    for u in range(2, zs):
        add(on_tiles, u, cross, 5, use)
        if u + 1 < zs:
            add(on_tiles, u + 1, base, 3, use)
    relay.reverse()

    for k in range(pairs):
        xt_ref[pair(k), :] = x_ref[:, pair(k)].T
    for conv, dil, nat, tra in ((conv1_ref, 1, band1, band1t), (conv2_ref, 2, band2, band2t)):
        band_map(conv, dil, nat)
        tra[...] = nat[...].T

    def earlier_t(ref, k):
        if k == 0:
            v = ref[0:128, :]
            return jnp.concatenate([jnp.zeros_like(v), v], axis=0)
        return ref[window2(k - 1), :]

    def gated(pre, d_ref, k):
        filt = jnp.tanh(pre[:128])
        gates = 0.5 * jnp.tanh(0.5 * pre[128:]) + 0.5
        d_ref[k, 0:128, :] = gates * (1.0 - filt * filt)
        d_ref[k, 128:256, :] = filt * gates * (1.0 - gates)
        return (filt * gates).astype(BF16)

    for k in range(pairs):
        first_ref[pair(k), :] = gated(dot(band1t[...], earlier_t(xt_ref, k)), d1_ref, k)
        if k % 2:
            step_relay()
    for k in range(1, pairs):
        hid_ref[pair(k - 1), :] = gated(dot(band2t[...], earlier_t(first_ref, k)), d2_ref, k)
        step_relay()

    for i in range(3):
        block_map(mix_ref, i, maps.at[i])
        mapst[i] = maps[i].T
    gh_ref[0:c, :] = jnp.zeros((c, nodes), BF16)

    for m in lists:
        m.wait_recv()
    node = lax.broadcasted_iota(jnp.int32, (nodes, BLK), 0)
    for q in range(parts):
        for o in range(1, parts):
            hit = node == lists_ref[q, o : o + 1, :]
            picks_ref[q, :, (o - 1) * BLK : o * BLK] = jnp.where(hit, 1.0, 0.0).astype(BF16)
        picks_t[q] = picks_ref[q].T
        step_relay(2)

    step_relay(len(relay))

    def back_owner(q):
        return (own_ref[q] + dot(part_t[q], picks_t[q])).astype(BF16)

    for q in range(parts):
        c1_ref[q] = back_owner(q)
    for p in range(parts):
        back_piece(c1_ref, p)
    for o in order + [0]:
        q = lax.rem(me + o, parts)
        c2 = back_owner(q)
        c2_ref[q] = c2
        grads = dot(maps[0], cf_ref[q]) + dot(maps[1], c1_ref[q]) + dot(maps[2], c2)
        ghs_ref[q] = grads.astype(BF16)
        go_home(2, o, ghs_ref, c, gh_ref)

    field_arrives(1, hid_round[0], hid_ref, hf_ref)
    mix = []
    for moved in (cf_ref, c1_ref, c2_ref):
        total = dot_t1(hf_ref[0], moved[0])
        for q in range(1, parts):
            total = total + dot_t1(hf_ref[q], moved[q])
        mix.append(total[:c, :c] + total[c:, c:])

    def reducer(g, pack, got, half, got_all, full, sums):
        def over_core(stage, src, dst):
            return [remote(src, dst, bsem.at[2 * g + stage], brsem.at[2 * g + stage], rep=crep)]

        def over_chips(stage, src_of, dst):
            made = []
            for o in range(1, chips):
                peer = lax.rem(chip + o, chips)
                made.append(remote(src_of(peer), dst, asem.at[2 * g + stage, o], arsem.at[2 * g + stage, o],
                                   dom=peer // 2, rep=lax.rem(peer, 2) * 2 + core))
            return made

        steps = (lambda: over_core(0, pack.at[1 - core], got),
                 lambda: over_chips(0, lambda peer: half.at[peer], got_all.at[chip]),
                 lambda: over_chips(1, lambda peer: full, sums.at[core, chip]),
                 lambda: over_core(1, sums.at[core], sums.at[core]))

        def start(i):
            for m in steps[i]():
                m.start()

        def arrive(i):
            for m in steps[i]():
                m.wait_recv()

        def first():
            start(0)

        def second():
            arrive(0)
            total = pack[core] + got[...]
            share = half.shape[1]
            for q in range(chips):
                half[q] = total[q * share : (q + 1) * share]
            start(1)
            got_all[chip] = half[chip]

        def third():
            arrive(1)
            total = got_all[0]
            for q in range(1, chips):
                total = total + got_all[q]
            full[...] = total * (1.0 / scale)
            start(2)
            sums[core, chip] = full[...]

        def fourth():
            arrive(2)
            start(3)

        def last():
            arrive(3)

        def sent():
            for i in range(4):
                for m in steps[i]():
                    m.wait_send()

        return first, second, third, fourth, last, sent

    early = reducer(0, pack0, got0, half0, all0, full0, sums0)
    late = reducer(1, pack1, got1, half1, all1, full1, sums1)
    pack0[...] = jnp.zeros(pack0.shape, F32)
    for i in range(3):
        pack0[i // 2, (i % 2) * c : (i % 2 + 1) * c, 0:c] = mix[i]
    early[0]()

    def extend(f_ref):
        for q in range(parts):
            ext_ref[q, :, 0:nodes] = f_ref[q]
            halo = dot(f_ref[q], picks_ref[q]).astype(BF16)
            for o in range(1, parts):
                at = nodes + (o - 1) * BLK
                ext_ref[(q + o) % parts, :, at : at + BLK] = halo[:, (o - 1) * BLK : o * BLK]

    extend(hf_ref)
    for p in range(parts):
        f1_ref[p] = dot(ext_ref[p], adj_t[p]).astype(BF16)
    extend(f1_ref)
    for o in order + [0]:
        q = lax.rem(me + o, parts)
        second = dot(ext_ref[q], adj_t[q]).astype(BF16)
        mixed = dot(mapst[0], hf_ref[q]) + dot(mapst[1], f1_ref[q]) + dot(mapst[2], second)
        mxs_ref[q] = mixed.astype(BF16)
        go_home(3, o, mxs_ref, 0, mx_ref)
    early[1]()

    home_arrives(2, ghs_ref, c, gh_ref)

    def conv_back(sig_ref, d_ref, up_of, band, low_of, first_pair, dilation, out):
        total, carry = None, None
        b = band[...]
        for k in range(first_pair, pairs):
            up = up_of(k)
            both = earlier_t(sig_ref, k)
            d = jnp.concatenate([up * d_ref[k, 0:128, :], up * d_ref[k, 128:256, :]], axis=0)
            d = d.astype(BF16)
            part = dot_t1(both, d)
            total = part if total is None else total + part
            back = dot(b, d)
            if k > 0:
                low_of(k - 1, back[:128] if carry is None else carry + back[:128])
            carry = back[128:]
        low_of(pairs - 1, carry)
        band_grad(total, dilation, out)

    def set_mid(k, low):
        mid_ref[pair(k), :] = low.astype(BF16)

    def set_grad(k, low):
        if k == 1:
            low = low + jnp.concatenate([jnp.zeros((c, nodes), F32), cot_ref[0:c, :].astype(F32)], axis=0)
        elif k > 1:
            low = low + cot_ref[(2 * k - 3) * c : (2 * k - 1) * c, :].astype(F32)
        low_ref[pair(k), :] = low.astype(BF16)

    conv_back(first_ref, d2_ref, lambda k: gh_ref[pair(k - 1), :].astype(F32), band2, set_mid, 1, 2, g2_ref)
    conv_back(xt_ref, d1_ref, lambda k: mid_ref[pair(k), :].astype(F32), band1, set_grad, 0, 1, g1_ref)

    for tap in range(2):
        pack1[0, tap * c : (tap + 1) * c, :] = g1_ref[tap]
        pack1[1, tap * c : (tap + 1) * c, :] = g2_ref[tap]
    late[0]()
    late[1]()
    for k in range(pairs):
        grad_ref[:, pair(k)] = low_ref[pair(k), :].T
    early[2]()
    home_arrives(3, mxs_ref, 0, mx_ref)
    kept = out_ref.shape[0]
    out_ref[...] = (mx_ref[...].astype(F32) + xt_ref[pairs * 128 - kept :, :].astype(F32)).astype(BF16)
    late[2]()
    early[3]()

    for m in cot_round[0] + hid_round[0] + lists:
        m.wait_send()
    pl.when(me != holder)(cot_round[1].wait_send)
    pl.when(me != holder)(hid_round[1].wait_send)
    home_sent(2, ghs_ref, c, gh_ref)
    home_sent(3, mxs_ref, 0, mx_ref)
    for t in range(zs):
        for w in ways(t):
            @pl.when(valid(t, w))
            def _():
                for sub in range(3):
                    go(lane_sends(t, w, sub) + side_sends(t, w, sub, base, 3)
                       + side_sends(t, w, sub, cross, 5) + core_sends(t, w, sub, base, 7)
                       + core_sends(t, w, sub, cross, 8), wait=True)
    late[3]()
    early[4]()
    share = sums0.shape[2]
    for q in range(chips):
        tap, at = divmod(q * share, c)
        mix_out[tap, at : at + share, :] = sums0[0, q, :, 0:c]
        if tap == 0:
            mix_out[2, at : at + share, :] = sums0[1, q, :, 0:c]
    early[5]()
    late[4]()
    for q in range(chips):
        tap, at = divmod(q * share, c)
        one_out[tap, at : at + share, :] = sums1[0, q]
        two_out[tap, at : at + share, :] = sums1[1, q]
    late[5]()


def finish_body(*refs):
    half = len(refs) // 2
    for a, b in zip(refs[:half], refs[half:]):
        b[...] = a[...]


def step_shards(inputs, cotangent, conv_one, conv_two, mix_weight, send_rows, counts, tile_cols,
                tile_vals):
    windows, nodes, flat = inputs.shape
    channels = mix_weight.shape[1]
    parts = lax.axis_size("dom")
    reps = lax.axis_size("rep")
    kept = flat // channels - 3
    c = channels
    pairs = flat // 128
    halo = (parts - 1) * BLK
    ext = nodes + halo
    scaling = math.sqrt(float(windows * reps * nodes * parts * kept))
    results = [((kept * c, nodes), BF16), ((nodes, flat), BF16), (conv_one.shape, F32),
               (conv_two.shape, F32), (mix_weight.shape, F32)]
    field = (parts, 2 * c, nodes)
    wide = flat - 2 * c
    scratch = [((nodes, BLK + halo), BF16), ((parts, BLK), jnp.int32),
               ((flat, nodes), BF16), ((flat, nodes), BF16), ((wide, nodes), BF16),
               ((pairs, 256, nodes), F32), ((pairs, 256, nodes), F32), ((flat, nodes), BF16),
               ((flat, nodes), BF16)]
    scratch += [((256, 256), BF16)] * 4 + [((3, 128, 128), BF16)] * 2
    scratch += [((parts, nodes, BLK + halo), BF16), ((parts, nodes, nodes), BF16),
                ((parts, ext, nodes), BF16), ((parts, parts, BLK), jnp.int32),
                ((parts, nodes, halo), BF16), ((parts, halo, nodes), BF16)]
    scratch += [(field, BF16)] * 5 + [(field, F32), ((parts, 2 * c, halo), BF16),
                                      ((parts, 2 * c, ext), BF16)]
    scratch += [((wide, nodes), BF16), ((kept * c, nodes), BF16), (field, BF16), (field, BF16)]
    scratch += [(conv_one.shape, F32), (conv_two.shape, F32)]
    chips = parts * reps // 2
    share = 2 * c // chips
    for _ in range(2):
        scratch += [((2, 2 * c, BLK), F32), ((2 * c, BLK), F32), ((chips, share, BLK), F32),
                    ((chips, share, BLK), F32), ((share, BLK), F32), ((2, chips, share, BLK), F32)]
    dma = pltpu.SemaphoreType.DMA
    sems = [(parts,), (parts,), (4, parts), (4, parts), (4, parts), (4, parts),
            (9, 3 * parts), (9, 3 * parts), (4, chips), (4, chips), (4,), (4,)]
    made = pl.pallas_call(
        functools.partial(steps_body, parts, reps, scaling),
        out_shape=[jax.ShapeDtypeStruct(s, d) for s, d in results],
        in_specs=[VM] * 6 + [SM, SM, VM],
        out_specs=[VM] * 5,
        scratch_shapes=[pltpu.VMEM(s, d) for s, d in scratch] + [dma(s) for s in sems],
        compiler_params=pltpu.CompilerParams(
            vmem_limit_bytes=60 * 1024 * 1024, collective_id=1, has_side_effects=True),
        name="steps",
    )(inputs[0], cotangent[0].T, conv_one, conv_two, mix_weight, send_rows[0], counts, tile_cols,
      tile_vals)
    output, grad_input, one, two, mix = pl.pallas_call(
        finish_body,
        out_shape=[jax.ShapeDtypeStruct(s, d) for s, d in results],
        in_specs=[VM] * 5,
        out_specs=[VM] * 5,
        compiler_params=LIMIT,
        name="finish",
    )(*made)
    return output.T[None], grad_input[None], one, two, mix


def solution(mesh):
    placed = (
        P("rep", "dom", None),
        P("rep", "dom", None),
        P(),
        P(),
        P(),
        P("dom", None, None),
        P("dom", None),
        P("dom", None),
        P("dom", None, None, None),
    )
    parts, reps = mesh.shape["dom"], mesh.shape["rep"]

    def layer(*args):
        kept = args[0].shape[2] // args[4].shape[1] - 3
        by_step = parts % 2 == 0 and reps == 4 and parts == kept - 1
        return step_shards(*args) if by_step else shards(*args)

    return jax.shard_map(
        layer,
        mesh=mesh,
        in_specs=placed,
        out_specs=(P("rep", "dom", None), P("rep", "dom", None), P(), P(), P()),
        check_vma=False,
    )
```

```python
import functools
import math

import jax
import jax.numpy as jnp
from jax import lax
from jax.experimental import pallas as pl
from jax.experimental.pallas import tpu as pltpu
from jax.sharding import PartitionSpec as P

F32 = jnp.float32
BF16 = jnp.bfloat16
BLK = 128
VM = pl.BlockSpec(memory_space=pltpu.VMEM)
SM = pl.BlockSpec(memory_space=pltpu.SMEM)
LIMIT = pltpu.CompilerParams(vmem_limit_bytes=56 * 1024 * 1024)


def dot(a, b):
    return jnp.dot(a, b, preferred_element_type=F32)


def dot_t0(a, b):
    return lax.dot_general(a, b, (((0,), (0,)), ((), ())), preferred_element_type=F32)


def dot_t1(a, b):
    return lax.dot_general(a, b, (((1,), (1,)), ((), ())), preferred_element_type=F32)


def pair(k):
    return slice(k * 128, (k + 1) * 128)


def window2(k):
    return slice(k * 128, (k + 2) * 128)


def block_map(weight_ref, index, out_ref):
    c = weight_ref.shape[1]
    w = weight_ref[index]
    out_ref[...] = jnp.zeros(out_ref.shape, BF16)
    out_ref[0:c, 0:c] = w
    out_ref[c : 2 * c, c : 2 * c] = w


def band_blocks(dilation):
    if dilation == 1:
        return ((0, 1, 0), (0, 2, 1), (1, 2, 0), (1, 3, 1))
    return ((0, 0, 0), (0, 1, 1), (1, 2, 0), (1, 3, 1))


def band_map(conv_ref, dilation, out_ref):
    c = conv_ref.shape[1]
    out_ref[...] = jnp.zeros(out_ref.shape, BF16)
    for tap, i, o in band_blocks(dilation):
        w = conv_ref[tap]
        rows = slice(i * c, (i + 1) * c)
        out_ref[rows, o * c : (o + 1) * c] = w[:, :c]
        out_ref[rows, (o + 2) * c : (o + 3) * c] = w[:, c:]


def band_grad(total, dilation, out_ref):
    c = out_ref.shape[1]
    for tap in range(2):
        for half in range(2):
            acc = None
            for t, i, o in band_blocks(dilation):
                if t != tap:
                    continue
                col = (o + 2 * half) * c
                part = total[i * c : (i + 1) * c, col : col + c]
                acc = part if acc is None else acc + part
            out_ref[tap, :, half * c : (half + 1) * c] = acc


def activations(pre):
    filt = jnp.tanh(pre[:, :128])
    gates = 0.5 * jnp.tanh(0.5 * pre[:, 128:]) + 0.5
    return filt, gates


def earlier(ref, k):
    if k == 0:
        x = ref[:, 0:128]
        return jnp.concatenate([jnp.zeros_like(x), x], axis=1)
    return ref[:, window2(k - 1)]


def build_tiles(cols_ref, vals_ref, acc_ref, dense_ref):
    rtiles, slots = vals_ref.shape[0], vals_ref.shape[1]
    ctiles = dense_ref.shape[1] // BLK
    for r in range(rtiles):
        acc_ref[...] = jnp.zeros(acc_ref.shape, F32)
        for j in range(slots):
            c = cols_ref[r, j]
            acc_ref[c] = acc_ref[c] + vals_ref[r, j].astype(F32)
        for c in range(ctiles):
            dense_ref[r * BLK : (r + 1) * BLK, c * BLK : (c + 1) * BLK] = acc_ref[c].astype(BF16)


def build_picks(send_ref, counts_ref, picks_ref):
    parts = send_ref.shape[0]
    nodes = picks_ref.shape[0]
    lane = lax.broadcasted_iota(jnp.int32, (1, BLK), 1)
    rows = lax.broadcasted_iota(jnp.int32, (nodes, BLK), 0)
    for q in range(parts):
        wanted = jnp.where(lane < counts_ref[0, q], send_ref[q : q + 1, :], -1)
        hit = rows == wanted
        picks_ref[:, q * BLK : (q + 1) * BLK] = jnp.where(hit, 1.0, 0.0).astype(BF16)


def prepare_body(cot_ref, mix_ref, send_ref, counts_ref, cols_ref, vals_ref,
                 dense_ref, picks_ref, cot_out, base_ref, pieces_ref,
                 acc_ref, map_ref, g_ref):
    nodes = cot_ref.shape[1]
    parts = send_ref.shape[0]
    c = mix_ref.shape[1]
    build_tiles(cols_ref, vals_ref, acc_ref, dense_ref)
    build_picks(send_ref, counts_ref, picks_ref)
    wide = cot_ref[...].astype(F32).T
    wide = jnp.concatenate([jnp.zeros((nodes, c), F32), wide], axis=1).astype(BF16)
    cot_out[...] = wide
    pairs = cot_out.shape[1] // 128
    block_map(mix_ref, 2, map_ref)
    m = map_ref[...]
    for k in range(pairs):
        g_ref[:, pair(k)] = dot_t1(cot_out[:, pair(k)], m).astype(BF16)
    block_map(mix_ref, 1, map_ref)
    m = map_ref[...]
    g = g_ref[...]
    pack_rows(g, dense_ref, nodes, parts, pieces_ref)
    base_ref[...] = dot_t0(dense_ref[:, :nodes], g)
    for k in range(pairs):
        base_ref[:, pair(k)] += dot_t1(cot_out[:, pair(k)], m)


def pack_rows(values, table_ref, start, parts, out_ref):
    flipped = values.astype(F32).T.astype(BF16)
    for q in range(parts):
        table = table_ref[:, start + q * BLK : start + (q + 1) * BLK]
        out_ref[q] = dot(flipped, table).astype(BF16)


def from_blocks(total, table_ref, start, parts, arrived_ref):
    for q in range(parts):
        table = table_ref[:, start + q * BLK : start + (q + 1) * BLK]
        total = total + dot_t1(table, arrived_ref[q])
    return total


def forward_part(x_ref, conv1_ref, conv2_ref, first_ref, hidden_ref, band_ref):
    pairs = x_ref.shape[1] // 128
    band_map(conv1_ref, 1, band_ref)
    b = band_ref[...]
    for k in range(pairs):
        filt, gates = activations(dot(earlier(x_ref, k), b))
        first_ref[:, pair(k)] = (filt * gates).astype(BF16)
    band_map(conv2_ref, 2, band_ref)
    b = band_ref[...]
    for k in range(1, pairs):
        filt, gates = activations(dot(earlier(first_ref, k), b))
        hidden_ref[:, pair(k - 1)] = (filt * gates).astype(BF16)


def gate_grad(pre, up):
    filt, gates = activations(pre)
    d_filt = up * gates * (1.0 - filt * filt)
    d_gate = up * filt * gates * (1.0 - gates)
    return jnp.concatenate([d_filt, d_gate], axis=1).astype(BF16)


def backward_part(x_ref, first_ref, cot_ref, conv1_ref, conv2_ref, grad_ref, g1_ref, g2_ref,
                  band_ref, up_ref, mid_ref):
    pairs = x_ref.shape[1] // 128
    band_map(conv2_ref, 2, band_ref)
    b = band_ref[...]
    total = None
    carry = None
    for k in range(1, pairs):
        both = earlier(first_ref, k)
        d = gate_grad(dot(both, b), up_ref[:, pair(k - 1)])
        part = dot_t0(both, d)
        total = part if total is None else total + part
        back = dot_t1(d, b)
        low = back[:, :128] if carry is None else carry + back[:, :128]
        mid_ref[:, pair(k - 1)] = low.astype(BF16)
        carry = back[:, 128:]
    mid_ref[:, pair(pairs - 1)] = carry.astype(BF16)
    band_grad(total, 2, g2_ref)
    band_map(conv1_ref, 1, band_ref)
    b = band_ref[...]
    total = None
    carry = None
    for k in range(pairs):
        both = earlier(x_ref, k)
        d = gate_grad(dot(both, b), mid_ref[:, pair(k)].astype(F32))
        part = dot_t0(both, d)
        total = part if total is None else total + part
        back = dot_t1(d, b)
        if k > 0:
            low = carry + back[:, :128]
            if k > 1:
                low = low + cot_ref[:, pair(k - 2)].astype(F32)
            grad_ref[:, pair(k - 1)] = low.astype(BF16)
        carry = back[:, 128:]
    last = carry + cot_ref[:, pair(pairs - 2)].astype(F32)
    grad_ref[:, pair(pairs - 1)] = last.astype(BF16)
    band_grad(total, 1, g1_ref)


def mix_grad(term_ref, cot_ref, c):
    acc = None
    for k in range(cot_ref.shape[1] // 128):
        part = dot_t0(term_ref[:, pair(k)], cot_ref[:, pair(k)])
        acc = part if acc is None else acc + part
    return acc[:c, :c] + acc[c:, c:]


def early_part(hidden_ref, hop_ref, x_ref, cot_ref, mix_ref, gm_ref, map0, map1, wide_ref):
    c = mix_ref.shape[1]
    block_map(mix_ref, 0, map0)
    block_map(mix_ref, 1, map1)
    for k in range(cot_ref.shape[1] // 128):
        acc = x_ref[:, pair(k + 1)].astype(F32)
        acc = acc + dot(hidden_ref[:, pair(k)], map0[...])
        wide_ref[:, pair(k)] = acc + dot(hop_ref[:, pair(k)], map1[...])
    gm_ref[0] = mix_grad(hidden_ref, cot_ref, c)
    gm_ref[1] = mix_grad(hop_ref, cot_ref, c)


def main_body(parts, reps, scale,
              x_ref, cot_ref, conv1_ref, conv2_ref, mix_ref, dense_ref, picks_ref, base_ref,
              pieces_ref,
              out_ref, grad_ref, sum_ref,
              first_ref, hidden_ref, hop_ref, second_ref, up_ref, mid_ref, band_ref,
              map0, map1, map2, g1_ref, g2_ref, gm_ref,
              wide_ref, send1, send2, send3, recv0, recv1, recv2, recv3,
              pack_ref, got_ref, part_ref, reps_ref, sums_ref,
              ssem, rsem, asem, arsem, bsem, brsem):
    me = lax.axis_index("dom")
    mine = lax.axis_index("rep")
    nodes = x_ref.shape[0]
    c = mix_ref.shape[1]
    pairs = cot_ref.shape[1] // 128
    feats = cot_ref.shape[1]

    barrier = pltpu.get_barrier_semaphore()
    for o in range(1, parts):
        pl.semaphore_signal(barrier, inc=1, device_id={"dom": lax.rem(me + o, parts)},
                            device_id_type=pl.DeviceIdType.MESH)
    for o in range(1, reps):
        pl.semaphore_signal(barrier, inc=1, device_id={"rep": lax.rem(mine + o, reps)},
                            device_id_type=pl.DeviceIdType.MESH)
    pl.semaphore_wait(barrier, parts - 1 + reps - 1)

    def copies(level, src, dst):
        made = []
        for o in sorted(range(1, parts), key=lambda o: abs(2 * o - parts)):
            peer = lax.rem(me + o, parts)
            made.append(pltpu.make_async_remote_copy(
                src_ref=src.at[peer, pl.ds(c, feats - c)],
                dst_ref=dst.at[me, pl.ds(c, feats - c)],
                send_sem=ssem.at[level, o],
                recv_sem=rsem.at[level, o],
                device_id={"dom": peer},
                device_id_type=pl.DeviceIdType.MESH,
            ))
        for m in made:
            m.start()
        return made

    def arrive(made):
        for m in made:
            m.wait_recv()

    round0 = copies(0, pieces_ref, recv0)
    for buf in (recv0, recv1, recv2, recv3):
        buf[:, 0:c, :] = jnp.zeros((parts, c, BLK), BF16)
        buf[me] = jnp.zeros((feats, BLK), BF16)

    forward_part(x_ref, conv1_ref, conv2_ref, first_ref, hidden_ref, band_ref)
    pack_rows(hidden_ref[...], picks_ref, 0, parts, send1)
    round1 = copies(1, send1, recv1)

    arrive(round0)
    g = from_blocks(base_ref[...], picks_ref, 0, parts, recv0).astype(BF16)
    pack_rows(g, dense_ref, nodes, parts, send2)
    round2 = copies(2, send2, recv2)
    up_ref[...] = dot_t0(dense_ref[:, :nodes], g)
    block_map(mix_ref, 0, map0)
    for k in range(pairs):
        up_ref[:, pair(k)] += dot_t1(cot_ref[:, pair(k)], map0[...])

    own = dot(dense_ref[:, :nodes], hidden_ref[...])
    arrive(round1)
    hop_ref[...] = from_blocks(own, dense_ref, nodes, parts, recv1).astype(BF16)
    pack_rows(hop_ref[...], picks_ref, 0, parts, send3)
    round3 = copies(3, send3, recv3)

    arrive(round2)
    up_ref[...] = from_blocks(up_ref[...], picks_ref, 0, parts, recv2)
    backward_part(x_ref, first_ref, cot_ref, conv1_ref, conv2_ref, grad_ref, g1_ref, g2_ref,
                  band_ref, up_ref, mid_ref)

    early_part(hidden_ref, hop_ref, x_ref, cot_ref, mix_ref, gm_ref, map0, map1, wide_ref)
    block_map(mix_ref, 2, map2)
    own = dot(dense_ref[:, :nodes], hop_ref[...])
    arrive(round3)
    second_ref[...] = from_blocks(own, dense_ref, nodes, parts, recv3).astype(BF16)
    gm_ref[2] = mix_grad(second_ref, cot_ref, c)

    per = pack_ref.shape[1]
    flat = pack_ref
    flat[...] = jnp.zeros(flat.shape, F32)

    def put(first_row, value):
        rows = value.shape[0]
        done = 0
        while done < rows:
            slot, at = divmod(first_row + done, per)
            step = min(per - at, rows - done)
            flat[slot, at : at + step, :] = value[done : done + step]
            done += step

    put(0, g1_ref[0])
    put(c, g1_ref[1])
    put(2 * c, g2_ref[0])
    put(3 * c, g2_ref[1])
    put(4 * c, jnp.concatenate([gm_ref[0], gm_ref[1]], axis=1))
    put(5 * c, jnp.concatenate([gm_ref[2], jnp.zeros((c, c), F32)], axis=1))

    scatter = []
    for o in range(1, parts):
        peer = lax.rem(me + o, parts)
        scatter.append(pltpu.make_async_remote_copy(
            src_ref=pack_ref.at[peer], dst_ref=got_ref.at[me],
            send_sem=asem.at[0, o], recv_sem=arsem.at[0, o],
            device_id={"dom": peer}, device_id_type=pl.DeviceIdType.MESH))
    for m in scatter:
        m.start()
    for k in range(pairs):
        wide_ref[:, pair(k)] += dot(second_ref[:, pair(k)], map2[...])
    out_ref[...] = wide_ref[...].T[c:].astype(BF16)
    got_ref[me] = pack_ref[me]
    arrive(scatter)
    total = got_ref[0]
    for q in range(1, parts):
        total = total + got_ref[q]
    part_ref[...] = total
    around = []
    for o in range(1, reps):
        peer = lax.rem(mine + o, reps)
        around.append(pltpu.make_async_remote_copy(
            src_ref=part_ref, dst_ref=reps_ref.at[mine],
            send_sem=bsem.at[o], recv_sem=brsem.at[o],
            device_id={"rep": peer}, device_id_type=pl.DeviceIdType.MESH))
    for m in around:
        m.start()
    reps_ref[mine] = total
    arrive(around)
    total = reps_ref[0]
    for q in range(1, reps):
        total = total + reps_ref[q]
    for m in around:
        m.wait_send()
    part_ref[...] = total * (1.0 / scale)
    final = []
    for o in range(1, parts):
        peer = lax.rem(me + o, parts)
        final.append(pltpu.make_async_remote_copy(
            src_ref=part_ref, dst_ref=sums_ref.at[me],
            send_sem=asem.at[1, o], recv_sem=arsem.at[1, o],
            device_id={"dom": peer}, device_id_type=pl.DeviceIdType.MESH))
    for m in final:
        m.start()
    sums_ref[me] = part_ref[...]
    arrive(final)

    sum_ref[...] = sums_ref[...]
    for m in round0 + round1 + round2 + round3 + scatter + final:
        m.wait_send()


def shards(inputs, cotangent, conv_one, conv_two, mix_weight, send_rows, counts, tile_cols,
           tile_vals):
    windows, nodes, flat = inputs.shape
    channels = mix_weight.shape[1]
    parts = lax.axis_size("dom")
    reps = lax.axis_size("rep")
    kept = flat // channels - 3
    wide = flat - 2 * channels
    halo = parts * BLK
    blocks = (parts, wide, BLK)
    prepared = [((nodes, nodes + halo), BF16), ((nodes, halo), BF16), ((nodes, wide), BF16),
                ((nodes, wide), F32), (blocks, BF16)]
    dense, picks, cot_wide, base, pieces = pl.pallas_call(
        prepare_body,
        out_shape=[jax.ShapeDtypeStruct(s, d) for s, d in prepared],
        in_specs=[VM, VM, VM, SM, SM, VM],
        out_specs=[VM] * 5,
        scratch_shapes=[pltpu.VMEM((parts + nodes // BLK, BLK, BLK), F32),
                        pltpu.VMEM((128, 128), BF16), pltpu.VMEM((nodes, wide), BF16)],
        compiler_params=LIMIT,
        name="prepare",
    )(cotangent[0].T, mix_weight, send_rows[0], counts, tile_cols, tile_vals)
    scaling = math.sqrt(float(windows * reps * nodes * parts * kept))
    unit = 8 * parts
    per = -(-6 * channels // unit) * unit // parts
    results = [((kept * channels, nodes), BF16), ((nodes, flat), BF16), ((parts, per, BLK), F32)]
    scratch = [((nodes, flat), BF16), ((nodes, wide), BF16), ((nodes, wide), BF16),
               ((nodes, wide), BF16), ((nodes, wide), F32), ((nodes, flat), BF16),
               ((256, 256), BF16), ((128, 128), BF16), ((128, 128), BF16), ((128, 128), BF16),
               (conv_one.shape, F32), (conv_two.shape, F32), (mix_weight.shape, F32)]
    scratch += [((nodes, wide), F32)] + [(blocks, BF16)] * 7
    scratch += [((parts, per, BLK), F32), ((parts, per, BLK), F32), ((per, BLK), F32),
                ((reps, per, BLK), F32), ((parts, per, BLK), F32)]
    dma = pltpu.SemaphoreType.DMA
    output, grad_input, packed = pl.pallas_call(
        functools.partial(main_body, parts, reps, scaling),
        out_shape=[jax.ShapeDtypeStruct(s, d) for s, d in results],
        in_specs=[VM] * 9,
        out_specs=[VM] * 3,
        scratch_shapes=[pltpu.VMEM(s, d) for s, d in scratch]
        + [dma((4, parts)), dma((4, parts)), dma((2, parts)), dma((2, parts)), dma((reps,)),
           dma((reps,))],
        compiler_params=pltpu.CompilerParams(
            vmem_limit_bytes=60 * 1024 * 1024, collective_id=0, has_side_effects=True),
        name="layer",
    )(inputs[0], cot_wide, conv_one, conv_two, mix_weight, dense, picks, base, pieces)
    c = channels
    rows = packed.reshape(parts * per, BLK)
    gm = jnp.stack([rows[4 * c : 5 * c, :c], rows[4 * c : 5 * c, c:], rows[5 * c : 6 * c, :c]])
    return (
        output.T[None],
        grad_input[None],
        rows[: 2 * c].reshape(conv_one.shape),
        rows[2 * c : 4 * c].reshape(conv_two.shape),
        gm,
    )


def place_tiles(r, me, parts, cols_ref, vals_ref, dense_ref):
    rtiles, slots = vals_ref.shape[0], vals_ref.shape[1]
    for c in range(dense_ref.shape[1] // BLK):
        named = r if c == 0 else rtiles + lax.rem(me - c + parts, parts)
        total = None
        for row in range(rtiles) if c == 0 else (r,):
            for j in range(slots):
                keep = jnp.where(cols_ref[row, j] == named, 1.0, 0.0)
                part = vals_ref[row, j].astype(F32) * keep
                total = part if total is None else total + part
        dense_ref[chunk(r * BLK, BLK), c * BLK : (c + 1) * BLK] = total.astype(BF16)


def own_places(cols_ref):
    code = 0
    for j in range(cols_ref.shape[1]):
        code = code + jnp.where(cols_ref[1, j] == 0, 1, 0) + jnp.where(cols_ref[1, j] == 1, 2, 0)
    return code


def chunk(first, size):
    return pl.ds(pl.multiple_of(first, size), size)


def steps_body(parts, reps, scale,
               x_ref, cot_ref, conv1_ref, conv2_ref, mix_ref, send_ref, counts_ref, cols_ref, vals_ref,
               out_ref, grad_ref, one_out, two_out, mix_out,
               dense_ref, wanted_ref, xt_ref, first_ref, hid_ref, d1_ref, d2_ref, mid_ref, low_ref,
               band1, band1t, band2, band2t, maps, mapst,
               adj_ref, own_adj, adj_t, lists_ref, picks_ref, picks_t,
               cf_ref, hf_ref, f1_ref, c1_ref, c2_ref, own_ref, part_t, ext_ref,
               gh_ref, mx_ref, ghs_ref, mxs_ref,
               g1_ref, g2_ref, pack0, got0, half0, all0, full0, sums0,
               pack1, got1, half1, all1, full1, sums1,
               lsend, lrecv, fsend, frecv, esend, erecv, tsend, trecv,
               asem, arsem, bsem, brsem):
    me = lax.axis_index("dom")
    mine = lax.axis_index("rep")
    nodes = x_ref.shape[0]
    c = mix_ref.shape[1]
    pairs = x_ref.shape[1] // 128
    mesh_ids = pl.DeviceIdType.MESH
    holder = lax.rem(parts // 2 - reps // 2 + mine + parts, parts)
    extra = parts * c
    zs = parts // 2
    z, xx = me // 2, lax.rem(me, 2)
    yy, core = mine // 2, lax.rem(mine, 2)
    chips = parts * reps // 2
    chip = me * 2 + yy
    crep = yy * 2 + 1 - core

    barrier = pltpu.get_barrier_semaphore()
    for o in range(1, chips):
        peer = lax.rem(chip + o, chips)
        pl.semaphore_signal(barrier, inc=1, device_id={"dom": peer // 2, "rep": lax.rem(peer, 2) * 2 + core},
                            device_id_type=mesh_ids)
    pl.semaphore_signal(barrier, inc=1, device_id={"rep": yy * 2 + 1 - core}, device_id_type=mesh_ids)
    place_tiles(core, me, parts, cols_ref, vals_ref, dense_ref)
    pl.semaphore_wait(barrier, chips)

    def remote(src, dst, ssem, rsem, **where):
        return pltpu.make_async_remote_copy(
            src_ref=src, dst_ref=dst, send_sem=ssem, recv_sem=rsem,
            device_id=where, device_id_type=mesh_ids)

    order = sorted(range(1, parts), key=lambda o: abs(2 * o - parts))

    own_rows = 3 * (nodes // 16)
    both_rows = nodes // 2 - 2 * own_rows

    def span(sub, cc, y):
        third = own_rows // 3
        first = (own_rows + both_rows) * y
        at, size = ((first, 2 * third), (first + 2 * third, third), (own_rows, both_rows))[sub]
        return pl.ds(pl.multiple_of(cc * (nodes // 2) + at, 16), size)

    def piece(p, sub, cc, y):
        return adj_ref.at[p, span(sub, cc, y)]

    def source_z(t, way):
        return z - t if way == 0 else z + t

    def valid(t, way):
        if t == 0:
            return z >= 0
        return z >= t if way == 0 else z + t < zs

    def slot(t, way, sub):
        return 3 * (0 if t == 0 else 2 * t - 1 + way) + sub

    def base(t, way):
        return source_z(t, way) * 2 + xx

    def cross(t, way):
        return source_z(t, way) * 2 + 1 - xx

    def first_source(t, way, sub):
        return dense_ref.at[span(sub, core, yy)] if t == 0 else piece(base(t, way), sub, core, yy)

    def along(t, way, sub, out_way):
        to = (z + 1 if out_way == 0 else z - 1) * 2 + xx
        return remote(first_source(t, way, sub), piece(base(t, way), sub, core, yy),
                      tsend.at[out_way, slot(t, way, sub)], trecv.at[0, slot(t + 1, out_way, sub)], dom=to)

    def across(t, way, sub):
        return remote(first_source(t, way, sub), piece(base(t, way), sub, core, yy),
                      tsend.at[2, slot(t, way, sub)], trecv.at[2, slot(t, way, sub)], dom=z * 2 + 1 - xx)

    def hand(kind, part, t, way, sub, y):
        ref = piece(part(t, way), sub, core, y)
        to = (1 - yy) * 2 + core if kind in (3, 5) else crep
        return remote(ref, ref, tsend.at[kind, slot(t, way, sub)], trecv.at[kind, slot(t, way, sub)], rep=to)

    def arrived(kind, ref, t, way, sub):
        remote(ref, ref, tsend.at[kind, slot(t, way, sub)], trecv.at[kind, slot(t, way, sub)],
               rep=crep).wait_recv()

    def ways(t):
        return (0,) if t == 0 else (0, 1)

    def lane_sends(t, way, sub):
        made = []
        if t + 1 < zs:
            for w in (0, 1) if t == 0 else (way,):
                made.append((z + 1 < zs if w == 0 else z >= 1, along(t, way, sub, w)))
        made.append((None, across(t, way, sub)))
        return made

    def side_sends(t, way, sub, part, kind):
        if t == 0 and part is base:
            return []
        made = [(None, hand(kind, part, t, way, sub, yy))] if sub < 2 else []
        return made + [(None, hand(kind + 1, part, t, way, sub, yy))]

    def core_sends(t, way, sub, part, kind):
        if t == 0 and part is base or sub == 2:
            return []
        return [(None, hand(kind, part, t, way, sub, 1 - yy))]

    def go(sends, wait=False):
        for cond, copy in sends:
            act = copy.wait_send if wait else copy.start
            if cond is None:
                act()
            else:
                pl.when(cond)(act)

    def on_base(t, way, sub):
        @pl.when(valid(t, way))
        def _():
            arrived(0, piece(base(t, way), sub, core, yy), t, way, sub)
            go(lane_sends(t, way, sub) + side_sends(t, way, sub, base, 3))

    def on_cross(t, way, sub):
        @pl.when(valid(t, way))
        def _():
            arrived(2, piece(cross(t, way), sub, core, yy), t, way, sub)
            go(side_sends(t, way, sub, cross, 5))

    def on_plane(t, way, sub, part, kind):
        @pl.when(valid(t, way))
        def _():
            arrived(kind, piece(part(t, way), sub, core, 1 - yy), t, way, sub)
            go(core_sends(t, way, sub, part, 7 if kind == 3 else 8))

    def on_tiles(t, way, part, kind, use):
        @pl.when(valid(t, way))
        def _():
            if t or part is cross:
                for sub in range(3):
                    arrived(kind + 1, piece(part(t, way), sub, 1 - core, yy), t, way, sub)
                for sub in range(2):
                    arrived(7 if kind == 3 else 8, piece(part(t, way), sub, 1 - core, 1 - yy), t, way, sub)
            use(part(t, way))

    relay = []

    def step_relay(count=1):
        for _ in range(count):
            if relay:
                relay.pop()()

    def scatter_field(level, src, first, dst):
        made = []
        for o in order:
            peer = lax.rem(me + o, parts)
            made.append(remote(src.at[chunk(first + peer * c, c)], dst.at[me, pl.ds(0, c)],
                               fsend.at[level, o], frecv.at[level, o], dom=peer))
        for m in made:
            m.start()
        off = lax.rem(holder - me + parts, parts)
        last = remote(src.at[pl.ds(first + extra, c)], dst.at[me, pl.ds(c, c)],
                      esend.at[level, 0], erecv.at[level, off], dom=holder)
        pl.when(me != holder)(last.start)
        dst[me, 0:c, :] = src[chunk(first + me * c, c), :]

        @pl.when(me == holder)
        def _():
            dst[me, c : 2 * c, :] = src[first + extra : first + extra + c, :]

        @pl.when(me != holder)
        def _():
            dst[:, c : 2 * c, :] = jnp.zeros((parts, c, nodes), BF16)
        return made, last

    def field_arrives(level, made, src, dst):
        for m in made:
            m.wait_recv()

        @pl.when(me == holder)
        def _():
            for o in range(1, parts):
                q = lax.rem(me - o + parts, parts)
                remote(dst.at[q, pl.ds(c, c)], dst.at[q, pl.ds(c, c)], esend.at[level, 0],
                       erecv.at[level, o], dom=q).wait_recv()

    def home_copies(level, o, src, first, dst):
        q = lax.rem(me + o, parts)
        one = remote(src.at[q, pl.ds(0, c)], dst.at[chunk(first + me * c, c)],
                     fsend.at[level, o], frecv.at[level, o], dom=q)
        two = remote(src.at[q, pl.ds(c, c)], dst.at[pl.ds(first + extra, c)],
                     esend.at[level, o], erecv.at[level, 0], dom=q)
        return one, two

    def go_home(level, o, src, first, dst):
        if o:
            one, two = home_copies(level, o, src, first, dst)
            one.start()
            pl.when(me == holder)(two.start)
            return
        dst[chunk(first + me * c, c), :] = src[me, 0:c, :]

        @pl.when(me == holder)
        def _():
            dst[first + extra : first + extra + c, :] = src[me, c : 2 * c, :]

    def home_arrives(level, src, first, dst):
        for o in range(1, parts):
            home_copies(level, o, src, first, dst)[0].wait_recv()
        pl.when(me != holder)(home_copies(level, 1, src, first, dst)[1].wait_recv)

    def home_sent(level, src, first, dst):
        for o in range(1, parts):
            one, two = home_copies(level, o, src, first, dst)
            one.wait_send()
            pl.when(me == holder)(two.wait_send)

    for sub in range(3):
        go(lane_sends(0, 0, sub))
    lane = lax.broadcasted_iota(jnp.int32, (1, BLK), 1)
    for o in range(1, parts):
        t = lax.rem(me + o, parts)
        wanted_ref[o : o + 1, :] = jnp.where(
            lane < counts_ref[0, t], send_ref[pl.ds(t, 1), :], -1)
    wanted_ref[0:1, :] = jnp.zeros((1, BLK), jnp.int32) + own_places(cols_ref)
    lists = []
    for o in order:
        peer = lax.rem(me + o, parts)
        lists.append(remote(wanted_ref, lists_ref.at[me], lsend.at[o], lrecv.at[o], dom=peer))
    for m in lists:
        m.start()
    lists_ref[me] = wanted_ref[...]
    place_tiles(1 - core, me, parts, cols_ref, vals_ref, dense_ref)
    adj_ref[me] = dense_ref[...]

    def back_piece(g_ref, p):
        own_ref[p] = dot(g_ref[p], own_adj[p])
        t = dot(g_ref[p], adj_ref[p, :, BLK:])
        for o in range(1, parts):
            at = (o - 1) * BLK
            owner = lax.rem(p - o + parts, parts)
            part_t[owner, :, at : at + BLK] = t[:, at : at + BLK].astype(BF16)

    def use(p):
        code = lists_ref[p, 0:1, :]
        for col in range(2):
            tile = adj_ref[p, col * BLK : (col + 1) * BLK, 0:BLK]
            second = jnp.where(jnp.bitwise_and(code, col + 1) > 0, 1.0, 0.0)
            for row, keep in enumerate((1.0 - second, second)):
                own_adj[p, row * BLK : (row + 1) * BLK, col * BLK : (col + 1) * BLK] = (
                    tile.astype(F32) * keep).astype(BF16)
        back_piece(cf_ref, p)
        adj_t[p, 0:nodes, :] = own_adj[p].T
        adj_t[p, nodes:, :] = adj_ref[p, :, BLK:].T

    hid_round, cot_round = [], []

    def first_piece():
        field_arrives(0, cot_round[0], cot_ref, cf_ref)
        use(me)

    def send_cotangent():
        cot_round.extend(scatter_field(0, cot_ref, 0, cf_ref))

    def send_hidden():
        hid_round.extend(scatter_field(1, hid_ref, c, hf_ref))

    def add(handler, t, *rest):
        for w in ways(t):
            relay.append(functools.partial(handler, t, w, *rest))

    for t in range(1, zs + 2):
        if t < zs:
            for sub in range(3):
                add(on_base, t, sub)
        if t == 2:
            relay.append(send_cotangent)
        if t <= zs:
            for sub in range(3):
                add(on_cross, t - 1, sub)
        for sub in range(2):
            if 2 <= t <= zs:
                add(on_plane, t - 1, sub, base, 3)
            if t >= 2:
                add(on_plane, t - 2, sub, cross, 5)
        if t == zs + 1:
            relay.append(send_hidden)
        if t >= zs:
            if t == zs:
                relay.append(first_piece)
            add(on_tiles, t - zs, cross, 5, use)
            add(on_tiles, t - zs + 1, base, 3, use)
    for u in range(2, zs):
        add(on_tiles, u, cross, 5, use)
        if u + 1 < zs:
            add(on_tiles, u + 1, base, 3, use)
    relay.reverse()

    for k in range(pairs):
        xt_ref[pair(k), :] = x_ref[:, pair(k)].T
    for conv, dil, nat, tra in ((conv1_ref, 1, band1, band1t), (conv2_ref, 2, band2, band2t)):
        band_map(conv, dil, nat)
        tra[...] = nat[...].T

    def earlier_t(ref, k):
        if k == 0:
            v = ref[0:128, :]
            return jnp.concatenate([jnp.zeros_like(v), v], axis=0)
        return ref[window2(k - 1), :]

    def gated(pre, d_ref, k):
        filt = jnp.tanh(pre[:128])
        gates = 0.5 * jnp.tanh(0.5 * pre[128:]) + 0.5
        d_ref[k, 0:128, :] = gates * (1.0 - filt * filt)
        d_ref[k, 128:256, :] = filt * gates * (1.0 - gates)
        return (filt * gates).astype(BF16)

    for k in range(pairs):
        first_ref[pair(k), :] = gated(dot(band1t[...], earlier_t(xt_ref, k)), d1_ref, k)
        if k % 2:
            step_relay()
    for k in range(1, pairs):
        hid_ref[pair(k - 1), :] = gated(dot(band2t[...], earlier_t(first_ref, k)), d2_ref, k)
        step_relay()

    for i in range(3):
        block_map(mix_ref, i, maps.at[i])
        mapst[i] = maps[i].T
    gh_ref[0:c, :] = jnp.zeros((c, nodes), BF16)

    for m in lists:
        m.wait_recv()
    node = lax.broadcasted_iota(jnp.int32, (nodes, BLK), 0)
    for q in range(parts):
        for o in range(1, parts):
            hit = node == lists_ref[q, o : o + 1, :]
            picks_ref[q, :, (o - 1) * BLK : o * BLK] = jnp.where(hit, 1.0, 0.0).astype(BF16)
        picks_t[q] = picks_ref[q].T
        step_relay(2)

    step_relay(len(relay))

    def back_owner(q):
        return (own_ref[q] + dot(part_t[q], picks_t[q])).astype(BF16)

    for q in range(parts):
        c1_ref[q] = back_owner(q)
    for p in range(parts):
        back_piece(c1_ref, p)
    for o in order + [0]:
        q = lax.rem(me + o, parts)
        c2 = back_owner(q)
        c2_ref[q] = c2
        grads = dot(maps[0], cf_ref[q]) + dot(maps[1], c1_ref[q]) + dot(maps[2], c2)
        ghs_ref[q] = grads.astype(BF16)
        go_home(2, o, ghs_ref, c, gh_ref)

    field_arrives(1, hid_round[0], hid_ref, hf_ref)
    mix = []
    for moved in (cf_ref, c1_ref, c2_ref):
        total = dot_t1(hf_ref[0], moved[0])
        for q in range(1, parts):
            total = total + dot_t1(hf_ref[q], moved[q])
        mix.append(total[:c, :c] + total[c:, c:])

    def reducer(g, pack, got, half, got_all, full, sums):
        def over_core(stage, src, dst):
            return [remote(src, dst, bsem.at[2 * g + stage], brsem.at[2 * g + stage], rep=crep)]

        def over_chips(stage, src_of, dst):
            made = []
            for o in range(1, chips):
                peer = lax.rem(chip + o, chips)
                made.append(remote(src_of(peer), dst, asem.at[2 * g + stage, o], arsem.at[2 * g + stage, o],
                                   dom=peer // 2, rep=lax.rem(peer, 2) * 2 + core))
            return made

        steps = (lambda: over_core(0, pack.at[1 - core], got),
                 lambda: over_chips(0, lambda peer: half.at[peer], got_all.at[chip]),
                 lambda: over_chips(1, lambda peer: full, sums.at[core, chip]),
                 lambda: over_core(1, sums.at[core], sums.at[core]))

        def start(i):
            for m in steps[i]():
                m.start()

        def arrive(i):
            for m in steps[i]():
                m.wait_recv()

        def first():
            start(0)

        def second():
            arrive(0)
            total = pack[core] + got[...]
            share = half.shape[1]
            for q in range(chips):
                half[q] = total[q * share : (q + 1) * share]
            start(1)
            got_all[chip] = half[chip]

        def third():
            arrive(1)
            total = got_all[0]
            for q in range(1, chips):
                total = total + got_all[q]
            full[...] = total * (1.0 / scale)
            start(2)
            sums[core, chip] = full[...]

        def fourth():
            arrive(2)
            start(3)

        def last():
            arrive(3)

        def sent():
            for i in range(4):
                for m in steps[i]():
                    m.wait_send()

        return first, second, third, fourth, last, sent

    early = reducer(0, pack0, got0, half0, all0, full0, sums0)
    late = reducer(1, pack1, got1, half1, all1, full1, sums1)
    pack0[...] = jnp.zeros(pack0.shape, F32)
    for i in range(3):
        pack0[i // 2, (i % 2) * c : (i % 2 + 1) * c, 0:c] = mix[i]
    early[0]()

    def extend(f_ref):
        for q in range(parts):
            ext_ref[q, :, 0:nodes] = f_ref[q]
            halo = dot(f_ref[q], picks_ref[q]).astype(BF16)
            for o in range(1, parts):
                at = nodes + (o - 1) * BLK
                ext_ref[(q + o) % parts, :, at : at + BLK] = halo[:, (o - 1) * BLK : o * BLK]

    extend(hf_ref)
    for p in range(parts):
        f1_ref[p] = dot(ext_ref[p], adj_t[p]).astype(BF16)
    extend(f1_ref)
    for o in order + [0]:
        q = lax.rem(me + o, parts)
        second = dot(ext_ref[q], adj_t[q]).astype(BF16)
        mixed = dot(mapst[0], hf_ref[q]) + dot(mapst[1], f1_ref[q]) + dot(mapst[2], second)
        mxs_ref[q] = mixed.astype(BF16)
        go_home(3, o, mxs_ref, 0, mx_ref)
    early[1]()

    home_arrives(2, ghs_ref, c, gh_ref)

    def conv_back(sig_ref, d_ref, up_of, band, low_of, first_pair, dilation, out):
        total, carry = None, None
        b = band[...]
        for k in range(first_pair, pairs):
            up = up_of(k)
            both = earlier_t(sig_ref, k)
            d = jnp.concatenate([up * d_ref[k, 0:128, :], up * d_ref[k, 128:256, :]], axis=0)
            d = d.astype(BF16)
            part = dot_t1(both, d)
            total = part if total is None else total + part
            back = dot(b, d)
            if k > 0:
                low_of(k - 1, back[:128] if carry is None else carry + back[:128])
            carry = back[128:]
        low_of(pairs - 1, carry)
        band_grad(total, dilation, out)

    def set_mid(k, low):
        mid_ref[pair(k), :] = low.astype(BF16)

    def set_grad(k, low):
        if k == 1:
            low = low + jnp.concatenate([jnp.zeros((c, nodes), F32), cot_ref[0:c, :].astype(F32)], axis=0)
        elif k > 1:
            low = low + cot_ref[(2 * k - 3) * c : (2 * k - 1) * c, :].astype(F32)
        low_ref[pair(k), :] = low.astype(BF16)

    conv_back(first_ref, d2_ref, lambda k: gh_ref[pair(k - 1), :].astype(F32), band2, set_mid, 1, 2, g2_ref)
    conv_back(xt_ref, d1_ref, lambda k: mid_ref[pair(k), :].astype(F32), band1, set_grad, 0, 1, g1_ref)

    for tap in range(2):
        pack1[0, tap * c : (tap + 1) * c, :] = g1_ref[tap]
        pack1[1, tap * c : (tap + 1) * c, :] = g2_ref[tap]
    late[0]()
    late[1]()
    for k in range(pairs):
        grad_ref[:, pair(k)] = low_ref[pair(k), :].T
    early[2]()
    home_arrives(3, mxs_ref, 0, mx_ref)
    kept = out_ref.shape[0]
    out_ref[...] = (mx_ref[...].astype(F32) + xt_ref[pairs * 128 - kept :, :].astype(F32)).astype(BF16)
    late[2]()
    early[3]()

    for m in cot_round[0] + hid_round[0] + lists:
        m.wait_send()
    pl.when(me != holder)(cot_round[1].wait_send)
    pl.when(me != holder)(hid_round[1].wait_send)
    home_sent(2, ghs_ref, c, gh_ref)
    home_sent(3, mxs_ref, 0, mx_ref)
    for t in range(zs):
        for w in ways(t):
            @pl.when(valid(t, w))
            def _():
                for sub in range(3):
                    go(lane_sends(t, w, sub) + side_sends(t, w, sub, base, 3)
                       + side_sends(t, w, sub, cross, 5) + core_sends(t, w, sub, base, 7)
                       + core_sends(t, w, sub, cross, 8), wait=True)
    late[3]()
    early[4]()
    share = sums0.shape[2]
    for q in range(chips):
        tap, at = divmod(q * share, c)
        mix_out[tap, at : at + share, :] = sums0[0, q, :, 0:c]
        if tap == 0:
            mix_out[2, at : at + share, :] = sums0[1, q, :, 0:c]
    early[5]()
    late[4]()
    for q in range(chips):
        tap, at = divmod(q * share, c)
        one_out[tap, at : at + share, :] = sums1[0, q]
        two_out[tap, at : at + share, :] = sums1[1, q]
    late[5]()


def finish_body(*refs):
    half = len(refs) // 2
    for a, b in zip(refs[:half], refs[half:]):
        b[...] = a[...]


def step_shards(inputs, cotangent, conv_one, conv_two, mix_weight, send_rows, counts, tile_cols,
                tile_vals):
    windows, nodes, flat = inputs.shape
    channels = mix_weight.shape[1]
    parts = lax.axis_size("dom")
    reps = lax.axis_size("rep")
    kept = flat // channels - 3
    c = channels
    pairs = flat // 128
    halo = (parts - 1) * BLK
    ext = nodes + halo
    scaling = math.sqrt(float(windows * reps * nodes * parts * kept))
    results = [((kept * c, nodes), BF16), ((nodes, flat), BF16), (conv_one.shape, F32),
               (conv_two.shape, F32), (mix_weight.shape, F32)]
    field = (parts, 2 * c, nodes)
    wide = flat - 2 * c
    scratch = [((nodes, BLK + halo), BF16), ((parts, BLK), jnp.int32),
               ((flat, nodes), BF16), ((flat, nodes), BF16), ((wide, nodes), BF16),
               ((pairs, 256, nodes), F32), ((pairs, 256, nodes), F32), ((flat, nodes), BF16),
               ((flat, nodes), BF16)]
    scratch += [((256, 256), BF16)] * 4 + [((3, 128, 128), BF16)] * 2
    scratch += [((parts, nodes, BLK + halo), BF16), ((parts, nodes, nodes), BF16),
                ((parts, ext, nodes), BF16), ((parts, parts, BLK), jnp.int32),
                ((parts, nodes, halo), BF16), ((parts, halo, nodes), BF16)]
    scratch += [(field, BF16)] * 5 + [(field, F32), ((parts, 2 * c, halo), BF16),
                                      ((parts, 2 * c, ext), BF16)]
    scratch += [((wide, nodes), BF16), ((kept * c, nodes), BF16), (field, BF16), (field, BF16)]
    scratch += [(conv_one.shape, F32), (conv_two.shape, F32)]
    chips = parts * reps // 2
    share = 2 * c // chips
    for _ in range(2):
        scratch += [((2, 2 * c, BLK), F32), ((2 * c, BLK), F32), ((chips, share, BLK), F32),
                    ((chips, share, BLK), F32), ((share, BLK), F32), ((2, chips, share, BLK), F32)]
    dma = pltpu.SemaphoreType.DMA
    sems = [(parts,), (parts,), (4, parts), (4, parts), (4, parts), (4, parts),
            (9, 3 * parts), (9, 3 * parts), (4, chips), (4, chips), (4,), (4,)]
    made = pl.pallas_call(
        functools.partial(steps_body, parts, reps, scaling),
        out_shape=[jax.ShapeDtypeStruct(s, d) for s, d in results],
        in_specs=[VM] * 6 + [SM, SM, VM],
        out_specs=[VM] * 5,
        scratch_shapes=[pltpu.VMEM(s, d) for s, d in scratch] + [dma(s) for s in sems],
        compiler_params=pltpu.CompilerParams(
            vmem_limit_bytes=60 * 1024 * 1024, collective_id=1, has_side_effects=True),
        name="steps",
    )(inputs[0], cotangent[0].T, conv_one, conv_two, mix_weight, send_rows[0], counts, tile_cols,
      tile_vals)
    output, grad_input, one, two, mix = pl.pallas_call(
        finish_body,
        out_shape=[jax.ShapeDtypeStruct(s, d) for s, d in results],
        in_specs=[VM] * 5,
        out_specs=[VM] * 5,
        compiler_params=LIMIT,
        name="finish",
    )(*made)
    return output.T[None], grad_input[None], one, two, mix


def solution(mesh):
    placed = (
        P("rep", "dom", None),
        P("rep", "dom", None),
        P(),
        P(),
        P(),
        P("dom", None, None),
        P("dom", None),
        P("dom", None),
        P("dom", None, None, None),
    )
    parts, reps = mesh.shape["dom"], mesh.shape["rep"]

    def layer(*args):
        kept = args[0].shape[2] // args[4].shape[1] - 3
        by_step = parts % 2 == 0 and reps == 4 and parts == kept - 1
        return step_shards(*args) if by_step else shards(*args)

    return jax.shard_map(
        layer,
        mesh=mesh,
        in_specs=placed,
        out_specs=(P("rep", "dom", None), P("rep", "dom", None), P(), P(), P()),
        check_vma=False,
    )
```
